32 devices in a mesh: ctx: 16 (over z, y, core), fsdp: 2 (over x).
Axes of the slice: x: 2, y: 2, z: 4, core: 2. Of those that a mesh axis runs over, the one named last changes fastest.
Arguments:
- tokens: bfloat16 [2, 2048, 1024], P('fsdp', 'ctx'), may hold values from -6 to 6
- w_qkv: bfloat16 [1024, 3072], P('fsdp'), may hold values from -0.1875 to 0.1875
- w_out: bfloat16 [1024, 1024], P('fsdp'), may hold values from -0.375 to 0.375
- w_up: bfloat16 [1024, 4096], P('fsdp'), may hold values from -0.1875 to 0.1875
- w_down: bfloat16 [4096, 1024], P('fsdp'), may hold values from -0.09375 to 0.09375
- w_time: bfloat16 [256, 2048], P('fsdp'), may hold values from -0.375 to 0.375
- gain_one: bfloat16 [1024], P('fsdp'), may hold values from 0.5 to 1.5
- bias_one: bfloat16 [1024], P('fsdp'), may hold values from -3 to 3
- gain_two: bfloat16 [1024], P('fsdp'), may hold values from 0.5 to 1.5
- bias_two: bfloat16 [1024], P('fsdp'), may hold values from -3 to 3
- bias_up: bfloat16 [4096], P('fsdp'), may hold values from -3 to 3
- bias_down: bfloat16 [1024], P('fsdp'), may hold values from -3 to 3
- lengths: int32 [2, 1], P('fsdp'), may hold values from 1024 to 2048, as said below
- time_steps: int32 [2, 1], P('fsdp'), may hold values from 0 to 999
- cotangent: bfloat16 [2, 2048, 1024], P('fsdp', 'ctx'), may hold values from -6 to 6
Outputs:
- output: bfloat16 [2, 2048, 1024], P('fsdp', 'ctx')
- grad_tokens: bfloat16 [2, 2048, 1024], P('fsdp', 'ctx')
- grad_qkv: float32 [1024, 3072], P('fsdp')
- grad_out: float32 [1024, 1024], P('fsdp')
- grad_up: float32 [1024, 4096], P('fsdp')
- grad_down: float32 [4096, 1024], P('fsdp')
- grad_time: float32 [256, 2048], P('fsdp')
- grad_gain_one: float32 [1024], P('fsdp')
- grad_bias_one: float32 [1024], P('fsdp')
- grad_gain_two: float32 [1024], P('fsdp')
- grad_bias_two: float32 [1024], P('fsdp')
- grad_bias_up: float32 [4096], P('fsdp')
- grad_bias_down: float32 [1024], P('fsdp')
The draws below stay inside these ranges and needn't reach their ends.
Inputs may be any that keep to these rules, and one draw needn't show every extreme that they name: The 1 lengths of a group add up to at most 2048; the group's tokens after them are padding; in every group some sequence has the largest length.
All inputs are finite; a program needn't handle non-finite values.
Results may differ from the reference program's by a relative error of at most 0.025.
Values may be sent and summed in bfloat16 or wider, within the bound.
No kernel may reach another device: no remote copies, remote signals or barrier semaphores. Data moves between devices by JAX's collectives and lax.ppermute only.
A program may use at most 256 MiB of HBM per device.

```python
import math
import jax
import jax.numpy as jnp
from jax import lax

D = 1024
HEADS = 16
FF = 4096
TE = 256
STEPS = 1000
CTX_TOKENS = 2048
GROUPS = 2
SEQS = 1


def draw_lengths(key, part):
    key_lengths, key_chosen = jax.random.split(key)
    shortest = CTX_TOKENS // (2 * SEQS)
    longest = CTX_TOKENS // SEQS
    drawn = jax.random.randint(key_lengths, (GROUPS, SEQS), shortest, longest + 1)
    chosen = jax.random.randint(key_chosen, (GROUPS, 1), 0, SEQS)
    marked = jnp.arange(SEQS)[None, :] == chosen
    return jnp.where(marked, longest, drawn).astype(jnp.int32)


def shard_levels(own_key, shape, shards, smallest, top_value):
    level = 1.0
    for axis_at, blocks in shards:
        heights = jax.random.uniform(jax.random.fold_in(jax.random.fold_in(own_key, 6), axis_at), (blocks,), jnp.float32, smallest / len(shards), top_value / len(shards))
        level = level * jnp.repeat(jnp.exp(heights), shape[axis_at] // blocks).reshape((-1,) + (1,) * (len(shape) - 1 - axis_at))
    return level


def normal_values(key, dims, scale, most, cuts=(), kind=jnp.bfloat16):
    array = jax.random.normal(key, dims, jnp.float32) * scale
    if len(cuts) > 0:
        array = shard_levels(key, dims, cuts, -0.22, 0.18) * array
    return jnp.clip(array, min=-most, max=most).astype(kind)


def setup_inputs(seed: int = 0) -> dict:
    streams_of = jax.random.split(jax.random.key(seed), 16)
    return {
        "tokens": normal_values(streams_of[0], (GROUPS, CTX_TOKENS, D), 1.0, 6.0, ((0, 2), (1, 16))),
        "w_qkv": normal_values(streams_of[1], (D, 3 * D), D ** -0.5, 0.1875, ((0, 2),)),
        "w_out": normal_values(streams_of[2], (D, D), (D // 4) ** -0.5, 0.375, ((0, 2),)),
        "w_up": normal_values(streams_of[3], (D, FF), D ** -0.5, 0.1875, ((0, 2),)),
        "w_down": normal_values(streams_of[4], (FF, D), FF ** -0.5, 0.09375, ((0, 2),)),
        "w_time": normal_values(streams_of[5], (TE, 2 * D), TE ** -0.5, 0.375, ((0, 2),)),
        "gain_one": jnp.clip(1.0 + 0.1 * jax.random.normal(streams_of[6], (D,), jnp.float32), 0.5, 1.5).astype(jnp.bfloat16),
        "bias_one": normal_values(streams_of[7], (D,), 0.5, 3.0, ((0, 2),)),
        "gain_two": jnp.clip(1.0 + 0.1 * jax.random.normal(streams_of[8], (D,), jnp.float32), 0.5, 1.5).astype(jnp.bfloat16),
        "bias_two": normal_values(streams_of[9], (D,), 0.5, 3.0, ((0, 2),)),
        "bias_up": normal_values(streams_of[10], (FF,), 0.5, 3.0, ((0, 2),)),
        "bias_down": normal_values(streams_of[11], (D,), 0.5, 3.0, ((0, 2),)),
        "lengths": draw_lengths(jax.random.fold_in(streams_of[15], 71), 0),
        "time_steps": jax.random.randint(streams_of[13], (GROUPS, SEQS), 0, STEPS).astype(jnp.int32),
        "cotangent": normal_values(streams_of[14], (GROUPS, CTX_TOKENS, D), 1.0, 6.0, ((0, 2), (1, 16))),
    }


@jax.custom_vjp
def low(v):
    return lax.optimization_barrier(v.astype(jnp.bfloat16)).astype(jnp.float32)

@jax.custom_vjp
def low_back(v):
    return v

def low_keep(v):
    return (low(v), None)

def low_pass(kept, grad):
    return (grad,)

def back_keep(v):
    return (v, None)

def back_low(kept, grad):
    return (low(grad),)
low.defvjp(low_keep, low_pass)
low_back.defvjp(back_keep, back_low)
HIGH = lax.Precision.HIGHEST
EPSILON = 1e-05
NEGATIVE = -1e+30

def layout(seq_lengths, offsets):
    ends = jnp.cumsum(seq_lengths).astype(jnp.int32)
    starts = jnp.concatenate([jnp.zeros((1,), jnp.int32), ends]).astype(jnp.int32)
    segment = lax.optimization_barrier(jnp.sum((offsets[:, None] >= ends[None, :]).astype(jnp.int32), axis=1)).astype(jnp.int32)
    onehot = segment[:, None] == jnp.arange(seq_lengths.shape[0] + 1, dtype=jnp.int32)[None, :]
    begin = lax.optimization_barrier(jnp.sum(jnp.where(onehot, starts[None, :], 0), axis=1)).astype(jnp.int32)
    return (segment, onehot, (offsets - begin).astype(jnp.int32))

def embed(steps_given, embed_width):
    half_width = embed_width // 2
    freq = jnp.exp(-math.log(10000.0) * jnp.arange(half_width, dtype=jnp.float32) / half_width)
    angle = steps_given.astype(jnp.float32)[..., None] * freq
    return jnp.concatenate([jnp.sin(angle), jnp.cos(angle)], axis=-1)

def rotary(values, position, heads):
    width = values.shape[-1]
    half_width = width // heads // 2
    inverse = jnp.exp(-math.log(10000.0) * jnp.arange(half_width, dtype=jnp.float32) / half_width)
    angle = position.astype(jnp.float32)[..., None] * inverse
    cosine = jnp.cos(angle)[..., None, :]
    sine = jnp.sin(angle)[..., None, :]
    split = values.reshape(values.shape[:-1] + (heads, 2, half_width))
    upper = split[..., 0, :]
    lower = split[..., 1, :]
    turned = jnp.stack([upper * cosine - lower * sine, lower * cosine + upper * sine], axis=-2)
    return turned.reshape(values.shape)

def normalize(values):
    centre = lax.optimization_barrier(jnp.mean(values, axis=-1, keepdims=True))
    centered = values - centre
    spread = lax.optimization_barrier(jnp.mean(centered * centered, axis=-1, keepdims=True))
    return centered * lax.rsqrt(spread + EPSILON)

def attend_group(query, key, value, segment):
    count = query.shape[0]
    block = min(512, count)
    head_size = query.shape[1] // HEADS
    scale = float(head_size) ** (-0.5)
    query_blocks = query.reshape(count // block, block, HEADS, head_size)
    segment_blocks = segment.reshape(count // block, block)
    key_heads = key.reshape(count, HEADS, head_size)
    value_heads = value.reshape(count, HEADS, head_size)

    @jax.checkpoint
    def one_block(item):
        query_block, segment_block = item
        score = jnp.einsum('qhd,khd->hqk', query_block, key_heads, precision=HIGH) * scale
        score = low_back(score)
        matches = (segment_block[:, None] == segment[None, :])[None]
        score = jnp.where(matches, score, NEGATIVE)
        prob = jax.nn.softmax(score, axis=-1)
        result = jnp.einsum('hqk,khd->qhd', low(prob), value_heads, precision=HIGH)
        return result.reshape(block, HEADS * head_size)
    return lax.map(one_block, (query_blocks, segment_blocks)).reshape(count, HEADS * head_size)

def forward(inputs, w_qkv, w_out, w_up, w_down, w_time, gain_one, bias_one, gain_two, bias_two, bias_up, bias_down, segment, onehot, position, live, temb):
    width = inputs.shape[-1]
    film = jnp.einsum('gst,tc->gsc', low(temb), w_time, precision=HIGH)
    film = jnp.concatenate([film, jnp.zeros((film.shape[0], 1, film.shape[2]), jnp.float32)], axis=1)
    film_tok = jnp.einsum('gns,gsc->gnc', onehot, film, precision=HIGH)
    norm_one = normalize(inputs) * (gain_one + film_tok[..., :width]) + (bias_one + film_tok[..., width:])
    mixed = low_back(jnp.einsum('gnd,de->gne', low(norm_one), w_qkv, precision=HIGH))
    query = low(rotary(mixed[..., :width], position, HEADS))
    key = low(rotary(mixed[..., width:2 * width], position, HEADS))
    value = low(mixed[..., 2 * width:])
    attended = lax.map(lambda item: attend_group(item[0], item[1], item[2], item[3]), (query, key, value, segment))
    attended = low(low_back(attended))
    resid = inputs + low_back(jnp.einsum('gnd,de->gne', attended, w_out, precision=HIGH))
    norm_two = normalize(resid) * gain_two + bias_two
    pre = low_back(jnp.einsum('gnd,df->gnf', low(norm_two), w_up, precision=HIGH)) + bias_up
    act = jax.nn.gelu(pre, approximate=False)
    branch = low_back(jnp.einsum('gnf,fd->gnd', low(act), w_down, precision=HIGH)) + bias_down
    return live[..., None] * (resid + branch)

def reference(tokens, w_qkv, w_out, w_up, w_down, w_time, gain_one, bias_one, gain_two, bias_two, bias_up, bias_down, lengths, time_steps, cotangent):
    count = tokens.shape[1]
    offsets = jnp.arange(count, dtype=jnp.int32)
    segment, onehot, position = jax.vmap(lambda seq_lengths: layout(seq_lengths, offsets))(lengths)
    live = (segment < SEQS).astype(jnp.float32)
    temb = embed(time_steps, TE)
    weights = (w_qkv.astype(jnp.float32), w_out.astype(jnp.float32), w_up.astype(jnp.float32), w_down.astype(jnp.float32), w_time.astype(jnp.float32), gain_one.astype(jnp.float32), bias_one.astype(jnp.float32), gain_two.astype(jnp.float32), bias_two.astype(jnp.float32), bias_up.astype(jnp.float32), bias_down.astype(jnp.float32))
    onehot_float = onehot.astype(jnp.float32)

    def run(inputs, p_qkv, p_out, p_up, p_down, p_time, p_gone, p_bone, p_gtwo, p_btwo, p_bup, p_bdown):
        return forward(inputs, p_qkv, p_out, p_up, p_down, p_time, p_gone, p_bone, p_gtwo, p_btwo, p_bup, p_bdown, segment, onehot_float, position, live, temb)
    output, pull = jax.vjp(run, tokens.astype(jnp.float32), *weights)
    grads = pull(cotangent.astype(jnp.float32))
    return (output.astype(jnp.bfloat16), grads[0].astype(jnp.bfloat16), grads[1], grads[2], grads[3], grads[4], grads[5], grads[6], grads[7], grads[8], grads[9], grads[10], grads[11])
```

```python
import functools
import math

import jax
import jax.numpy as jnp
from jax import lax
from jax.experimental import pallas as pl
from jax.experimental.pallas import tpu as pltpu
from jax.sharding import PartitionSpec as P

HEADS = 16
EPSILON = 1e-05
NEGATIVE = -1e30
HIGH = lax.Precision.HIGHEST
F32 = jnp.float32
BF16 = jnp.bfloat16
VMEM_BYTES = 56 << 20


def dims(left, right, left_dim, right_dim):
    return lax.dot_general(
        left, right, (((left_dim,), (right_dim,)), ((), ())), preferred_element_type=F32
    )


def segments(ends, index):
    return sum((index >= end).astype(jnp.int32) for end in ends)


def positions(ends, index, segment):
    begin = jnp.zeros_like(index)
    for at, end in enumerate(ends):
        begin = jnp.where(segment > at, end, begin)
    return index - begin


def embed(steps_given, embed_width):
    half_width = embed_width // 2
    freq = jnp.exp(-math.log(10000.0) * jnp.arange(half_width, dtype=F32) / half_width)
    angle = steps_given.astype(F32)[..., None] * freq
    return jnp.concatenate([jnp.sin(angle), jnp.cos(angle)], axis=-1)


def stats(values):
    centre = jnp.mean(values, axis=-1, keepdims=True)
    centered = values - centre
    spread = jnp.mean(centered * centered, axis=-1, keepdims=True)
    scale = lax.rsqrt(spread + EPSILON)
    return centered * scale, scale


def stats_back(grad, normal, scale):
    return (
        grad
        - jnp.mean(grad, axis=-1, keepdims=True)
        - normal * jnp.mean(grad * normal, axis=-1, keepdims=True)
    ) * scale


def gelu_parts(pre):
    below = 0.5 * (1.0 + lax.erf(pre * math.sqrt(0.5)))
    density = jnp.exp(-0.5 * pre * pre) * (1.0 / math.sqrt(2.0 * math.pi))
    return pre * below, below + pre * density


def qkv_kernel(
    rows, head_size, ends_ref, base_ref, tokens_ref, gains_ref, shifts_ref, w_ref,
    cos_ref, sin_ref, norm_ref, query_t_ref, key_ref, key_t_ref, value_t_ref, pair_ref,
):
    step = pl.program_id(0)
    block = tokens_ref.shape[0]
    seq_count = ends_ref.shape[0]
    half = head_size // 2
    values = tokens_ref[...].astype(F32)
    normal, _ = stats(values)
    chunks = block // rows

    def token_index(shape, axis):
        within = lax.broadcasted_iota(jnp.int32, shape, axis)
        index = within + base_ref[step * chunks]
        for at in range(1, chunks):
            index = jnp.where(
                within >= at * rows,
                within - at * rows + base_ref[step * chunks + at],
                index,
            )
        return index

    ends = [ends_ref[s] for s in range(seq_count)]
    seg_col = segments(ends, token_index((block, 1), 0))
    seg_row = segments(ends, token_index((1, block), 1))
    gains = gains_ref[0:1, :]
    shifts = shifts_ref[0:1, :]
    for s in range(1, seq_count + 1):
        gains = jnp.where(seg_col == s, gains_ref[s : s + 1, :], gains)
        shifts = jnp.where(seg_col == s, shifts_ref[s : s + 1, :], shifts)
    norm = (normal * gains + shifts).astype(BF16)
    norm_ref[...] = norm
    mixed = jnp.dot(norm, w_ref[...], preferred_element_type=F32)
    turned = mixed.T
    cos = cos_ref[...]
    sin = sin_ref[...]

    def turn(at):
        upper = turned[at : at + half]
        lower = turned[at + half : at + head_size]
        return jnp.concatenate(
            [upper * cos - lower * sin, lower * cos + upper * sin], axis=0
        ).astype(BF16)

    query = turn(0).astype(F32) * (float(head_size) ** -0.5)
    key = turn(head_size).astype(F32)
    value = turned[2 * head_size : 3 * head_size].astype(BF16).astype(F32)
    spare = 128 - head_size
    row_id = lax.broadcasted_iota(jnp.int32, (spare, block), 0)
    same = row_id == seg_row
    used = row_id <= seq_count
    key_tail = jnp.where(same & used, 1.0, 0.0)
    query_tail = jnp.where(used & jnp.logical_not(same), NEGATIVE, 0.0)
    query_t_ref[...] = jnp.concatenate([query, query_tail], axis=0).astype(BF16)
    key_t_ref[...] = key.astype(BF16)
    value_t_ref[...] = value.astype(BF16)
    key_ref[...] = jnp.concatenate([key, key_tail], axis=0).T.astype(BF16)
    pair_ref[...] = jnp.concatenate([value, query], axis=0).T.astype(BF16)


def attend_kernel(chunk, rows, query_ref, key_ref, value_ref, out_ref, sent_ref, lse_ref, score_ref):
    count = key_ref.shape[0]
    query = query_ref[...]
    top = None
    for at in range(0, count, chunk):
        score = jnp.dot(key_ref[at : at + chunk, :], query, preferred_element_type=F32)
        score_ref[at : at + chunk, :] = score
        high = jnp.max(score, axis=0, keepdims=True)
        top = high if top is None else jnp.maximum(top, high)
    total = jnp.zeros_like(top)
    out = jnp.zeros(out_ref.shape, F32)
    for at in range(0, count, chunk):
        weight = jnp.exp(score_ref[at : at + chunk, :] - top)
        total = total + jnp.sum(weight, axis=0, keepdims=True)
        out = out + jnp.dot(
            value_ref[:, at : at + chunk],
            weight.astype(BF16),
            preferred_element_type=F32,
        )
    out = out / total
    out_ref[...] = out
    for at in range(sent_ref.shape[0]):
        sent_ref[at] = out[:, at * rows : (at + 1) * rows].astype(BF16)
    lse_ref[...] = top + jnp.log(total)


def attend_back_kernel(
    chunk, rows, head_size, query_ref, grad_ref, out_ref, lse_ref, key_ref, key_t_ref, pair_ref,
    pair_block_ref, cos_block_ref, sin_block_ref, cos_ref, sin_ref, mixed_ref, key_acc, value_acc,
):
    step = pl.program_id(0)
    count = key_ref.shape[0]
    block = query_ref.shape[1]
    half = head_size // 2
    scale = float(head_size) ** -0.5

    @pl.when(step == 0)
    def _():
        key_acc[...] = jnp.zeros_like(key_acc)
        value_acc[...] = jnp.zeros_like(value_acc)

    query = query_ref[...]
    grad = jnp.concatenate(
        [grad_ref[at] for at in range(grad_ref.shape[0])], axis=1
    ).astype(F32)
    delta = jnp.sum(grad * out_ref[...], axis=0, keepdims=True)
    lse = lse_ref[...]
    grad_t = jnp.concatenate(
        [grad, jnp.zeros((128 - head_size, block), F32)], axis=0
    )
    grad_rows = grad_t.T.astype(BF16)
    grad_t = grad_t.astype(BF16)
    pair = pair_block_ref[...]
    grad_query = jnp.zeros((head_size, block), F32)
    for at in range(0, count, chunk):
        part = slice(at, at + chunk)
        score = jnp.dot(key_ref[part, :], query, preferred_element_type=F32)
        prob = jnp.exp(score - lse)
        grad_prob = jnp.dot(pair_ref[part, :], grad_t, preferred_element_type=F32)
        grad_score = (prob * (grad_prob - delta)).astype(BF16)
        grad_query = grad_query + jnp.dot(
            key_t_ref[:, part], grad_score, preferred_element_type=F32
        )
        key_acc[part, :] += jnp.dot(grad_score, pair, preferred_element_type=F32)
        value_acc[part, :] += jnp.dot(
            prob.astype(BF16), grad_rows, preferred_element_type=F32
        )

    def turn_back(values, cos, sin):
        upper = values[:half]
        lower = values[half:]
        return jnp.concatenate(
            [upper * cos + lower * sin, lower * cos - upper * sin], axis=0
        ).astype(BF16)

    at = pl.multiple_of(step * block, block)
    mixed_ref[0:head_size, pl.ds(at, block)] = turn_back(
        grad_query * scale, cos_block_ref[...], sin_block_ref[...]
    )

    @pl.when(step == pl.num_programs(0) - 1)
    def _():
        mixed_ref[head_size : 2 * head_size, :] = turn_back(
            key_acc[...].T[head_size : 2 * head_size], cos_ref[...], sin_ref[...]
        )
        mixed_ref[2 * head_size : 3 * head_size, :] = value_acc[...].T[
            :head_size
        ].astype(BF16)


def whole(shape):
    return pl.BlockSpec(shape, lambda i, *_: (0,) * len(shape))


def project(tokens, base, ends, gains, shifts, w_head, cos, sin, rows, head_size):
    count, width = tokens.shape
    block = min(count, 2 * rows)
    grid_spec = pltpu.PrefetchScalarGridSpec(
        num_scalar_prefetch=2,
        grid=(count // block,),
        in_specs=[
            pl.BlockSpec((block, width), lambda i, *_: (i, 0)),
            whole(gains.shape),
            whole(shifts.shape),
            whole(w_head.shape),
            pl.BlockSpec((head_size // 2, block), lambda i, *_: (0, i)),
            pl.BlockSpec((head_size // 2, block), lambda i, *_: (0, i)),
        ],
        out_specs=[
            pl.BlockSpec((block, width), lambda i, *_: (i, 0)),
            pl.BlockSpec((128, block), lambda i, *_: (0, i)),
            pl.BlockSpec((block, 128), lambda i, *_: (i, 0)),
            pl.BlockSpec((head_size, block), lambda i, *_: (0, i)),
            pl.BlockSpec((head_size, block), lambda i, *_: (0, i)),
            pl.BlockSpec((block, 128), lambda i, *_: (i, 0)),
        ],
    )
    return pl.pallas_call(
        functools.partial(qkv_kernel, rows, head_size),
        grid_spec=grid_spec,
        out_shape=[
            jax.ShapeDtypeStruct((count, width), BF16),
            jax.ShapeDtypeStruct((128, count), BF16),
            jax.ShapeDtypeStruct((count, 128), BF16),
            jax.ShapeDtypeStruct((head_size, count), BF16),
            jax.ShapeDtypeStruct((head_size, count), BF16),
            jax.ShapeDtypeStruct((count, 128), BF16),
        ],
        compiler_params=pltpu.CompilerParams(vmem_limit_bytes=VMEM_BYTES),
        cost_estimate=pl.CostEstimate(
            flops=2 * count * width * 256,
            bytes_accessed=4 * count * width,
            transcendentals=0,
        ),
        name="project_head",
    )(ends, base, tokens, gains, shifts, w_head, cos, sin)


def attend(query_t, key, value_t, rows):
    count = key.shape[0]
    head_size = value_t.shape[0]
    block = min(count, 2 * rows)
    chunk = min(count, 512)
    return pl.pallas_call(
        functools.partial(attend_kernel, chunk, rows),
        grid=(count // block,),
        in_specs=[
            pl.BlockSpec((128, block), lambda i: (0, i)),
            whole((count, 128)),
            whole((head_size, count)),
        ],
        out_specs=[
            pl.BlockSpec((head_size, block), lambda i: (0, i)),
            pl.BlockSpec((block // rows, head_size, rows), lambda i: (i, 0, 0)),
            pl.BlockSpec((1, block), lambda i: (0, i)),
        ],
        out_shape=[
            jax.ShapeDtypeStruct((head_size, count), F32),
            jax.ShapeDtypeStruct((count // rows, head_size, rows), BF16),
            jax.ShapeDtypeStruct((1, count), F32),
        ],
        scratch_shapes=[pltpu.VMEM((count, block), F32)],
        compiler_params=pltpu.CompilerParams(vmem_limit_bytes=VMEM_BYTES),
        cost_estimate=pl.CostEstimate(
            flops=8 * count * count * 128,
            bytes_accessed=8 * count * 128,
            transcendentals=count * count,
        ),
        name="attend_head",
    )(query_t, key, value_t)


def attend_back(query_t, grad, out, lse, key, key_t, pair, cos, sin, rows):
    count = key.shape[0]
    head_size = key_t.shape[0]
    half = head_size // 2
    block = min(count, 2 * rows)
    chunk = min(count, 512)
    return pl.pallas_call(
        functools.partial(attend_back_kernel, chunk, rows, head_size),
        grid=(count // block,),
        in_specs=[
            pl.BlockSpec((128, block), lambda i: (0, i)),
            pl.BlockSpec((block // rows, head_size, rows), lambda i: (i, 0, 0)),
            pl.BlockSpec((head_size, block), lambda i: (0, i)),
            pl.BlockSpec((1, block), lambda i: (0, i)),
            whole((count, 128)),
            whole((head_size, count)),
            whole((count, 128)),
            pl.BlockSpec((block, 128), lambda i: (i, 0)),
            pl.BlockSpec((half, block), lambda i: (0, i)),
            pl.BlockSpec((half, block), lambda i: (0, i)),
            whole((half, count)),
            whole((half, count)),
        ],
        out_specs=whole((3 * head_size, count)),
        out_shape=jax.ShapeDtypeStruct((3 * head_size, count), BF16),
        scratch_shapes=[pltpu.VMEM((count, 128), F32), pltpu.VMEM((count, 128), F32)],
        compiler_params=pltpu.CompilerParams(vmem_limit_bytes=VMEM_BYTES),
        cost_estimate=pl.CostEstimate(
            flops=20 * count * count * 128,
            bytes_accessed=16 * count * 128,
            transcendentals=count * count,
        ),
        name="attend_head_back",
    )(query_t, grad, out, lse, key, key_t, pair, pair, cos, sin, cos, sin)


def times_rows(values, pieces):
    return sum(
        jnp.dot(
            lax.dynamic_slice_in_dim(values, at, piece.shape[0], 1),
            piece,
            preferred_element_type=F32,
        )
        for piece, at in pieces
    )


def times_rows_t(values_t, pieces):
    return sum(
        dims(lax.dynamic_slice_in_dim(values_t, at, piece.shape[0], 0), piece, 0, 0)
        for piece, at in pieces
    )


def joined(parts, pieces, dim):
    if len(parts) == 1:
        return parts[0]
    shape = list(parts[0].shape)
    shape[dim] = sum(part.shape[dim] for part in parts)
    out = jnp.zeros(shape, parts[0].dtype)
    for part, (_, at) in zip(parts, pieces):
        out = lax.dynamic_update_slice_in_dim(out, part, at, dim)
    return out


def rows_of(pieces, start, size):
    out = None
    for piece, at in pieces:
        length = piece.shape[0]
        local = jnp.clip(start - at, 0, length - size)
        found = lax.dynamic_slice_in_dim(piece, local, size, 0)
        inside = (start >= at) & (start < at + length)
        out = found if out is None else jnp.where(inside, found, out)
    return out


def body(
    ctx_size, fsdp_size,
    tokens, w_qkv, w_out, w_up, w_down, w_time, gain_one, bias_one, gain_two, bias_two, bias_up,
    bias_down, lengths, time_steps, cotangent,
):
    me = lax.axis_index("ctx")
    shard = lax.axis_index("fsdp")
    core = me % 2
    rows = tokens.shape[1]
    width = tokens.shape[2]
    count = rows * ctx_size
    head_size = width // HEADS
    repeats = ctx_size // HEADS
    columns = head_size // repeats
    seq_count = lengths.shape[1]
    hidden = w_up.shape[1]
    paired = fsdp_size == 2

    def across(values):
        return lax.ppermute(values, "fsdp", [(0, 1), (1, 0)])

    def core_swap(values):
        return lax.ppermute(values, "ctx", [(i, i ^ 1) for i in range(ctx_size)])

    def gather_small(values):
        if not paired:
            return lax.all_gather(values, "fsdp", axis=0, tiled=True)
        other = across(values)
        first = jnp.where(shard == 0, values, other)
        second = jnp.where(shard == 0, other, values)
        return jnp.concatenate([first, second], axis=0)

    def fetch(weight):
        if not paired:
            return [(lax.all_gather(weight, "fsdp", axis=0, tiled=True), 0)]
        size = weight.shape[0]
        half = size // 2
        mine = across(lax.dynamic_slice_in_dim(weight, core * half, half, 0))
        theirs = core_swap(mine)
        other = (1 - shard) * size
        return [
            (weight, shard * size),
            (mine, other + core * half),
            (theirs, other + (1 - core) * half),
        ]

    def scatter_sum(values, dim):
        if not paired:
            return lax.psum_scatter(
                values.astype(BF16), "fsdp", scatter_dimension=dim, tiled=True
            )
        half = values.shape[dim] // 2
        keep = lax.dynamic_slice_in_dim(values, shard * half, half, dim)
        send = lax.dynamic_slice_in_dim(values, (1 - shard) * half, half, dim)
        return (keep + across(send.astype(BF16)).astype(F32)).astype(BF16)

    def gather(values):
        return lax.all_gather(values, "ctx", axis=0, tiled=False)

    ends = []
    for s in range(seq_count):
        ends.append(lengths[0, s] + (ends[-1] if ends else 0))
    ends_vector = jnp.stack(ends)
    index = me * rows + jnp.arange(rows, dtype=jnp.int32)
    segment = segments(ends, index)
    live = (segment < seq_count).astype(F32)[:, None]
    all_index = jnp.arange(count, dtype=jnp.int32)
    all_position = positions(ends, all_index, segments(ends, all_index))
    half_width = head_size // 2
    inverse = jnp.exp(
        -math.log(10000.0) * jnp.arange(half_width, dtype=F32) / half_width
    )
    angle = inverse[:, None] * all_position.astype(F32)[None, :]
    cos = jnp.cos(angle)
    sin = jnp.sin(angle)

    all_tokens = gather(tokens[0]).reshape(count, width)
    inputs = tokens[0].astype(F32)
    grad_y = cotangent[0].astype(F32) * live
    grad_y_b = grad_y.astype(BF16)
    all_grad_y = gather(grad_y_b).reshape(count, width)

    small = [gain_one, bias_one, gain_two, bias_two, bias_down, bias_up]
    packed = gather_small(jnp.concatenate(small)[None, :])
    vectors = []
    at = 0
    for vector in small:
        size = vector.shape[0]
        vectors.append(packed[:, at : at + size].reshape(1, -1).astype(F32))
        at += size
    gain_first, bias_first, gain_second, bias_second, bias_output, bias_hidden = vectors

    all_steps = lax.all_gather(time_steps.astype(F32), "fsdp", axis=0, tiled=True)
    all_embedded = embed(all_steps, w_time.shape[0] * fsdp_size).astype(BF16)
    embedded = lax.dynamic_index_in_dim(all_embedded, shard, 0, keepdims=False)
    film = times_rows(embedded, fetch(w_time))
    film = jnp.concatenate([film, jnp.zeros((1, 2 * width), F32)], axis=0)
    gains = gain_first + film[:, :width]
    shifts = bias_first + film[:, width:]

    head = me // repeats
    w_head = jnp.concatenate(
        [
            lax.dynamic_slice_in_dim(w_qkv, k * width + head * head_size, head_size, 1)
            for k in range(3)
        ]
        + [jnp.zeros((w_qkv.shape[0], head_size), BF16)],
        axis=1,
    )
    w_head = gather_small(w_head)

    base = jnp.arange(ctx_size, dtype=jnp.int32) * rows
    all_norm, query_t, key, key_t, value_t, pair = project(
        all_tokens, base, ends_vector, gains, shifts, w_head, cos, sin, rows, head_size
    )
    out_t, sent, lse = attend(query_t, key, value_t, rows)

    part = (me % repeats) * columns
    if repeats > 1:
        sent = lax.dynamic_slice_in_dim(sent, part, columns, 1)
    attended_t = lax.all_to_all(sent, "ctx", 0, 0, tiled=True).reshape(width, rows)

    out_pieces = fetch(w_out)
    up_pieces = fetch(w_up)
    down_pieces = fetch(w_down)
    qkv_pieces = fetch(w_qkv)
    resid = inputs + times_rows_t(attended_t, out_pieces)
    normal_two, scale_two = stats(resid)
    norm_two_b = (normal_two * gain_second + bias_second).astype(BF16)
    all_norm_two = gather(norm_two_b).reshape(count, width)
    pre = times_rows(norm_two_b, up_pieces) + bias_hidden
    act, slope = gelu_parts(pre)
    branch = times_rows(act.astype(BF16), down_pieces) + bias_output
    output = (live * (resid + branch)).astype(BF16)
    grad_act = joined([dims(grad_y_b, p, 1, 1) for p, _ in down_pieces], down_pieces, 1)
    grad_pre = grad_act * slope
    grad_bias_up = jnp.sum(grad_pre, axis=0)
    grad_pre_b = grad_pre.astype(BF16)
    grad_norm_two = joined([dims(grad_pre_b, p, 1, 1) for p, _ in up_pieces], up_pieces, 1)
    grad_resid = grad_y + stats_back(grad_norm_two * gain_second, normal_two, scale_two)
    grad_resid_b = grad_resid.astype(BF16)
    grad_att_t = joined(
        [dims(p, grad_resid_b, 1, 1) for p, _ in out_pieces], out_pieces, 0
    ).astype(BF16)
    grad_att_t = grad_att_t.reshape(HEADS, head_size, rows)
    if repeats > 1:
        grad_att_t = jnp.repeat(grad_att_t, repeats, axis=0)
    grad_att = lax.all_to_all(grad_att_t, "ctx", 0, 0, tiled=True)

    mixed_t = attend_back(
        query_t, grad_att, out_t, lse, key, key_t, pair, cos, sin, rows
    )
    mixed_t = mixed_t.reshape(3, head_size, count)
    if repeats > 1:
        mixed_t = lax.dynamic_slice_in_dim(mixed_t, part, columns, 1)
    mixed_t = mixed_t.reshape(3 * columns, count)
    mixed_sent = mixed_t.reshape(3 * columns, ctx_size, rows).transpose(1, 0, 2)
    mixed_got = lax.all_to_all(mixed_sent, "ctx", 0, 0, tiled=True)
    grad_mixed_t = (
        mixed_got.reshape(ctx_size, 3, columns, rows)
        .transpose(1, 0, 2, 3)
        .reshape(3 * width, rows)
    )
    grad_norm_one = joined(
        [dims(grad_mixed_t, p, 0, 1) for p, _ in qkv_pieces], qkv_pieces, 1
    )
    normal_one, scale_one = stats(inputs)
    seg_col = segment[:, None]
    gain_tok = gains[0:1]
    for s in range(1, seq_count + 1):
        gain_tok = jnp.where(seg_col == s, gains[s : s + 1], gain_tok)
    grad_tokens = (
        grad_resid + stats_back(grad_norm_one * gain_tok, normal_one, scale_one)
    ).astype(BF16)
    film_terms = jnp.concatenate([grad_norm_one * normal_one, grad_norm_one], axis=1)
    film_sums = [
        jnp.sum(jnp.where(seg_col == s, film_terms, 0.0), axis=0)
        for s in range(seq_count + 1)
    ]

    sums = [
        jnp.sum(grad_norm_two * normal_two, axis=0),
        jnp.sum(grad_norm_two, axis=0),
        jnp.sum(grad_y, axis=0),
        grad_bias_up,
    ] + film_sums
    sizes = [vector.shape[0] for vector in sums]
    total = lax.psum(jnp.concatenate(sums)[None, :], "ctx")
    total = lax.all_gather(total, "fsdp", axis=0, tiled=True)
    split = []
    at = 0
    for size in sizes:
        split.append(total[:, at : at + size])
        at += size

    def own(vector):
        size = vector.shape[0] // fsdp_size
        return lax.dynamic_slice_in_dim(vector, shard * size, size, 0)

    sum_gain_two, sum_bias_two, sum_bias_down, sum_bias_up = (
        own(jnp.sum(vector, axis=0)) for vector in split[:4]
    )
    film_all = jnp.sum(sum(split[4:]), axis=0)
    sum_gain_one = own(film_all[:width])
    sum_bias_one = own(film_all[width:])
    film_grad = jnp.stack(split[4 : 4 + seq_count], axis=1).reshape(-1, 2 * width)
    embedded_rows = lax.dynamic_slice_in_dim(
        all_embedded.astype(F32).reshape(film_grad.shape[0], -1),
        shard * w_time.shape[0],
        w_time.shape[0],
        1,
    )
    grad_time = sum(
        embedded_rows[g][:, None] * film_grad[g][None, :]
        for g in range(film_grad.shape[0])
    )

    slice_width = hidden // (ctx_size * fsdp_size)
    starts = [
        k * (hidden // fsdp_size) + me * slice_width for k in range(fsdp_size)
    ]
    w_up_cols = []
    for piece, _ in up_pieces:
        w_up_cols.append(
            jnp.concatenate(
                [
                    lax.dynamic_slice_in_dim(piece, start, slice_width, 1)
                    for start in starts
                ],
                axis=1,
            )
        )
    w_up_slice = joined(w_up_cols, up_pieces, 0)
    w_down_slice = jnp.concatenate(
        [rows_of(down_pieces, start, slice_width) for start in starts], axis=0
    )
    bias_slice = jnp.concatenate(
        [
            lax.dynamic_slice_in_dim(bias_hidden, start, slice_width, 1)
            for start in starts
        ],
        axis=1,
    )
    pre_slice = dims(all_norm_two, w_up_slice, 1, 0) + bias_slice
    act_slice, slope_slice = gelu_parts(pre_slice)
    grad_pre_slice = (dims(all_grad_y, w_down_slice, 1, 1) * slope_slice).astype(BF16)
    down_slice = dims(act_slice.astype(BF16), all_grad_y, 0, 0)
    up_slice = dims(all_norm_two, grad_pre_slice, 0, 0)
    grad_down = gather(scatter_sum(down_slice, 0)).reshape(-1, width).astype(F32)
    up_parts = gather(scatter_sum(up_slice, 0))
    grad_up = (
        up_parts.reshape(ctx_size, width // fsdp_size, fsdp_size, slice_width)
        .transpose(1, 2, 0, 3)
        .reshape(width // fsdp_size, hidden)
        .astype(F32)
    )
    out_part = jnp.dot(attended_t, grad_resid_b, preferred_element_type=F32)
    out_rows = lax.psum_scatter(
        out_part.astype(BF16), ("fsdp", "ctx"), scatter_dimension=0, tiled=True
    )
    grad_out = gather(out_rows).reshape(-1, width).astype(F32)
    qkv_slice = jnp.dot(mixed_t, all_norm, preferred_element_type=F32)
    qkv_parts = gather(scatter_sum(qkv_slice, 1))
    grad_qkv = (
        qkv_parts.reshape(ctx_size, 3, columns, width // fsdp_size)
        .transpose(3, 1, 0, 2)
        .reshape(width // fsdp_size, 3 * width)
        .astype(F32)
    )
    return (
        output[None],
        grad_tokens[None],
        grad_qkv,
        grad_out,
        grad_up,
        grad_down,
        grad_time,
        sum_gain_one,
        sum_bias_one,
        sum_gain_two,
        sum_bias_two,
        sum_bias_up,
        sum_bias_down,
    )


def solution(mesh):
    in_specs = (
        (P("fsdp", "ctx", None),)
        + (P("fsdp", None),) * 5
        + (P("fsdp"),) * 6
        + (P("fsdp", None), P("fsdp", None), P("fsdp", "ctx", None))
    )
    out_specs = (
        (P("fsdp", "ctx", None),) * 2 + (P("fsdp", None),) * 5 + (P("fsdp"),) * 6
    )
    return jax.shard_map(
        functools.partial(body, mesh.shape["ctx"], mesh.shape["fsdp"]),
        mesh=mesh,
        in_specs=in_specs,
        out_specs=out_specs,
        check_vma=False,
    )
```

```python
import functools
import math

import jax
import jax.numpy as jnp
import numpy as np
from jax import lax
from jax.experimental import pallas as pl
from jax.experimental.pallas import tpu as pltpu
from jax.sharding import PartitionSpec as P

HEADS = 16
EPSILON = 1e-05
NEGATIVE = -1e30
HIGH = lax.Precision.HIGHEST
F32 = jnp.float32
BF16 = jnp.bfloat16
VMEM_BYTES = 56 << 20


def dims(left, right, left_dim, right_dim):
    return lax.dot_general(
        left, right, (((left_dim,), (right_dim,)), ((), ())), preferred_element_type=F32
    )


def segments(ends, index):
    return sum((index >= end).astype(jnp.int32) for end in ends)


def positions(ends, index, segment):
    begin = jnp.zeros_like(index)
    for at, end in enumerate(ends):
        begin = jnp.where(segment > at, end, begin)
    return index - begin


def embed(steps_given, embed_width):
    half_width = embed_width // 2
    freq = jnp.exp(-math.log(10000.0) * jnp.arange(half_width, dtype=F32) / half_width)
    angle = steps_given.astype(F32)[..., None] * freq
    return jnp.concatenate([jnp.sin(angle), jnp.cos(angle)], axis=-1)


def stats(values):
    centre = jnp.mean(values, axis=-1, keepdims=True)
    centered = values - centre
    spread = jnp.mean(centered * centered, axis=-1, keepdims=True)
    scale = lax.rsqrt(spread + EPSILON)
    return centered * scale, scale


def stats_back(grad, normal, scale):
    return (
        grad
        - jnp.mean(grad, axis=-1, keepdims=True)
        - normal * jnp.mean(grad * normal, axis=-1, keepdims=True)
    ) * scale


def gelu_parts(pre):
    below = 0.5 * (1.0 + lax.erf(pre * math.sqrt(0.5)))
    density = jnp.exp(-0.5 * pre * pre) * (1.0 / math.sqrt(2.0 * math.pi))
    return pre * below, below + pre * density


def qkv_kernel(
    rows, head_size, ends_ref, base_ref, tokens_ref, gains_ref, shifts_ref, w_ref,
    cos_ref, sin_ref, norm_ref, query_t_ref, key_ref, key_t_ref, value_t_ref, pair_ref,
):
    step = pl.program_id(0)
    block = tokens_ref.shape[0]
    seq_count = ends_ref.shape[0]
    half = head_size // 2
    values = tokens_ref[...].astype(F32)
    normal, _ = stats(values)
    chunks = block // rows

    def token_index(shape, axis):
        within = lax.broadcasted_iota(jnp.int32, shape, axis)
        index = within + base_ref[step * chunks]
        for at in range(1, chunks):
            index = jnp.where(
                within >= at * rows,
                within - at * rows + base_ref[step * chunks + at],
                index,
            )
        return index

    ends = [ends_ref[s] for s in range(seq_count)]
    seg_col = segments(ends, token_index((block, 1), 0))
    seg_row = segments(ends, token_index((1, block), 1))
    gains = gains_ref[0:1, :]
    shifts = shifts_ref[0:1, :]
    for s in range(1, seq_count + 1):
        gains = jnp.where(seg_col == s, gains_ref[s : s + 1, :], gains)
        shifts = jnp.where(seg_col == s, shifts_ref[s : s + 1, :], shifts)
    norm = (normal * gains + shifts).astype(BF16)
    norm_ref[...] = norm
    mixed = jnp.dot(norm, w_ref[...], preferred_element_type=F32)
    turned = mixed.T
    cos = cos_ref[...]
    sin = sin_ref[...]

    def turn(at):
        upper = turned[at : at + half]
        lower = turned[at + half : at + head_size]
        return jnp.concatenate(
            [upper * cos - lower * sin, lower * cos + upper * sin], axis=0
        ).astype(BF16)

    query = turn(0).astype(F32) * (float(head_size) ** -0.5)
    key = turn(head_size).astype(F32)
    value = turned[2 * head_size : 3 * head_size].astype(BF16).astype(F32)
    spare = 128 - head_size
    row_id = lax.broadcasted_iota(jnp.int32, (spare, block), 0)
    same = row_id == seg_row
    used = row_id <= seq_count
    key_tail = jnp.where(same & used, 1.0, 0.0)
    query_tail = jnp.where(used & jnp.logical_not(same), NEGATIVE, 0.0)
    query_t_ref[...] = jnp.concatenate([query, query_tail], axis=0).astype(BF16)
    key_t_ref[...] = key.astype(BF16)
    value_t_ref[...] = value.astype(BF16)
    key_ref[...] = jnp.concatenate([key, key_tail], axis=0).T.astype(BF16)
    pair_ref[...] = jnp.concatenate([value, query], axis=0).T.astype(BF16)


def attend_kernel(
    chunk, rows, place_ref, query_ref, key_ref, value_ref, out_ref, sent_ref, lse_ref, score_ref,
):
    core = place_ref[0] % 2
    count = key_ref.shape[0]
    query = query_ref[...]
    top = None
    for at in range(0, count, chunk):
        score = jnp.dot(key_ref[at : at + chunk, :], query, preferred_element_type=F32)
        score_ref[at : at + chunk, :] = score
        high = jnp.max(score, axis=0, keepdims=True)
        top = high if top is None else jnp.maximum(top, high)
    total = jnp.zeros_like(top)
    out = jnp.zeros(out_ref.shape, F32)
    for at in range(0, count, chunk):
        weight = jnp.exp(score_ref[at : at + chunk, :] - top)
        total = total + jnp.sum(weight, axis=0, keepdims=True)
        out = out + jnp.dot(
            value_ref[:, at : at + chunk],
            weight.astype(BF16),
            preferred_element_type=F32,
        )
    out = out / total
    out_ref[...] = out
    for at in range(sent_ref.shape[0]):
        sent_ref[at ^ core] = out[:, at * rows : (at + 1) * rows].astype(BF16)
    lse_ref[...] = top + jnp.log(total)


def attend_back_kernel(
    chunk, rows, head_size, place_ref, query_ref, grad_ref, out_ref, lse_ref, key_ref, key_t_ref, pair_ref,
    pair_block_ref, cos_block_ref, sin_block_ref, cos_ref, sin_ref, mixed_ref, sent_ref, key_acc, value_acc,
):
    step = pl.program_id(0)
    core = place_ref[0] % 2
    per_step = grad_ref.shape[0]
    count = key_ref.shape[0]
    block = query_ref.shape[1]
    half = head_size // 2
    scale = float(head_size) ** -0.5

    @pl.when(step == 0)
    def _():
        key_acc[...] = jnp.zeros_like(key_acc)
        value_acc[...] = jnp.zeros_like(value_acc)

    query = query_ref[...]
    grad = jnp.concatenate(
        [grad_ref[at ^ core] for at in range(per_step)], axis=1
    ).astype(F32)
    delta = jnp.sum(grad * out_ref[...], axis=0, keepdims=True)
    lse = lse_ref[...]
    grad_t = jnp.concatenate(
        [grad, jnp.zeros((128 - head_size, block), F32)], axis=0
    )
    grad_rows = grad_t.T.astype(BF16)
    grad_t = grad_t.astype(BF16)
    pair = pair_block_ref[...]
    grad_query = jnp.zeros((head_size, block), F32)
    for at in range(0, count, chunk):
        part = slice(at, at + chunk)
        score = jnp.dot(key_ref[part, :], query, preferred_element_type=F32)
        prob = jnp.exp(score - lse)
        grad_prob = jnp.dot(pair_ref[part, :], grad_t, preferred_element_type=F32)
        grad_score = (prob * (grad_prob - delta)).astype(BF16)
        grad_query = grad_query + jnp.dot(
            key_t_ref[:, part], grad_score, preferred_element_type=F32
        )
        key_acc[part, :] += jnp.dot(grad_score, pair, preferred_element_type=F32)
        value_acc[part, :] += jnp.dot(
            prob.astype(BF16), grad_rows, preferred_element_type=F32
        )

    def turn_back(values, cos, sin):
        upper = values[:half]
        lower = values[half:]
        return jnp.concatenate(
            [upper * cos + lower * sin, lower * cos - upper * sin], axis=0
        ).astype(BF16)

    at = pl.multiple_of(step * block, block)
    query_part = turn_back(
        grad_query * scale, cos_block_ref[...], sin_block_ref[...]
    )
    mixed_ref[0:head_size, pl.ds(at, block)] = query_part
    for k in range(per_step):
        sent_ref[place_ref[step * per_step + k], 0:head_size, :] = query_part[
            :, k * rows : (k + 1) * rows
        ]

    @pl.when(step == pl.num_programs(0) - 1)
    def _():
        key_part = turn_back(
            key_acc[...].T[head_size : 2 * head_size], cos_ref[...], sin_ref[...]
        )
        value_part = value_acc[...].T[:head_size].astype(BF16)
        both = jnp.concatenate([key_part, value_part], axis=0)
        mixed_ref[head_size : 3 * head_size, :] = both
        for k in range(count // rows):
            sent_ref[place_ref[k], head_size : 3 * head_size, :] = both[
                :, k * rows : (k + 1) * rows
            ]


def whole(shape):
    return pl.BlockSpec(shape, lambda i, *_: (0,) * len(shape))


def project(tokens, base, ends, gains, shifts, w_head, cos, sin, rows, head_size):
    count, width = tokens.shape
    block = min(count, 2 * rows)
    grid_spec = pltpu.PrefetchScalarGridSpec(
        num_scalar_prefetch=2,
        grid=(count // block,),
        in_specs=[
            pl.BlockSpec((block, width), lambda i, *_: (i, 0)),
            whole(gains.shape),
            whole(shifts.shape),
            whole(w_head.shape),
            pl.BlockSpec((head_size // 2, block), lambda i, *_: (0, i)),
            pl.BlockSpec((head_size // 2, block), lambda i, *_: (0, i)),
        ],
        out_specs=[
            pl.BlockSpec((block, width), lambda i, *_: (i, 0)),
            pl.BlockSpec((128, block), lambda i, *_: (0, i)),
            pl.BlockSpec((block, 128), lambda i, *_: (i, 0)),
            pl.BlockSpec((head_size, block), lambda i, *_: (0, i)),
            pl.BlockSpec((head_size, block), lambda i, *_: (0, i)),
            pl.BlockSpec((block, 128), lambda i, *_: (i, 0)),
        ],
    )
    return pl.pallas_call(
        functools.partial(qkv_kernel, rows, head_size),
        grid_spec=grid_spec,
        out_shape=[
            jax.ShapeDtypeStruct((count, width), BF16),
            jax.ShapeDtypeStruct((128, count), BF16),
            jax.ShapeDtypeStruct((count, 128), BF16),
            jax.ShapeDtypeStruct((head_size, count), BF16),
            jax.ShapeDtypeStruct((head_size, count), BF16),
            jax.ShapeDtypeStruct((count, 128), BF16),
        ],
        compiler_params=pltpu.CompilerParams(vmem_limit_bytes=VMEM_BYTES),
        cost_estimate=pl.CostEstimate(
            flops=2 * count * width * 256,
            bytes_accessed=4 * count * width,
            transcendentals=0,
        ),
        name="project_head",
    )(ends, base, tokens, gains, shifts, w_head, cos, sin)


def attend(place, query_t, key, value_t, rows):
    count = key.shape[0]
    head_size = value_t.shape[0]
    block = min(count, 2 * rows)
    chunk = min(count, 512)
    grid_spec = pltpu.PrefetchScalarGridSpec(
        num_scalar_prefetch=1,
        grid=(count // block,),
        in_specs=[
            pl.BlockSpec((128, block), lambda i, _: (0, i)),
            whole((count, 128)),
            whole((head_size, count)),
        ],
        out_specs=[
            pl.BlockSpec((head_size, block), lambda i, _: (0, i)),
            pl.BlockSpec(
                (2, head_size, rows), lambda i, place: (place[2 * i] // 2, 0, 0)
            ),
            pl.BlockSpec((1, block), lambda i, _: (0, i)),
        ],
        scratch_shapes=[pltpu.VMEM((count, block), F32)],
    )
    return pl.pallas_call(
        functools.partial(attend_kernel, chunk, rows),
        grid_spec=grid_spec,
        out_shape=[
            jax.ShapeDtypeStruct((head_size, count), F32),
            jax.ShapeDtypeStruct((count // rows, head_size, rows), BF16),
            jax.ShapeDtypeStruct((1, count), F32),
        ],
        compiler_params=pltpu.CompilerParams(vmem_limit_bytes=VMEM_BYTES),
        cost_estimate=pl.CostEstimate(
            flops=8 * count * count * 128,
            bytes_accessed=8 * count * 128,
            transcendentals=count * count,
        ),
        name="attend_head",
    )(place, query_t, key, value_t)


def attend_back(place, query_t, grad, out, lse, key, key_t, pair, cos, sin, rows):
    count = key.shape[0]
    head_size = key_t.shape[0]
    half = head_size // 2
    block = min(count, 2 * rows)
    chunk = min(count, 512)
    grid_spec = pltpu.PrefetchScalarGridSpec(
        num_scalar_prefetch=1,
        grid=(count // block,),
        in_specs=[
            pl.BlockSpec((128, block), lambda i, _: (0, i)),
            pl.BlockSpec(
                (2, head_size, rows), lambda i, place: (place[2 * i] // 2, 0, 0)
            ),
            pl.BlockSpec((head_size, block), lambda i, _: (0, i)),
            pl.BlockSpec((1, block), lambda i, _: (0, i)),
            whole((count, 128)),
            whole((head_size, count)),
            whole((count, 128)),
            pl.BlockSpec((block, 128), lambda i, _: (i, 0)),
            pl.BlockSpec((half, block), lambda i, _: (0, i)),
            pl.BlockSpec((half, block), lambda i, _: (0, i)),
            whole((half, count)),
            whole((half, count)),
        ],
        out_specs=[
            whole((3 * head_size, count)),
            whole((count // rows, 3 * head_size, rows)),
        ],
        scratch_shapes=[pltpu.VMEM((count, 128), F32), pltpu.VMEM((count, 128), F32)],
    )
    return pl.pallas_call(
        functools.partial(attend_back_kernel, chunk, rows, head_size),
        grid_spec=grid_spec,
        out_shape=[
            jax.ShapeDtypeStruct((3 * head_size, count), BF16),
            jax.ShapeDtypeStruct((count // rows, 3 * head_size, rows), BF16),
        ],
        compiler_params=pltpu.CompilerParams(vmem_limit_bytes=VMEM_BYTES),
        cost_estimate=pl.CostEstimate(
            flops=20 * count * count * 128,
            bytes_accessed=16 * count * 128,
            transcendentals=count * count,
        ),
        name="attend_head_back",
    )(place, query_t, grad, out, lse, key, key_t, pair, pair, cos, sin, cos, sin)


def up_kernel(in_ref, out_ref):
    for j in range(in_ref.shape[0]):
        out_ref[:, j * 128 : (j + 1) * 128] = in_ref[j].astype(F32)


def down_kernel(in_ref, out_ref):
    for j in range(in_ref.shape[0]):
        for k in range(out_ref.shape[1] // 128):
            out_ref[j * 128 : (j + 1) * 128, k * 128 : (k + 1) * 128] = in_ref[
                j, k * 128 : (k + 1) * 128, :
            ].astype(F32)


def expand_up(packed, up_rows, shards):
    devices = packed.shape[0]
    many = min(devices, 8)
    groups = devices // many
    return pl.pallas_call(
        up_kernel,
        grid=(shards, groups),
        in_specs=[pl.BlockSpec((many, up_rows, 128), lambda k, g: (g, k, 0))],
        out_specs=pl.BlockSpec((up_rows, many * 128), lambda k, g: (0, k * groups + g)),
        out_shape=jax.ShapeDtypeStruct((up_rows, shards * devices * 128), F32),
        compiler_params=pltpu.CompilerParams(vmem_limit_bytes=VMEM_BYTES),
        name="expand_up",
    )(packed)


def expand_down(packed, width):
    devices = packed.shape[0]
    many = 4
    return pl.pallas_call(
        down_kernel,
        grid=(devices // many,),
        in_specs=[pl.BlockSpec((many, width, 128), lambda g: (g, 1, 0))],
        out_specs=pl.BlockSpec((many * 128, width), lambda g: (g, 0)),
        out_shape=jax.ShapeDtypeStruct((devices * 128, width), F32),
        compiler_params=pltpu.CompilerParams(vmem_limit_bytes=VMEM_BYTES),
        name="expand_down",
    )(packed)


def last_kernel(head_size, place_ref, where_ref, in_ref, qkv_ref, out_ref):
    chip = pl.program_id(0)
    core = place_ref[0] % 2
    width = out_ref.shape[1]
    depth = in_ref.shape[2]
    pair = [in_ref[at ^ core] for at in range(2)]
    for k in range(3):
        part = slice(k * head_size, (k + 1) * head_size)
        both = jnp.concatenate([pair[0][part], pair[1][part]], axis=0).astype(F32)
        at = pl.multiple_of(k * width + chip * 2 * head_size, 128)
        qkv_ref[:, pl.ds(at, 2 * head_size)] = both.T
    rows = out_ref.shape[0] // 2
    top = 3 * head_size
    for at in range(2):
        for k in range(width // depth):
            out_ref[at * rows : (at + 1) * rows, k * depth : (k + 1) * depth] = pair[at][
                top + k * rows : top + (k + 1) * rows
            ].astype(F32)


def expand_last(place, where, packed, width, head_size):
    devices, tall, depth = packed.shape
    grid_spec = pltpu.PrefetchScalarGridSpec(
        num_scalar_prefetch=2,
        grid=(devices // 2,),
        in_specs=[
            pl.BlockSpec((2, tall, depth), lambda i, place, where: (where[i], 0, 0))
        ],
        out_specs=[
            whole((depth, 3 * width)),
            pl.BlockSpec((2 * (depth // devices), width), lambda i, *_: (i, 0)),
        ],
    )
    return pl.pallas_call(
        functools.partial(last_kernel, head_size),
        grid_spec=grid_spec,
        out_shape=[
            jax.ShapeDtypeStruct((depth, 3 * width), F32),
            jax.ShapeDtypeStruct((depth, width), F32),
        ],
        compiler_params=pltpu.CompilerParams(vmem_limit_bytes=VMEM_BYTES),
        name="expand_last",
    )(place, where, packed)


def times(values, blocks, columns):
    total = None
    placed = {}
    for block, row, column in blocks:
        term = jnp.dot(
            lax.dynamic_slice_in_dim(values, row, block.shape[0], 1),
            block,
            preferred_element_type=F32,
        )
        if block.shape[1] == columns:
            total = term if total is None else total + term
        elif id(column) in placed:
            placed[id(column)][0] += term
        else:
            placed[id(column)] = [term, column]
    if placed:
        side = jnp.zeros(total.shape, F32)
        for term, column in placed.values():
            side = lax.dynamic_update_slice_in_dim(side, term, column, 1)
        total = total + side
    return total


def times_t(values, blocks, length):
    found = {}
    for block, row, column in blocks:
        part = values
        if block.shape[1] != values.shape[1]:
            part = lax.dynamic_slice_in_dim(values, column, block.shape[1], 1)
        term = dims(part, block, 1, 1)
        if id(row) in found:
            found[id(row)][0] += term
        else:
            found[id(row)] = [term, row]
    if len(found) == 1:
        return term
    out = jnp.zeros((values.shape[0], length), F32)
    for term, row in found.values():
        out = lax.dynamic_update_slice_in_dim(out, term, row, 1)
    return out


def columns_of(blocks, start, size, length):
    found = {}
    for block, row, column in blocks:
        last = block.shape[1] - size
        local = jnp.clip(start - column, 0, last)
        part = lax.dynamic_slice_in_dim(block, local, size, 1)
        if id(row) in found:
            inside = (start >= column) & (start <= column + last)
            found[id(row)][0] = jnp.where(inside, part, found[id(row)][0])
        else:
            found[id(row)] = [part, row]
    if len(found) == 1:
        return part
    out = jnp.zeros((length, size), blocks[0][0].dtype)
    for part, row in found.values():
        out = lax.dynamic_update_slice_in_dim(out, part, row, 0)
    return out


def ring_chips(chips):
    if chips == 8:
        return [0, 2, 4, 6, 7, 5, 3, 1]
    return list(range(chips))


def ring_tables(ctx_size):
    chips = ctx_size // 2
    order = ring_chips(chips)
    offsets = [0]
    for step in range(1, chips // 2 + 1):
        offsets.append(-step)
        if step <= (chips - 1) // 2:
            offsets.append(step)
    place = np.zeros((ctx_size, ctx_size), np.int32)
    where = np.zeros((ctx_size, chips), np.int32)
    for me in range(ctx_size):
        at = order.index(me // 2)
        for k, offset in enumerate(offsets):
            chip = order[(at + offset) % chips]
            place[me, 2 * k] = 2 * chip + me % 2
            place[me, 2 * k + 1] = 2 * chip + 1 - me % 2
            where[me, chip] = k
    return order, place, where


def after(values, *earlier):
    return lax.optimization_barrier((values, *earlier))[0]


def body(
    ctx_size, fsdp_size,
    tokens, w_qkv, w_out, w_up, w_down, w_time, gain_one, bias_one, gain_two, bias_two, bias_up,
    bias_down, lengths, time_steps, cotangent,
):
    me = lax.axis_index("ctx")
    shard = lax.axis_index("fsdp")
    core = me % 2
    rows = tokens.shape[1]
    width = tokens.shape[2]
    count = rows * ctx_size
    head_size = width // HEADS
    repeats = ctx_size // HEADS
    columns = head_size // repeats
    seq_count = lengths.shape[1]
    hidden = w_up.shape[1]
    paired = fsdp_size == 2
    other = 1 - shard
    chips = ctx_size // 2
    order, place_table, where_table = ring_tables(ctx_size)
    place = jnp.asarray(place_table)[me]
    where = jnp.asarray(where_table)[me]

    def across(values):
        return lax.ppermute(values, "fsdp", [(0, 1), (1, 0)])

    def flip(values, bit):
        return lax.ppermute(
            values, "ctx", [(i, i ^ (1 << bit)) for i in range(ctx_size)]
        )

    def hop(values, step):
        return lax.ppermute(
            values,
            "ctx",
            [
                (2 * order[at] + c, 2 * order[(at + step) % chips] + c)
                for at in range(chips)
                for c in range(2)
            ],
        )

    def ring_gather(values):
        right = left = values
        kept = [values]
        for step in range(1, chips // 2 + 1):
            right = hop(right, 1)
            kept.append(right)
            if step <= (chips - 1) // 2:
                left = hop(left, -1)
                kept.append(left)
        return [part for mine in kept for part in (mine, flip(mine, 0))]

    def by_shard(mine, others, axis):
        first = jnp.where(shard == 0, mine, others)
        second = jnp.where(shard == 0, others, mine)
        return jnp.concatenate([first, second], axis=axis)

    def gather_small(values, earlier=()):
        if not paired:
            return lax.all_gather(values, "fsdp", axis=0, tiled=True)
        return by_shard(values, across(after(values, *earlier)), 0)

    def fetch(weight, earlier=()):
        if not paired:
            return [(lax.all_gather(weight, "fsdp", axis=0, tiled=True), 0, 0)]
        size = weight.shape[0]
        half = size // 2
        send = after(lax.dynamic_slice_in_dim(weight, core * half, half, 0), *earlier)
        mine = across(send)
        return [
            (weight, shard * size, 0),
            (mine, other * size + core * half, 0),
            (flip(mine, 0), other * size + (1 - core) * half, 0),
        ]

    def fetch_four(weight, parts, earlier):
        if not paired:
            return [(lax.all_gather(weight, "fsdp", axis=0, tiled=True), 0, 0)]
        size, length = weight.shape
        side = me % 4
        quarter = length // 4
        deep = size // parts
        blocks = [(weight, shard * size, 0)]
        starts = [(side ^ k) * quarter for k in range(4)]
        for part in range(parts):
            send = lax.dynamic_slice(
                weight, (part * deep, starts[0]), (deep, quarter)
            )
            got = across(after(send, *earlier))
            earlier = (got,)
            beside = flip(got, 1)
            row = other * size + part * deep
            four = [got, flip(got, 0), beside, flip(beside, 0)]
            blocks += [(four[k], row, starts[k]) for k in range(4)]
        return blocks

    def scatter_sum(values, dim):
        if not paired:
            return lax.psum_scatter(
                values.astype(BF16), "fsdp", scatter_dimension=dim, tiled=True
            )
        half = values.shape[dim] // 2
        keep = lax.dynamic_slice_in_dim(values, shard * half, half, dim)
        send = lax.dynamic_slice_in_dim(values, other * half, half, dim)
        return (keep + across(send.astype(BF16)).astype(F32)).astype(BF16)

    def gather(values):
        return lax.all_gather(values, "ctx", axis=0, tiled=False)

    bits = ctx_size.bit_length() - 1

    def halve(values, axis, mine, send):
        keep = lax.dynamic_index_in_dim(values, mine, axis, keepdims=False)
        give = lax.dynamic_index_in_dim(values, 1 - mine, axis, keepdims=False)
        return keep + send(give.astype(BF16)).astype(F32)

    def scatter_rows(values):
        length = values.shape[1]
        deep = values.shape[0] // (ctx_size * fsdp_size)
        values = values.reshape(fsdp_size, -1, 2, deep, length)
        values = halve(values, 2, core, lambda v: flip(v, 0))
        if paired:
            values = halve(values, 0, shard, across)[None]
        for bit in range(1, bits):
            values = values.reshape(values.shape[0], -1, 2, deep, length)
            values = halve(
                values, 2, (me >> bit) % 2, lambda v, bit=bit: flip(v, bit)
            )
        values = values.reshape(-1, deep, length)
        if not paired:
            values = lax.psum_scatter(
                values.astype(BF16), "fsdp", scatter_dimension=0, tiled=True
            )
        return values.reshape(deep, length).astype(BF16)

    ends = []
    for s in range(seq_count):
        ends.append(lengths[0, s] + (ends[-1] if ends else 0))
    ends_vector = jnp.stack(ends)
    base = place * rows
    index = me * rows + jnp.arange(rows, dtype=jnp.int32)
    segment = segments(ends, index)
    seg_col = segment[:, None]
    live = (segment < seq_count).astype(F32)[:, None]
    all_index = (base[:, None] + jnp.arange(rows, dtype=jnp.int32)[None, :]).reshape(-1)
    all_position = positions(ends, all_index, segments(ends, all_index))
    half_width = head_size // 2
    inverse = jnp.exp(
        -math.log(10000.0) * jnp.arange(half_width, dtype=F32) / half_width
    )
    angle = inverse[:, None] * all_position.astype(F32)[None, :]
    cos = jnp.cos(angle)
    sin = jnp.sin(angle)

    all_tokens = jnp.concatenate(ring_gather(tokens[0]), axis=0)
    inputs = tokens[0].astype(F32)
    grad_y = cotangent[0].astype(F32) * live
    grad_y_b = grad_y.astype(BF16)
    all_grad_y = gather(grad_y_b).reshape(count, width)

    steps_row = time_steps.reshape(1, seq_count)
    high = (steps_row // 256).astype(BF16)
    low = (steps_row % 256).astype(BF16)
    small = [v[None, :] for v in (gain_one, bias_one, gain_two, bias_two, bias_down, bias_up)]
    packed = gather_small(jnp.concatenate(small + [high, low], axis=1))
    vectors = []
    at = 0
    for vector in small:
        size = vector.shape[1]
        vectors.append(packed[:, at : at + size].reshape(1, -1).astype(F32))
        at += size
    gain_first, bias_first, gain_second, bias_second, bias_output, bias_hidden = vectors
    all_steps = packed[:, at : at + seq_count].astype(F32) * 256.0 + packed[
        :, at + seq_count :
    ].astype(F32)
    all_embedded = embed(all_steps, w_time.shape[0] * fsdp_size).astype(BF16)

    head = me // repeats
    w_head = jnp.concatenate(
        [
            lax.dynamic_slice_in_dim(w_qkv, k * width + head * head_size, head_size, 1)
            for k in range(3)
        ]
        + [jnp.zeros((w_qkv.shape[0], head_size), BF16)],
        axis=1,
    )
    w_head = gather_small(w_head, (packed,))

    if paired:
        other_grad_y = across(after(grad_y_b, w_head))
        time_blocks = fetch(w_time, (other_grad_y,))
        grad_act_part = dims(
            jnp.concatenate([grad_y_b, other_grad_y], axis=0), w_down, 1, 1
        )
        grad_act_send = after(grad_act_part[rows:].astype(BF16), time_blocks[1][0])
        grad_act_got = across(grad_act_send)
        grad_act = by_shard(grad_act_part[:rows], grad_act_got.astype(F32), 1)
        out_blocks = fetch(w_out, (grad_act_got,))
        up_blocks = fetch_four(w_up, 2, (out_blocks[1][0],))
        slice_width = hidden // (ctx_size * fsdp_size)
        other_rows = across(
            after(
                lax.dynamic_slice_in_dim(w_down, me * slice_width, slice_width, 0),
                up_blocks[-4][0],
            )
        )
        own_rows = lax.dynamic_slice_in_dim(w_down, me * slice_width, slice_width, 0)
        w_down_slice = by_shard(own_rows, other_rows, 0)
        qkv_blocks = fetch(w_qkv, (other_rows,))
        down_blocks = fetch(w_down, (qkv_blocks[1][0],))
    else:
        time_blocks = fetch(w_time)
        out_blocks = fetch(w_out)
        up_blocks = fetch(w_up)
        down_blocks = fetch(w_down)
        qkv_blocks = fetch(w_qkv)
        grad_act = times_t(grad_y_b, down_blocks, hidden)
        slice_width = hidden // (ctx_size * fsdp_size)
        full_down = down_blocks[0][0].reshape(fsdp_size, ctx_size, slice_width, width)
        w_down_slice = lax.dynamic_index_in_dim(full_down, me, 1, keepdims=False)
        w_down_slice = w_down_slice.reshape(-1, width)

    embedded = lax.dynamic_index_in_dim(all_embedded, shard, 0, keepdims=False)
    film = times(embedded.reshape(seq_count, -1), time_blocks, 2 * width)
    film = jnp.concatenate([film, jnp.zeros((1, 2 * width), F32)], axis=0)
    gains = gain_first + film[:, :width]
    shifts = bias_first + film[:, width:]

    all_norm, query_t, key, key_t, value_t, pair = project(
        all_tokens, base, ends_vector, gains, shifts, w_head, cos, sin, rows, head_size
    )
    out_t, sent, lse = attend(place, query_t, key, value_t, rows)
    part = (me % repeats) * columns
    if repeats > 1:
        sent = lax.dynamic_slice_in_dim(sent, part, columns, 1)
    attended_t = lax.all_to_all(sent, "ctx", 0, 0, tiled=True).reshape(width, rows)

    resid = inputs + sum(
        dims(lax.dynamic_slice_in_dim(attended_t, row, b.shape[0], 0), b, 0, 0)
        for b, row, _ in out_blocks
    )
    normal_two, scale_two = stats(resid)
    norm_two_b = (normal_two * gain_second + bias_second).astype(BF16)
    all_norm_two = gather(norm_two_b).reshape(count, width)
    pre = times(norm_two_b, up_blocks, hidden) + bias_hidden
    act, slope = gelu_parts(pre)
    act_b = act.astype(BF16)
    grad_pre = grad_act * slope
    grad_bias_up = jnp.sum(grad_pre, axis=0)
    grad_pre_b = grad_pre.astype(BF16)
    grad_norm_two = times_t(grad_pre_b, up_blocks, width)
    grad_resid = grad_y + stats_back(grad_norm_two * gain_second, normal_two, scale_two)
    grad_resid_b = grad_resid.astype(BF16)
    if len(out_blocks) == 1:
        grad_att_t = dims(out_blocks[0][0], grad_resid_b, 1, 1)
    else:
        grad_att_t = jnp.zeros((width, rows), F32)
        for b, row, _ in out_blocks:
            grad_att_t = lax.dynamic_update_slice_in_dim(
                grad_att_t, dims(b, grad_resid_b, 1, 1), row, 0
            )
    grad_att_t = grad_att_t.astype(BF16).reshape(HEADS, head_size, rows)
    if repeats > 1:
        grad_att_t = jnp.repeat(grad_att_t, repeats, axis=0)
    grad_att = lax.all_to_all(grad_att_t, "ctx", 0, 0, tiled=True)

    mixed_t, mixed_sent = attend_back(
        place, query_t, grad_att, out_t, lse, key, key_t, pair, cos, sin, rows
    )
    if repeats > 1:
        mixed_t = mixed_t.reshape(3, head_size, count)
        mixed_t = lax.dynamic_slice_in_dim(mixed_t, part, columns, 1)
        mixed_t = mixed_t.reshape(3 * columns, count)
        mixed_sent = mixed_sent.reshape(ctx_size, 3, head_size, rows)
        mixed_sent = lax.dynamic_slice_in_dim(mixed_sent, part, columns, 2)
        mixed_sent = mixed_sent.reshape(ctx_size, 3 * columns, rows)
    mixed_got = lax.all_to_all(mixed_sent, "ctx", 0, 0, tiled=True)
    grad_mixed_t = (
        mixed_got.reshape(ctx_size, 3, columns, rows)
        .transpose(1, 0, 2, 3)
        .reshape(3 * width, rows)
    )

    starts = [k * (hidden // fsdp_size) + me * slice_width for k in range(fsdp_size)]
    w_up_slice = jnp.concatenate(
        [columns_of(up_blocks, start, slice_width, width) for start in starts], axis=1
    )
    bias_slice = jnp.concatenate(
        [
            lax.dynamic_slice_in_dim(bias_hidden, start, slice_width, 1)
            for start in starts
        ],
        axis=1,
    )
    pre_slice = dims(all_norm_two, w_up_slice, 1, 0) + bias_slice
    act_slice, slope_slice = gelu_parts(pre_slice)
    grad_pre_slice = (dims(all_grad_y, w_down_slice, 1, 1) * slope_slice).astype(BF16)
    down_slice = scatter_sum(dims(act_slice.astype(BF16), all_grad_y, 0, 0), 0)
    up_slice = scatter_sum(dims(all_norm_two, grad_pre_slice, 0, 0), 0)
    packable = paired and slice_width == 128
    if packable:
        sliced = jnp.concatenate(
            [up_slice[:, k * 128 : (k + 1) * 128] for k in range(fsdp_size)]
            + [down_slice[:, k * 128 : (k + 1) * 128] for k in range(width // 128)],
            axis=0,
        )
        sliced = gather(sliced)
        grad_up = expand_up(sliced, width // fsdp_size, fsdp_size)
        grad_down = expand_down(sliced, width)
    else:
        grad_down = gather(down_slice).reshape(-1, width).astype(F32)
        grad_up = (
            gather(up_slice)
            .reshape(ctx_size, width // fsdp_size, fsdp_size, slice_width)
            .transpose(1, 2, 0, 3)
            .reshape(width // fsdp_size, hidden)
            .astype(F32)
        )

    out_rows = scatter_rows(jnp.dot(attended_t, grad_resid_b, preferred_element_type=F32))
    qkv_slice = scatter_sum(jnp.dot(mixed_t, all_norm, preferred_element_type=F32), 1)
    if packable and repeats == 1:
        deep = width // fsdp_size
        last = jnp.concatenate(
            [qkv_slice] + [out_rows[:, k * deep : (k + 1) * deep] for k in range(fsdp_size)],
            axis=0,
        )
        last = jnp.stack(ring_gather(last))
        grad_qkv, grad_out = expand_last(place, where, last, width, head_size)
    else:
        grad_out = gather(out_rows).reshape(-1, width).astype(F32)
        grad_qkv = (
            gather(qkv_slice)
            .reshape(ctx_size, 3, columns, width // fsdp_size)
            .transpose(3, 1, 0, 2)
            .reshape(width // fsdp_size, 3 * width)
            .astype(F32)
        )

    grad_norm_one = times_t(grad_mixed_t.T, qkv_blocks, width)
    normal_one, scale_one = stats(inputs)
    gain_tok = gains[0:1]
    for s in range(1, seq_count + 1):
        gain_tok = jnp.where(seg_col == s, gains[s : s + 1], gain_tok)
    grad_tokens = (
        grad_resid + stats_back(grad_norm_one * gain_tok, normal_one, scale_one)
    ).astype(BF16)
    film_terms = jnp.concatenate([grad_norm_one * normal_one, grad_norm_one], axis=1)
    film_sums = [
        jnp.sum(jnp.where(seg_col == s, film_terms, 0.0), axis=0)
        for s in range(seq_count + 1)
    ]
    branch = times(act_b, down_blocks, width) + bias_output
    output = (live * (resid + branch)).astype(BF16)

    sums = [
        jnp.sum(grad_norm_two * normal_two, axis=0),
        jnp.sum(grad_norm_two, axis=0),
        jnp.sum(grad_y, axis=0),
        grad_bias_up,
    ] + film_sums
    sizes = [vector.shape[0] for vector in sums]
    total = jnp.concatenate(sums)[None, :]
    for bit in range(bits):
        total = total + flip(total, bit)
    total = gather_small(total)
    split = []
    at = 0
    for size in sizes:
        split.append(total[:, at : at + size])
        at += size

    def own(vector):
        size = vector.shape[0] // fsdp_size
        return lax.dynamic_slice_in_dim(vector, shard * size, size, 0)

    sum_gain_two, sum_bias_two, sum_bias_down, sum_bias_up = (
        own(jnp.sum(vector, axis=0)) for vector in split[:4]
    )
    film_all = jnp.sum(sum(split[4:]), axis=0)
    sum_gain_one = own(film_all[:width])
    sum_bias_one = own(film_all[width:])
    film_grad = jnp.stack(split[4 : 4 + seq_count], axis=1).reshape(-1, 2 * width)
    embedded_rows = lax.dynamic_slice_in_dim(
        all_embedded.astype(F32).reshape(film_grad.shape[0], -1),
        shard * w_time.shape[0],
        w_time.shape[0],
        1,
    )
    grad_time = sum(
        embedded_rows[g][:, None] * film_grad[g][None, :]
        for g in range(film_grad.shape[0])
    )
    return (
        output[None],
        grad_tokens[None],
        grad_qkv,
        grad_out,
        grad_up,
        grad_down,
        grad_time,
        sum_gain_one,
        sum_bias_one,
        sum_gain_two,
        sum_bias_two,
        sum_bias_up,
        sum_bias_down,
    )


def solution(mesh):
    in_specs = (
        (P("fsdp", "ctx", None),)
        + (P("fsdp", None),) * 5
        + (P("fsdp"),) * 6
        + (P("fsdp", None), P("fsdp", None), P("fsdp", "ctx", None))
    )
    out_specs = (
        (P("fsdp", "ctx", None),) * 2 + (P("fsdp", None),) * 5 + (P("fsdp"),) * 6
    )
    return jax.shard_map(
        functools.partial(body, mesh.shape["ctx"], mesh.shape["fsdp"]),
        mesh=mesh,
        in_specs=in_specs,
        out_specs=out_specs,
        check_vma=False,
    )
```

```python
import functools
import math

import jax
import jax.numpy as jnp
import numpy as np
from jax import lax
from jax.experimental import pallas as pl
from jax.experimental.pallas import tpu as pltpu
from jax.sharding import PartitionSpec as P

HEADS = 16
EPSILON = 1e-05
NEGATIVE = -1e30
HIGH = lax.Precision.HIGHEST
F32 = jnp.float32
BF16 = jnp.bfloat16
VMEM_BYTES = 56 << 20


def dims(left, right, left_dim, right_dim):
    return lax.dot_general(
        left, right, (((left_dim,), (right_dim,)), ((), ())), preferred_element_type=F32
    )


def segments(ends, index):
    return sum((index >= end).astype(jnp.int32) for end in ends)


def positions(ends, index, segment):
    begin = jnp.zeros_like(index)
    for at, end in enumerate(ends):
        begin = jnp.where(segment > at, end, begin)
    return index - begin


def embed(steps_given, embed_width):
    half_width = embed_width // 2
    freq = jnp.exp(-math.log(10000.0) * jnp.arange(half_width, dtype=F32) / half_width)
    angle = steps_given.astype(F32)[..., None] * freq
    return jnp.concatenate([jnp.sin(angle), jnp.cos(angle)], axis=-1)


def stats(values):
    centre = jnp.mean(values, axis=-1, keepdims=True)
    centered = values - centre
    spread = jnp.mean(centered * centered, axis=-1, keepdims=True)
    scale = lax.rsqrt(spread + EPSILON)
    return centered * scale, scale


def stats_back(grad, normal, scale):
    return (
        grad
        - jnp.mean(grad, axis=-1, keepdims=True)
        - normal * jnp.mean(grad * normal, axis=-1, keepdims=True)
    ) * scale


def gelu_parts(pre):
    below = 0.5 * (1.0 + lax.erf(pre * math.sqrt(0.5)))
    density = jnp.exp(-0.5 * pre * pre) * (1.0 / math.sqrt(2.0 * math.pi))
    return pre * below, below + pre * density


def qkv_kernel(
    rows, head_size, first, ends_ref, base_ref, tokens_ref, gains_ref, shifts_ref, w_ref,
    cos_ref, sin_ref, *refs,
):
    norm_ref, query_t_ref, key_ref, key_t_ref, value_t_ref, pair_ref = refs[-6:]
    step = pl.program_id(0) + first
    block = tokens_ref.shape[0]
    seq_count = ends_ref.shape[0]
    half = head_size // 2
    values = tokens_ref[...].astype(F32)
    normal, _ = stats(values)
    chunks = block // rows

    def token_index(shape, axis):
        within = lax.broadcasted_iota(jnp.int32, shape, axis)
        index = within + base_ref[step * chunks]
        for at in range(1, chunks):
            index = jnp.where(
                within >= at * rows,
                within - at * rows + base_ref[step * chunks + at],
                index,
            )
        return index

    ends = [ends_ref[s] for s in range(seq_count)]
    seg_col = segments(ends, token_index((block, 1), 0))
    seg_row = segments(ends, token_index((1, block), 1))
    gains = gains_ref[0:1, :]
    shifts = shifts_ref[0:1, :]
    for s in range(1, seq_count + 1):
        gains = jnp.where(seg_col == s, gains_ref[s : s + 1, :], gains)
        shifts = jnp.where(seg_col == s, shifts_ref[s : s + 1, :], shifts)
    norm = (normal * gains + shifts).astype(BF16)
    norm_ref[...] = norm
    mixed = jnp.dot(norm, w_ref[...], preferred_element_type=F32)
    turned = mixed.T
    cos = cos_ref[...]
    sin = sin_ref[...]

    def turn(at):
        upper = turned[at : at + half]
        lower = turned[at + half : at + head_size]
        return jnp.concatenate(
            [upper * cos - lower * sin, lower * cos + upper * sin], axis=0
        ).astype(BF16)

    query = turn(0).astype(F32) * (float(head_size) ** -0.5)
    key = turn(head_size).astype(F32)
    value = turned[2 * head_size : 3 * head_size].astype(BF16).astype(F32)
    spare = 128 - head_size
    row_id = lax.broadcasted_iota(jnp.int32, (spare, block), 0)
    same = row_id == seg_row
    used = row_id <= seq_count
    key_tail = jnp.where(same & used, 1.0, 0.0)
    query_tail = jnp.where(used & jnp.logical_not(same), NEGATIVE, 0.0)
    query_t_ref[...] = jnp.concatenate([query, query_tail], axis=0).astype(BF16)
    key_t_ref[...] = key.astype(BF16)
    value_t_ref[...] = value.astype(BF16)
    key_ref[...] = jnp.concatenate([key, key_tail], axis=0).T.astype(BF16)
    pair_ref[...] = jnp.concatenate([value, query], axis=0).T.astype(BF16)


def attend_kernel(
    chunk, rows, place_ref, query_ref, key_ref, value_ref, out_ref, sent_ref, lse_ref, score_ref,
):
    core = place_ref[0] % 2
    count = key_ref.shape[0]
    query = query_ref[...]
    top = None
    for at in range(0, count, chunk):
        score = jnp.dot(key_ref[at : at + chunk, :], query, preferred_element_type=F32)
        score_ref[at : at + chunk, :] = score
        high = jnp.max(score, axis=0, keepdims=True)
        top = high if top is None else jnp.maximum(top, high)
    total = jnp.zeros_like(top)
    out = jnp.zeros(out_ref.shape, F32)
    for at in range(0, count, chunk):
        weight = jnp.exp(score_ref[at : at + chunk, :] - top)
        total = total + jnp.sum(weight, axis=0, keepdims=True)
        out = out + jnp.dot(
            value_ref[:, at : at + chunk],
            weight.astype(BF16),
            preferred_element_type=F32,
        )
    out = out / total
    out_ref[...] = out
    for at in range(sent_ref.shape[0]):
        sent_ref[at ^ core] = out[:, at * rows : (at + 1) * rows].astype(BF16)
    lse_ref[...] = top + jnp.log(total)


def attend_back_kernel(
    chunk, rows, head_size, place_ref, query_ref, grad_ref, out_ref, lse_ref, key_ref, key_t_ref, pair_ref,
    pair_block_ref, cos_block_ref, sin_block_ref, cos_ref, sin_ref, mixed_ref, sent_ref, key_acc, value_acc,
):
    step = pl.program_id(0)
    core = place_ref[0] % 2
    per_step = grad_ref.shape[0]
    count = key_ref.shape[0]
    block = query_ref.shape[1]
    half = head_size // 2
    scale = float(head_size) ** -0.5

    @pl.when(step == 0)
    def _():
        key_acc[...] = jnp.zeros_like(key_acc)
        value_acc[...] = jnp.zeros_like(value_acc)

    query = query_ref[...]
    grad = jnp.concatenate(
        [grad_ref[at ^ core] for at in range(per_step)], axis=1
    ).astype(F32)
    delta = jnp.sum(grad * out_ref[...], axis=0, keepdims=True)
    lse = lse_ref[...]
    grad_t = jnp.concatenate(
        [grad, jnp.zeros((128 - head_size, block), F32)], axis=0
    )
    grad_rows = grad_t.T.astype(BF16)
    grad_t = grad_t.astype(BF16)
    pair = pair_block_ref[...]
    grad_query = jnp.zeros((head_size, block), F32)
    for at in range(0, count, chunk):
        part = slice(at, at + chunk)
        score = jnp.dot(key_ref[part, :], query, preferred_element_type=F32)
        prob = jnp.exp(score - lse)
        grad_prob = jnp.dot(pair_ref[part, :], grad_t, preferred_element_type=F32)
        grad_score = (prob * (grad_prob - delta)).astype(BF16)
        grad_query = grad_query + jnp.dot(
            key_t_ref[:, part], grad_score, preferred_element_type=F32
        )
        key_acc[part, :] += jnp.dot(grad_score, pair, preferred_element_type=F32)
        value_acc[part, :] += jnp.dot(
            prob.astype(BF16), grad_rows, preferred_element_type=F32
        )

    def turn_back(values, cos, sin):
        upper = values[:half]
        lower = values[half:]
        return jnp.concatenate(
            [upper * cos + lower * sin, lower * cos - upper * sin], axis=0
        ).astype(BF16)

    at = pl.multiple_of(step * block, block)
    query_part = turn_back(
        grad_query * scale, cos_block_ref[...], sin_block_ref[...]
    )
    mixed_ref[0:head_size, pl.ds(at, block)] = query_part
    for k in range(per_step):
        sent_ref[place_ref[step * per_step + k], 0:head_size, :] = query_part[
            :, k * rows : (k + 1) * rows
        ]

    @pl.when(step == pl.num_programs(0) - 1)
    def _():
        key_part = turn_back(
            key_acc[...].T[head_size : 2 * head_size], cos_ref[...], sin_ref[...]
        )
        value_part = value_acc[...].T[:head_size].astype(BF16)
        both = jnp.concatenate([key_part, value_part], axis=0)
        mixed_ref[head_size : 3 * head_size, :] = both
        for k in range(count // rows):
            sent_ref[place_ref[k], head_size : 3 * head_size, :] = both[
                :, k * rows : (k + 1) * rows
            ]


def whole(shape):
    return pl.BlockSpec(shape, lambda i, *_: (0,) * len(shape))


def project(
    tokens, base, ends, gains, shifts, w_head, cos, sin, rows, head_size, first=0, earlier=None,
):
    width = tokens.shape[1]
    count = base.shape[0] * rows
    block = min(count, 2 * rows)
    earlier = list(earlier or ())
    grid_spec = pltpu.PrefetchScalarGridSpec(
        num_scalar_prefetch=2,
        grid=(tokens.shape[0] // block,),
        in_specs=[
            pl.BlockSpec((block, width), lambda i, *_: (i, 0)),
            whole(gains.shape),
            whole(shifts.shape),
            whole(w_head.shape),
            pl.BlockSpec((head_size // 2, block), lambda i, *_: (0, i + first)),
            pl.BlockSpec((head_size // 2, block), lambda i, *_: (0, i + first)),
        ]
        + [pl.BlockSpec(memory_space=pl.ANY)] * len(earlier),
        out_specs=[
            pl.BlockSpec((block, width), lambda i, *_: (i + first, 0)),
            pl.BlockSpec((128, block), lambda i, *_: (0, i + first)),
            pl.BlockSpec((block, 128), lambda i, *_: (i + first, 0)),
            pl.BlockSpec((head_size, block), lambda i, *_: (0, i + first)),
            pl.BlockSpec((head_size, block), lambda i, *_: (0, i + first)),
            pl.BlockSpec((block, 128), lambda i, *_: (i + first, 0)),
        ],
    )
    return pl.pallas_call(
        functools.partial(qkv_kernel, rows, head_size, first),
        grid_spec=grid_spec,
        out_shape=[
            jax.ShapeDtypeStruct((count, width), BF16),
            jax.ShapeDtypeStruct((128, count), BF16),
            jax.ShapeDtypeStruct((count, 128), BF16),
            jax.ShapeDtypeStruct((head_size, count), BF16),
            jax.ShapeDtypeStruct((head_size, count), BF16),
            jax.ShapeDtypeStruct((count, 128), BF16),
        ],
        input_output_aliases={8 + k: k for k in range(len(earlier))},
        compiler_params=pltpu.CompilerParams(vmem_limit_bytes=VMEM_BYTES),
        cost_estimate=pl.CostEstimate(
            flops=2 * tokens.shape[0] * width * 1024,
            bytes_accessed=4 * tokens.shape[0] * width,
            transcendentals=0,
        ),
        name="project_head",
    )(ends, base, tokens, gains, shifts, w_head, cos, sin, *earlier)


def project_chunks_kernel(rows, head_size, first, chunks, who_ref, ends_ref, base_ref, *refs):
    tokens = refs[:chunks]
    gains_ref, shifts_ref, own_ref, other_ref, cos_ref, sin_ref = refs[chunks : chunks + 6]
    block_ref, w_ref = refs[-2:]
    step = pl.program_id(0)
    size = own_ref.shape[0]

    @pl.when(step == 0)
    def _():
        w_ref[:, 128:] = jnp.zeros((2 * size, 128), BF16)
        shard = who_ref[1]
        own_at = pl.multiple_of(shard * size, size)
        other_at = pl.multiple_of((1 - shard) * size, size)
        width = own_ref.shape[1]
        w_ref[pl.ds(own_at, size), :width] = own_ref[...]
        w_ref[pl.ds(other_at, size), :width] = other_ref[...]

    for at in range(chunks // 2):

        @pl.when(step == at)
        def _():
            block_ref[:rows] = tokens[2 * at][...]
            block_ref[rows:] = tokens[2 * at + 1][...]

    qkv_kernel(
        rows, head_size, first, ends_ref, base_ref, block_ref, gains_ref, shifts_ref, w_ref,
        cos_ref, sin_ref, *refs[-8:-2],
    )


def project_chunks(
    who, tokens, base, ends, gains, shifts, w_own, w_other, cos, sin, head_size, first=0, earlier=None,
):
    rows, width = tokens[0].shape
    count = base.shape[0] * rows
    block = 2 * rows
    earlier = list(earlier or ())
    grid_spec = pltpu.PrefetchScalarGridSpec(
        num_scalar_prefetch=3,
        grid=(len(tokens) // 2,),
        in_specs=[whole((rows, width))] * len(tokens)
        + [
            whole(gains.shape),
            whole(shifts.shape),
            whole(w_own.shape),
            whole(w_other.shape),
            pl.BlockSpec((head_size // 2, block), lambda i, *_: (0, i + first)),
            pl.BlockSpec((head_size // 2, block), lambda i, *_: (0, i + first)),
        ]
        + [pl.BlockSpec(memory_space=pl.ANY)] * len(earlier),
        out_specs=[
            pl.BlockSpec((block, width), lambda i, *_: (i + first, 0)),
            pl.BlockSpec((128, block), lambda i, *_: (0, i + first)),
            pl.BlockSpec((block, 128), lambda i, *_: (i + first, 0)),
            pl.BlockSpec((head_size, block), lambda i, *_: (0, i + first)),
            pl.BlockSpec((head_size, block), lambda i, *_: (0, i + first)),
            pl.BlockSpec((block, 128), lambda i, *_: (i + first, 0)),
        ],
        scratch_shapes=[
            pltpu.VMEM((block, width), BF16),
            pltpu.VMEM((width, 256), BF16),
        ],
    )
    return pl.pallas_call(
        functools.partial(project_chunks_kernel, rows, head_size, first, len(tokens)),
        grid_spec=grid_spec,
        out_shape=[
            jax.ShapeDtypeStruct((count, width), BF16),
            jax.ShapeDtypeStruct((128, count), BF16),
            jax.ShapeDtypeStruct((count, 128), BF16),
            jax.ShapeDtypeStruct((head_size, count), BF16),
            jax.ShapeDtypeStruct((head_size, count), BF16),
            jax.ShapeDtypeStruct((count, 128), BF16),
        ],
        input_output_aliases={9 + len(tokens) + k: k for k in range(len(earlier))},
        compiler_params=pltpu.CompilerParams(vmem_limit_bytes=VMEM_BYTES),
        cost_estimate=pl.CostEstimate(
            flops=2 * len(tokens) * rows * width * 1024,
            bytes_accessed=4 * len(tokens) * rows * width,
            transcendentals=0,
        ),
        name="project_chunks",
    )(who, ends, base, *tokens, gains, shifts, w_own, w_other, cos, sin, *earlier)


def attend(place, query_t, key, value_t, rows):
    count = key.shape[0]
    head_size = value_t.shape[0]
    block = min(count, 2 * rows)
    chunk = min(count, 512)
    grid_spec = pltpu.PrefetchScalarGridSpec(
        num_scalar_prefetch=1,
        grid=(count // block,),
        in_specs=[
            pl.BlockSpec((128, block), lambda i, _: (0, i)),
            whole((count, 128)),
            whole((head_size, count)),
        ],
        out_specs=[
            pl.BlockSpec((head_size, block), lambda i, _: (0, i)),
            pl.BlockSpec(
                (2, head_size, rows), lambda i, place: (place[2 * i] // 2, 0, 0)
            ),
            pl.BlockSpec((1, block), lambda i, _: (0, i)),
        ],
        scratch_shapes=[pltpu.VMEM((count, block), F32)],
    )
    return pl.pallas_call(
        functools.partial(attend_kernel, chunk, rows),
        grid_spec=grid_spec,
        out_shape=[
            jax.ShapeDtypeStruct((head_size, count), F32),
            jax.ShapeDtypeStruct((count // rows, head_size, rows), BF16),
            jax.ShapeDtypeStruct((1, count), F32),
        ],
        compiler_params=pltpu.CompilerParams(vmem_limit_bytes=VMEM_BYTES),
        cost_estimate=pl.CostEstimate(
            flops=8 * count * count * 128,
            bytes_accessed=8 * count * 128,
            transcendentals=count * count,
        ),
        name="attend_head",
    )(place, query_t, key, value_t)


def attend_back(place, query_t, grad, out, lse, key, key_t, pair, cos, sin, rows):
    count = key.shape[0]
    head_size = key_t.shape[0]
    half = head_size // 2
    block = min(count, 2 * rows)
    chunk = min(count, 512)
    grid_spec = pltpu.PrefetchScalarGridSpec(
        num_scalar_prefetch=1,
        grid=(count // block,),
        in_specs=[
            pl.BlockSpec((128, block), lambda i, _: (0, i)),
            pl.BlockSpec(
                (2, head_size, rows), lambda i, place: (place[2 * i] // 2, 0, 0)
            ),
            pl.BlockSpec((head_size, block), lambda i, _: (0, i)),
            pl.BlockSpec((1, block), lambda i, _: (0, i)),
            whole((count, 128)),
            whole((head_size, count)),
            whole((count, 128)),
            pl.BlockSpec((block, 128), lambda i, _: (i, 0)),
            pl.BlockSpec((half, block), lambda i, _: (0, i)),
            pl.BlockSpec((half, block), lambda i, _: (0, i)),
            whole((half, count)),
            whole((half, count)),
        ],
        out_specs=[
            whole((3 * head_size, count)),
            whole((count // rows, 3 * head_size, rows)),
        ],
        scratch_shapes=[pltpu.VMEM((count, 128), F32), pltpu.VMEM((count, 128), F32)],
    )
    return pl.pallas_call(
        functools.partial(attend_back_kernel, chunk, rows, head_size),
        grid_spec=grid_spec,
        out_shape=[
            jax.ShapeDtypeStruct((3 * head_size, count), BF16),
            jax.ShapeDtypeStruct((count // rows, 3 * head_size, rows), BF16),
        ],
        compiler_params=pltpu.CompilerParams(vmem_limit_bytes=VMEM_BYTES),
        cost_estimate=pl.CostEstimate(
            flops=20 * count * count * 128,
            bytes_accessed=16 * count * 128,
            transcendentals=count * count,
        ),
        name="attend_head_back",
    )(place, query_t, grad, out, lse, key, key_t, pair, pair, cos, sin, cos, sin)


def slices_kernel(chunks, me_ref, *refs):
    norms = refs[:chunks]
    grads = refs[chunks : 2 * chunks]
    up_own, up_other, down_own, down_other, bias_ref, out_ref, down_w, down_acc, up_acc, up_t = refs[
        2 * chunks :
    ]
    shard = me_ref[1]
    size, units = up_own.shape
    width = 2 * size
    half = units // 2
    own_at = pl.multiple_of(shard * size, size)
    other_at = pl.multiple_of((1 - shard) * size, size)
    down_w[:half] = down_own[...]
    down_w[half:] = down_other[...]
    for c in range(0, chunks, 2):
        own = jnp.concatenate(
            [norms[c + j][:, pl.ds(own_at, size)] for j in range(2)], axis=0
        )
        other = jnp.concatenate(
            [norms[c + j][:, pl.ds(other_at, size)] for j in range(2)], axis=0
        )
        pre = jnp.dot(own, up_own[...], preferred_element_type=F32)
        pre = pre + jnp.dot(other, up_other[...], preferred_element_type=F32)
        act, slope = gelu_parts(pre + bias_ref[...])
        grad_y = jnp.concatenate([grads[c][...], grads[c + 1][...]], axis=0)
        grad = dims(grad_y, down_w[...], 1, 1) * slope
        norm = jnp.concatenate([norms[c][...], norms[c + 1][...]], axis=0)
        down = jnp.dot(act.T.astype(BF16), grad_y, preferred_element_type=F32)
        up = jnp.dot(grad.T.astype(BF16), norm, preferred_element_type=F32)
        if c == 0:
            down_acc[...] = down
            up_acc[...] = up
        else:
            down_acc[...] += down
            up_acc[...] += up
    up_t[...] = up_acc[...].T
    first = pl.multiple_of(shard * size, size)
    second = pl.multiple_of((1 - shard) * size, size)
    for at, rows in enumerate((own_at, other_at)):
        values = up_t[pl.ds(rows, size), :]
        out_ref[at, pl.ds(first, size), :] = values[:, :half]
        out_ref[at, pl.ds(second, size), :] = values[:, half:]
        for k in range(width // half):
            out_ref[at, width + k * half : width + (k + 1) * half, :] = down_acc[
                at * half : (at + 1) * half, k * half : (k + 1) * half
            ]


def slices(me, norms, grads, up_own, up_other, down_own, down_other, bias):
    size, units = up_own.shape
    width = 2 * size
    chunks = len(norms)
    count = chunks * norms[0].shape[0]
    vmem = pl.BlockSpec(memory_space=pltpu.VMEM)
    return pl.pallas_call(
        functools.partial(slices_kernel, chunks),
        in_specs=[pl.BlockSpec(memory_space=pltpu.SMEM)] + [vmem] * (2 * chunks + 5),
        out_specs=vmem,
        out_shape=jax.ShapeDtypeStruct((2, 2 * width, units // 2), F32),
        scratch_shapes=[
            pltpu.VMEM((units, width), BF16),
            pltpu.VMEM((units, width), F32),
            pltpu.VMEM((units, width), F32),
            pltpu.VMEM((width, units), F32),
        ],
        compiler_params=pltpu.CompilerParams(vmem_limit_bytes=VMEM_BYTES),
        cost_estimate=pl.CostEstimate(
            flops=8 * count * width * units,
            bytes_accessed=4 * count * width,
            transcendentals=2 * count * units,
        ),
        name="feed_forward_slices",
    )(me, *norms, *grads, up_own, up_other, down_own, down_other, bias)


def row_starts(who_ref, size):
    core = who_ref[0] % 2
    shard = who_ref[1]
    half = size // 2
    other = (1 - shard) * size
    return (
        pl.multiple_of(shard * size, size),
        pl.multiple_of(other + core * half, half),
        pl.multiple_of(other + (1 - core) * half, half),
    )


def middle_kernel(
    who_ref, att_ref, own_ref, mine_ref, flip_ref, tokens_ref, gain_ref, bias_ref,
    resid_ref, normal_ref, scale_ref, norm_ref, turned,
):
    turned[...] = att_ref[...].astype(F32).T.astype(BF16)
    resid = tokens_ref[...].astype(F32)
    pieces = (own_ref, mine_ref, flip_ref)
    for at, piece in zip(row_starts(who_ref, own_ref.shape[0]), pieces):
        resid = resid + jnp.dot(
            turned[:, pl.ds(at, piece.shape[0])],
            piece[...],
            preferred_element_type=F32,
        )
    resid_ref[...] = resid
    normal, scale = stats(resid)
    normal_ref[...] = normal
    scale_ref[...] = scale
    norm_ref[...] = (normal * gain_ref[...] + bias_ref[...]).astype(BF16)


def middle(who, attended, pieces, tokens, gain, bias):
    rows, width = tokens.shape
    vmem = pl.BlockSpec(memory_space=pltpu.VMEM)
    return pl.pallas_call(
        middle_kernel,
        in_specs=[pl.BlockSpec(memory_space=pltpu.SMEM)] + [vmem] * 7,
        out_specs=[vmem] * 4,
        out_shape=[
            jax.ShapeDtypeStruct((rows, width), F32),
            jax.ShapeDtypeStruct((rows, width), F32),
            jax.ShapeDtypeStruct((rows, 1), F32),
            jax.ShapeDtypeStruct((rows, width), BF16),
        ],
        scratch_shapes=[pltpu.VMEM((rows, width), BF16)],
        compiler_params=pltpu.CompilerParams(vmem_limit_bytes=VMEM_BYTES),
        cost_estimate=pl.CostEstimate(
            flops=8 * rows * width * width,
            bytes_accessed=4 * width * width,
            transcendentals=0,
        ),
        name="output_projection",
    )(who, attended, *pieces, tokens, gain, bias)


def feed_kernel(parts, who_ref, norm_ref, own_ref, *refs):
    pieces = refs[: 4 * parts]
    (
        near_ref, far_ref, bias_ref, normal_ref, scale_ref, gain_ref, grad_y_ref, out_own, out_mine,
        out_flip, act_ref, resid_ref, resid_b_ref, att_ref, sums_ref, grad_ref,
    ) = refs[4 * parts :]
    side = who_ref[0] % 4
    shard = who_ref[1]
    size, hidden = own_ref.shape
    quarter = hidden // 4
    deep = size // parts
    own_at = pl.multiple_of(shard * size, size)
    other_at = pl.multiple_of((1 - shard) * size, size)
    own_norm = norm_ref[:, pl.ds(own_at, size)]
    part_at = [pl.multiple_of(other_at + p * deep, deep) for p in range(parts)]
    norms = [norm_ref[:, pl.ds(at, deep)] for at in part_at]
    for k in range(4):
        block = side ^ k
        columns = pl.ds(pl.multiple_of(block * quarter, quarter), quarter)
        weight = own_ref[:, columns]
        pre = jnp.dot(own_norm, weight, preferred_element_type=F32)
        for p in range(parts):
            pre = pre + jnp.dot(
                norms[p], pieces[4 * p + k][...], preferred_element_type=F32
            )
        act, slope = gelu_parts(pre + bias_ref[:, columns])
        act_ref[:, columns] = act.astype(BF16)
        within = pl.ds(pl.multiple_of((block % 2) * quarter, quarter), quarter)
        near = near_ref[:, within]
        far = far_ref[:, within].astype(F32)
        grad = jnp.where(block // 2 == shard, near, far) * slope
        sums_ref[pl.ds(3 + block, 1), :] = jnp.sum(grad, axis=0, keepdims=True)
        grad = grad.astype(BF16)
        terms = [(own_at, size, weight)]
        terms += [(part_at[p], deep, pieces[4 * p + k][...]) for p in range(parts)]
        for at, length, piece in terms:
            term = dims(grad, piece, 1, 1)
            if k == 0:
                grad_ref[:, pl.ds(at, length)] = term
            else:
                grad_ref[:, pl.ds(at, length)] += term
    grad = grad_ref[...]
    normal = normal_ref[...]
    grad_y = grad_y_ref[...].astype(F32)
    sums_ref[0:1, :] = jnp.sum(grad * normal, axis=0, keepdims=True)
    sums_ref[1:2, :] = jnp.sum(grad, axis=0, keepdims=True)
    sums_ref[2:3, :] = jnp.sum(grad_y, axis=0, keepdims=True)
    sums_ref[7:8, :] = jnp.zeros((1, quarter), F32)
    resid = grad_y + stats_back(grad * gain_ref[...], normal, scale_ref[...])
    resid_ref[...] = resid
    resid = resid.astype(BF16)
    resid_b_ref[...] = resid
    out_pieces = (out_own, out_mine, out_flip)
    for at, piece in zip(row_starts(who_ref, out_own.shape[0]), out_pieces):
        att_ref[pl.ds(at, piece.shape[0]), :] = dims(piece[...], resid, 1, 1).astype(
            BF16
        )


def feed(who, norm, own, pieces, near, far, bias, normal, scale, gain, grad_y, out_pieces):
    rows, width = norm.shape
    hidden = own.shape[1]
    vmem = pl.BlockSpec(memory_space=pltpu.VMEM)
    return pl.pallas_call(
        functools.partial(feed_kernel, len(pieces) // 4),
        in_specs=[pl.BlockSpec(memory_space=pltpu.SMEM)] + [vmem] * (12 + len(pieces)),
        out_specs=[vmem] * 5,
        out_shape=[
            jax.ShapeDtypeStruct((rows, hidden), BF16),
            jax.ShapeDtypeStruct((rows, width), F32),
            jax.ShapeDtypeStruct((rows, width), BF16),
            jax.ShapeDtypeStruct((width, rows), BF16),
            jax.ShapeDtypeStruct((8, width), F32),
        ],
        scratch_shapes=[pltpu.VMEM((rows, width), F32)],
        compiler_params=pltpu.CompilerParams(vmem_limit_bytes=VMEM_BYTES),
        cost_estimate=pl.CostEstimate(
            flops=16 * rows * width * hidden,
            bytes_accessed=4 * width * hidden,
            transcendentals=2 * rows * hidden,
        ),
        name="feed_forward",
    )(who, norm, own, *pieces, near, far, bias, normal, scale, gain, grad_y, *out_pieces)


def first_back_kernel(
    head_size, who_ref, ends_ref, got_ref, own_ref, mine_ref, flip_ref, tokens_ref, resid_ref,
    gains_ref, sums_ref, grad_ref, total_ref, mixed, turned,
):
    heads = got_ref.shape[0]
    rows, width = tokens_ref.shape
    seq_count = ends_ref.shape[0]
    for h in range(heads):
        for k in range(3):
            at = k * width + h * head_size
            mixed[at : at + head_size, :] = got_ref[
                h, k * head_size : (k + 1) * head_size, :
            ]
    pieces = (own_ref, mine_ref, flip_ref)
    for at, piece in zip(row_starts(who_ref, own_ref.shape[0]), pieces):
        turned[pl.ds(at, piece.shape[0]), :] = jnp.dot(
            piece[...], mixed[...], preferred_element_type=F32
        )
    grad = turned[...].T
    normal, scale = stats(tokens_ref[...].astype(F32))
    index = who_ref[0] * rows + lax.broadcasted_iota(jnp.int32, (rows, 1), 0)
    segment = segments([ends_ref[s] for s in range(seq_count)], index)
    gains = gains_ref[0:1, :]
    for s in range(1, seq_count + 1):
        gains = jnp.where(segment == s, gains_ref[s : s + 1, :], gains)
    grad_ref[...] = (
        resid_ref[...] + stats_back(grad * gains, normal, scale)
    ).astype(BF16)
    total_ref[0:8, :] = sums_ref[...]
    product = grad * normal
    for s in range(seq_count + 1):
        here = segment == s
        for k, terms in enumerate((product, grad)):
            total_ref[8 + 2 * s + k : 9 + 2 * s + k, :] = jnp.sum(
                jnp.where(here, terms, 0.0), axis=0, keepdims=True
            )


def first_back(who, ends, got, pieces, tokens, resid, gains, sums):
    rows, width = tokens.shape
    heads, tall, _ = got.shape
    seq_count = ends.shape[0]
    lines = 8 + 2 * (seq_count + 1)
    vmem = pl.BlockSpec(memory_space=pltpu.VMEM)
    return pl.pallas_call(
        functools.partial(first_back_kernel, tall // 3),
        in_specs=[pl.BlockSpec(memory_space=pltpu.SMEM)] * 2 + [vmem] * 8,
        out_specs=[vmem] * 2,
        out_shape=[
            jax.ShapeDtypeStruct((rows, width), BF16),
            jax.ShapeDtypeStruct((lines, width), F32),
        ],
        scratch_shapes=[
            pltpu.VMEM((3 * width, rows), BF16),
            pltpu.VMEM((width, rows), F32),
        ],
        compiler_params=pltpu.CompilerParams(vmem_limit_bytes=VMEM_BYTES),
        cost_estimate=pl.CostEstimate(
            flops=12 * rows * width * width,
            bytes_accessed=8 * width * width,
            transcendentals=0,
        ),
        name="first_norm_back",
    )(who, ends, got, *pieces, tokens, resid, gains, sums)


def small_kernel(seq_count, top, chunks, who_ref, own_embed, other_embed, *refs):
    parts = refs[:chunks]
    (
        time_ref, gain_one, bias_one, gain_two, bias_two, bias_up, bias_down, total,
    ) = refs[chunks:]
    lines, width = total.shape
    half = width // 2
    shard = who_ref[1]
    for k in range(width // 128):
        at = top + k * lines
        value = parts[0][at : at + lines, :].astype(F32)
        for ref in parts[1:]:
            value = value + ref[at : at + lines, :].astype(F32)
        total[:, k * 128 : (k + 1) * 128] = value
    part = pl.ds(pl.multiple_of(shard * half, half), half)
    gain_two[...] = total[0:1, part]
    bias_two[...] = total[1:2, part]
    bias_down[...] = total[2:3, part]
    bias_up[:, :width] = total[pl.ds(3 + 2 * shard, 1), :]
    bias_up[:, width:] = total[pl.ds(4 + 2 * shard, 1), :]
    films = 2 * (seq_count + 1)
    gain = total[8:9, part]
    bias = total[9:10, part]
    for s in range(1, films):
        gain = gain + total[8 + 2 * s : 9 + 2 * s, part]
        bias = bias + total[9 + 2 * s : 10 + 2 * s, part]
    gain_one[...] = gain
    bias_one[...] = bias
    for k in range(2):
        value = None
        for g, embed_ref in enumerate((own_embed, other_embed)):
            for s in range(seq_count):
                line = 8 + g * films + 2 * s + k
                term = embed_ref[:, s : s + 1] * total[line : line + 1, :]
                value = term if value is None else value + term
        time_ref[:, k * width : (k + 1) * width] = value


def small_sums(who, own_embed, other_embed, parts, top, lines, width):
    vmem = pl.BlockSpec(memory_space=pltpu.VMEM)
    return pl.pallas_call(
        functools.partial(small_kernel, own_embed.shape[1], top, len(parts)),
        in_specs=[pl.BlockSpec(memory_space=pltpu.SMEM)] + [vmem] * (2 + len(parts)),
        out_specs=[vmem] * 7,
        out_shape=[jax.ShapeDtypeStruct((own_embed.shape[0], 2 * width), F32)]
        + [jax.ShapeDtypeStruct((1, width // 2), F32)] * 4
        + [
            jax.ShapeDtypeStruct((1, 2 * width), F32),
            jax.ShapeDtypeStruct((1, width // 2), F32),
        ],
        scratch_shapes=[pltpu.VMEM((lines, width), F32)],
        compiler_params=pltpu.CompilerParams(vmem_limit_bytes=VMEM_BYTES),
        cost_estimate=pl.CostEstimate(
            flops=1000000, bytes_accessed=2000000, transcendentals=0
        ),
        name="small_gradients",
    )(who, own_embed, other_embed, *parts)


def stream(chips, copies_of, fill):
    pending = [None, None]
    for at in range(chips):
        slot = at % 2
        if pending[slot] is not None:
            for copy in pending[slot]:
                copy.wait()
        fill(at, slot)
        pending[slot] = copies_of(at, slot)
        for copy in pending[slot]:
            copy.start()
    for copies in pending:
        if copies is not None:
            for copy in copies:
                copy.wait()


def wide_kernel(first, chunks, place_ref, *refs):
    parts = refs[:chunks]
    up_ref, down_ref, out_ref, up_slots, down_slots, out_slots, sems = refs[-7:]
    core = place_ref[0] % 2
    deep = out_slots.shape[1] // 2
    size = up_ref.shape[0]
    hidden = up_ref.shape[1]
    width = down_ref.shape[1]

    def fill(at, slot):
        for j in range(2):
            ref = parts[2 * at + j]
            column = pl.ds(pl.multiple_of((j ^ core) * 128, 128), 128)
            for k in range(2):
                up_slots[slot, k, :, column] = ref[k * size : (k + 1) * size, :].astype(
                    F32
                )
            row = pl.ds(pl.multiple_of((j ^ core) * 128, 128), 128)
            for k in range(width // 128):
                top = 2 * size + k * 128
                down_slots[slot, row, k * 128 : (k + 1) * 128] = ref[
                    top : top + 128, :
                ].astype(F32)
            row = pl.ds(pl.multiple_of((j ^ core) * deep, deep), deep)
            for k in range(width // 128):
                top = 2 * size + width + k * deep
                out_slots[slot, row, k * 128 : (k + 1) * 128] = ref[
                    top : top + deep, :
                ].astype(F32)

    def copies_of(at, slot):
        chip = place_ref[2 * (at + first)] // 2
        copies = []
        for k in range(2):
            column = pl.multiple_of(k * (hidden // 2) + chip * 256, 256)
            copies.append(
                pltpu.make_async_copy(
                    up_slots.at[slot, k],
                    up_ref.at[:, pl.ds(column, 256)],
                    sems.at[slot, k],
                )
            )
        row = pl.multiple_of(chip * 256, 256)
        copies.append(
            pltpu.make_async_copy(
                down_slots.at[slot], down_ref.at[pl.ds(row, 256), :], sems.at[slot, 2]
            )
        )
        row = pl.multiple_of(chip * 2 * deep, 2 * deep)
        copies.append(
            pltpu.make_async_copy(
                out_slots.at[slot], out_ref.at[pl.ds(row, 2 * deep), :], sems.at[slot, 3]
            )
        )
        return copies

    stream(chunks // 2, copies_of, fill)


def expand_wide(place, first, parts, width, earlier):
    devices = place.shape[0]
    size = width // 2
    vmem = pl.BlockSpec(memory_space=pltpu.VMEM)
    hbm = pl.BlockSpec(memory_space=pl.ANY)
    return pl.pallas_call(
        functools.partial(wide_kernel, first, len(parts)),
        in_specs=[pl.BlockSpec(memory_space=pltpu.SMEM)]
        + [vmem] * len(parts)
        + [hbm] * len(earlier),
        out_specs=[hbm, hbm, hbm],
        out_shape=[
            jax.ShapeDtypeStruct((size, 2 * devices * 128), F32),
            jax.ShapeDtypeStruct((devices * 128, width), F32),
            jax.ShapeDtypeStruct((size, width), F32),
        ],
        scratch_shapes=[
            pltpu.VMEM((2, 2, size, 256), F32),
            pltpu.VMEM((2, 256, width), F32),
            pltpu.VMEM((2, 2 * size // devices, width), F32),
            pltpu.SemaphoreType.DMA((2, 4)),
        ],
        input_output_aliases={1 + len(parts) + k: k for k in range(len(earlier))},
        compiler_params=pltpu.CompilerParams(vmem_limit_bytes=VMEM_BYTES),
        cost_estimate=pl.CostEstimate(
            flops=parts[0].size * len(parts),
            bytes_accessed=6 * parts[0].size * len(parts),
            transcendentals=0,
        ),
        name="expand_wide",
    )(place, *parts, *earlier)


def last_kernel(head_size, width, chunks, place_ref, *refs):
    parts = refs[:chunks]
    qkv_ref, slots, sems = refs[-3:]
    core = place_ref[0] % 2

    def fill(at, slot):
        for k in range(3):
            part = slice(k * head_size, (k + 1) * head_size)
            mine = parts[2 * at][part, :].astype(F32)
            flip = parts[2 * at + 1][part, :].astype(F32)
            both = jnp.concatenate(
                [jnp.where(core == 0, mine, flip), jnp.where(core == 0, flip, mine)],
                axis=0,
            )
            slots[slot, k] = both.T

    def copies_of(at, slot):
        chip = place_ref[2 * at] // 2
        copies = []
        for k in range(3):
            column = pl.multiple_of(k * width + chip * 2 * head_size, 128)
            copies.append(
                pltpu.make_async_copy(
                    slots.at[slot, k],
                    qkv_ref.at[:, pl.ds(column, 2 * head_size)],
                    sems.at[slot, k],
                )
            )
        return copies

    stream(chunks // 2, copies_of, fill)


def expand_last(place, parts, head_size):
    depth = parts[0].shape[1]
    width = place.shape[0] * head_size
    vmem = pl.BlockSpec(memory_space=pltpu.VMEM)
    return pl.pallas_call(
        functools.partial(last_kernel, head_size, width, len(parts)),
        in_specs=[pl.BlockSpec(memory_space=pltpu.SMEM)] + [vmem] * len(parts),
        out_specs=pl.BlockSpec(memory_space=pl.ANY),
        out_shape=jax.ShapeDtypeStruct((depth, 3 * width), F32),
        scratch_shapes=[
            pltpu.VMEM((2, 3, depth, 2 * head_size), F32),
            pltpu.SemaphoreType.DMA((2, 3)),
        ],
        compiler_params=pltpu.CompilerParams(vmem_limit_bytes=VMEM_BYTES),
        cost_estimate=pl.CostEstimate(
            flops=parts[0].size * len(parts),
            bytes_accessed=6 * parts[0].size * len(parts),
            transcendentals=0,
        ),
        name="expand_last",
    )(place, *parts)


def times_rows(values, pieces):
    return sum(
        jnp.dot(
            lax.dynamic_slice_in_dim(values, at, piece.shape[0], 1),
            piece,
            preferred_element_type=F32,
        )
        for piece, at in pieces
    )


def times_rows_t(values_t, pieces):
    return sum(
        dims(lax.dynamic_slice_in_dim(values_t, at, piece.shape[0], 0), piece, 0, 0)
        for piece, at in pieces
    )


def joined(parts, pieces, dim):
    if len(parts) == 1:
        return parts[0]
    shape = list(parts[0].shape)
    shape[dim] = sum(part.shape[dim] for part in parts)
    out = jnp.zeros(shape, parts[0].dtype)
    for part, (_, at) in zip(parts, pieces):
        out = lax.dynamic_update_slice_in_dim(out, part, at, dim)
    return out


def rows_of(pieces, start, size):
    out = None
    for piece, at in pieces:
        length = piece.shape[0]
        local = jnp.clip(start - at, 0, length - size)
        found = lax.dynamic_slice_in_dim(piece, local, size, 0)
        inside = (start >= at) & (start < at + length)
        out = found if out is None else jnp.where(inside, found, out)
    return out


def body_general(
    ctx_size, fsdp_size,
    tokens, w_qkv, w_out, w_up, w_down, w_time, gain_one, bias_one, gain_two, bias_two, bias_up,
    bias_down, lengths, time_steps, cotangent,
):
    me = lax.axis_index("ctx")
    shard = lax.axis_index("fsdp")
    rows = tokens.shape[1]
    width = tokens.shape[2]
    count = rows * ctx_size
    head_size = width // HEADS
    repeats = ctx_size // HEADS
    columns = head_size // repeats
    seq_count = lengths.shape[1]
    hidden = w_up.shape[1]

    def gather_small(values):
        return lax.all_gather(values, "fsdp", axis=0, tiled=True)

    def fetch(weight):
        return [(gather_small(weight), 0)]

    def scatter_sum(values, dim):
        return lax.psum_scatter(
            values.astype(BF16), "fsdp", scatter_dimension=dim, tiled=True
        )

    def gather(values):
        return lax.all_gather(values, "ctx", axis=0, tiled=False)

    ends = []
    for s in range(seq_count):
        ends.append(lengths[0, s] + (ends[-1] if ends else 0))
    ends_vector = jnp.stack(ends)
    index = me * rows + jnp.arange(rows, dtype=jnp.int32)
    segment = segments(ends, index)
    live = (segment < seq_count).astype(F32)[:, None]
    all_index = jnp.arange(count, dtype=jnp.int32)
    all_position = positions(ends, all_index, segments(ends, all_index))
    half_width = head_size // 2
    inverse = jnp.exp(
        -math.log(10000.0) * jnp.arange(half_width, dtype=F32) / half_width
    )
    angle = inverse[:, None] * all_position.astype(F32)[None, :]
    cos = jnp.cos(angle)
    sin = jnp.sin(angle)

    all_tokens = gather(tokens[0]).reshape(count, width)
    inputs = tokens[0].astype(F32)
    grad_y = cotangent[0].astype(F32) * live
    grad_y_b = grad_y.astype(BF16)
    all_grad_y = gather(grad_y_b).reshape(count, width)

    small = [gain_one, bias_one, gain_two, bias_two, bias_down, bias_up]
    packed = gather_small(jnp.concatenate(small)[None, :])
    vectors = []
    at = 0
    for vector in small:
        size = vector.shape[0]
        vectors.append(packed[:, at : at + size].reshape(1, -1).astype(F32))
        at += size
    gain_first, bias_first, gain_second, bias_second, bias_output, bias_hidden = vectors

    all_steps = lax.all_gather(time_steps.astype(F32), "fsdp", axis=0, tiled=True)
    all_embedded = embed(all_steps, w_time.shape[0] * fsdp_size).astype(BF16)
    embedded = lax.dynamic_index_in_dim(all_embedded, shard, 0, keepdims=False)
    film = times_rows(embedded, fetch(w_time))
    film = jnp.concatenate([film, jnp.zeros((1, 2 * width), F32)], axis=0)
    gains = gain_first + film[:, :width]
    shifts = bias_first + film[:, width:]

    head = me // repeats
    w_head = jnp.concatenate(
        [
            lax.dynamic_slice_in_dim(w_qkv, k * width + head * head_size, head_size, 1)
            for k in range(3)
        ]
        + [jnp.zeros((w_qkv.shape[0], head_size), BF16)],
        axis=1,
    )
    w_head = gather_small(w_head)

    base = jnp.arange(ctx_size, dtype=jnp.int32) * rows
    all_norm, query_t, key, key_t, value_t, pair = project(
        all_tokens, base, ends_vector, gains, shifts, w_head, cos, sin, rows, head_size
    )
    place = jnp.arange(ctx_size, dtype=jnp.int32)
    out_t, sent, lse = attend(place, query_t, key, value_t, rows)

    part = (me % repeats) * columns
    if repeats > 1:
        sent = lax.dynamic_slice_in_dim(sent, part, columns, 1)
    attended_t = lax.all_to_all(sent, "ctx", 0, 0, tiled=True).reshape(width, rows)

    out_pieces = fetch(w_out)
    up_pieces = fetch(w_up)
    down_pieces = fetch(w_down)
    qkv_pieces = fetch(w_qkv)
    resid = inputs + times_rows_t(attended_t, out_pieces)
    normal_two, scale_two = stats(resid)
    norm_two_b = (normal_two * gain_second + bias_second).astype(BF16)
    all_norm_two = gather(norm_two_b).reshape(count, width)
    pre = times_rows(norm_two_b, up_pieces) + bias_hidden
    act, slope = gelu_parts(pre)
    branch = times_rows(act.astype(BF16), down_pieces) + bias_output
    output = (live * (resid + branch)).astype(BF16)
    grad_act = joined([dims(grad_y_b, p, 1, 1) for p, _ in down_pieces], down_pieces, 1)
    grad_pre = grad_act * slope
    grad_bias_up = jnp.sum(grad_pre, axis=0)
    grad_pre_b = grad_pre.astype(BF16)
    grad_norm_two = joined([dims(grad_pre_b, p, 1, 1) for p, _ in up_pieces], up_pieces, 1)
    grad_resid = grad_y + stats_back(grad_norm_two * gain_second, normal_two, scale_two)
    grad_resid_b = grad_resid.astype(BF16)
    grad_att_t = joined(
        [dims(p, grad_resid_b, 1, 1) for p, _ in out_pieces], out_pieces, 0
    ).astype(BF16)
    grad_att_t = grad_att_t.reshape(HEADS, head_size, rows)
    if repeats > 1:
        grad_att_t = jnp.repeat(grad_att_t, repeats, axis=0)
    grad_att = lax.all_to_all(grad_att_t, "ctx", 0, 0, tiled=True)

    mixed_t, _ = attend_back(
        place, query_t, grad_att, out_t, lse, key, key_t, pair, cos, sin, rows
    )
    mixed_t = mixed_t.reshape(3, head_size, count)
    if repeats > 1:
        mixed_t = lax.dynamic_slice_in_dim(mixed_t, part, columns, 1)
    mixed_t = mixed_t.reshape(3 * columns, count)
    mixed_sent = mixed_t.reshape(3 * columns, ctx_size, rows).transpose(1, 0, 2)
    mixed_got = lax.all_to_all(mixed_sent, "ctx", 0, 0, tiled=True)
    grad_mixed_t = (
        mixed_got.reshape(ctx_size, 3, columns, rows)
        .transpose(1, 0, 2, 3)
        .reshape(3 * width, rows)
    )
    grad_norm_one = joined(
        [dims(grad_mixed_t, p, 0, 1) for p, _ in qkv_pieces], qkv_pieces, 1
    )
    normal_one, scale_one = stats(inputs)
    seg_col = segment[:, None]
    gain_tok = gains[0:1]
    for s in range(1, seq_count + 1):
        gain_tok = jnp.where(seg_col == s, gains[s : s + 1], gain_tok)
    grad_tokens = (
        grad_resid + stats_back(grad_norm_one * gain_tok, normal_one, scale_one)
    ).astype(BF16)
    film_terms = jnp.concatenate([grad_norm_one * normal_one, grad_norm_one], axis=1)
    film_sums = [
        jnp.sum(jnp.where(seg_col == s, film_terms, 0.0), axis=0)
        for s in range(seq_count + 1)
    ]

    sums = [
        jnp.sum(grad_norm_two * normal_two, axis=0),
        jnp.sum(grad_norm_two, axis=0),
        jnp.sum(grad_y, axis=0),
        grad_bias_up,
    ] + film_sums
    sizes = [vector.shape[0] for vector in sums]
    total = lax.psum(jnp.concatenate(sums)[None, :], "ctx")
    total = lax.all_gather(total, "fsdp", axis=0, tiled=True)
    split = []
    at = 0
    for size in sizes:
        split.append(total[:, at : at + size])
        at += size

    def own(vector):
        size = vector.shape[0] // fsdp_size
        return lax.dynamic_slice_in_dim(vector, shard * size, size, 0)

    sum_gain_two, sum_bias_two, sum_bias_down, sum_bias_up = (
        own(jnp.sum(vector, axis=0)) for vector in split[:4]
    )
    film_all = jnp.sum(sum(split[4:]), axis=0)
    sum_gain_one = own(film_all[:width])
    sum_bias_one = own(film_all[width:])
    film_grad = jnp.stack(split[4 : 4 + seq_count], axis=1).reshape(-1, 2 * width)
    embedded_rows = lax.dynamic_slice_in_dim(
        all_embedded.astype(F32).reshape(film_grad.shape[0], -1),
        shard * w_time.shape[0],
        w_time.shape[0],
        1,
    )
    grad_time = sum(
        embedded_rows[g][:, None] * film_grad[g][None, :]
        for g in range(film_grad.shape[0])
    )

    slice_width = hidden // (ctx_size * fsdp_size)
    starts = [
        k * (hidden // fsdp_size) + me * slice_width for k in range(fsdp_size)
    ]
    w_up_cols = []
    for piece, _ in up_pieces:
        w_up_cols.append(
            jnp.concatenate(
                [
                    lax.dynamic_slice_in_dim(piece, start, slice_width, 1)
                    for start in starts
                ],
                axis=1,
            )
        )
    w_up_slice = joined(w_up_cols, up_pieces, 0)
    w_down_slice = jnp.concatenate(
        [rows_of(down_pieces, start, slice_width) for start in starts], axis=0
    )
    bias_slice = jnp.concatenate(
        [
            lax.dynamic_slice_in_dim(bias_hidden, start, slice_width, 1)
            for start in starts
        ],
        axis=1,
    )
    pre_slice = dims(all_norm_two, w_up_slice, 1, 0) + bias_slice
    act_slice, slope_slice = gelu_parts(pre_slice)
    grad_pre_slice = (dims(all_grad_y, w_down_slice, 1, 1) * slope_slice).astype(BF16)
    down_slice = dims(act_slice.astype(BF16), all_grad_y, 0, 0)
    up_slice = dims(all_norm_two, grad_pre_slice, 0, 0)
    grad_down = gather(scatter_sum(down_slice, 0)).reshape(-1, width).astype(F32)
    up_parts = gather(scatter_sum(up_slice, 0))
    grad_up = (
        up_parts.reshape(ctx_size, width // fsdp_size, fsdp_size, slice_width)
        .transpose(1, 2, 0, 3)
        .reshape(width // fsdp_size, hidden)
        .astype(F32)
    )
    out_part = jnp.dot(attended_t, grad_resid_b, preferred_element_type=F32)
    out_rows = lax.psum_scatter(
        out_part.astype(BF16), ("fsdp", "ctx"), scatter_dimension=0, tiled=True
    )
    grad_out = gather(out_rows).reshape(-1, width).astype(F32)
    qkv_slice = jnp.dot(mixed_t, all_norm, preferred_element_type=F32)
    qkv_parts = gather(scatter_sum(qkv_slice, 1))
    grad_qkv = (
        qkv_parts.reshape(ctx_size, 3, columns, width // fsdp_size)
        .transpose(3, 1, 0, 2)
        .reshape(width // fsdp_size, 3 * width)
        .astype(F32)
    )
    return (
        output[None],
        grad_tokens[None],
        grad_qkv,
        grad_out,
        grad_up,
        grad_down,
        grad_time,
        sum_gain_one,
        sum_bias_one,
        sum_gain_two,
        sum_bias_two,
        sum_bias_up,
        sum_bias_down,
    )


def ring_tables(ctx_size):
    chips = ctx_size // 2
    order = list(range(0, chips, 2)) + list(range(1, chips, 2))[::-1]
    offsets = [0]
    for step in range(1, chips // 2 + 1):
        offsets.append(-step)
        if step <= (chips - 1) // 2:
            offsets.append(step)
    place = np.zeros((ctx_size, ctx_size), np.int32)
    for me in range(ctx_size):
        at = order.index(me // 2)
        for k, offset in enumerate(offsets):
            chip = order[(at + offset) % chips]
            place[me, 2 * k] = 2 * chip + me % 2
            place[me, 2 * k + 1] = 2 * chip + 1 - me % 2
    return order, place


def fence(*values):
    return lax.optimization_barrier(values)


def after(values, *earlier):
    return lax.optimization_barrier((values, *earlier))[0]


def body(
    ctx_size, fsdp_size,
    tokens, w_qkv, w_out, w_up, w_down, w_time, gain_one, bias_one, gain_two, bias_two, bias_up,
    bias_down, lengths, time_steps, cotangent,
):
    me = lax.axis_index("ctx")
    shard = lax.axis_index("fsdp")
    core = me % 2
    rows = tokens.shape[1]
    width = tokens.shape[2]
    head_size = width // HEADS
    seq_count = lengths.shape[1]
    hidden = w_up.shape[1]
    other = 1 - shard
    chips = ctx_size // 2
    half = width // 2
    units = hidden // (ctx_size * fsdp_size)
    order, place_table = ring_tables(ctx_size)
    place = jnp.asarray(place_table)[me]
    who = jnp.stack([me, shard]).astype(jnp.int32)

    def across(values):
        return lax.ppermute(values, "fsdp", [(0, 1), (1, 0)])

    def flip(values, bit=0):
        return lax.ppermute(
            values, "ctx", [(i, i ^ (1 << bit)) for i in range(ctx_size)]
        )

    def hop(values, step):
        return lax.ppermute(
            values,
            "ctx",
            [
                (2 * order[at] + c, 2 * order[(at + step) % chips] + c)
                for at in range(chips)
                for c in range(2)
            ],
        )

    def by_shard(mine, others, axis):
        first = jnp.where(shard == 0, mine, others)
        second = jnp.where(shard == 0, others, mine)
        return jnp.concatenate([first, second], axis=axis)

    def cut(values, start, size, axis):
        return lax.dynamic_slice_in_dim(values, start, size, axis)

    def halve(values, axis, mine, send):
        keep = lax.dynamic_index_in_dim(values, mine, axis, keepdims=False)
        give = lax.dynamic_index_in_dim(values, 1 - mine, axis, keepdims=False)
        return keep + send(give.astype(BF16)).astype(F32)

    ends = []
    for s in range(seq_count):
        ends.append(lengths[0, s] + (ends[-1] if ends else 0))
    ends_vector = jnp.stack(ends)
    base = place * rows
    index = me * rows + jnp.arange(rows, dtype=jnp.int32)
    segment = segments(ends, index)
    seg_col = segment[:, None]
    live = (segment < seq_count).astype(F32)[:, None]
    all_index = (base[:, None] + jnp.arange(rows, dtype=jnp.int32)[None, :]).reshape(-1)
    all_position = positions(ends, all_index, segments(ends, all_index))
    half_width = head_size // 2
    inverse = jnp.exp(
        -math.log(10000.0) * jnp.arange(half_width, dtype=F32) / half_width
    )
    angle = inverse[:, None] * all_position.astype(F32)[None, :]
    cos = jnp.cos(angle)
    sin = jnp.sin(angle)

    own_tokens = tokens[0]
    steps_row = time_steps.reshape(1, seq_count)
    small = [
        v[None, :]
        for v in (gain_one, bias_one, gain_two, bias_two, bias_down, bias_up)
    ]
    packed = jnp.concatenate(
        small + [(steps_row // 256).astype(BF16), (steps_row % 256).astype(BF16)], axis=1
    )
    w_head = jnp.concatenate(
        [cut(w_qkv, k * width + me * head_size, head_size, 1) for k in range(3)], axis=1
    )
    class Ring:
        def __init__(self, values):
            self.right = self.left = values
            self.parts = [values]
            self.step = 0

        def go(self, *earlier):
            right, left = self.right, self.left
            if earlier:
                right, left = (
                    after(right, *earlier),
                    after(left, *earlier),
                )
            self.step += 1
            self.right = hop(right, 1)
            if self.step <= (chips - 1) // 2:
                self.left = hop(left, -1)
                return [self.right, self.left]
            return [self.right]

        def came(self, values):
            self.right = values[0]
            if len(values) > 1:
                self.left = values[1]
            self.parts += values

    def fenced(groups):
        flat = [v for group in groups for v in group]
        flat = list(fence(*flat))
        out = []
        for group in groups:
            out.append(flat[: len(group)])
            flat = flat[len(group) :]
        return out

    def with_flips(values):
        return [part for v in values for part in (v, flip(v))]

    tok = Ring(own_tokens)
    tok_new = tok.go()
    tok_new, (packed, w_head) = fenced([tok_new, [packed, w_head]])
    tok.came(tok_new)

    tok_new = tok.go()
    packed_other = across(packed)
    w_head_other = across(w_head)
    inputs = own_tokens.astype(F32)
    grad_y = cotangent[0].astype(F32) * live
    grad_y_b = grad_y.astype(BF16)
    out_half = w_out.shape[0] // 2
    out_send = cut(w_out, core * out_half, out_half, 0)
    tok_new, (packed_other, w_head_other, cos, sin, out_send) = fenced(
        [tok_new, [packed_other, w_head_other, cos, sin, out_send]]
    )
    tok.came(tok_new)

    tok_new = tok.go()
    out_mine = across(out_send)
    packed_all = by_shard(packed, packed_other, 0)
    vectors = []
    at = 0
    for vector in small:
        size = vector.shape[1]
        vectors.append(packed_all[:, at : at + size].reshape(1, -1).astype(F32))
        at += size
    gain_first, bias_first, gain_second, bias_second, bias_output, bias_hidden = vectors
    all_steps = packed_all[:, at : at + seq_count].astype(F32) * 256.0 + packed_all[
        :, at + seq_count :
    ].astype(F32)
    all_embedded = embed(all_steps, w_time.shape[0] * fsdp_size).astype(BF16)
    own_part = cut(all_embedded, shard * w_time.shape[0], w_time.shape[0], 2)
    film_part = jnp.dot(
        own_part.reshape(fsdp_size * seq_count, -1), w_time, preferred_element_type=F32
    ).reshape(fsdp_size, seq_count, 2 * width)
    film_other = across(lax.dynamic_index_in_dim(film_part, other, 0, keepdims=False))
    film = film_other + lax.dynamic_index_in_dim(film_part, shard, 0, keepdims=False)
    film = jnp.concatenate([film, jnp.zeros((1, 2 * width), F32)], axis=0)
    gains = gain_first + film[:, :width]
    shifts = bias_first + film[:, width:]
    up_parts = 2
    up_deep = w_up.shape[0] // up_parts
    quarter = hidden // 4
    up_send = [
        lax.dynamic_slice(w_up, (p * up_deep, (me % 4) * quarter), (up_deep, quarter))
        for p in range(up_parts)
    ]
    tok_new, (gains, shifts, grad_y_b, out_mine), up_send = fenced(
        [tok_new, [gains, shifts, grad_y_b, out_mine], up_send]
    )
    tok_flips = with_flips(tok.parts)
    tok.came(tok_new)

    tok_last = tok.go()
    grad_y_other = across(grad_y_b)
    up_mine = [across(up_send[0])]
    tok_flips += with_flips(tok_new)
    constants = (base, ends_vector, gains, shifts, w_head, w_head_other, cos, sin, head_size)
    head_values = project_chunks(who, tok_flips, *constants)
    head_values, tok_last, (grad_y_other, up_mine[0]) = fenced(
        [head_values, tok_last, [grad_y_other, up_mine[0]]]
    )

    cot = Ring(grad_y_b)
    cot_new = cot.go(tok_last[0])
    up_mine.append(across(after(up_send[1], up_mine[0])))
    up_side = [flip(up_mine[0], 1)]
    all_norm, query_t, key, key_t, value_t, pair = project_chunks(
        who, with_flips(tok_last), *constants, first=chips - 1, earlier=head_values
    )
    out_t, sent, lse = attend(place, query_t, key, value_t, rows)
    (out_t, sent, lse, up_mine[1], up_side[0]), cot_new = fenced(
        [[out_t, sent, lse, up_mine[1], up_side[0]], cot_new]
    )
    cot.came(cot_new)

    attended = lax.all_to_all(sent, "ctx", 0, 0, tiled=True).reshape(width, rows)
    up_side.append(flip(up_mine[1], 1))
    far_send = dims(after(grad_y_other, lse), w_down, 1, 1).astype(BF16)
    far_grad = across(far_send)
    near_grad = dims(after(grad_y_b, lse), w_down, 1, 1)
    first_units = shard * (hidden // 2) + me * units
    second_units = other * (hidden // 2) + me * units
    up_first = cut(w_up, first_units, units, 1)
    up_second = cut(w_up, second_units, units, 1)
    up_own = jnp.concatenate([up_first, up_second], axis=1)
    up_give = jnp.concatenate([up_second, up_first], axis=1)
    down_own = cut(w_down, me * units, units, 0)
    out_pieces = (w_out, out_mine, flip(out_mine))
    pieces = []
    for p in range(up_parts):
        pieces += [up_mine[p], flip(up_mine[p])]
    (attended, up_side[1], near_grad, up_own, up_give, down_own), pieces = fenced(
        [[attended, up_side[1], near_grad, up_own, up_give, down_own], pieces]
    )

    cot_new = cot.go(attended)
    resid, normal_two, scale_two, norm_two_b = middle(
        who, attended, out_pieces, own_tokens, gain_second, bias_second
    )
    side = with_flips(up_side)
    (norm_two_b, far_grad), cot_new, side = fenced([[norm_two_b, far_grad], cot_new, side])
    cot.came(cot_new)
    pieces = pieces[:2] + side[:2] + pieces[2:] + side[2:]

    two = Ring(norm_two_b)
    two_new = two.go()
    cot_new = cot.go()
    up_other = across(after(up_give, norm_two_b))
    down_other = across(after(down_own, norm_two_b))
    act_b, grad_resid, grad_resid_b, grad_att, sums = feed(
        who, norm_two_b, w_up, pieces, near_grad, far_grad, bias_hidden, normal_two, scale_two,
        gain_second, grad_y_b, out_pieces,
    )
    two_new, cot_new, (grad_att, grad_resid_b) = fenced(
        [two_new, cot_new, [grad_att, grad_resid_b]]
    )
    two.came(two_new)
    cot.came(cot_new)

    grad_att = grad_att.reshape(HEADS, head_size, rows)
    grad_att = lax.all_to_all(grad_att, "ctx", 0, 0, tiled=True)
    two_new = two.go()
    qkv_half = w_qkv.shape[0] // 2
    qkv_send = cut(w_qkv, core * qkv_half, qkv_half, 0)
    out_part = jnp.dot(attended, grad_resid_b, preferred_element_type=F32)
    deep = width // (ctx_size * fsdp_size)
    out_part = out_part.reshape(fsdp_size, ctx_size // 2, 2, deep, width)
    out_part = halve(out_part, 2, core, flip)
    two_new, (grad_att, out_part, up_other, down_other, qkv_send) = fenced(
        [two_new, [grad_att, out_part, up_other, down_other, qkv_send]]
    )
    two.came(two_new)

    two_new = two.go()
    cot_new = cot.go(grad_att)
    out_part = halve(out_part, 0, shard, across)
    qkv_mine = across(after(qkv_send, out_part))
    mixed, mixed_sent = attend_back(
        place, query_t, grad_att, out_t, lse, key, key_t, pair, cos, sin, rows
    )
    two_new, cot_new, (mixed, mixed_sent, out_part) = fenced(
        [two_new, cot_new, [mixed, mixed_sent, out_part]]
    )
    two.came(two_new)
    cot.came(cot_new)

    mixed_got = lax.all_to_all(mixed_sent, "ctx", 0, 0, tiled=True)
    two_new = two.go()
    qkv_slice = jnp.dot(mixed, all_norm, preferred_element_type=F32)
    qkv_keep = cut(qkv_slice, shard * half, half, 1)
    qkv_other = across(cut(qkv_slice, other * half, half, 1).astype(BF16))
    qkv_sum = (qkv_keep + qkv_other.astype(F32)).astype(BF16)
    out_part = halve(
        out_part.reshape(-1, 2, deep, width), 1, (me >> 1) % 2, lambda v: flip(v, 1)
    )
    bias_slice = jnp.concatenate(
        [cut(bias_hidden, at, units, 1) for at in (first_units, second_units)], axis=1
    )
    cot_parts = with_flips(cot.parts)
    two_new, (mixed_got, qkv_sum, bias_slice, out_part), cot_parts = fenced(
        [two_new, [mixed_got, qkv_sum, bias_slice, out_part], cot_parts]
    )
    two.came(two_new)

    last_ring = Ring(qkv_sum)
    last_new = last_ring.go()
    out_part = halve(
        out_part.reshape(-1, 2, deep, width), 1, (me >> 2) % 2, lambda v: flip(v, 2)
    )
    sliced = slices(
        who, with_flips(two.parts), cot_parts, up_own, up_other, down_own, down_other, bias_slice
    )
    last_new, (sliced, qkv_mine, out_part) = fenced(
        [last_new, [sliced, qkv_mine, out_part]]
    )
    last_ring.came(last_new)

    wide_other = across(sliced[1].astype(BF16))
    last_new = last_ring.go()
    grad_tokens, total = first_back(
        who, ends_vector, mixed_got, (w_qkv, qkv_mine, flip(qkv_mine)), own_tokens, grad_resid,
        gains, sums,
    )
    out_part = halve(
        out_part.reshape(-1, 2, deep, width), 1, (me >> 3) % 2, lambda v: flip(v, 3)
    )
    total_other = across(total)
    down_half = w_down.shape[0] // 2
    down_send = cut(w_down, core * down_half, down_half, 0)
    last_new, (wide_other, total, total_other, out_part, down_send) = fenced(
        [last_new, [wide_other, total, total_other, out_part, down_send]]
    )
    last_ring.came(last_new)

    total = jnp.concatenate(
        [total[:8] + total_other[:8], total[8:], total_other[8:]], axis=0
    )
    total = jnp.pad(total, ((0, -total.shape[0] % 16), (0, 0))).astype(BF16)
    lines = total.shape[0]

    def narrow(values):
        return [values[:, k * 128 : (k + 1) * 128] for k in range(width // 128)]

    wide = jnp.concatenate(
        [(sliced[0] + wide_other.astype(F32)).astype(BF16)]
        + narrow(out_part.reshape(deep, width).astype(BF16))
        + narrow(total),
        axis=0,
    )
    wide_ring = Ring(wide)
    wide_new = wide_ring.go()
    last_new = last_ring.go()
    down_mine = across(after(down_send, wide))
    wide_new, last_new = fenced([wide_new, last_new])
    wide_ring.came(wide_new)
    last_ring.came(last_new)

    wide_new = wide_ring.go()
    last_new = last_ring.go()
    wide_new, last_new = fenced([wide_new, last_new])
    wide_ring.came(wide_new)
    last_ring.came(last_new)

    wide_new = wide_ring.go()
    wide_flips = with_flips(wide_ring.parts)
    grad_qkv = expand_last(place, with_flips(last_ring.parts), head_size)
    wide_new, (grad_qkv, down_mine), wide_flips = fenced(
        [wide_new, [grad_qkv, down_mine], wide_flips]
    )
    wide_ring.came(wide_new)

    wide_flips += with_flips(wide_new)
    wide_last = wide_ring.go()
    down_flip = flip(down_mine)
    grads = expand_wide(place, 0, wide_flips, width, ())
    branch = bias_output
    for b, row in (
        (w_down, shard * (hidden // 2)),
        (down_mine, other * (hidden // 2) + core * down_half),
        (down_flip, other * (hidden // 2) + (1 - core) * down_half),
    ):
        branch = branch + jnp.dot(
            cut(act_b, row, b.shape[0], 1), b, preferred_element_type=F32
        )
    output = (live * (resid + branch)).astype(BF16)
    own_embed = lax.dynamic_index_in_dim(own_part, shard, 0, keepdims=False)
    other_embed = lax.dynamic_index_in_dim(own_part, other, 0, keepdims=False)
    grads, wide_last, (output, own_embed, other_embed) = fenced(
        [
            grads,
            wide_last,
            [output, own_embed.astype(F32).T, other_embed.astype(F32).T],
        ]
    )

    wide_last = with_flips(wide_last)
    grad_time, *vectors = small_sums(
        who, own_embed, other_embed, wide_flips + wide_last, 2 * width + deep * width // 128,
        lines, width,
    )
    grad_up, grad_down, grad_out = expand_wide(
        place, chips - 1, wide_last, width, grads
    )
    return (
        output[None],
        grad_tokens[None],
        grad_qkv,
        grad_out,
        grad_up,
        grad_down,
        grad_time,
        *[vector.reshape(-1) for vector in vectors],
    )


def solution(mesh):
    in_specs = (
        (P("fsdp", "ctx", None),)
        + (P("fsdp", None),) * 5
        + (P("fsdp"),) * 6
        + (P("fsdp", None), P("fsdp", None), P("fsdp", "ctx", None))
    )
    out_specs = (
        (P("fsdp", "ctx", None),) * 2 + (P("fsdp", None),) * 5 + (P("fsdp"),) * 6
    )
    ctx_size, fsdp_size = mesh.shape["ctx"], mesh.shape["fsdp"]
    paired = ctx_size == HEADS and fsdp_size == 2
    return jax.shard_map(
        functools.partial(body if paired else body_general, ctx_size, fsdp_size),
        mesh=mesh,
        in_specs=in_specs,
        out_specs=out_specs,
        check_vma=False,
    )
```

```python
import functools
import math

import jax
import jax.numpy as jnp
import numpy as np
from jax import lax
from jax.experimental import pallas as pl
from jax.experimental.pallas import tpu as pltpu
from jax.sharding import PartitionSpec as P

HEADS = 16
EPSILON = 1e-05
NEGATIVE = -1e30
HIGH = lax.Precision.HIGHEST
F32 = jnp.float32
BF16 = jnp.bfloat16
VMEM_BYTES = 56 << 20


def dims(left, right, left_dim, right_dim):
    return lax.dot_general(
        left, right, (((left_dim,), (right_dim,)), ((), ())), preferred_element_type=F32
    )


def segments(ends, index):
    return sum((index >= end).astype(jnp.int32) for end in ends)


def positions(ends, index, segment):
    begin = jnp.zeros_like(index)
    for at, end in enumerate(ends):
        begin = jnp.where(segment > at, end, begin)
    return index - begin


def embed(steps_given, embed_width):
    half_width = embed_width // 2
    freq = jnp.exp(-math.log(10000.0) * jnp.arange(half_width, dtype=F32) / half_width)
    angle = steps_given.astype(F32)[..., None] * freq
    return jnp.concatenate([jnp.sin(angle), jnp.cos(angle)], axis=-1)


def stats(values):
    centre = jnp.mean(values, axis=-1, keepdims=True)
    centered = values - centre
    spread = jnp.mean(centered * centered, axis=-1, keepdims=True)
    scale = lax.rsqrt(spread + EPSILON)
    return centered * scale, scale


def stats_back(grad, normal, scale):
    return (
        grad
        - jnp.mean(grad, axis=-1, keepdims=True)
        - normal * jnp.mean(grad * normal, axis=-1, keepdims=True)
    ) * scale


def gelu_parts(pre):
    below = 0.5 * (1.0 + lax.erf(pre * math.sqrt(0.5)))
    density = jnp.exp(-0.5 * pre * pre) * (1.0 / math.sqrt(2.0 * math.pi))
    return pre * below, below + pre * density


def qkv_kernel(
    rows, head_size, first, ends_ref, base_ref, tokens_ref, gains_ref, shifts_ref, w_ref,
    cos_ref, sin_ref, *refs,
):
    norm_ref, query_t_ref, key_ref, key_t_ref, value_t_ref, pair_ref = refs[-6:]
    step = pl.program_id(0) + first
    block = tokens_ref.shape[0]
    seq_count = ends_ref.shape[0]
    half = head_size // 2
    values = tokens_ref[...].astype(F32)
    normal, _ = stats(values)
    chunks = block // rows

    def token_index(shape, axis):
        within = lax.broadcasted_iota(jnp.int32, shape, axis)
        index = within + base_ref[step * chunks]
        for at in range(1, chunks):
            index = jnp.where(
                within >= at * rows,
                within - at * rows + base_ref[step * chunks + at],
                index,
            )
        return index

    ends = [ends_ref[s] for s in range(seq_count)]
    seg_col = segments(ends, token_index((block, 1), 0))
    seg_row = segments(ends, token_index((1, block), 1))
    gains = gains_ref[0:1, :]
    shifts = shifts_ref[0:1, :]
    for s in range(1, seq_count + 1):
        gains = jnp.where(seg_col == s, gains_ref[s : s + 1, :], gains)
        shifts = jnp.where(seg_col == s, shifts_ref[s : s + 1, :], shifts)
    norm = (normal * gains + shifts).astype(BF16)
    norm_ref[...] = norm
    mixed = jnp.dot(norm, w_ref[...], preferred_element_type=F32)
    turned = mixed.T
    cos = cos_ref[...]
    sin = sin_ref[...]

    def turn(at):
        upper = turned[at : at + half]
        lower = turned[at + half : at + head_size]
        return jnp.concatenate(
            [upper * cos - lower * sin, lower * cos + upper * sin], axis=0
        ).astype(BF16)

    query = turn(0).astype(F32) * (float(head_size) ** -0.5)
    key = turn(head_size).astype(F32)
    value = turned[2 * head_size : 3 * head_size].astype(BF16).astype(F32)
    spare = 128 - head_size
    row_id = lax.broadcasted_iota(jnp.int32, (spare, block), 0)
    same = row_id == seg_row
    used = row_id <= seq_count
    key_tail = jnp.where(same & used, 1.0, 0.0)
    query_tail = jnp.where(used & jnp.logical_not(same), NEGATIVE, 0.0)
    query_t_ref[...] = jnp.concatenate([query, query_tail], axis=0).astype(BF16)
    key_t_ref[...] = key.astype(BF16)
    value_t_ref[...] = value.astype(BF16)
    key_ref[...] = jnp.concatenate([key, key_tail], axis=0).T.astype(BF16)
    pair_ref[...] = jnp.concatenate([value, query], axis=0).T.astype(BF16)


def attend_kernel(
    chunk, rows, place_ref, query_ref, key_ref, value_ref, out_ref, sent_ref, lse_ref, score_ref,
):
    core = place_ref[0] % 2
    count = key_ref.shape[0]
    query = query_ref[...]
    top = None
    for at in range(0, count, chunk):
        score = jnp.dot(key_ref[at : at + chunk, :], query, preferred_element_type=F32)
        score_ref[at : at + chunk, :] = score
        high = jnp.max(score, axis=0, keepdims=True)
        top = high if top is None else jnp.maximum(top, high)
    total = jnp.zeros_like(top)
    out = jnp.zeros(out_ref.shape, F32)
    for at in range(0, count, chunk):
        weight = jnp.exp(score_ref[at : at + chunk, :] - top)
        total = total + jnp.sum(weight, axis=0, keepdims=True)
        out = out + jnp.dot(
            value_ref[:, at : at + chunk],
            weight.astype(BF16),
            preferred_element_type=F32,
        )
    out = out / total
    out_ref[...] = out
    for at in range(sent_ref.shape[0]):
        sent_ref[at ^ core] = out[:, at * rows : (at + 1) * rows].astype(BF16)
    lse_ref[...] = top + jnp.log(total)


def attend_back_kernel(
    chunk, rows, head_size, place_ref, query_ref, grad_ref, out_ref, lse_ref, key_ref, key_t_ref, pair_ref,
    pair_block_ref, cos_block_ref, sin_block_ref, cos_ref, sin_ref, mixed_ref, sent_ref, key_acc, value_acc,
):
    step = pl.program_id(0)
    core = place_ref[0] % 2
    per_step = grad_ref.shape[0]
    count = key_ref.shape[0]
    block = query_ref.shape[1]
    half = head_size // 2
    scale = float(head_size) ** -0.5

    @pl.when(step == 0)
    def _():
        key_acc[...] = jnp.zeros_like(key_acc)
        value_acc[...] = jnp.zeros_like(value_acc)

    query = query_ref[...]
    grad = jnp.concatenate(
        [grad_ref[at ^ core] for at in range(per_step)], axis=1
    ).astype(F32)
    delta = jnp.sum(grad * out_ref[...], axis=0, keepdims=True)
    lse = lse_ref[...]
    grad_t = jnp.concatenate(
        [grad, jnp.zeros((128 - head_size, block), F32)], axis=0
    )
    grad_rows = grad_t.T.astype(BF16)
    grad_t = grad_t.astype(BF16)
    pair = pair_block_ref[...]
    grad_query = jnp.zeros((head_size, block), F32)
    for at in range(0, count, chunk):
        part = slice(at, at + chunk)
        score = jnp.dot(key_ref[part, :], query, preferred_element_type=F32)
        prob = jnp.exp(score - lse)
        grad_prob = jnp.dot(pair_ref[part, :], grad_t, preferred_element_type=F32)
        grad_score = (prob * (grad_prob - delta)).astype(BF16)
        grad_query = grad_query + jnp.dot(
            key_t_ref[:, part], grad_score, preferred_element_type=F32
        )
        key_acc[part, :] += jnp.dot(grad_score, pair, preferred_element_type=F32)
        value_acc[part, :] += jnp.dot(
            prob.astype(BF16), grad_rows, preferred_element_type=F32
        )

    def turn_back(values, cos, sin):
        upper = values[:half]
        lower = values[half:]
        return jnp.concatenate(
            [upper * cos + lower * sin, lower * cos - upper * sin], axis=0
        ).astype(BF16)

    at = pl.multiple_of(step * block, block)
    query_part = turn_back(
        grad_query * scale, cos_block_ref[...], sin_block_ref[...]
    )
    mixed_ref[0:head_size, pl.ds(at, block)] = query_part
    for k in range(per_step):
        sent_ref[place_ref[step * per_step + k], 0:head_size, :] = query_part[
            :, k * rows : (k + 1) * rows
        ]

    @pl.when(step == pl.num_programs(0) - 1)
    def _():
        key_part = turn_back(
            key_acc[...].T[head_size : 2 * head_size], cos_ref[...], sin_ref[...]
        )
        value_part = value_acc[...].T[:head_size].astype(BF16)
        both = jnp.concatenate([key_part, value_part], axis=0)
        mixed_ref[head_size : 3 * head_size, :] = both
        for k in range(count // rows):
            sent_ref[place_ref[k], head_size : 3 * head_size, :] = both[
                :, k * rows : (k + 1) * rows
            ]


def whole(shape):
    return pl.BlockSpec(shape, lambda i, *_: (0,) * len(shape))


def project(
    tokens, base, ends, gains, shifts, w_head, cos, sin, rows, head_size, first=0, earlier=None,
):
    width = tokens.shape[1]
    count = base.shape[0] * rows
    block = min(count, 2 * rows)
    earlier = list(earlier or ())
    grid_spec = pltpu.PrefetchScalarGridSpec(
        num_scalar_prefetch=2,
        grid=(tokens.shape[0] // block,),
        in_specs=[
            pl.BlockSpec((block, width), lambda i, *_: (i, 0)),
            whole(gains.shape),
            whole(shifts.shape),
            whole(w_head.shape),
            pl.BlockSpec((head_size // 2, block), lambda i, *_: (0, i + first)),
            pl.BlockSpec((head_size // 2, block), lambda i, *_: (0, i + first)),
        ]
        + [pl.BlockSpec(memory_space=pl.ANY)] * len(earlier),
        out_specs=[
            pl.BlockSpec((block, width), lambda i, *_: (i + first, 0)),
            pl.BlockSpec((128, block), lambda i, *_: (0, i + first)),
            pl.BlockSpec((block, 128), lambda i, *_: (i + first, 0)),
            pl.BlockSpec((head_size, block), lambda i, *_: (0, i + first)),
            pl.BlockSpec((head_size, block), lambda i, *_: (0, i + first)),
            pl.BlockSpec((block, 128), lambda i, *_: (i + first, 0)),
        ],
    )
    return pl.pallas_call(
        functools.partial(qkv_kernel, rows, head_size, first),
        grid_spec=grid_spec,
        out_shape=[
            jax.ShapeDtypeStruct((count, width), BF16),
            jax.ShapeDtypeStruct((128, count), BF16),
            jax.ShapeDtypeStruct((count, 128), BF16),
            jax.ShapeDtypeStruct((head_size, count), BF16),
            jax.ShapeDtypeStruct((head_size, count), BF16),
            jax.ShapeDtypeStruct((count, 128), BF16),
        ],
        input_output_aliases={8 + k: k for k in range(len(earlier))},
        compiler_params=pltpu.CompilerParams(vmem_limit_bytes=VMEM_BYTES),
        cost_estimate=pl.CostEstimate(
            flops=2 * tokens.shape[0] * width * 1024,
            bytes_accessed=4 * tokens.shape[0] * width,
            transcendentals=0,
        ),
        name="project_head",
    )(ends, base, tokens, gains, shifts, w_head, cos, sin, *earlier)


def project_chunks_kernel(rows, head_size, first, chunks, who_ref, ends_ref, base_ref, *refs):
    tokens = refs[:chunks]
    gains_ref, shifts_ref, own_ref, other_ref, cos_ref, sin_ref = refs[chunks : chunks + 6]
    block_ref, w_ref = refs[-2:]
    step = pl.program_id(0)
    size = own_ref.shape[0]

    @pl.when(step == 0)
    def _():
        w_ref[:, 128:] = jnp.zeros((2 * size, 128), BF16)
        shard = who_ref[1]
        own_at = pl.multiple_of(shard * size, size)
        other_at = pl.multiple_of((1 - shard) * size, size)
        width = own_ref.shape[1]
        w_ref[pl.ds(own_at, size), :width] = own_ref[...]
        w_ref[pl.ds(other_at, size), :width] = other_ref[...]

    for at in range(chunks // 2):

        @pl.when(step == at)
        def _():
            block_ref[:rows] = tokens[2 * at][...]
            block_ref[rows:] = tokens[2 * at + 1][...]

    qkv_kernel(
        rows, head_size, first, ends_ref, base_ref, block_ref, gains_ref, shifts_ref, w_ref,
        cos_ref, sin_ref, *refs[-8:-2],
    )


def project_chunks(
    who, tokens, base, ends, gains, shifts, w_own, w_other, cos, sin, head_size, first=0, earlier=None,
):
    rows, width = tokens[0].shape
    count = base.shape[0] * rows
    block = 2 * rows
    earlier = list(earlier or ())
    grid_spec = pltpu.PrefetchScalarGridSpec(
        num_scalar_prefetch=3,
        grid=(len(tokens) // 2,),
        in_specs=[whole((rows, width))] * len(tokens)
        + [
            whole(gains.shape),
            whole(shifts.shape),
            whole(w_own.shape),
            whole(w_other.shape),
            pl.BlockSpec((head_size // 2, block), lambda i, *_: (0, i + first)),
            pl.BlockSpec((head_size // 2, block), lambda i, *_: (0, i + first)),
        ]
        + [pl.BlockSpec(memory_space=pl.ANY)] * len(earlier),
        out_specs=[
            pl.BlockSpec((block, width), lambda i, *_: (i + first, 0)),
            pl.BlockSpec((128, block), lambda i, *_: (0, i + first)),
            pl.BlockSpec((block, 128), lambda i, *_: (i + first, 0)),
            pl.BlockSpec((head_size, block), lambda i, *_: (0, i + first)),
            pl.BlockSpec((head_size, block), lambda i, *_: (0, i + first)),
            pl.BlockSpec((block, 128), lambda i, *_: (i + first, 0)),
        ],
        scratch_shapes=[
            pltpu.VMEM((block, width), BF16),
            pltpu.VMEM((width, 256), BF16),
        ],
    )
    return pl.pallas_call(
        functools.partial(project_chunks_kernel, rows, head_size, first, len(tokens)),
        grid_spec=grid_spec,
        out_shape=[
            jax.ShapeDtypeStruct((count, width), BF16),
            jax.ShapeDtypeStruct((128, count), BF16),
            jax.ShapeDtypeStruct((count, 128), BF16),
            jax.ShapeDtypeStruct((head_size, count), BF16),
            jax.ShapeDtypeStruct((head_size, count), BF16),
            jax.ShapeDtypeStruct((count, 128), BF16),
        ],
        input_output_aliases={9 + len(tokens) + k: k for k in range(len(earlier))},
        compiler_params=pltpu.CompilerParams(vmem_limit_bytes=VMEM_BYTES),
        cost_estimate=pl.CostEstimate(
            flops=2 * len(tokens) * rows * width * 1024,
            bytes_accessed=4 * len(tokens) * rows * width,
            transcendentals=0,
        ),
        name="project_chunks",
    )(who, ends, base, *tokens, gains, shifts, w_own, w_other, cos, sin, *earlier)


def attend(place, query_t, key, value_t, rows):
    count = key.shape[0]
    head_size = value_t.shape[0]
    block = min(count, 2 * rows)
    chunk = min(count, 512)
    grid_spec = pltpu.PrefetchScalarGridSpec(
        num_scalar_prefetch=1,
        grid=(count // block,),
        in_specs=[
            pl.BlockSpec((128, block), lambda i, _: (0, i)),
            whole((count, 128)),
            whole((head_size, count)),
        ],
        out_specs=[
            pl.BlockSpec((head_size, block), lambda i, _: (0, i)),
            pl.BlockSpec(
                (2, head_size, rows), lambda i, place: (place[2 * i] // 2, 0, 0)
            ),
            pl.BlockSpec((1, block), lambda i, _: (0, i)),
        ],
        scratch_shapes=[pltpu.VMEM((count, block), F32)],
    )
    return pl.pallas_call(
        functools.partial(attend_kernel, chunk, rows),
        grid_spec=grid_spec,
        out_shape=[
            jax.ShapeDtypeStruct((head_size, count), F32),
            jax.ShapeDtypeStruct((count // rows, head_size, rows), BF16),
            jax.ShapeDtypeStruct((1, count), F32),
        ],
        compiler_params=pltpu.CompilerParams(vmem_limit_bytes=VMEM_BYTES),
        cost_estimate=pl.CostEstimate(
            flops=8 * count * count * 128,
            bytes_accessed=8 * count * 128,
            transcendentals=count * count,
        ),
        name="attend_head",
    )(place, query_t, key, value_t)


def attend_back(place, query_t, grad, out, lse, key, key_t, pair, cos, sin, rows):
    count = key.shape[0]
    head_size = key_t.shape[0]
    half = head_size // 2
    block = min(count, 2 * rows)
    chunk = min(count, 512)
    grid_spec = pltpu.PrefetchScalarGridSpec(
        num_scalar_prefetch=1,
        grid=(count // block,),
        in_specs=[
            pl.BlockSpec((128, block), lambda i, _: (0, i)),
            pl.BlockSpec(
                (2, head_size, rows), lambda i, place: (place[2 * i] // 2, 0, 0)
            ),
            pl.BlockSpec((head_size, block), lambda i, _: (0, i)),
            pl.BlockSpec((1, block), lambda i, _: (0, i)),
            whole((count, 128)),
            whole((head_size, count)),
            whole((count, 128)),
            pl.BlockSpec((block, 128), lambda i, _: (i, 0)),
            pl.BlockSpec((half, block), lambda i, _: (0, i)),
            pl.BlockSpec((half, block), lambda i, _: (0, i)),
            whole((half, count)),
            whole((half, count)),
        ],
        out_specs=[
            whole((3 * head_size, count)),
            whole((count // rows, 3 * head_size, rows)),
        ],
        scratch_shapes=[pltpu.VMEM((count, 128), F32), pltpu.VMEM((count, 128), F32)],
    )
    return pl.pallas_call(
        functools.partial(attend_back_kernel, chunk, rows, head_size),
        grid_spec=grid_spec,
        out_shape=[
            jax.ShapeDtypeStruct((3 * head_size, count), BF16),
            jax.ShapeDtypeStruct((count // rows, 3 * head_size, rows), BF16),
        ],
        compiler_params=pltpu.CompilerParams(vmem_limit_bytes=VMEM_BYTES),
        cost_estimate=pl.CostEstimate(
            flops=20 * count * count * 128,
            bytes_accessed=16 * count * 128,
            transcendentals=count * count,
        ),
        name="attend_head_back",
    )(place, query_t, grad, out, lse, key, key_t, pair, pair, cos, sin, cos, sin)


def slices_kernel(
    who_ref, norm_ref, grad_ref, up_own, up_other, down_own, down_other, bias_ref, keep_ref,
    give_ref, down_w, down_acc, up_acc, up_t,
):
    step = pl.program_id(0)
    shard = who_ref[1]
    size, units = up_own.shape
    width = 2 * size
    half = units // 2
    own_at = pl.multiple_of(shard * size, size)
    other_at = pl.multiple_of((1 - shard) * size, size)

    @pl.when(step == 0)
    def _():
        down_w[:half] = down_own[...]
        down_w[half:] = down_other[...]
        down_acc[...] = jnp.zeros_like(down_acc)
        up_acc[...] = jnp.zeros_like(up_acc)

    pre = jnp.dot(
        norm_ref[:, pl.ds(own_at, size)], up_own[...], preferred_element_type=F32
    )
    pre = pre + jnp.dot(
        norm_ref[:, pl.ds(other_at, size)], up_other[...], preferred_element_type=F32
    )
    act, slope = gelu_parts(pre + bias_ref[...])
    grad_y = grad_ref[...]
    grad = dims(grad_y, down_w[...], 1, 1) * slope
    down_acc[...] += jnp.dot(act.T.astype(BF16), grad_y, preferred_element_type=F32)
    up_acc[...] += jnp.dot(
        grad.T.astype(BF16), norm_ref[...], preferred_element_type=F32
    )

    @pl.when(step == pl.num_programs(0) - 1)
    def _():
        up_t[...] = up_acc[...].T
        for at, (rows, out_ref) in enumerate(((own_at, keep_ref), (other_at, give_ref))):
            values = up_t[pl.ds(rows, size), :].astype(out_ref.dtype)
            out_ref[pl.ds(own_at, size), :] = values[:, :half]
            out_ref[pl.ds(other_at, size), :] = values[:, half:]
            for k in range(width // half):
                out_ref[width + k * half : width + (k + 1) * half, :] = down_acc[
                    at * half : (at + 1) * half, k * half : (k + 1) * half
                ].astype(out_ref.dtype)


def slices(
    who, norm, grad_y, up_own, up_other, down_own, down_other, bias,
):
    count, width = norm.shape
    size, units = up_own.shape
    block = 256
    tall = 2 * width
    token = pl.BlockSpec((block, width), lambda i: (i, 0))
    return pl.pallas_call(
        slices_kernel,
        grid=(count // block,),
        in_specs=[pl.BlockSpec(memory_space=pltpu.SMEM), token, token]
        + [
            pl.BlockSpec(v.shape, lambda i: (0, 0))
            for v in (up_own, up_other, down_own, down_other, bias)
        ],
        out_specs=[pl.BlockSpec((tall, units // 2), lambda i: (0, 0))] * 2,
        out_shape=[
            jax.ShapeDtypeStruct((tall, units // 2), F32),
            jax.ShapeDtypeStruct((tall, units // 2), BF16),
        ],
        scratch_shapes=[
            pltpu.VMEM((units, width), BF16),
            pltpu.VMEM((units, width), F32),
            pltpu.VMEM((units, width), F32),
            pltpu.VMEM((width, units), F32),
        ],
        compiler_params=pltpu.CompilerParams(vmem_limit_bytes=VMEM_BYTES),
        cost_estimate=pl.CostEstimate(
            flops=8 * count * width * units,
            bytes_accessed=6 * count * width,
            transcendentals=2 * count * units,
        ),
        name="weight_slices",
    )(
        who, norm, grad_y, up_own, up_other, down_own, down_other, bias
    )


def head_of(device, devices):
    return device % 2 * (devices // 2) + device // 2


def row_starts(who_ref, size):
    core = who_ref[0] % 2
    shard = who_ref[1]
    half = size // 2
    other = (1 - shard) * size
    return (
        pl.multiple_of(shard * size, size),
        pl.multiple_of(other + core * half, half),
        pl.multiple_of(other + (1 - core) * half, half),
    )


def middle_kernel(
    who_ref, att_ref, own_ref, mine_ref, flip_ref, tokens_ref, gain_ref, bias_ref,
    resid_ref, normal_ref, scale_ref, norm_ref, turned,
):
    devices, head_size, _ = att_ref.shape
    for d in range(devices):
        at = head_of(d, devices) * head_size
        turned[:, at : at + head_size] = att_ref[d].astype(F32).T.astype(BF16)
    resid = tokens_ref[...].astype(F32)
    pieces = (own_ref, mine_ref, flip_ref)
    for at, piece in zip(row_starts(who_ref, own_ref.shape[0]), pieces):
        resid = resid + jnp.dot(
            turned[:, pl.ds(at, piece.shape[0])],
            piece[...],
            preferred_element_type=F32,
        )
    resid_ref[...] = resid
    normal, scale = stats(resid)
    normal_ref[...] = normal
    scale_ref[...] = scale
    norm_ref[...] = (normal * gain_ref[...] + bias_ref[...]).astype(BF16)


def middle(who, attended, pieces, tokens, gain, bias):
    rows, width = tokens.shape
    vmem = pl.BlockSpec(memory_space=pltpu.VMEM)
    return pl.pallas_call(
        middle_kernel,
        in_specs=[pl.BlockSpec(memory_space=pltpu.SMEM)] + [vmem] * 7,
        out_specs=[vmem] * 4,
        out_shape=[
            jax.ShapeDtypeStruct((rows, width), F32),
            jax.ShapeDtypeStruct((rows, width), F32),
            jax.ShapeDtypeStruct((rows, 1), F32),
            jax.ShapeDtypeStruct((rows, width), BF16),
        ],
        scratch_shapes=[pltpu.VMEM((rows, width), BF16)],
        compiler_params=pltpu.CompilerParams(vmem_limit_bytes=VMEM_BYTES),
        cost_estimate=pl.CostEstimate(
            flops=8 * rows * width * width,
            bytes_accessed=4 * width * width,
            transcendentals=0,
        ),
        name="output_projection",
    )(who, attended, *pieces, tokens, gain, bias)


def feed_kernel(parts, who_ref, norm_ref, own_ref, *refs):
    pieces = refs[: 4 * parts]
    (
        near_ref, far_ref, bias_ref, normal_ref, scale_ref, gain_ref, grad_y_ref, out_own, out_mine,
        out_flip, act_ref, resid_ref, resid_b_ref, sent_ref, sums_ref, grad_ref, att_ref,
    ) = refs[4 * parts :]
    side = who_ref[0] % 4
    shard = who_ref[1]
    size, hidden = own_ref.shape
    quarter = hidden // 4
    deep = size // parts
    own_at = pl.multiple_of(shard * size, size)
    other_at = pl.multiple_of((1 - shard) * size, size)
    own_norm = norm_ref[:, pl.ds(own_at, size)]
    part_at = [pl.multiple_of(other_at + p * deep, deep) for p in range(parts)]
    norms = [norm_ref[:, pl.ds(at, deep)] for at in part_at]
    for k in range(4):
        block = side ^ k
        columns = pl.ds(pl.multiple_of(block * quarter, quarter), quarter)
        weight = own_ref[:, columns]
        pre = jnp.dot(own_norm, weight, preferred_element_type=F32)
        for p in range(parts):
            pre = pre + jnp.dot(
                norms[p], pieces[4 * p + k][...], preferred_element_type=F32
            )
        act, slope = gelu_parts(pre + bias_ref[:, columns])
        act_ref[:, columns] = act.astype(BF16)
        within = pl.ds(pl.multiple_of((block % 2) * quarter, quarter), quarter)
        near = near_ref[:, within]
        far = far_ref[:, within].astype(F32)
        grad = jnp.where(block // 2 == shard, near, far) * slope
        sums_ref[pl.ds(3 + block, 1), :] = jnp.sum(grad, axis=0, keepdims=True)
        grad = grad.astype(BF16)
        terms = [(own_at, size, weight)]
        terms += [(part_at[p], deep, pieces[4 * p + k][...]) for p in range(parts)]
        for at, length, piece in terms:
            term = dims(grad, piece, 1, 1)
            if k == 0:
                grad_ref[:, pl.ds(at, length)] = term
            else:
                grad_ref[:, pl.ds(at, length)] += term
    grad = grad_ref[...]
    normal = normal_ref[...]
    grad_y = grad_y_ref[...].astype(F32)
    sums_ref[0:1, :] = jnp.sum(grad * normal, axis=0, keepdims=True)
    sums_ref[1:2, :] = jnp.sum(grad, axis=0, keepdims=True)
    sums_ref[2:3, :] = jnp.sum(grad_y, axis=0, keepdims=True)
    sums_ref[7:8, :] = jnp.zeros((1, quarter), F32)
    resid = grad_y + stats_back(grad * gain_ref[...], normal, scale_ref[...])
    resid_ref[...] = resid
    resid = resid.astype(BF16)
    resid_b_ref[...] = resid
    out_pieces = (out_own, out_mine, out_flip)
    for at, piece in zip(row_starts(who_ref, out_own.shape[0]), out_pieces):
        att_ref[pl.ds(at, piece.shape[0]), :] = dims(piece[...], resid, 1, 1).astype(
            BF16
        )
    devices, head_size, _ = sent_ref.shape
    for d in range(devices):
        at = head_of(d, devices) * head_size
        sent_ref[d] = att_ref[at : at + head_size, :]


def feed(who, norm, own, pieces, near, far, bias, normal, scale, gain, grad_y, out_pieces):
    rows, width = norm.shape
    hidden = own.shape[1]
    vmem = pl.BlockSpec(memory_space=pltpu.VMEM)
    return pl.pallas_call(
        functools.partial(feed_kernel, len(pieces) // 4),
        in_specs=[pl.BlockSpec(memory_space=pltpu.SMEM)] + [vmem] * (12 + len(pieces)),
        out_specs=[vmem] * 5,
        out_shape=[
            jax.ShapeDtypeStruct((rows, hidden), BF16),
            jax.ShapeDtypeStruct((rows, width), F32),
            jax.ShapeDtypeStruct((rows, width), BF16),
            jax.ShapeDtypeStruct((HEADS, width // HEADS, rows), BF16),
            jax.ShapeDtypeStruct((8, width), F32),
        ],
        scratch_shapes=[pltpu.VMEM((rows, width), F32), pltpu.VMEM((width, rows), BF16)],
        compiler_params=pltpu.CompilerParams(vmem_limit_bytes=VMEM_BYTES),
        cost_estimate=pl.CostEstimate(
            flops=16 * rows * width * hidden,
            bytes_accessed=4 * width * hidden,
            transcendentals=2 * rows * hidden,
        ),
        name="feed_forward",
    )(who, norm, own, *pieces, near, far, bias, normal, scale, gain, grad_y, *out_pieces)


def first_back_kernel(
    head_size, who_ref, ends_ref, got_ref, own_ref, mine_0, mine_1, flip_0, flip_1, tokens_ref,
    resid_ref, gains_ref, sums_ref, grad_ref, total_ref, mixed, turned,
):
    heads = got_ref.shape[0]
    rows, width = tokens_ref.shape
    seq_count = ends_ref.shape[0]
    for d in range(heads):
        for k in range(3):
            at = k * width + head_of(d, heads) * head_size
            mixed[at : at + head_size, :] = got_ref[
                d, k * head_size : (k + 1) * head_size, :
            ]
    own_at, mine_at, flip_at = row_starts(who_ref, own_ref.shape[0])
    part = mine_0.shape[0]
    starts = (own_at, mine_at, mine_at + part, flip_at, flip_at + part)
    for at, piece in zip(starts, (own_ref, mine_0, mine_1, flip_0, flip_1)):
        turned[pl.ds(at, piece.shape[0]), :] = jnp.dot(
            piece[...], mixed[...], preferred_element_type=F32
        )
    grad = turned[...].T
    normal, scale = stats(tokens_ref[...].astype(F32))
    index = who_ref[0] * rows + lax.broadcasted_iota(jnp.int32, (rows, 1), 0)
    segment = segments([ends_ref[s] for s in range(seq_count)], index)
    gains = gains_ref[0:1, :]
    for s in range(1, seq_count + 1):
        gains = jnp.where(segment == s, gains_ref[s : s + 1, :], gains)
    grad_ref[...] = (
        resid_ref[...] + stats_back(grad * gains, normal, scale)
    ).astype(BF16)
    total_ref[0:8, :] = sums_ref[...]
    product = grad * normal
    for s in range(seq_count + 1):
        here = segment == s
        for k, terms in enumerate((product, grad)):
            total_ref[8 + 2 * s + k : 9 + 2 * s + k, :] = jnp.sum(
                jnp.where(here, terms, 0.0), axis=0, keepdims=True
            )


def first_back(who, ends, got, pieces, tokens, resid, gains, sums):
    rows, width = tokens.shape
    heads, tall, _ = got.shape
    seq_count = ends.shape[0]
    lines = 8 + 2 * (seq_count + 1)
    vmem = pl.BlockSpec(memory_space=pltpu.VMEM)
    return pl.pallas_call(
        functools.partial(first_back_kernel, tall // 3),
        in_specs=[pl.BlockSpec(memory_space=pltpu.SMEM)] * 2 + [vmem] * 10,
        out_specs=[vmem] * 2,
        out_shape=[
            jax.ShapeDtypeStruct((rows, width), BF16),
            jax.ShapeDtypeStruct((lines, width), F32),
        ],
        scratch_shapes=[
            pltpu.VMEM((3 * width, rows), BF16),
            pltpu.VMEM((width, rows), F32),
        ],
        compiler_params=pltpu.CompilerParams(vmem_limit_bytes=VMEM_BYTES),
        cost_estimate=pl.CostEstimate(
            flops=12 * rows * width * width,
            bytes_accessed=8 * width * width,
            transcendentals=0,
        ),
        name="first_norm_back",
    )(who, ends, got, *pieces, tokens, resid, gains, sums)


def small_kernel(seq_count, chunks, who_ref, own_embed, other_embed, *refs):
    parts = refs[:chunks]
    (
        time_ref, gain_one, bias_one, gain_two, bias_two, bias_up, bias_down, total,
    ) = refs[chunks:]
    lines, width = total.shape
    half = width // 2
    shard = who_ref[1]
    for k in range(width // 128):
        at = k * lines
        value = parts[0][at : at + lines, :].astype(F32)
        for ref in parts[1:]:
            value = value + ref[at : at + lines, :].astype(F32)
        total[:, k * 128 : (k + 1) * 128] = value
    part = pl.ds(pl.multiple_of(shard * half, half), half)
    gain_two[...] = total[0:1, part]
    bias_two[...] = total[1:2, part]
    bias_down[...] = total[2:3, part]
    bias_up[:, :width] = total[pl.ds(3 + 2 * shard, 1), :]
    bias_up[:, width:] = total[pl.ds(4 + 2 * shard, 1), :]
    films = 2 * (seq_count + 1)
    gain = total[8:9, part]
    bias = total[9:10, part]
    for s in range(1, films):
        gain = gain + total[8 + 2 * s : 9 + 2 * s, part]
        bias = bias + total[9 + 2 * s : 10 + 2 * s, part]
    gain_one[...] = gain
    bias_one[...] = bias
    embeds = []
    for embed_ref in (own_embed, other_embed):
        columns = []
        for s in range(seq_count):
            line = embed_ref[s : s + 1, :]
            columns.append(jnp.broadcast_to(line, (8, line.shape[1])).T[:, 0:1])
        embeds.append(columns)
    for k in range(2):
        value = None
        for g, columns in enumerate(embeds):
            for s in range(seq_count):
                line = 8 + g * films + 2 * s + k
                term = columns[s] * total[line : line + 1, :]
                value = term if value is None else value + term
        time_ref[:, k * width : (k + 1) * width] = value


def small_sums(who, own_embed, other_embed, parts, top, lines, width):
    vmem = pl.BlockSpec(memory_space=pltpu.VMEM)
    tall = lines * width // 128
    tail = pl.BlockSpec((tall, 128), lambda i: (top // tall, 0))
    return pl.pallas_call(
        functools.partial(small_kernel, own_embed.shape[0], len(parts)),
        grid=(1,),
        in_specs=[pl.BlockSpec(memory_space=pltpu.SMEM)]
        + [vmem] * 2
        + [tail] * len(parts),
        out_specs=[vmem] * 7,
        out_shape=[jax.ShapeDtypeStruct((own_embed.shape[1], 2 * width), F32)]
        + [jax.ShapeDtypeStruct((1, width // 2), F32)] * 4
        + [
            jax.ShapeDtypeStruct((1, 2 * width), F32),
            jax.ShapeDtypeStruct((1, width // 2), F32),
        ],
        scratch_shapes=[pltpu.VMEM((lines, width), F32)],
        compiler_params=pltpu.CompilerParams(vmem_limit_bytes=VMEM_BYTES),
        cost_estimate=pl.CostEstimate(
            flops=1000000, bytes_accessed=2000000, transcendentals=0
        ),
        name="small_gradients",
    )(who, own_embed, other_embed, *parts)


def stream(chips, copies_of, fill):
    pending = [None, None]
    for at in range(chips):
        slot = at % 2
        if pending[slot] is not None:
            for copy in pending[slot]:
                copy.wait()
        fill(at, slot)
        pending[slot] = copies_of(at, slot)
        for copy in pending[slot]:
            copy.start()
    for copies in pending:
        if copies is not None:
            for copy in copies:
                copy.wait()


def wide_kernel(first, chunks, place_ref, *refs):
    parts = refs[:chunks]
    up_ref, down_ref, out_ref, up_slots, down_slots, out_slots, sems = refs[-7:]
    core = place_ref[0] % 2
    deep = out_slots.shape[1] // 2
    size = up_ref.shape[0]
    hidden = up_ref.shape[1]
    width = down_ref.shape[1]

    def fill(at, slot):
        for j in range(2):
            ref = parts[2 * at + j]
            column = pl.ds(pl.multiple_of((j ^ core) * 128, 128), 128)
            for k in range(2):
                up_slots[slot, k, :, column] = ref[k * size : (k + 1) * size, :].astype(
                    F32
                )
            row = pl.ds(pl.multiple_of((j ^ core) * 128, 128), 128)
            for k in range(width // 128):
                top = 2 * size + k * 128
                down_slots[slot, row, k * 128 : (k + 1) * 128] = ref[
                    top : top + 128, :
                ].astype(F32)
            row = pl.ds(pl.multiple_of((j ^ core) * deep, deep), deep)
            for k in range(width // 128):
                top = 2 * size + width + k * deep
                out_slots[slot, row, k * 128 : (k + 1) * 128] = ref[
                    top : top + deep, :
                ].astype(F32)

    def copies_of(at, slot):
        chip = place_ref[2 * (at + first)] // 2
        copies = []
        for k in range(2):
            column = pl.multiple_of(k * (hidden // 2) + chip * 256, 256)
            copies.append(
                pltpu.make_async_copy(
                    up_slots.at[slot, k],
                    up_ref.at[:, pl.ds(column, 256)],
                    sems.at[slot, k],
                )
            )
        row = pl.multiple_of(chip * 256, 256)
        copies.append(
            pltpu.make_async_copy(
                down_slots.at[slot], down_ref.at[pl.ds(row, 256), :], sems.at[slot, 2]
            )
        )
        row = pl.multiple_of(chip * 2 * deep, 2 * deep)
        copies.append(
            pltpu.make_async_copy(
                out_slots.at[slot], out_ref.at[pl.ds(row, 2 * deep), :], sems.at[slot, 3]
            )
        )
        return copies

    stream(chunks // 2, copies_of, fill)


def expand_wide(place, first, parts, width, earlier):
    devices = place.shape[0]
    size = width // 2
    vmem = pl.BlockSpec(memory_space=pltpu.VMEM)
    hbm = pl.BlockSpec(memory_space=pl.ANY)
    return pl.pallas_call(
        functools.partial(wide_kernel, first, len(parts)),
        in_specs=[pl.BlockSpec(memory_space=pltpu.SMEM)]
        + [vmem] * len(parts)
        + [hbm] * len(earlier),
        out_specs=[hbm, hbm, hbm],
        out_shape=[
            jax.ShapeDtypeStruct((size, 2 * devices * 128), F32),
            jax.ShapeDtypeStruct((devices * 128, width), F32),
            jax.ShapeDtypeStruct((size, width), F32),
        ],
        scratch_shapes=[
            pltpu.VMEM((2, 2, size, 256), F32),
            pltpu.VMEM((2, 256, width), F32),
            pltpu.VMEM((2, 2 * size // devices, width), F32),
            pltpu.SemaphoreType.DMA((2, 4)),
        ],
        input_output_aliases={1 + len(parts) + k: k for k in range(len(earlier))},
        compiler_params=pltpu.CompilerParams(vmem_limit_bytes=VMEM_BYTES),
        cost_estimate=pl.CostEstimate(
            flops=parts[0].size * len(parts),
            bytes_accessed=6 * parts[0].size * len(parts),
            transcendentals=0,
        ),
        name="expand_wide",
    )(place, *parts, *earlier)


def last_kernel(head_size, in_ref, out_ref):
    pairs = []
    for j in range(2):
        for k in range(in_ref.shape[0] // 4):
            pairs.append((in_ref[4 * k + j], in_ref[4 * k + 2 + j]))
    for at, (first, second) in enumerate(pairs):
        both = jnp.concatenate([first, second], axis=0).astype(F32)
        out_ref[:, at * 2 * head_size : (at + 1) * 2 * head_size] = both.T


def expand_last(parts, head_size):
    devices, tall, depth = parts.shape
    width = devices * head_size
    return pl.pallas_call(
        functools.partial(last_kernel, head_size),
        grid=(3,),
        in_specs=[pl.BlockSpec((devices, head_size, depth), lambda k: (0, k, 0))],
        out_specs=pl.BlockSpec((depth, width), lambda k: (0, k)),
        out_shape=jax.ShapeDtypeStruct((depth, 3 * width), F32),
        compiler_params=pltpu.CompilerParams(vmem_limit_bytes=VMEM_BYTES),
        cost_estimate=pl.CostEstimate(
            flops=parts.size, bytes_accessed=6 * parts.size, transcendentals=0
        ),
        name="expand_last",
    )(parts)


def times_rows(values, pieces):
    return sum(
        jnp.dot(
            lax.dynamic_slice_in_dim(values, at, piece.shape[0], 1),
            piece,
            preferred_element_type=F32,
        )
        for piece, at in pieces
    )


def times_rows_t(values_t, pieces):
    return sum(
        dims(lax.dynamic_slice_in_dim(values_t, at, piece.shape[0], 0), piece, 0, 0)
        for piece, at in pieces
    )


def joined(parts, pieces, dim):
    if len(parts) == 1:
        return parts[0]
    shape = list(parts[0].shape)
    shape[dim] = sum(part.shape[dim] for part in parts)
    out = jnp.zeros(shape, parts[0].dtype)
    for part, (_, at) in zip(parts, pieces):
        out = lax.dynamic_update_slice_in_dim(out, part, at, dim)
    return out


def rows_of(pieces, start, size):
    out = None
    for piece, at in pieces:
        length = piece.shape[0]
        local = jnp.clip(start - at, 0, length - size)
        found = lax.dynamic_slice_in_dim(piece, local, size, 0)
        inside = (start >= at) & (start < at + length)
        out = found if out is None else jnp.where(inside, found, out)
    return out


def body_general(
    ctx_size, fsdp_size,
    tokens, w_qkv, w_out, w_up, w_down, w_time, gain_one, bias_one, gain_two, bias_two, bias_up,
    bias_down, lengths, time_steps, cotangent,
):
    me = lax.axis_index("ctx")
    shard = lax.axis_index("fsdp")
    rows = tokens.shape[1]
    width = tokens.shape[2]
    count = rows * ctx_size
    head_size = width // HEADS
    repeats = ctx_size // HEADS
    columns = head_size // repeats
    seq_count = lengths.shape[1]
    hidden = w_up.shape[1]

    def gather_small(values):
        return lax.all_gather(values, "fsdp", axis=0, tiled=True)

    def fetch(weight):
        return [(gather_small(weight), 0)]

    def scatter_sum(values, dim):
        return lax.psum_scatter(
            values.astype(BF16), "fsdp", scatter_dimension=dim, tiled=True
        )

    def gather(values):
        return lax.all_gather(values, "ctx", axis=0, tiled=False)

    ends = []
    for s in range(seq_count):
        ends.append(lengths[0, s] + (ends[-1] if ends else 0))
    ends_vector = jnp.stack(ends)
    index = me * rows + jnp.arange(rows, dtype=jnp.int32)
    segment = segments(ends, index)
    live = (segment < seq_count).astype(F32)[:, None]
    all_index = jnp.arange(count, dtype=jnp.int32)
    all_position = positions(ends, all_index, segments(ends, all_index))
    half_width = head_size // 2
    inverse = jnp.exp(
        -math.log(10000.0) * jnp.arange(half_width, dtype=F32) / half_width
    )
    angle = inverse[:, None] * all_position.astype(F32)[None, :]
    cos = jnp.cos(angle)
    sin = jnp.sin(angle)

    all_tokens = gather(tokens[0]).reshape(count, width)
    inputs = tokens[0].astype(F32)
    grad_y = cotangent[0].astype(F32) * live
    grad_y_b = grad_y.astype(BF16)
    all_grad_y = gather(grad_y_b).reshape(count, width)

    small = [gain_one, bias_one, gain_two, bias_two, bias_down, bias_up]
    packed = gather_small(jnp.concatenate(small)[None, :])
    vectors = []
    at = 0
    for vector in small:
        size = vector.shape[0]
        vectors.append(packed[:, at : at + size].reshape(1, -1).astype(F32))
        at += size
    gain_first, bias_first, gain_second, bias_second, bias_output, bias_hidden = vectors

    all_steps = lax.all_gather(time_steps.astype(F32), "fsdp", axis=0, tiled=True)
    all_embedded = embed(all_steps, w_time.shape[0] * fsdp_size).astype(BF16)
    embedded = lax.dynamic_index_in_dim(all_embedded, shard, 0, keepdims=False)
    film = times_rows(embedded, fetch(w_time))
    film = jnp.concatenate([film, jnp.zeros((1, 2 * width), F32)], axis=0)
    gains = gain_first + film[:, :width]
    shifts = bias_first + film[:, width:]

    head = me // repeats
    w_head = jnp.concatenate(
        [
            lax.dynamic_slice_in_dim(w_qkv, k * width + head * head_size, head_size, 1)
            for k in range(3)
        ]
        + [jnp.zeros((w_qkv.shape[0], head_size), BF16)],
        axis=1,
    )
    w_head = gather_small(w_head)

    base = jnp.arange(ctx_size, dtype=jnp.int32) * rows
    all_norm, query_t, key, key_t, value_t, pair = project(
        all_tokens, base, ends_vector, gains, shifts, w_head, cos, sin, rows, head_size
    )
    place = jnp.arange(ctx_size, dtype=jnp.int32)
    out_t, sent, lse = attend(place, query_t, key, value_t, rows)

    part = (me % repeats) * columns
    if repeats > 1:
        sent = lax.dynamic_slice_in_dim(sent, part, columns, 1)
    attended_t = lax.all_to_all(sent, "ctx", 0, 0, tiled=True).reshape(width, rows)

    out_pieces = fetch(w_out)
    up_pieces = fetch(w_up)
    down_pieces = fetch(w_down)
    qkv_pieces = fetch(w_qkv)
    resid = inputs + times_rows_t(attended_t, out_pieces)
    normal_two, scale_two = stats(resid)
    norm_two_b = (normal_two * gain_second + bias_second).astype(BF16)
    all_norm_two = gather(norm_two_b).reshape(count, width)
    pre = times_rows(norm_two_b, up_pieces) + bias_hidden
    act, slope = gelu_parts(pre)
    branch = times_rows(act.astype(BF16), down_pieces) + bias_output
    output = (live * (resid + branch)).astype(BF16)
    grad_act = joined([dims(grad_y_b, p, 1, 1) for p, _ in down_pieces], down_pieces, 1)
    grad_pre = grad_act * slope
    grad_bias_up = jnp.sum(grad_pre, axis=0)
    grad_pre_b = grad_pre.astype(BF16)
    grad_norm_two = joined([dims(grad_pre_b, p, 1, 1) for p, _ in up_pieces], up_pieces, 1)
    grad_resid = grad_y + stats_back(grad_norm_two * gain_second, normal_two, scale_two)
    grad_resid_b = grad_resid.astype(BF16)
    grad_att_t = joined(
        [dims(p, grad_resid_b, 1, 1) for p, _ in out_pieces], out_pieces, 0
    ).astype(BF16)
    grad_att_t = grad_att_t.reshape(HEADS, head_size, rows)
    if repeats > 1:
        grad_att_t = jnp.repeat(grad_att_t, repeats, axis=0)
    grad_att = lax.all_to_all(grad_att_t, "ctx", 0, 0, tiled=True)

    mixed_t, _ = attend_back(
        place, query_t, grad_att, out_t, lse, key, key_t, pair, cos, sin, rows
    )
    mixed_t = mixed_t.reshape(3, head_size, count)
    if repeats > 1:
        mixed_t = lax.dynamic_slice_in_dim(mixed_t, part, columns, 1)
    mixed_t = mixed_t.reshape(3 * columns, count)
    mixed_sent = mixed_t.reshape(3 * columns, ctx_size, rows).transpose(1, 0, 2)
    mixed_got = lax.all_to_all(mixed_sent, "ctx", 0, 0, tiled=True)
    grad_mixed_t = (
        mixed_got.reshape(ctx_size, 3, columns, rows)
        .transpose(1, 0, 2, 3)
        .reshape(3 * width, rows)
    )
    grad_norm_one = joined(
        [dims(grad_mixed_t, p, 0, 1) for p, _ in qkv_pieces], qkv_pieces, 1
    )
    normal_one, scale_one = stats(inputs)
    seg_col = segment[:, None]
    gain_tok = gains[0:1]
    for s in range(1, seq_count + 1):
        gain_tok = jnp.where(seg_col == s, gains[s : s + 1], gain_tok)
    grad_tokens = (
        grad_resid + stats_back(grad_norm_one * gain_tok, normal_one, scale_one)
    ).astype(BF16)
    film_terms = jnp.concatenate([grad_norm_one * normal_one, grad_norm_one], axis=1)
    film_sums = [
        jnp.sum(jnp.where(seg_col == s, film_terms, 0.0), axis=0)
        for s in range(seq_count + 1)
    ]

    sums = [
        jnp.sum(grad_norm_two * normal_two, axis=0),
        jnp.sum(grad_norm_two, axis=0),
        jnp.sum(grad_y, axis=0),
        grad_bias_up,
    ] + film_sums
    sizes = [vector.shape[0] for vector in sums]
    total = lax.psum(jnp.concatenate(sums)[None, :], "ctx")
    total = lax.all_gather(total, "fsdp", axis=0, tiled=True)
    split = []
    at = 0
    for size in sizes:
        split.append(total[:, at : at + size])
        at += size

    def own(vector):
        size = vector.shape[0] // fsdp_size
        return lax.dynamic_slice_in_dim(vector, shard * size, size, 0)

    sum_gain_two, sum_bias_two, sum_bias_down, sum_bias_up = (
        own(jnp.sum(vector, axis=0)) for vector in split[:4]
    )
    film_all = jnp.sum(sum(split[4:]), axis=0)
    sum_gain_one = own(film_all[:width])
    sum_bias_one = own(film_all[width:])
    film_grad = jnp.stack(split[4 : 4 + seq_count], axis=1).reshape(-1, 2 * width)
    embedded_rows = lax.dynamic_slice_in_dim(
        all_embedded.astype(F32).reshape(film_grad.shape[0], -1),
        shard * w_time.shape[0],
        w_time.shape[0],
        1,
    )
    grad_time = sum(
        embedded_rows[g][:, None] * film_grad[g][None, :]
        for g in range(film_grad.shape[0])
    )

    slice_width = hidden // (ctx_size * fsdp_size)
    starts = [
        k * (hidden // fsdp_size) + me * slice_width for k in range(fsdp_size)
    ]
    w_up_cols = []
    for piece, _ in up_pieces:
        w_up_cols.append(
            jnp.concatenate(
                [
                    lax.dynamic_slice_in_dim(piece, start, slice_width, 1)
                    for start in starts
                ],
                axis=1,
            )
        )
    w_up_slice = joined(w_up_cols, up_pieces, 0)
    w_down_slice = jnp.concatenate(
        [rows_of(down_pieces, start, slice_width) for start in starts], axis=0
    )
    bias_slice = jnp.concatenate(
        [
            lax.dynamic_slice_in_dim(bias_hidden, start, slice_width, 1)
            for start in starts
        ],
        axis=1,
    )
    pre_slice = dims(all_norm_two, w_up_slice, 1, 0) + bias_slice
    act_slice, slope_slice = gelu_parts(pre_slice)
    grad_pre_slice = (dims(all_grad_y, w_down_slice, 1, 1) * slope_slice).astype(BF16)
    down_slice = dims(act_slice.astype(BF16), all_grad_y, 0, 0)
    up_slice = dims(all_norm_two, grad_pre_slice, 0, 0)
    grad_down = gather(scatter_sum(down_slice, 0)).reshape(-1, width).astype(F32)
    up_parts = gather(scatter_sum(up_slice, 0))
    grad_up = (
        up_parts.reshape(ctx_size, width // fsdp_size, fsdp_size, slice_width)
        .transpose(1, 2, 0, 3)
        .reshape(width // fsdp_size, hidden)
        .astype(F32)
    )
    out_part = jnp.dot(attended_t, grad_resid_b, preferred_element_type=F32)
    out_rows = lax.psum_scatter(
        out_part.astype(BF16), ("fsdp", "ctx"), scatter_dimension=0, tiled=True
    )
    grad_out = gather(out_rows).reshape(-1, width).astype(F32)
    qkv_slice = jnp.dot(mixed_t, all_norm, preferred_element_type=F32)
    qkv_parts = gather(scatter_sum(qkv_slice, 1))
    grad_qkv = (
        qkv_parts.reshape(ctx_size, 3, columns, width // fsdp_size)
        .transpose(3, 1, 0, 2)
        .reshape(width // fsdp_size, 3 * width)
        .astype(F32)
    )
    return (
        output[None],
        grad_tokens[None],
        grad_qkv,
        grad_out,
        grad_up,
        grad_down,
        grad_time,
        sum_gain_one,
        sum_bias_one,
        sum_gain_two,
        sum_bias_two,
        sum_bias_up,
        sum_bias_down,
    )


def ring_tables(ctx_size):
    chips = ctx_size // 2
    order = list(range(0, chips, 2)) + list(range(1, chips, 2))[::-1]
    offsets = [0]
    for step in range(1, chips // 2 + 1):
        offsets.append(-step)
        if step <= (chips - 1) // 2:
            offsets.append(step)
    place = np.zeros((ctx_size, ctx_size), np.int32)
    for me in range(ctx_size):
        at = order.index(me // 2)
        for k, offset in enumerate(offsets):
            chip = order[(at + offset) % chips]
            place[me, 2 * k] = 2 * chip + me % 2
            place[me, 2 * k + 1] = 2 * chip + 1 - me % 2
    return order, place


def fence(*values):
    return lax.optimization_barrier(values)


def after(values, *earlier):
    return lax.optimization_barrier((values, *earlier))[0]


def body(
    ctx_size, fsdp_size,
    tokens, w_qkv, w_out, w_up, w_down, w_time, gain_one, bias_one, gain_two, bias_two, bias_up,
    bias_down, lengths, time_steps, cotangent,
):
    me = lax.axis_index("ctx")
    shard = lax.axis_index("fsdp")
    core = me % 2
    rows = tokens.shape[1]
    width = tokens.shape[2]
    head_size = width // HEADS
    seq_count = lengths.shape[1]
    hidden = w_up.shape[1]
    other = 1 - shard
    chips = ctx_size // 2
    half = width // 2
    units = hidden // (ctx_size * fsdp_size)
    order, place_table = ring_tables(ctx_size)
    place = jnp.asarray(place_table)[me]
    who = jnp.stack([me, shard]).astype(jnp.int32)

    def across(values):
        return lax.ppermute(values, "fsdp", [(0, 1), (1, 0)])

    def gather(values):
        return lax.all_gather(values, "ctx", axis=0, tiled=True)

    def flip(values, bit=0):
        return lax.ppermute(
            values, "ctx", [(i, i ^ (1 << bit)) for i in range(ctx_size)]
        )

    def hop(values, step):
        return lax.ppermute(
            values,
            "ctx",
            [
                (2 * order[at] + c, 2 * order[(at + step) % chips] + c)
                for at in range(chips)
                for c in range(2)
            ],
        )

    def by_shard(mine, others, axis):
        first = jnp.where(shard == 0, mine, others)
        second = jnp.where(shard == 0, others, mine)
        return jnp.concatenate([first, second], axis=axis)

    def cut(values, start, size, axis):
        return lax.dynamic_slice_in_dim(values, start, size, axis)

    def halve(values, axis, mine, send):
        keep = lax.dynamic_index_in_dim(values, mine, axis, keepdims=False)
        give = lax.dynamic_index_in_dim(values, 1 - mine, axis, keepdims=False)
        return keep + send(give.astype(BF16)).astype(F32)

    ends = []
    for s in range(seq_count):
        ends.append(lengths[0, s] + (ends[-1] if ends else 0))
    ends_vector = jnp.stack(ends)
    base = place * rows
    index = me * rows + jnp.arange(rows, dtype=jnp.int32)
    segment = segments(ends, index)
    seg_col = segment[:, None]
    live = (segment < seq_count).astype(F32)[:, None]
    own_tokens = tokens[0]
    steps_row = time_steps.reshape(1, seq_count)
    high = (steps_row // 256).astype(BF16)
    low = (steps_row % 256).astype(BF16)
    head = core * chips + me // 2
    w_head = jnp.concatenate(
        [cut(w_qkv, k * width + head * head_size, head_size, 1) for k in range(3)], axis=1
    )
    class Ring:
        def __init__(self, values):
            self.right = self.left = values
            self.parts = [values]
            self.step = 0

        def go(self, *earlier):
            right, left = self.right, self.left
            if earlier:
                right, left = (
                    after(right, *earlier),
                    after(left, *earlier),
                )
            self.step += 1
            self.right = hop(right, 1)
            if self.step <= (chips - 1) // 2:
                self.left = hop(left, -1)
                return [self.right, self.left]
            return [self.right]

        def came(self, values):
            self.right = values[0]
            if len(values) > 1:
                self.left = values[1]
            self.parts += values

    def fenced(groups):
        flat = [v for group in groups for v in group]
        flat = list(fence(*flat))
        out = []
        for group in groups:
            out.append(flat[: len(group)])
            flat = flat[len(group) :]
        return out

    def with_flips(values):
        return [part for v in values for part in (v, flip(v))]

    tok = Ring(own_tokens)
    tok_new = tok.go()
    packed = jnp.concatenate([gain_one[None, :], bias_one[None, :], high, low], axis=1)
    tok_new, (packed, w_head) = fenced([tok_new, [packed, w_head]])
    tok.came(tok_new)

    tok_new = tok.go()
    packed_other = across(packed)
    w_head_other = across(w_head)
    base = after(base, packed)
    all_index = (base[:, None] + jnp.arange(rows, dtype=jnp.int32)[None, :]).reshape(-1)
    all_position = positions(ends, all_index, segments(ends, all_index))
    half_width = head_size // 2
    inverse = jnp.exp(
        -math.log(10000.0) * jnp.arange(half_width, dtype=F32) / half_width
    )
    angle = inverse[:, None] * all_position.astype(F32)[None, :]
    cos = jnp.cos(angle)
    sin = jnp.sin(angle)

    inputs = own_tokens.astype(F32)
    grad_y = cotangent[0].astype(F32) * live
    grad_y_b = grad_y.astype(BF16)
    out_half = w_out.shape[0] // 2
    me_1 = after(me, packed)
    out_mine = across(cut(w_out, (me_1 % 2) * out_half, out_half, 0))
    tok_new, (packed_other, w_head, cos, sin, grad_y_b, me_2, place, who, base, w_head_other) = fenced(
        [tok_new, [packed_other, w_head, cos, sin, grad_y_b, me, place, who, base, w_head_other]]
    )
    tok.came(tok_new)

    tok_new = tok.go()
    packed_all = by_shard(packed, packed_other, 0)

    def vector_of(values, at, size):
        return values[:, at : at + size].reshape(1, -1).astype(F32)

    gain_first = vector_of(packed_all, 0, half)
    bias_first = vector_of(packed_all, half, half)
    all_steps = packed_all[:, width : width + seq_count].astype(F32) * 256.0 + packed_all[
        :, width + seq_count :
    ].astype(F32)
    all_embedded = embed(all_steps, w_time.shape[0] * fsdp_size).astype(BF16)
    own_part = cut(all_embedded, shard * w_time.shape[0], w_time.shape[0], 2)
    film_part = jnp.dot(
        own_part.reshape(fsdp_size * seq_count, -1), w_time, preferred_element_type=F32
    ).reshape(fsdp_size, seq_count, 2 * width)
    film_other = across(lax.dynamic_index_in_dim(film_part, other, 0, keepdims=False))
    film = film_other + lax.dynamic_index_in_dim(film_part, shard, 0, keepdims=False)
    film = jnp.concatenate([film, jnp.zeros((1, 2 * width), F32)], axis=0)
    gains = gain_first + film[:, :width]
    shifts = bias_first + film[:, width:]
    up_parts = 2
    up_deep = w_up.shape[0] // up_parts
    quarter = hidden // 4
    up_send = [
        lax.dynamic_slice(w_up, (p * up_deep, (me_2 % 4) * quarter), (up_deep, quarter))
        for p in range(up_parts)
    ]
    tok_new, (gains, shifts, out_mine), up_send = fenced(
        [tok_new, [gains, shifts, out_mine], up_send]
    )
    tok_flips = with_flips(tok.parts)
    tok.came(tok_new)

    tok_last = tok.go()
    all_grad_y = gather(after(grad_y_b, gains))
    grad_y_other = across(grad_y_b)
    up_mine = [across(after(up_send[0], gains))]
    tok_flips += with_flips(tok_new)
    constants = (base, ends_vector, gains, shifts, w_head, w_head_other, cos, sin, head_size)
    head_values = project_chunks(who, tok_flips, *constants)
    head_values, tok_last, (grad_y_other, gain_two, up_send[1]) = fenced(
        [head_values, tok_last, [grad_y_other, gain_two, up_send[1]]]
    )

    up_mine.append(across(up_send[1]))
    all_norm, query_t, key, key_t, value_t, pair = project_chunks(
        who, with_flips(tok_last), *constants, first=chips - 1, earlier=head_values
    )
    out_t, sent, lse = attend(place, query_t, key, value_t, rows)
    rest = jnp.concatenate(
        [v[None, :] for v in (gain_two, bias_two, bias_down, bias_up)], axis=1
    )
    out_t, sent, lse, *up_mine, rest, me_5, grad_y_other = fence(
        out_t, sent, lse, *up_mine, rest, me, grad_y_other
    )

    attended = lax.all_to_all(sent, "ctx", 0, 0, tiled=True)
    rest_other = across(rest)
    up_side = [flip(up_mine[0], 1), flip(up_mine[1], 1)]
    qkv_half = w_qkv.shape[0] // 2
    qkv_send = [
        cut(w_qkv, (me_5 % 2) * qkv_half + k * (qkv_half // 2), qkv_half // 2, 0)
        for k in range(2)
    ]
    qkv_mine = [across(qkv_send[0])]
    far_grad = across(dims(grad_y_other, w_down, 1, 1).astype(BF16))
    near_grad = dims(after(grad_y_b, lse), w_down, 1, 1)
    out_pieces = (w_out, out_mine, flip(out_mine))
    pieces = [with_flips([v]) for v in up_mine]
    rest_5 = [rest_other, me_5, qkv_send[1], qkv_mine[0]]
    (attended, up_side[0], near_grad), rest_5, *pieces = fenced(
        [[attended, up_side[0], near_grad], rest_5, *pieces]
    )
    rest_other, me_6, qkv_send[1], qkv_mine[0] = rest_5

    rest = by_shard(rest, rest_other, 0)
    gain_second = vector_of(rest, 0, half)
    bias_second = vector_of(rest, half, half)
    bias_output = vector_of(rest, width, half)
    bias_hidden = vector_of(rest, width + half, hidden // 2)
    resid, normal_two, scale_two, norm_two_b = middle(
        who, attended, out_pieces, own_tokens, gain_second, bias_second
    )
    first_units = shard * (hidden // 2) + me_6 * units
    second_units = other * (hidden // 2) + me_6 * units
    up_first = cut(w_up, first_units, units, 1)
    up_second = cut(w_up, second_units, units, 1)
    up_own = jnp.concatenate([up_first, up_second], axis=1)
    down_own = cut(w_down, me_6 * units, units, 0)
    up_give = jnp.concatenate([up_second, up_first], axis=1)
    pieces[0] = pieces[0] + with_flips([up_side[0]])
    rest_6 = [up_own, up_give, down_own]
    (norm_two_b, far_grad, up_side[1]), rest_6, *pieces = fenced(
        [[norm_two_b, far_grad, up_side[1]], rest_6, *pieces]
    )
    up_own, up_give, down_own = rest_6
    pieces = pieces[0] + pieces[1] + with_flips([up_side[1]])

    all_norm_two = gather(norm_two_b)
    up_other = across(after(up_give, norm_two_b))
    down_other = across(after(down_own, norm_two_b))
    act_b, grad_resid, grad_resid_b, grad_att, sums = feed(
        who, norm_two_b, w_up, pieces, near_grad, far_grad, bias_hidden, normal_two, scale_two,
        gain_second, grad_y_b, out_pieces,
    )
    grad_att, grad_resid_b, me_8, up_other, down_other = fence(
        grad_att, grad_resid_b, me, up_other, down_other
    )

    grad_att = grad_att.reshape(HEADS, head_size, rows)
    grad_att = lax.all_to_all(grad_att, "ctx", 0, 0, tiled=True)
    qkv_mine.append(across(after(qkv_send[1], up_other, down_other)))
    deep = width // (ctx_size * fsdp_size)
    out_part = jnp.dot(
        attended.reshape(width, rows), grad_resid_b, preferred_element_type=F32
    )
    out_part = out_part.reshape(chips, fsdp_size, 2, deep, width)
    out_part = halve(out_part, 2, core, flip)
    down_half = w_down.shape[0] // 2
    down_send = cut(w_down, (me_8 % 2) * down_half, down_half, 0)
    grad_att, down_send, out_part = fence(grad_att, down_send, out_part)

    out_part = halve(out_part, 1, shard, across)
    mixed, mixed_sent = attend_back(
        place, query_t, grad_att, out_t, lse, key, key_t, pair, cos, sin, rows
    )
    mixed, mixed_sent, out_part, qkv_mine[1] = fence(
        mixed, mixed_sent, out_part, qkv_mine[1]
    )

    mixed_got = lax.all_to_all(mixed_sent, "ctx", 0, 0, tiled=True)
    qkv_slice = jnp.dot(mixed, all_norm, preferred_element_type=F32)
    qkv_keep = cut(qkv_slice, shard * half, half, 1)
    qkv_give = cut(qkv_slice, other * half, half, 1).astype(BF16)
    bias_slice = jnp.concatenate(
        [cut(bias_hidden, at, units, 1) for at in (first_units, second_units)], axis=1
    )
    qkv_other = across(qkv_give)
    out_part = halve(
        out_part.reshape(-1, 2, deep, width), 1, (me >> 1) % 2, lambda v: flip(v, 1)
    )
    qkv_sum = (qkv_keep + qkv_other.astype(F32)).astype(BF16)
    qkv_sum, bias_slice, all_norm_two, all_grad_y, out_part = fence(
        qkv_sum, bias_slice, all_norm_two, all_grad_y, out_part
    )

    all_qkv = gather(qkv_sum)
    out_part = halve(
        out_part.reshape(-1, 2, deep, width), 1, (me >> 2) % 2, lambda v: flip(v, 2)
    )
    wide_keep, wide_give = slices(
        who, all_norm_two, all_grad_y, up_own, up_other, down_own, down_other, bias_slice
    )
    wide_keep, wide_give, mixed_got, out_part = fence(
        wide_keep, wide_give, mixed_got, out_part
    )

    wide_other = across(wide_give)
    qkv_mine = fence(*qkv_mine, wide_give)[:-1]
    qkv_pieces = (w_qkv, *qkv_mine, *[flip(v) for v in qkv_mine])
    grad_tokens, total = first_back(
        who, ends_vector, mixed_got, qkv_pieces, own_tokens, grad_resid, gains, sums
    )
    total_other = across(total)
    out_part = halve(
        out_part.reshape(-1, 2, deep, width), 1, (me >> 3) % 2, lambda v: flip(v, 3)
    )
    wide_other, total, total_other, out_part = fence(
        wide_other, total, total_other, out_part
    )

    total = jnp.concatenate(
        [total[:8] + total_other[:8], total[8:], total_other[8:]], axis=0
    )
    total = jnp.pad(total, ((0, -total.shape[0] % 16), (0, 0))).astype(BF16)
    lines = total.shape[0]

    def narrow(values):
        return [values[:, k * 128 : (k + 1) * 128] for k in range(width // 128)]

    wide = jnp.concatenate(
        [(wide_keep + wide_other.astype(F32)).astype(BF16)]
        + narrow(out_part.reshape(deep, width).astype(BF16))
        + narrow(total),
        axis=0,
    )
    wide_ring = Ring(wide)
    wide_new = wide_ring.go()
    down_mine = across(after(down_send, wide))
    wide_new = list(fence(*wide_new))
    wide_flips = with_flips(wide_ring.parts)
    wide_ring.came(wide_new)

    wide_flips += with_flips(wide_new)
    wide_new = wide_ring.go()
    grads = expand_wide(place, 0, wide_flips, width, ())
    own_embed = lax.dynamic_index_in_dim(own_part, shard, 0, keepdims=False)
    other_embed = lax.dynamic_index_in_dim(own_part, other, 0, keepdims=False)
    own_embed = own_embed.astype(F32)
    other_embed = other_embed.astype(F32)
    wide_new, grads, (down_mine, own_embed, other_embed, all_qkv) = fenced(
        [wide_new, grads, [down_mine, own_embed, other_embed, all_qkv]]
    )
    wide_ring.came(wide_new)

    more_flips = with_flips(wide_new)
    wide_new = wide_ring.go()
    grad_qkv = expand_last(all_qkv.reshape(ctx_size, 3 * head_size, half), head_size)
    down_flip = flip(down_mine)
    branch = bias_output
    for b, row in (
        (w_down, shard * (hidden // 2)),
        (down_mine, other * (hidden // 2) + core * down_half),
        (down_flip, other * (hidden // 2) + (1 - core) * down_half),
    ):
        branch = branch + jnp.dot(
            cut(act_b, row, b.shape[0], 1), b, preferred_element_type=F32
        )
    output = (live * (resid + branch)).astype(BF16)
    wide_new, (output, grad_qkv), more_flips = fenced(
        [wide_new, [output, grad_qkv], more_flips]
    )

    tall = wide.shape[0] // 2
    last_top = hop(wide_new[0][:tall], 1)
    last_low = hop(wide_new[1][tall:], -1)
    more_flips += with_flips(wide_new)
    grads = expand_wide(place, len(wide_flips) // 2, more_flips, width, grads)
    grads, (last_top, last_low) = fenced([grads, [last_top, last_low]])

    wide_last = with_flips([jnp.concatenate([last_top, last_low], axis=0)])
    grad_up, grad_down, grad_out = expand_wide(
        place, chips - 1, wide_last, width, grads
    )
    grad_time, *vectors = small_sums(
        who, own_embed, other_embed, wide_flips + more_flips + wide_last,
        wide.shape[0] - lines * width // 128, lines, width,
    )
    return (
        output[None],
        grad_tokens[None],
        grad_qkv,
        grad_out,
        grad_up,
        grad_down,
        grad_time,
        *[vector.reshape(-1) for vector in vectors],
    )


def solution(mesh):
    in_specs = (
        (P("fsdp", "ctx", None),)
        + (P("fsdp", None),) * 5
        + (P("fsdp"),) * 6
        + (P("fsdp", None), P("fsdp", None), P("fsdp", "ctx", None))
    )
    out_specs = (
        (P("fsdp", "ctx", None),) * 2 + (P("fsdp", None),) * 5 + (P("fsdp"),) * 6
    )
    ctx_size, fsdp_size = mesh.shape["ctx"], mesh.shape["fsdp"]
    paired = ctx_size == HEADS and fsdp_size == 2
    return jax.shard_map(
        functools.partial(body if paired else body_general, ctx_size, fsdp_size),
        mesh=mesh,
        in_specs=in_specs,
        out_specs=out_specs,
        check_vma=False,
    )
```

```python
import functools
import math

import jax
import jax.numpy as jnp
import numpy as np
from jax import lax
from jax.experimental import pallas as pl
from jax.experimental.pallas import tpu as pltpu
from jax.sharding import PartitionSpec as P

HEADS = 16
EPSILON = 1e-05
NEGATIVE = -1e30
HIGH = lax.Precision.HIGHEST
F32 = jnp.float32
BF16 = jnp.bfloat16
VMEM_BYTES = 56 << 20


def dims(left, right, left_dim, right_dim):
    return lax.dot_general(
        left, right, (((left_dim,), (right_dim,)), ((), ())), preferred_element_type=F32
    )


def segments(ends, index):
    return sum((index >= end).astype(jnp.int32) for end in ends)


def positions(ends, index, segment):
    begin = jnp.zeros_like(index)
    for at, end in enumerate(ends):
        begin = jnp.where(segment > at, end, begin)
    return index - begin


def embed(steps_given, embed_width):
    half_width = embed_width // 2
    freq = jnp.exp(-math.log(10000.0) * jnp.arange(half_width, dtype=F32) / half_width)
    angle = steps_given.astype(F32)[..., None] * freq
    return jnp.concatenate([jnp.sin(angle), jnp.cos(angle)], axis=-1)


def stats(values):
    centre = jnp.mean(values, axis=-1, keepdims=True)
    centered = values - centre
    spread = jnp.mean(centered * centered, axis=-1, keepdims=True)
    scale = lax.rsqrt(spread + EPSILON)
    return centered * scale, scale


def stats_back(grad, normal, scale):
    return (
        grad
        - jnp.mean(grad, axis=-1, keepdims=True)
        - normal * jnp.mean(grad * normal, axis=-1, keepdims=True)
    ) * scale


def gelu_parts(pre):
    below = 0.5 * (1.0 + lax.erf(pre * math.sqrt(0.5)))
    density = jnp.exp(-0.5 * pre * pre) * (1.0 / math.sqrt(2.0 * math.pi))
    return pre * below, below + pre * density


def qkv_kernel(
    rows, head_size, first, ends_ref, base_ref, tokens_ref, gains_ref, shifts_ref, w_ref,
    cos_ref, sin_ref, *refs,
):
    norm_ref, query_t_ref, key_ref, key_t_ref, value_t_ref, pair_ref = refs[-6:]
    step = pl.program_id(0) + first
    block = tokens_ref.shape[0]
    seq_count = ends_ref.shape[0]
    half = head_size // 2
    values = tokens_ref[...].astype(F32)
    normal, _ = stats(values)
    chunks = block // rows

    def token_index(shape, axis):
        within = lax.broadcasted_iota(jnp.int32, shape, axis)
        index = within + base_ref[step * chunks]
        for at in range(1, chunks):
            index = jnp.where(
                within >= at * rows,
                within - at * rows + base_ref[step * chunks + at],
                index,
            )
        return index

    ends = [ends_ref[s] for s in range(seq_count)]
    seg_col = segments(ends, token_index((block, 1), 0))
    seg_row = segments(ends, token_index((1, block), 1))
    gains = gains_ref[0:1, :]
    shifts = shifts_ref[0:1, :]
    for s in range(1, seq_count + 1):
        gains = jnp.where(seg_col == s, gains_ref[s : s + 1, :], gains)
        shifts = jnp.where(seg_col == s, shifts_ref[s : s + 1, :], shifts)
    norm = (normal * gains + shifts).astype(BF16)
    norm_ref[...] = norm
    mixed = jnp.dot(norm, w_ref[...], preferred_element_type=F32)
    turned = mixed.T
    cos = cos_ref[...]
    sin = sin_ref[...]

    def turn(at):
        upper = turned[at : at + half]
        lower = turned[at + half : at + head_size]
        return jnp.concatenate(
            [upper * cos - lower * sin, lower * cos + upper * sin], axis=0
        ).astype(BF16)

    query = turn(0).astype(F32) * (float(head_size) ** -0.5)
    key = turn(head_size).astype(F32)
    value = turned[2 * head_size : 3 * head_size].astype(BF16).astype(F32)
    spare = 128 - head_size
    row_id = lax.broadcasted_iota(jnp.int32, (spare, block), 0)
    same = row_id == seg_row
    used = row_id <= seq_count
    key_tail = jnp.where((same & used) | ((row_id >= 8) & (row_id < 11)), 1.0, 0.0)
    query_tail = jnp.where(used & jnp.logical_not(same), NEGATIVE, 0.0)
    query_t_ref[...] = jnp.concatenate([query, query_tail], axis=0).astype(BF16)
    key_t_ref[...] = key.astype(BF16)
    value_t_ref[...] = value.astype(BF16)
    key_ref[...] = jnp.concatenate([key, key_tail], axis=0).T.astype(BF16)
    pair_ref[...] = jnp.concatenate([value, query], axis=0).T.astype(BF16)


def attend_kernel(
    chunk, rows, place_ref, query_ref, key_ref, value_ref, out_ref, sent_ref, lse_ref, score_ref, top_ref,
):
    core = place_ref[0] % 2
    count = key_ref.shape[0]
    step = pl.program_id(0)
    now = step % 2
    before = 1 - now
    query = query_ref[...]
    last_top = top_ref[before]
    top = None
    total = jnp.zeros_like(last_top)
    out = jnp.zeros(out_ref.shape, F32)
    for at in range(0, count, chunk):
        part = slice(at, at + chunk)
        score = jnp.dot(key_ref[part, :], query, preferred_element_type=F32)
        weight = jnp.exp(score_ref[before, part, :] - last_top)
        score_ref[now, part, :] = score
        high = jnp.max(score, axis=0, keepdims=True)
        top = high if top is None else jnp.maximum(top, high)
        total = total + jnp.sum(weight, axis=0, keepdims=True)
        out = out + jnp.dot(
            value_ref[:, part], weight.astype(BF16), preferred_element_type=F32
        )
    top_ref[now] = top

    @pl.when(step > 0)
    def _():
        result = out / total
        out_ref[...] = result
        for at in range(sent_ref.shape[0]):
            sent_ref[at ^ core] = result[:, at * rows : (at + 1) * rows].astype(BF16)
        lse_ref[...] = last_top + jnp.log(total)


def attend_back_kernel(
    chunk, rows, head_size, place_ref, query_ref, grad_ref, out_ref, lse_ref, key_ref, key_t_ref, pair_ref,
    pair_block_ref, cos_block_ref, sin_block_ref, cos_ref, sin_ref, mixed_ref, sent_ref, acc_ref,
):
    step = pl.program_id(0)
    core = place_ref[0] % 2
    per_step = grad_ref.shape[0]
    count = key_ref.shape[0]
    block = query_ref.shape[1]
    half = head_size // 2
    scale = float(head_size) ** -0.5

    @pl.when(step == 0)
    def _():
        acc_ref[...] = jnp.zeros_like(acc_ref)

    rest = -lse_ref[...]
    query = query_ref[...].astype(F32)
    row_id = lax.broadcasted_iota(jnp.int32, query.shape, 0)
    for k in range(3):
        piece = rest.astype(BF16).astype(F32)
        query = jnp.where(row_id == head_size + 8 + k, piece, query)
        rest = rest - piece
    query = query.astype(BF16)
    grad = jnp.concatenate(
        [grad_ref[at ^ core] for at in range(per_step)], axis=1
    ).astype(F32)
    delta = jnp.sum(grad * out_ref[...], axis=0, keepdims=True)
    grad_t = jnp.concatenate([grad, jnp.zeros((128 - head_size, block), F32)], axis=0)
    pair = pair_block_ref[...]
    lane = lax.broadcasted_iota(jnp.int32, pair.shape, 1)
    queries = jnp.where(lane >= head_size, pair.astype(F32), 0.0).astype(BF16)
    both = jnp.concatenate([queries, grad_t.T.astype(BF16)], axis=0)
    grad_t = grad_t.astype(BF16)
    grad_query = jnp.zeros((head_size, block), F32)
    for at in range(0, count, chunk):
        part = slice(at, at + chunk)
        score = jnp.dot(key_ref[part, :], query, preferred_element_type=F32)
        prob = jnp.exp(score)
        grad_prob = jnp.dot(pair_ref[part, :], grad_t, preferred_element_type=F32)
        grad_score = (prob * (grad_prob - delta)).astype(BF16)
        grad_query = grad_query + jnp.dot(
            key_t_ref[:, part], grad_score, preferred_element_type=F32
        )
        acc_ref[part, :] += jnp.dot(
            jnp.concatenate([grad_score, prob.astype(BF16)], axis=1),
            both,
            preferred_element_type=F32,
        )

    def turn_back(values, cos, sin):
        upper = values[:half]
        lower = values[half:]
        return jnp.concatenate(
            [upper * cos + lower * sin, lower * cos - upper * sin], axis=0
        ).astype(BF16)

    at = pl.multiple_of(step * block, block)
    query_part = turn_back(
        grad_query * scale, cos_block_ref[...], sin_block_ref[...]
    )
    mixed_ref[0:head_size, pl.ds(at, block)] = query_part
    for k in range(per_step):
        sent_ref[place_ref[step * per_step + k], 0:head_size, :] = query_part[
            :, k * rows : (k + 1) * rows
        ]

    @pl.when(step == pl.num_programs(0) - 1)
    def _():
        acc = acc_ref[...].T
        key_part = turn_back(acc[head_size : 2 * head_size], cos_ref[...], sin_ref[...])
        value_part = acc[:head_size].astype(BF16)
        parts = jnp.concatenate([key_part, value_part], axis=0)
        mixed_ref[head_size : 3 * head_size, :] = parts
        for k in range(count // rows):
            sent_ref[place_ref[k], head_size : 3 * head_size, :] = parts[
                :, k * rows : (k + 1) * rows
            ]


def whole(shape):
    return pl.BlockSpec(shape, lambda i, *_: (0,) * len(shape))


def project(
    tokens, base, ends, gains, shifts, w_head, cos, sin, rows, head_size, first=0, earlier=None,
):
    width = tokens.shape[1]
    count = base.shape[0] * rows
    block = min(count, 2 * rows)
    earlier = list(earlier or ())
    grid_spec = pltpu.PrefetchScalarGridSpec(
        num_scalar_prefetch=2,
        grid=(tokens.shape[0] // block,),
        in_specs=[
            pl.BlockSpec((block, width), lambda i, *_: (i, 0)),
            whole(gains.shape),
            whole(shifts.shape),
            whole(w_head.shape),
            pl.BlockSpec((head_size // 2, block), lambda i, *_: (0, i + first)),
            pl.BlockSpec((head_size // 2, block), lambda i, *_: (0, i + first)),
        ]
        + [pl.BlockSpec(memory_space=pl.ANY)] * len(earlier),
        out_specs=[
            pl.BlockSpec((block, width), lambda i, *_: (i + first, 0)),
            pl.BlockSpec((128, block), lambda i, *_: (0, i + first)),
            pl.BlockSpec((block, 128), lambda i, *_: (i + first, 0)),
            pl.BlockSpec((head_size, block), lambda i, *_: (0, i + first)),
            pl.BlockSpec((head_size, block), lambda i, *_: (0, i + first)),
            pl.BlockSpec((block, 128), lambda i, *_: (i + first, 0)),
        ],
    )
    return pl.pallas_call(
        functools.partial(qkv_kernel, rows, head_size, first),
        grid_spec=grid_spec,
        out_shape=[
            jax.ShapeDtypeStruct((count, width), BF16),
            jax.ShapeDtypeStruct((128, count), BF16),
            jax.ShapeDtypeStruct((count, 128), BF16),
            jax.ShapeDtypeStruct((head_size, count), BF16),
            jax.ShapeDtypeStruct((head_size, count), BF16),
            jax.ShapeDtypeStruct((count, 128), BF16),
        ],
        input_output_aliases={8 + k: k for k in range(len(earlier))},
        compiler_params=pltpu.CompilerParams(vmem_limit_bytes=VMEM_BYTES),
        cost_estimate=pl.CostEstimate(
            flops=2 * tokens.shape[0] * width * 1024,
            bytes_accessed=4 * tokens.shape[0] * width,
            transcendentals=0,
        ),
        name="project_head",
    )(ends, base, tokens, gains, shifts, w_head, cos, sin, *earlier)


def project_chunks_kernel(rows, head_size, first, chunks, who_ref, ends_ref, base_ref, *refs):
    tokens = refs[:chunks]
    gains_ref, shifts_ref, own_ref, other_ref, cos_ref, sin_ref = refs[chunks : chunks + 6]
    block_ref, w_ref = refs[-2:]
    step = pl.program_id(0)
    size = own_ref.shape[0]

    @pl.when(step == 0)
    def _():
        w_ref[:, 128:] = jnp.zeros((2 * size, 128), BF16)
        shard = who_ref[1]
        own_at = pl.multiple_of(shard * size, size)
        other_at = pl.multiple_of((1 - shard) * size, size)
        width = own_ref.shape[1]
        w_ref[pl.ds(own_at, size), :width] = own_ref[...]
        w_ref[pl.ds(other_at, size), :width] = other_ref[...]

    for at in range(chunks // 2):

        @pl.when(step == at)
        def _():
            block_ref[:rows] = tokens[2 * at][...]
            block_ref[rows:] = tokens[2 * at + 1][...]

    qkv_kernel(
        rows, head_size, first, ends_ref, base_ref, block_ref, gains_ref, shifts_ref, w_ref,
        cos_ref, sin_ref, *refs[-8:-2],
    )


def project_chunks(
    who, tokens, base, ends, gains, shifts, w_own, w_other, cos, sin, head_size, first=0, earlier=None,
):
    rows, width = tokens[0].shape
    count = base.shape[0] * rows
    block = 2 * rows
    earlier = list(earlier or ())
    grid_spec = pltpu.PrefetchScalarGridSpec(
        num_scalar_prefetch=3,
        grid=(len(tokens) // 2,),
        in_specs=[whole((rows, width))] * len(tokens)
        + [
            whole(gains.shape),
            whole(shifts.shape),
            whole(w_own.shape),
            whole(w_other.shape),
            pl.BlockSpec((head_size // 2, block), lambda i, *_: (0, i + first)),
            pl.BlockSpec((head_size // 2, block), lambda i, *_: (0, i + first)),
        ]
        + [pl.BlockSpec(memory_space=pl.ANY)] * len(earlier),
        out_specs=[
            pl.BlockSpec((block, width), lambda i, *_: (i + first, 0)),
            pl.BlockSpec((128, block), lambda i, *_: (0, i + first)),
            pl.BlockSpec((block, 128), lambda i, *_: (i + first, 0)),
            pl.BlockSpec((head_size, block), lambda i, *_: (0, i + first)),
            pl.BlockSpec((head_size, block), lambda i, *_: (0, i + first)),
            pl.BlockSpec((block, 128), lambda i, *_: (i + first, 0)),
        ],
        scratch_shapes=[
            pltpu.VMEM((block, width), BF16),
            pltpu.VMEM((width, 256), BF16),
        ],
    )
    return pl.pallas_call(
        functools.partial(project_chunks_kernel, rows, head_size, first, len(tokens)),
        grid_spec=grid_spec,
        out_shape=[
            jax.ShapeDtypeStruct((count, width), BF16),
            jax.ShapeDtypeStruct((128, count), BF16),
            jax.ShapeDtypeStruct((count, 128), BF16),
            jax.ShapeDtypeStruct((head_size, count), BF16),
            jax.ShapeDtypeStruct((head_size, count), BF16),
            jax.ShapeDtypeStruct((count, 128), BF16),
        ],
        input_output_aliases={9 + len(tokens) + k: k for k in range(len(earlier))},
        compiler_params=pltpu.CompilerParams(vmem_limit_bytes=VMEM_BYTES),
        cost_estimate=pl.CostEstimate(
            flops=2 * len(tokens) * rows * width * 1024,
            bytes_accessed=4 * len(tokens) * rows * width,
            transcendentals=0,
        ),
        name="project_chunks",
    )(who, ends, base, *tokens, gains, shifts, w_own, w_other, cos, sin, *earlier)


def attend(place, query_t, key, value_t, rows):
    count = key.shape[0]
    head_size = value_t.shape[0]
    block = min(count, 2 * rows)
    chunk = min(count, 512)
    blocks = count // block

    def before(i):
        return jnp.maximum(i - 1, 0)

    grid_spec = pltpu.PrefetchScalarGridSpec(
        num_scalar_prefetch=1,
        grid=(blocks + 1,),
        in_specs=[
            pl.BlockSpec((128, block), lambda i, _: (0, jnp.minimum(i, blocks - 1))),
            whole((count, 128)),
            whole((head_size, count)),
        ],
        out_specs=[
            pl.BlockSpec((head_size, block), lambda i, _: (0, before(i))),
            pl.BlockSpec(
                (2, head_size, rows), lambda i, place: (place[2 * before(i)] // 2, 0, 0)
            ),
            pl.BlockSpec((1, block), lambda i, _: (0, before(i))),
        ],
        scratch_shapes=[
            pltpu.VMEM((2, count, block), F32),
            pltpu.VMEM((2, 1, block), F32),
        ],
    )
    return pl.pallas_call(
        functools.partial(attend_kernel, chunk, rows),
        grid_spec=grid_spec,
        out_shape=[
            jax.ShapeDtypeStruct((head_size, count), F32),
            jax.ShapeDtypeStruct((count // rows, head_size, rows), BF16),
            jax.ShapeDtypeStruct((1, count), F32),
        ],
        compiler_params=pltpu.CompilerParams(vmem_limit_bytes=VMEM_BYTES),
        cost_estimate=pl.CostEstimate(
            flops=8 * count * count * 128,
            bytes_accessed=8 * count * 128,
            transcendentals=count * count,
        ),
        name="attend_head",
    )(place, query_t, key, value_t)


def attend_back(place, query_t, grad, out, lse, key, key_t, pair, cos, sin, rows):
    count = key.shape[0]
    head_size = key_t.shape[0]
    half = head_size // 2
    block = min(count, 2 * rows)
    chunk = min(count, 512)
    grid_spec = pltpu.PrefetchScalarGridSpec(
        num_scalar_prefetch=1,
        grid=(count // block,),
        in_specs=[
            pl.BlockSpec((128, block), lambda i, _: (0, i)),
            pl.BlockSpec(
                (2, head_size, rows), lambda i, place: (place[2 * i] // 2, 0, 0)
            ),
            pl.BlockSpec((head_size, block), lambda i, _: (0, i)),
            pl.BlockSpec((1, block), lambda i, _: (0, i)),
            whole((count, 128)),
            whole((head_size, count)),
            whole((count, 128)),
            pl.BlockSpec((block, 128), lambda i, _: (i, 0)),
            pl.BlockSpec((half, block), lambda i, _: (0, i)),
            pl.BlockSpec((half, block), lambda i, _: (0, i)),
            whole((half, count)),
            whole((half, count)),
        ],
        out_specs=[
            whole((3 * head_size, count)),
            whole((count // rows, 3 * head_size, rows)),
        ],
        scratch_shapes=[pltpu.VMEM((count, 128), F32)],
    )
    return pl.pallas_call(
        functools.partial(attend_back_kernel, chunk, rows, head_size),
        grid_spec=grid_spec,
        out_shape=[
            jax.ShapeDtypeStruct((3 * head_size, count), BF16),
            jax.ShapeDtypeStruct((count // rows, 3 * head_size, rows), BF16),
        ],
        compiler_params=pltpu.CompilerParams(vmem_limit_bytes=VMEM_BYTES),
        cost_estimate=pl.CostEstimate(
            flops=20 * count * count * 128,
            bytes_accessed=16 * count * 128,
            transcendentals=count * count,
        ),
        name="attend_head_back",
    )(place, query_t, grad, out, lse, key, key_t, pair, pair, cos, sin, cos, sin)


def slices_kernel(
    who_ref, norm_ref, grad_ref, up_own, up_other, down_own, down_other, bias_ref, keep_ref,
    give_ref, down_w, down_acc, up_acc, up_t,
):
    step = pl.program_id(0)
    shard = who_ref[1]
    size, units = up_own.shape
    width = 2 * size
    half = units // 2
    own_at = pl.multiple_of(shard * size, size)
    other_at = pl.multiple_of((1 - shard) * size, size)

    @pl.when(step == 0)
    def _():
        down_w[:half] = down_own[...]
        down_w[half:] = down_other[...]
        down_acc[...] = jnp.zeros_like(down_acc)
        up_acc[...] = jnp.zeros_like(up_acc)

    pre = jnp.dot(
        norm_ref[:, pl.ds(own_at, size)], up_own[...], preferred_element_type=F32
    )
    pre = pre + jnp.dot(
        norm_ref[:, pl.ds(other_at, size)], up_other[...], preferred_element_type=F32
    )
    act, slope = gelu_parts(pre + bias_ref[...])
    grad_y = grad_ref[...]
    grad = dims(grad_y, down_w[...], 1, 1) * slope
    down_acc[...] += jnp.dot(act.T.astype(BF16), grad_y, preferred_element_type=F32)
    up_acc[...] += jnp.dot(
        grad.T.astype(BF16), norm_ref[...], preferred_element_type=F32
    )

    @pl.when(step == pl.num_programs(0) - 1)
    def _():
        up_t[...] = up_acc[...].T
        for at, (rows, out_ref) in enumerate(((own_at, keep_ref), (other_at, give_ref))):
            values = up_t[pl.ds(rows, size), :].astype(out_ref.dtype)
            out_ref[pl.ds(own_at, size), :] = values[:, :half]
            out_ref[pl.ds(other_at, size), :] = values[:, half:]
            for k in range(width // half):
                out_ref[width + k * half : width + (k + 1) * half, :] = down_acc[
                    at * half : (at + 1) * half, k * half : (k + 1) * half
                ].astype(out_ref.dtype)


def slices(
    who, norm, grad_y, up_own, up_other, down_own, down_other, bias,
):
    count, width = norm.shape
    size, units = up_own.shape
    block = 256
    tall = 2 * width
    token = pl.BlockSpec((block, width), lambda i: (i, 0))
    return pl.pallas_call(
        slices_kernel,
        grid=(count // block,),
        in_specs=[pl.BlockSpec(memory_space=pltpu.SMEM), token, token]
        + [
            pl.BlockSpec(v.shape, lambda i: (0, 0))
            for v in (up_own, up_other, down_own, down_other, bias)
        ],
        out_specs=[pl.BlockSpec((tall, units // 2), lambda i: (0, 0))] * 2,
        out_shape=[
            jax.ShapeDtypeStruct((tall, units // 2), F32),
            jax.ShapeDtypeStruct((tall, units // 2), BF16),
        ],
        scratch_shapes=[
            pltpu.VMEM((units, width), BF16),
            pltpu.VMEM((units, width), F32),
            pltpu.VMEM((units, width), F32),
            pltpu.VMEM((width, units), F32),
        ],
        compiler_params=pltpu.CompilerParams(vmem_limit_bytes=VMEM_BYTES),
        cost_estimate=pl.CostEstimate(
            flops=8 * count * width * units,
            bytes_accessed=6 * count * width,
            transcendentals=2 * count * units,
        ),
        name="weight_slices",
    )(
        who, norm, grad_y, up_own, up_other, down_own, down_other, bias
    )


def head_of(device, devices):
    return device % 2 * (devices // 2) + device // 2


def row_starts(who_ref, size):
    core = who_ref[0] % 2
    shard = who_ref[1]
    half = size // 2
    other = (1 - shard) * size
    return (
        pl.multiple_of(shard * size, size),
        pl.multiple_of(other + core * half, half),
        pl.multiple_of(other + (1 - core) * half, half),
    )


def middle_kernel(
    who_ref, att_ref, own_ref, mine_ref, flip_ref, tokens_ref, gain_ref, bias_ref,
    resid_ref, normal_ref, scale_ref, norm_ref, turned,
):
    devices, head_size, _ = att_ref.shape
    for d in range(devices):
        at = head_of(d, devices) * head_size
        turned[:, at : at + head_size] = att_ref[d].astype(F32).T.astype(BF16)
    resid = tokens_ref[...].astype(F32)
    pieces = (own_ref, mine_ref, flip_ref)
    for at, piece in zip(row_starts(who_ref, own_ref.shape[0]), pieces):
        resid = resid + jnp.dot(
            turned[:, pl.ds(at, piece.shape[0])],
            piece[...],
            preferred_element_type=F32,
        )
    resid_ref[...] = resid
    normal, scale = stats(resid)
    normal_ref[...] = normal
    scale_ref[...] = scale
    norm_ref[...] = (normal * gain_ref[...] + bias_ref[...]).astype(BF16)


def middle(who, attended, pieces, tokens, gain, bias):
    rows, width = tokens.shape
    vmem = pl.BlockSpec(memory_space=pltpu.VMEM)
    return pl.pallas_call(
        middle_kernel,
        in_specs=[pl.BlockSpec(memory_space=pltpu.SMEM)] + [vmem] * 7,
        out_specs=[vmem] * 4,
        out_shape=[
            jax.ShapeDtypeStruct((rows, width), F32),
            jax.ShapeDtypeStruct((rows, width), F32),
            jax.ShapeDtypeStruct((rows, 1), F32),
            jax.ShapeDtypeStruct((rows, width), BF16),
        ],
        scratch_shapes=[pltpu.VMEM((rows, width), BF16)],
        compiler_params=pltpu.CompilerParams(vmem_limit_bytes=VMEM_BYTES),
        cost_estimate=pl.CostEstimate(
            flops=8 * rows * width * width,
            bytes_accessed=4 * width * width,
            transcendentals=0,
        ),
        name="output_projection",
    )(who, attended, *pieces, tokens, gain, bias)


def feed_kernel(parts, who_ref, norm_ref, own_ref, *refs):
    pieces = refs[: 4 * parts]
    (
        near_ref, far_ref, bias_ref, normal_ref, scale_ref, gain_ref, grad_y_ref, out_own, out_mine,
        out_flip, act_ref, resid_ref, resid_b_ref, sent_ref, sums_ref, grad_ref, att_ref,
    ) = refs[4 * parts :]
    side = who_ref[0] % 4
    shard = who_ref[1]
    size, hidden = own_ref.shape
    quarter = hidden // 4
    deep = size // parts
    own_at = pl.multiple_of(shard * size, size)
    other_at = pl.multiple_of((1 - shard) * size, size)
    own_norm = norm_ref[:, pl.ds(own_at, size)]
    part_at = [pl.multiple_of(other_at + p * deep, deep) for p in range(parts)]
    norms = [norm_ref[:, pl.ds(at, deep)] for at in part_at]
    for k in range(4):
        block = side ^ k
        columns = pl.ds(pl.multiple_of(block * quarter, quarter), quarter)
        weight = own_ref[:, columns]
        pre = jnp.dot(own_norm, weight, preferred_element_type=F32)
        for p in range(parts):
            pre = pre + jnp.dot(
                norms[p], pieces[4 * p + k][...], preferred_element_type=F32
            )
        act, slope = gelu_parts(pre + bias_ref[:, columns])
        act_ref[:, columns] = act.astype(BF16)
        within = pl.ds(pl.multiple_of((block % 2) * quarter, quarter), quarter)
        near = near_ref[:, within]
        far = far_ref[:, within].astype(F32)
        grad = jnp.where(block // 2 == shard, near, far) * slope
        sums_ref[pl.ds(3 + block, 1), :] = jnp.sum(grad, axis=0, keepdims=True)
        grad = grad.astype(BF16)
        terms = [(own_at, size, weight)]
        terms += [(part_at[p], deep, pieces[4 * p + k][...]) for p in range(parts)]
        for at, length, piece in terms:
            term = dims(grad, piece, 1, 1)
            if k == 0:
                grad_ref[:, pl.ds(at, length)] = term
            else:
                grad_ref[:, pl.ds(at, length)] += term
    grad = grad_ref[...]
    normal = normal_ref[...]
    grad_y = grad_y_ref[...].astype(F32)
    sums_ref[0:1, :] = jnp.sum(grad * normal, axis=0, keepdims=True)
    sums_ref[1:2, :] = jnp.sum(grad, axis=0, keepdims=True)
    sums_ref[2:3, :] = jnp.sum(grad_y, axis=0, keepdims=True)
    sums_ref[7:8, :] = jnp.zeros((1, quarter), F32)
    resid = grad_y + stats_back(grad * gain_ref[...], normal, scale_ref[...])
    resid_ref[...] = resid
    resid = resid.astype(BF16)
    resid_b_ref[...] = resid
    out_pieces = (out_own, out_mine, out_flip)
    for at, piece in zip(row_starts(who_ref, out_own.shape[0]), out_pieces):
        att_ref[pl.ds(at, piece.shape[0]), :] = dims(piece[...], resid, 1, 1).astype(
            BF16
        )
    devices, head_size, _ = sent_ref.shape
    for d in range(devices):
        at = head_of(d, devices) * head_size
        sent_ref[d] = att_ref[at : at + head_size, :]


def feed(who, norm, own, pieces, near, far, bias, normal, scale, gain, grad_y, out_pieces):
    rows, width = norm.shape
    hidden = own.shape[1]
    vmem = pl.BlockSpec(memory_space=pltpu.VMEM)
    return pl.pallas_call(
        functools.partial(feed_kernel, len(pieces) // 4),
        in_specs=[pl.BlockSpec(memory_space=pltpu.SMEM)] + [vmem] * (12 + len(pieces)),
        out_specs=[vmem] * 5,
        out_shape=[
            jax.ShapeDtypeStruct((rows, hidden), BF16),
            jax.ShapeDtypeStruct((rows, width), F32),
            jax.ShapeDtypeStruct((rows, width), BF16),
            jax.ShapeDtypeStruct((HEADS, width // HEADS, rows), BF16),
            jax.ShapeDtypeStruct((8, width), F32),
        ],
        scratch_shapes=[pltpu.VMEM((rows, width), F32), pltpu.VMEM((width, rows), BF16)],
        compiler_params=pltpu.CompilerParams(vmem_limit_bytes=VMEM_BYTES),
        cost_estimate=pl.CostEstimate(
            flops=16 * rows * width * hidden,
            bytes_accessed=4 * width * hidden,
            transcendentals=2 * rows * hidden,
        ),
        name="feed_forward",
    )(who, norm, own, *pieces, near, far, bias, normal, scale, gain, grad_y, *out_pieces)


def first_back_kernel(
    head_size, who_ref, ends_ref, got_ref, own_ref, mine_0, mine_1, flip_0, flip_1, tokens_ref,
    resid_ref, gains_ref, sums_ref, grad_ref, total_ref, mixed, turned,
):
    heads = got_ref.shape[0]
    rows, width = tokens_ref.shape
    seq_count = ends_ref.shape[0]
    for d in range(heads):
        for k in range(3):
            at = k * width + head_of(d, heads) * head_size
            mixed[at : at + head_size, :] = got_ref[
                d, k * head_size : (k + 1) * head_size, :
            ]
    own_at, mine_at, flip_at = row_starts(who_ref, own_ref.shape[0])
    part = mine_0.shape[0]
    starts = (own_at, mine_at, mine_at + part, flip_at, flip_at + part)
    for at, piece in zip(starts, (own_ref, mine_0, mine_1, flip_0, flip_1)):
        turned[pl.ds(at, piece.shape[0]), :] = jnp.dot(
            piece[...], mixed[...], preferred_element_type=F32
        )
    grad = turned[...].T
    normal, scale = stats(tokens_ref[...].astype(F32))
    index = who_ref[0] * rows + lax.broadcasted_iota(jnp.int32, (rows, 1), 0)
    segment = segments([ends_ref[s] for s in range(seq_count)], index)
    gains = gains_ref[0:1, :]
    for s in range(1, seq_count + 1):
        gains = jnp.where(segment == s, gains_ref[s : s + 1, :], gains)
    grad_ref[...] = (
        resid_ref[...] + stats_back(grad * gains, normal, scale)
    ).astype(BF16)
    total_ref[0:8, :] = sums_ref[...]
    product = grad * normal
    for s in range(seq_count + 1):
        here = segment == s
        for k, terms in enumerate((product, grad)):
            total_ref[8 + 2 * s + k : 9 + 2 * s + k, :] = jnp.sum(
                jnp.where(here, terms, 0.0), axis=0, keepdims=True
            )


def first_back(who, ends, got, pieces, tokens, resid, gains, sums):
    rows, width = tokens.shape
    heads, tall, _ = got.shape
    seq_count = ends.shape[0]
    lines = 8 + 2 * (seq_count + 1)
    vmem = pl.BlockSpec(memory_space=pltpu.VMEM)
    return pl.pallas_call(
        functools.partial(first_back_kernel, tall // 3),
        in_specs=[pl.BlockSpec(memory_space=pltpu.SMEM)] * 2 + [vmem] * 10,
        out_specs=[vmem] * 2,
        out_shape=[
            jax.ShapeDtypeStruct((rows, width), BF16),
            jax.ShapeDtypeStruct((lines, width), F32),
        ],
        scratch_shapes=[
            pltpu.VMEM((3 * width, rows), BF16),
            pltpu.VMEM((width, rows), F32),
        ],
        compiler_params=pltpu.CompilerParams(vmem_limit_bytes=VMEM_BYTES),
        cost_estimate=pl.CostEstimate(
            flops=12 * rows * width * width,
            bytes_accessed=8 * width * width,
            transcendentals=0,
        ),
        name="first_norm_back",
    )(who, ends, got, *pieces, tokens, resid, gains, sums)


def small_kernel(seq_count, chunks, who_ref, own_embed, other_embed, *refs):
    parts = refs[:chunks]
    (
        time_ref, gain_one, bias_one, gain_two, bias_two, bias_up, bias_down, total,
    ) = refs[chunks:]
    lines, width = total.shape
    half = width // 2
    shard = who_ref[1]
    for k in range(width // 128):
        at = k * lines
        value = parts[0][at : at + lines, :].astype(F32)
        for ref in parts[1:]:
            value = value + ref[at : at + lines, :].astype(F32)
        total[:, k * 128 : (k + 1) * 128] = value
    part = pl.ds(pl.multiple_of(shard * half, half), half)
    gain_two[...] = total[0:1, part]
    bias_two[...] = total[1:2, part]
    bias_down[...] = total[2:3, part]
    bias_up[:, :width] = total[pl.ds(3 + 2 * shard, 1), :]
    bias_up[:, width:] = total[pl.ds(4 + 2 * shard, 1), :]
    films = 2 * (seq_count + 1)
    gain = total[8:9, part]
    bias = total[9:10, part]
    for s in range(1, films):
        gain = gain + total[8 + 2 * s : 9 + 2 * s, part]
        bias = bias + total[9 + 2 * s : 10 + 2 * s, part]
    gain_one[...] = gain
    bias_one[...] = bias
    embeds = []
    for embed_ref in (own_embed, other_embed):
        columns = []
        for s in range(seq_count):
            line = embed_ref[s : s + 1, :]
            columns.append(jnp.broadcast_to(line, (8, line.shape[1])).T[:, 0:1])
        embeds.append(columns)
    for k in range(2):
        value = None
        for g, columns in enumerate(embeds):
            for s in range(seq_count):
                line = 8 + g * films + 2 * s + k
                term = columns[s] * total[line : line + 1, :]
                value = term if value is None else value + term
        time_ref[:, k * width : (k + 1) * width] = value


def small_sums(who, own_embed, other_embed, parts, top, lines, width):
    vmem = pl.BlockSpec(memory_space=pltpu.VMEM)
    tall = lines * width // 128
    tail = pl.BlockSpec((tall, 128), lambda i: (top // tall, 0))
    return pl.pallas_call(
        functools.partial(small_kernel, own_embed.shape[0], len(parts)),
        grid=(1,),
        in_specs=[pl.BlockSpec(memory_space=pltpu.SMEM)]
        + [vmem] * 2
        + [tail] * len(parts),
        out_specs=[vmem] * 7,
        out_shape=[jax.ShapeDtypeStruct((own_embed.shape[1], 2 * width), F32)]
        + [jax.ShapeDtypeStruct((1, width // 2), F32)] * 4
        + [
            jax.ShapeDtypeStruct((1, 2 * width), F32),
            jax.ShapeDtypeStruct((1, width // 2), F32),
        ],
        scratch_shapes=[pltpu.VMEM((lines, width), F32)],
        compiler_params=pltpu.CompilerParams(vmem_limit_bytes=VMEM_BYTES),
        cost_estimate=pl.CostEstimate(
            flops=1000000, bytes_accessed=2000000, transcendentals=0
        ),
        name="small_gradients",
    )(who, own_embed, other_embed, *parts)


def stream(chips, copies_of, fill):
    pending = [None, None]
    for at in range(chips):
        slot = at % 2
        if pending[slot] is not None:
            for copy in pending[slot]:
                copy.wait()
        fill(at, slot)
        pending[slot] = copies_of(at, slot)
        for copy in pending[slot]:
            copy.start()
    for copies in pending:
        if copies is not None:
            for copy in copies:
                copy.wait()


def wide_kernel(first, chunks, place_ref, *refs):
    parts = refs[:chunks]
    up_ref, down_ref, out_ref, up_slots, down_slots, out_slots, sems = refs[-7:]
    core = place_ref[0] % 2
    deep = out_slots.shape[1] // 2
    size = up_ref.shape[0]
    hidden = up_ref.shape[1]
    width = down_ref.shape[1]

    def fill(at, slot):
        for j in range(2):
            ref = parts[2 * at + j]
            column = pl.ds(pl.multiple_of((j ^ core) * 128, 128), 128)
            for k in range(2):
                up_slots[slot, k, :, column] = ref[k * size : (k + 1) * size, :].astype(
                    F32
                )
            row = pl.ds(pl.multiple_of((j ^ core) * 128, 128), 128)
            for k in range(width // 128):
                top = 2 * size + k * 128
                down_slots[slot, row, k * 128 : (k + 1) * 128] = ref[
                    top : top + 128, :
                ].astype(F32)
            row = pl.ds(pl.multiple_of((j ^ core) * deep, deep), deep)
            for k in range(width // 128):
                top = 2 * size + width + k * deep
                out_slots[slot, row, k * 128 : (k + 1) * 128] = ref[
                    top : top + deep, :
                ].astype(F32)

    def copies_of(at, slot):
        chip = place_ref[2 * (at + first)] // 2
        copies = []
        for k in range(2):
            column = pl.multiple_of(k * (hidden // 2) + chip * 256, 256)
            copies.append(
                pltpu.make_async_copy(
                    up_slots.at[slot, k],
                    up_ref.at[:, pl.ds(column, 256)],
                    sems.at[slot, k],
                )
            )
        row = pl.multiple_of(chip * 256, 256)
        copies.append(
            pltpu.make_async_copy(
                down_slots.at[slot], down_ref.at[pl.ds(row, 256), :], sems.at[slot, 2]
            )
        )
        row = pl.multiple_of(chip * 2 * deep, 2 * deep)
        copies.append(
            pltpu.make_async_copy(
                out_slots.at[slot], out_ref.at[pl.ds(row, 2 * deep), :], sems.at[slot, 3]
            )
        )
        return copies

    stream(chunks // 2, copies_of, fill)


def expand_wide(place, first, parts, width, earlier):
    devices = place.shape[0]
    size = width // 2
    vmem = pl.BlockSpec(memory_space=pltpu.VMEM)
    hbm = pl.BlockSpec(memory_space=pl.ANY)
    return pl.pallas_call(
        functools.partial(wide_kernel, first, len(parts)),
        in_specs=[pl.BlockSpec(memory_space=pltpu.SMEM)]
        + [vmem] * len(parts)
        + [hbm] * len(earlier),
        out_specs=[hbm, hbm, hbm],
        out_shape=[
            jax.ShapeDtypeStruct((size, 2 * devices * 128), F32),
            jax.ShapeDtypeStruct((devices * 128, width), F32),
            jax.ShapeDtypeStruct((size, width), F32),
        ],
        scratch_shapes=[
            pltpu.VMEM((2, 2, size, 256), F32),
            pltpu.VMEM((2, 256, width), F32),
            pltpu.VMEM((2, 2 * size // devices, width), F32),
            pltpu.SemaphoreType.DMA((2, 4)),
        ],
        input_output_aliases={1 + len(parts) + k: k for k in range(len(earlier))},
        compiler_params=pltpu.CompilerParams(vmem_limit_bytes=VMEM_BYTES),
        cost_estimate=pl.CostEstimate(
            flops=parts[0].size * len(parts),
            bytes_accessed=6 * parts[0].size * len(parts),
            transcendentals=0,
        ),
        name="expand_wide",
    )(place, *parts, *earlier)


def last_kernel(head_size, in_ref, out_ref):
    pairs = []
    for j in range(2):
        for k in range(in_ref.shape[0] // 4):
            pairs.append((in_ref[4 * k + j], in_ref[4 * k + 2 + j]))
    for at, (first, second) in enumerate(pairs):
        both = jnp.concatenate([first, second], axis=0).astype(F32)
        out_ref[:, at * 2 * head_size : (at + 1) * 2 * head_size] = both.T


def expand_last(parts, head_size):
    devices, tall, depth = parts.shape
    width = devices * head_size
    return pl.pallas_call(
        functools.partial(last_kernel, head_size),
        grid=(3,),
        in_specs=[pl.BlockSpec((devices, head_size, depth), lambda k: (0, k, 0))],
        out_specs=pl.BlockSpec((depth, width), lambda k: (0, k)),
        out_shape=jax.ShapeDtypeStruct((depth, 3 * width), F32),
        compiler_params=pltpu.CompilerParams(vmem_limit_bytes=VMEM_BYTES),
        cost_estimate=pl.CostEstimate(
            flops=parts.size, bytes_accessed=6 * parts.size, transcendentals=0
        ),
        name="expand_last",
    )(parts)


def times_rows(values, pieces):
    return sum(
        jnp.dot(
            lax.dynamic_slice_in_dim(values, at, piece.shape[0], 1),
            piece,
            preferred_element_type=F32,
        )
        for piece, at in pieces
    )


def times_rows_t(values_t, pieces):
    return sum(
        dims(lax.dynamic_slice_in_dim(values_t, at, piece.shape[0], 0), piece, 0, 0)
        for piece, at in pieces
    )


def joined(parts, pieces, dim):
    if len(parts) == 1:
        return parts[0]
    shape = list(parts[0].shape)
    shape[dim] = sum(part.shape[dim] for part in parts)
    out = jnp.zeros(shape, parts[0].dtype)
    for part, (_, at) in zip(parts, pieces):
        out = lax.dynamic_update_slice_in_dim(out, part, at, dim)
    return out


def rows_of(pieces, start, size):
    out = None
    for piece, at in pieces:
        length = piece.shape[0]
        local = jnp.clip(start - at, 0, length - size)
        found = lax.dynamic_slice_in_dim(piece, local, size, 0)
        inside = (start >= at) & (start < at + length)
        out = found if out is None else jnp.where(inside, found, out)
    return out


def body_general(
    ctx_size, fsdp_size,
    tokens, w_qkv, w_out, w_up, w_down, w_time, gain_one, bias_one, gain_two, bias_two, bias_up,
    bias_down, lengths, time_steps, cotangent,
):
    me = lax.axis_index("ctx")
    shard = lax.axis_index("fsdp")
    rows = tokens.shape[1]
    width = tokens.shape[2]
    count = rows * ctx_size
    head_size = width // HEADS
    repeats = ctx_size // HEADS
    columns = head_size // repeats
    seq_count = lengths.shape[1]
    hidden = w_up.shape[1]

    def gather_small(values):
        return lax.all_gather(values, "fsdp", axis=0, tiled=True)

    def fetch(weight):
        return [(gather_small(weight), 0)]

    def scatter_sum(values, dim):
        return lax.psum_scatter(
            values.astype(BF16), "fsdp", scatter_dimension=dim, tiled=True
        )

    def gather(values):
        return lax.all_gather(values, "ctx", axis=0, tiled=False)

    ends = []
    for s in range(seq_count):
        ends.append(lengths[0, s] + (ends[-1] if ends else 0))
    ends_vector = jnp.stack(ends)
    index = me * rows + jnp.arange(rows, dtype=jnp.int32)
    segment = segments(ends, index)
    live = (segment < seq_count).astype(F32)[:, None]
    all_index = jnp.arange(count, dtype=jnp.int32)
    all_position = positions(ends, all_index, segments(ends, all_index))
    half_width = head_size // 2
    inverse = jnp.exp(
        -math.log(10000.0) * jnp.arange(half_width, dtype=F32) / half_width
    )
    angle = inverse[:, None] * all_position.astype(F32)[None, :]
    cos = jnp.cos(angle)
    sin = jnp.sin(angle)

    all_tokens = gather(tokens[0]).reshape(count, width)
    inputs = tokens[0].astype(F32)
    grad_y = cotangent[0].astype(F32) * live
    grad_y_b = grad_y.astype(BF16)
    all_grad_y = gather(grad_y_b).reshape(count, width)

    small = [gain_one, bias_one, gain_two, bias_two, bias_down, bias_up]
    packed = gather_small(jnp.concatenate(small)[None, :])
    vectors = []
    at = 0
    for vector in small:
        size = vector.shape[0]
        vectors.append(packed[:, at : at + size].reshape(1, -1).astype(F32))
        at += size
    gain_first, bias_first, gain_second, bias_second, bias_output, bias_hidden = vectors

    all_steps = lax.all_gather(time_steps.astype(F32), "fsdp", axis=0, tiled=True)
    all_embedded = embed(all_steps, w_time.shape[0] * fsdp_size).astype(BF16)
    embedded = lax.dynamic_index_in_dim(all_embedded, shard, 0, keepdims=False)
    film = times_rows(embedded, fetch(w_time))
    film = jnp.concatenate([film, jnp.zeros((1, 2 * width), F32)], axis=0)
    gains = gain_first + film[:, :width]
    shifts = bias_first + film[:, width:]

    head = me // repeats
    w_head = jnp.concatenate(
        [
            lax.dynamic_slice_in_dim(w_qkv, k * width + head * head_size, head_size, 1)
            for k in range(3)
        ]
        + [jnp.zeros((w_qkv.shape[0], head_size), BF16)],
        axis=1,
    )
    w_head = gather_small(w_head)

    base = jnp.arange(ctx_size, dtype=jnp.int32) * rows
    all_norm, query_t, key, key_t, value_t, pair = project(
        all_tokens, base, ends_vector, gains, shifts, w_head, cos, sin, rows, head_size
    )
    place = jnp.arange(ctx_size, dtype=jnp.int32)
    out_t, sent, lse = attend(place, query_t, key, value_t, rows)

    part = (me % repeats) * columns
    if repeats > 1:
        sent = lax.dynamic_slice_in_dim(sent, part, columns, 1)
    attended_t = lax.all_to_all(sent, "ctx", 0, 0, tiled=True).reshape(width, rows)

    out_pieces = fetch(w_out)
    up_pieces = fetch(w_up)
    down_pieces = fetch(w_down)
    qkv_pieces = fetch(w_qkv)
    resid = inputs + times_rows_t(attended_t, out_pieces)
    normal_two, scale_two = stats(resid)
    norm_two_b = (normal_two * gain_second + bias_second).astype(BF16)
    all_norm_two = gather(norm_two_b).reshape(count, width)
    pre = times_rows(norm_two_b, up_pieces) + bias_hidden
    act, slope = gelu_parts(pre)
    branch = times_rows(act.astype(BF16), down_pieces) + bias_output
    output = (live * (resid + branch)).astype(BF16)
    grad_act = joined([dims(grad_y_b, p, 1, 1) for p, _ in down_pieces], down_pieces, 1)
    grad_pre = grad_act * slope
    grad_bias_up = jnp.sum(grad_pre, axis=0)
    grad_pre_b = grad_pre.astype(BF16)
    grad_norm_two = joined([dims(grad_pre_b, p, 1, 1) for p, _ in up_pieces], up_pieces, 1)
    grad_resid = grad_y + stats_back(grad_norm_two * gain_second, normal_two, scale_two)
    grad_resid_b = grad_resid.astype(BF16)
    grad_att_t = joined(
        [dims(p, grad_resid_b, 1, 1) for p, _ in out_pieces], out_pieces, 0
    ).astype(BF16)
    grad_att_t = grad_att_t.reshape(HEADS, head_size, rows)
    if repeats > 1:
        grad_att_t = jnp.repeat(grad_att_t, repeats, axis=0)
    grad_att = lax.all_to_all(grad_att_t, "ctx", 0, 0, tiled=True)

    mixed_t, _ = attend_back(
        place, query_t, grad_att, out_t, lse, key, key_t, pair, cos, sin, rows
    )
    mixed_t = mixed_t.reshape(3, head_size, count)
    if repeats > 1:
        mixed_t = lax.dynamic_slice_in_dim(mixed_t, part, columns, 1)
    mixed_t = mixed_t.reshape(3 * columns, count)
    mixed_sent = mixed_t.reshape(3 * columns, ctx_size, rows).transpose(1, 0, 2)
    mixed_got = lax.all_to_all(mixed_sent, "ctx", 0, 0, tiled=True)
    grad_mixed_t = (
        mixed_got.reshape(ctx_size, 3, columns, rows)
        .transpose(1, 0, 2, 3)
        .reshape(3 * width, rows)
    )
    grad_norm_one = joined(
        [dims(grad_mixed_t, p, 0, 1) for p, _ in qkv_pieces], qkv_pieces, 1
    )
    normal_one, scale_one = stats(inputs)
    seg_col = segment[:, None]
    gain_tok = gains[0:1]
    for s in range(1, seq_count + 1):
        gain_tok = jnp.where(seg_col == s, gains[s : s + 1], gain_tok)
    grad_tokens = (
        grad_resid + stats_back(grad_norm_one * gain_tok, normal_one, scale_one)
    ).astype(BF16)
    film_terms = jnp.concatenate([grad_norm_one * normal_one, grad_norm_one], axis=1)
    film_sums = [
        jnp.sum(jnp.where(seg_col == s, film_terms, 0.0), axis=0)
        for s in range(seq_count + 1)
    ]

    sums = [
        jnp.sum(grad_norm_two * normal_two, axis=0),
        jnp.sum(grad_norm_two, axis=0),
        jnp.sum(grad_y, axis=0),
        grad_bias_up,
    ] + film_sums
    sizes = [vector.shape[0] for vector in sums]
    total = lax.psum(jnp.concatenate(sums)[None, :], "ctx")
    total = lax.all_gather(total, "fsdp", axis=0, tiled=True)
    split = []
    at = 0
    for size in sizes:
        split.append(total[:, at : at + size])
        at += size

    def own(vector):
        size = vector.shape[0] // fsdp_size
        return lax.dynamic_slice_in_dim(vector, shard * size, size, 0)

    sum_gain_two, sum_bias_two, sum_bias_down, sum_bias_up = (
        own(jnp.sum(vector, axis=0)) for vector in split[:4]
    )
    film_all = jnp.sum(sum(split[4:]), axis=0)
    sum_gain_one = own(film_all[:width])
    sum_bias_one = own(film_all[width:])
    film_grad = jnp.stack(split[4 : 4 + seq_count], axis=1).reshape(-1, 2 * width)
    embedded_rows = lax.dynamic_slice_in_dim(
        all_embedded.astype(F32).reshape(film_grad.shape[0], -1),
        shard * w_time.shape[0],
        w_time.shape[0],
        1,
    )
    grad_time = sum(
        embedded_rows[g][:, None] * film_grad[g][None, :]
        for g in range(film_grad.shape[0])
    )

    slice_width = hidden // (ctx_size * fsdp_size)
    starts = [
        k * (hidden // fsdp_size) + me * slice_width for k in range(fsdp_size)
    ]
    w_up_cols = []
    for piece, _ in up_pieces:
        w_up_cols.append(
            jnp.concatenate(
                [
                    lax.dynamic_slice_in_dim(piece, start, slice_width, 1)
                    for start in starts
                ],
                axis=1,
            )
        )
    w_up_slice = joined(w_up_cols, up_pieces, 0)
    w_down_slice = jnp.concatenate(
        [rows_of(down_pieces, start, slice_width) for start in starts], axis=0
    )
    bias_slice = jnp.concatenate(
        [
            lax.dynamic_slice_in_dim(bias_hidden, start, slice_width, 1)
            for start in starts
        ],
        axis=1,
    )
    pre_slice = dims(all_norm_two, w_up_slice, 1, 0) + bias_slice
    act_slice, slope_slice = gelu_parts(pre_slice)
    grad_pre_slice = (dims(all_grad_y, w_down_slice, 1, 1) * slope_slice).astype(BF16)
    down_slice = dims(act_slice.astype(BF16), all_grad_y, 0, 0)
    up_slice = dims(all_norm_two, grad_pre_slice, 0, 0)
    grad_down = gather(scatter_sum(down_slice, 0)).reshape(-1, width).astype(F32)
    up_parts = gather(scatter_sum(up_slice, 0))
    grad_up = (
        up_parts.reshape(ctx_size, width // fsdp_size, fsdp_size, slice_width)
        .transpose(1, 2, 0, 3)
        .reshape(width // fsdp_size, hidden)
        .astype(F32)
    )
    out_part = jnp.dot(attended_t, grad_resid_b, preferred_element_type=F32)
    out_rows = lax.psum_scatter(
        out_part.astype(BF16), ("fsdp", "ctx"), scatter_dimension=0, tiled=True
    )
    grad_out = gather(out_rows).reshape(-1, width).astype(F32)
    qkv_slice = jnp.dot(mixed_t, all_norm, preferred_element_type=F32)
    qkv_parts = gather(scatter_sum(qkv_slice, 1))
    grad_qkv = (
        qkv_parts.reshape(ctx_size, 3, columns, width // fsdp_size)
        .transpose(3, 1, 0, 2)
        .reshape(width // fsdp_size, 3 * width)
        .astype(F32)
    )
    return (
        output[None],
        grad_tokens[None],
        grad_qkv,
        grad_out,
        grad_up,
        grad_down,
        grad_time,
        sum_gain_one,
        sum_bias_one,
        sum_gain_two,
        sum_bias_two,
        sum_bias_up,
        sum_bias_down,
    )


def ring_tables(ctx_size):
    chips = ctx_size // 2
    order = list(range(0, chips, 2)) + list(range(1, chips, 2))[::-1]
    offsets = [0]
    for step in range(1, chips // 2 + 1):
        offsets.append(-step)
        if step <= (chips - 1) // 2:
            offsets.append(step)
    place = np.zeros((ctx_size, ctx_size), np.int32)
    for me in range(ctx_size):
        at = order.index(me // 2)
        for k, offset in enumerate(offsets):
            chip = order[(at + offset) % chips]
            place[me, 2 * k] = 2 * chip + me % 2
            place[me, 2 * k + 1] = 2 * chip + 1 - me % 2
    return order, place


def fence(*values):
    return lax.optimization_barrier(values)


def after(values, *earlier):
    return lax.optimization_barrier((values, *earlier))[0]


def body(
    ctx_size, fsdp_size,
    tokens, w_qkv, w_out, w_up, w_down, w_time, gain_one, bias_one, gain_two, bias_two, bias_up,
    bias_down, lengths, time_steps, cotangent,
):
    me = lax.axis_index("ctx")
    shard = lax.axis_index("fsdp")
    core = me % 2
    rows = tokens.shape[1]
    width = tokens.shape[2]
    head_size = width // HEADS
    seq_count = lengths.shape[1]
    hidden = w_up.shape[1]
    other = 1 - shard
    chips = ctx_size // 2
    half = width // 2
    units = hidden // (ctx_size * fsdp_size)
    order, place_table = ring_tables(ctx_size)
    place = jnp.asarray(place_table)[me]
    who = jnp.stack([me, shard]).astype(jnp.int32)

    def across(values):
        return lax.ppermute(values, "fsdp", [(0, 1), (1, 0)])

    def gather(values):
        return lax.all_gather(values, "ctx", axis=0, tiled=True)

    def flip(values, bit=0):
        return lax.ppermute(
            values, "ctx", [(i, i ^ (1 << bit)) for i in range(ctx_size)]
        )

    def hop(values, step):
        return lax.ppermute(
            values,
            "ctx",
            [
                (2 * order[at] + c, 2 * order[(at + step) % chips] + c)
                for at in range(chips)
                for c in range(2)
            ],
        )

    def by_shard(mine, others, axis):
        first = jnp.where(shard == 0, mine, others)
        second = jnp.where(shard == 0, others, mine)
        return jnp.concatenate([first, second], axis=axis)

    def cut(values, start, size, axis):
        return lax.dynamic_slice_in_dim(values, start, size, axis)

    def halve(values, axis, mine, send):
        keep = lax.dynamic_index_in_dim(values, mine, axis, keepdims=False)
        give = lax.dynamic_index_in_dim(values, 1 - mine, axis, keepdims=False)
        return keep + send(give.astype(BF16)).astype(F32)

    ends = []
    for s in range(seq_count):
        ends.append(lengths[0, s] + (ends[-1] if ends else 0))
    ends_vector = jnp.stack(ends)
    base = place * rows
    index = me * rows + jnp.arange(rows, dtype=jnp.int32)
    segment = segments(ends, index)
    seg_col = segment[:, None]
    live = (segment < seq_count).astype(F32)[:, None]
    own_tokens = tokens[0]
    steps_row = time_steps.reshape(1, seq_count)
    high = (steps_row // 256).astype(BF16)
    low = (steps_row % 256).astype(BF16)
    head = core * chips + me // 2
    w_head = jnp.concatenate(
        [cut(w_qkv, k * width + head * head_size, head_size, 1) for k in range(3)], axis=1
    )
    class Ring:
        def __init__(self, values):
            self.right = self.left = values
            self.parts = [values]
            self.step = 0

        def go(self, *earlier):
            right, left = self.right, self.left
            if earlier:
                right, left = (
                    after(right, *earlier),
                    after(left, *earlier),
                )
            self.step += 1
            self.right = hop(right, 1)
            if self.step <= (chips - 1) // 2:
                self.left = hop(left, -1)
                return [self.right, self.left]
            return [self.right]

        def came(self, values):
            self.right = values[0]
            if len(values) > 1:
                self.left = values[1]
            self.parts += values

    def fenced(groups):
        flat = [v for group in groups for v in group]
        flat = list(fence(*flat))
        out = []
        for group in groups:
            out.append(flat[: len(group)])
            flat = flat[len(group) :]
        return out

    def with_flips(values):
        return [part for v in values for part in (v, flip(v))]

    tok = Ring(own_tokens)
    tok_new = tok.go()
    packed = jnp.concatenate([gain_one[None, :], bias_one[None, :], high, low], axis=1)
    tok_new, (packed, w_head) = fenced([tok_new, [packed, w_head]])
    tok.came(tok_new)

    tok_new = tok.go()
    packed_other = across(packed)
    w_head_other = across(w_head)
    base = after(base, packed)
    all_index = (base[:, None] + jnp.arange(rows, dtype=jnp.int32)[None, :]).reshape(-1)
    all_position = positions(ends, all_index, segments(ends, all_index))
    half_width = head_size // 2
    inverse = jnp.exp(
        -math.log(10000.0) * jnp.arange(half_width, dtype=F32) / half_width
    )
    angle = inverse[:, None] * all_position.astype(F32)[None, :]
    cos = jnp.cos(angle)
    sin = jnp.sin(angle)

    inputs = own_tokens.astype(F32)
    grad_y = cotangent[0].astype(F32) * live
    grad_y_b = grad_y.astype(BF16)
    out_half = w_out.shape[0] // 2
    tok_new, (packed_other, w_head, cos, sin, grad_y_b, me_2, place, who, base, w_head_other) = fenced(
        [tok_new, [packed_other, w_head, cos, sin, grad_y_b, me, place, who, base, w_head_other]]
    )
    tok.came(tok_new)

    tok_new = tok.go()
    packed_all = by_shard(packed, packed_other, 0)

    def vector_of(values, at, size):
        return values[:, at : at + size].reshape(1, -1).astype(F32)

    gain_first = vector_of(packed_all, 0, half)
    bias_first = vector_of(packed_all, half, half)
    all_steps = packed_all[:, width : width + seq_count].astype(F32) * 256.0 + packed_all[
        :, width + seq_count :
    ].astype(F32)
    all_embedded = embed(all_steps, w_time.shape[0] * fsdp_size).astype(BF16)
    own_part = cut(all_embedded, shard * w_time.shape[0], w_time.shape[0], 2)
    film_part = jnp.dot(
        own_part.reshape(fsdp_size * seq_count, -1), w_time, preferred_element_type=F32
    ).reshape(fsdp_size, seq_count, 2 * width)
    film_other = across(lax.dynamic_index_in_dim(film_part, other, 0, keepdims=False))
    film = film_other + lax.dynamic_index_in_dim(film_part, shard, 0, keepdims=False)
    film = jnp.concatenate([film, jnp.zeros((1, 2 * width), F32)], axis=0)
    gains = gain_first + film[:, :width]
    shifts = bias_first + film[:, width:]
    up_parts = 2
    up_deep = w_up.shape[0] // up_parts
    quarter = hidden // 4
    up_send = [
        lax.dynamic_slice(w_up, (p * up_deep, (me_2 % 4) * quarter), (up_deep, quarter))
        for p in range(up_parts)
    ]
    tok_new, (gains, shifts), up_send = fenced([tok_new, [gains, shifts], up_send])
    tok_flips = with_flips(tok.parts)
    tok.came(tok_new)

    tok_last = tok.go()
    all_grad_y = gather(after(grad_y_b, gains))
    grad_y_other = across(grad_y_b)
    up_mine = [across(after(up_send[0], gains))]
    tok_flips += with_flips(tok_new)
    constants = (base, ends_vector, gains, shifts, w_head, w_head_other, cos, sin, head_size)
    head_values = project_chunks(who, tok_flips, *constants)
    head_values, tok_last, (grad_y_other, gain_two, up_send[1]) = fenced(
        [head_values, tok_last, [grad_y_other, gain_two, up_send[1]]]
    )

    up_mine.append(across(up_send[1]))
    far_send = dims(grad_y_other, w_down, 1, 1).astype(BF16)
    all_norm, query_t, key, key_t, value_t, pair = project_chunks(
        who, with_flips(tok_last), *constants, first=chips - 1, earlier=head_values
    )
    out_t, sent, lse = attend(place, query_t, key, value_t, rows)
    rest = jnp.concatenate(
        [v[None, :] for v in (gain_two, bias_two, bias_down, bias_up)], axis=1
    )
    out_t, sent, lse, *up_mine, rest, me_5, far_send = fence(
        out_t, sent, lse, *up_mine, rest, me, far_send
    )

    attended = lax.all_to_all(sent, "ctx", 0, 0, tiled=True)
    rest_other = across(rest)
    up_side = [flip(up_mine[0], 1), flip(up_mine[1], 1)]
    qkv_half = w_qkv.shape[0] // 2
    qkv_send = [
        cut(w_qkv, (me_5 % 2) * qkv_half + k * (qkv_half // 2), qkv_half // 2, 0)
        for k in range(2)
    ]
    out_mine = across(cut(w_out, (me_5 % 2) * out_half, out_half, 0))
    far_grad = across(far_send)
    near_grad = dims(after(grad_y_b, lse), w_down, 1, 1)
    pieces = [with_flips([v]) for v in up_mine]
    rest_5 = [out_mine, rest_other, me_5, qkv_send[1], qkv_send[0]]
    (attended, up_side[0], near_grad), rest_5, *pieces = fenced(
        [[attended, up_side[0], near_grad], rest_5, *pieces]
    )
    out_mine, rest_other, me_6, qkv_send[1], qkv_send[0] = rest_5

    rest = by_shard(rest, rest_other, 0)
    gain_second = vector_of(rest, 0, half)
    bias_second = vector_of(rest, half, half)
    bias_output = vector_of(rest, width, half)
    bias_hidden = vector_of(rest, width + half, hidden // 2)
    out_pieces = (w_out, out_mine, flip(out_mine))
    resid, normal_two, scale_two, norm_two_b = middle(
        who, attended, out_pieces, own_tokens, gain_second, bias_second
    )
    first_units = shard * (hidden // 2) + me_6 * units
    second_units = other * (hidden // 2) + me_6 * units
    up_first = cut(w_up, first_units, units, 1)
    up_second = cut(w_up, second_units, units, 1)
    up_own = jnp.concatenate([up_first, up_second], axis=1)
    down_own = cut(w_down, me_6 * units, units, 0)
    up_give = jnp.concatenate([up_second, up_first], axis=1)
    pieces[0] = pieces[0] + with_flips([up_side[0]])
    rest_6 = [up_own, up_give, down_own]
    (norm_two_b, far_grad, up_side[1]), rest_6, *pieces = fenced(
        [[norm_two_b, far_grad, up_side[1]], rest_6, *pieces]
    )
    up_own, up_give, down_own = rest_6
    pieces = pieces[0] + pieces[1] + with_flips([up_side[1]])

    all_norm_two = gather(norm_two_b)
    up_other = across(after(up_give, norm_two_b))
    down_other = across(after(down_own, norm_two_b))
    act_b, grad_resid, grad_resid_b, grad_att, sums = feed(
        who, norm_two_b, w_up, pieces, near_grad, far_grad, bias_hidden, normal_two, scale_two,
        gain_second, grad_y_b, out_pieces,
    )
    grad_att, grad_resid_b, me_8, up_other, down_other = fence(
        grad_att, grad_resid_b, me, up_other, down_other
    )

    grad_att = grad_att.reshape(HEADS, head_size, rows)
    grad_att = lax.all_to_all(grad_att, "ctx", 0, 0, tiled=True)
    qkv_mine = [across(after(qkv_send[0], up_other, down_other))]
    deep = width // (ctx_size * fsdp_size)
    out_part = jnp.dot(
        attended.reshape(width, rows), grad_resid_b, preferred_element_type=F32
    )
    out_part = out_part.reshape(chips, fsdp_size, 2, deep, width)
    out_part = halve(out_part, 2, core, flip)
    down_half = w_down.shape[0] // 2
    down_send = cut(w_down, (me_8 % 2) * down_half, down_half, 0)
    grad_att, down_send, out_part = fence(grad_att, down_send, out_part)

    out_part = halve(out_part, 1, shard, across)
    qkv_mine.append(across(after(qkv_send[1], out_part)))
    mixed, mixed_sent = attend_back(
        place, query_t, grad_att, out_t, lse, key, key_t, pair, cos, sin, rows
    )
    mixed, mixed_sent, out_part, qkv_mine[0] = fence(
        mixed, mixed_sent, out_part, qkv_mine[0]
    )

    mixed_got = lax.all_to_all(mixed_sent, "ctx", 0, 0, tiled=True)
    qkv_slice = jnp.dot(mixed, all_norm, preferred_element_type=F32)
    qkv_keep = cut(qkv_slice, shard * half, half, 1)
    qkv_give = cut(qkv_slice, other * half, half, 1).astype(BF16)
    bias_slice = jnp.concatenate(
        [cut(bias_hidden, at, units, 1) for at in (first_units, second_units)], axis=1
    )
    qkv_other = across(qkv_give)
    out_part = halve(
        out_part.reshape(-1, 2, deep, width), 1, (me >> 1) % 2, lambda v: flip(v, 1)
    )
    qkv_sum = (qkv_keep + qkv_other.astype(F32)).astype(BF16)
    qkv_sum, bias_slice, all_norm_two, all_grad_y, out_part = fence(
        qkv_sum, bias_slice, all_norm_two, all_grad_y, out_part
    )

    all_qkv = gather(qkv_sum)
    out_part = halve(
        out_part.reshape(-1, 2, deep, width), 1, (me >> 2) % 2, lambda v: flip(v, 2)
    )
    wide_keep, wide_give = slices(
        who, all_norm_two, all_grad_y, up_own, up_other, down_own, down_other, bias_slice
    )
    wide_keep, wide_give, mixed_got, out_part = fence(
        wide_keep, wide_give, mixed_got, out_part
    )

    wide_other = across(wide_give)
    qkv_mine = fence(*qkv_mine, wide_give)[:-1]
    qkv_pieces = (w_qkv, *qkv_mine, *[flip(v) for v in qkv_mine])
    grad_tokens, total = first_back(
        who, ends_vector, mixed_got, qkv_pieces, own_tokens, grad_resid, gains, sums
    )
    total_other = across(total)
    out_part = halve(
        out_part.reshape(-1, 2, deep, width), 1, (me >> 3) % 2, lambda v: flip(v, 3)
    )
    wide_other, total, total_other, out_part = fence(
        wide_other, total, total_other, out_part
    )

    total = jnp.concatenate(
        [total[:8] + total_other[:8], total[8:], total_other[8:]], axis=0
    )
    total = jnp.pad(total, ((0, -total.shape[0] % 16), (0, 0))).astype(BF16)
    lines = total.shape[0]

    def narrow(values):
        return [values[:, k * 128 : (k + 1) * 128] for k in range(width // 128)]

    wide = jnp.concatenate(
        [(wide_keep + wide_other.astype(F32)).astype(BF16)]
        + narrow(out_part.reshape(deep, width).astype(BF16))
        + narrow(total),
        axis=0,
    )
    wide_ring = Ring(wide)
    wide_new = wide_ring.go()
    down_mine = across(after(down_send, wide))
    wide_new = list(fence(*wide_new))
    wide_flips = with_flips(wide_ring.parts)
    wide_ring.came(wide_new)

    wide_flips += with_flips(wide_new)
    wide_new = wide_ring.go()
    grads = expand_wide(place, 0, wide_flips, width, ())
    own_embed = lax.dynamic_index_in_dim(own_part, shard, 0, keepdims=False)
    other_embed = lax.dynamic_index_in_dim(own_part, other, 0, keepdims=False)
    own_embed = own_embed.astype(F32)
    other_embed = other_embed.astype(F32)
    wide_new, grads, (down_mine, own_embed, other_embed, all_qkv) = fenced(
        [wide_new, grads, [down_mine, own_embed, other_embed, all_qkv]]
    )
    wide_ring.came(wide_new)

    more_flips = with_flips(wide_new)
    wide_new = wide_ring.go()
    grad_qkv = expand_last(all_qkv.reshape(ctx_size, 3 * head_size, half), head_size)
    down_flip = flip(down_mine)
    branch = bias_output
    for b, row in (
        (w_down, shard * (hidden // 2)),
        (down_mine, other * (hidden // 2) + core * down_half),
        (down_flip, other * (hidden // 2) + (1 - core) * down_half),
    ):
        branch = branch + jnp.dot(
            cut(act_b, row, b.shape[0], 1), b, preferred_element_type=F32
        )
    output = (live * (resid + branch)).astype(BF16)
    wide_new, (output, grad_qkv), more_flips = fenced(
        [wide_new, [output, grad_qkv], more_flips]
    )

    tall = wide.shape[0] // 2
    last_top = hop(wide_new[0][:tall], 1)
    last_low = hop(wide_new[1][tall:], -1)
    more_flips += with_flips(wide_new)
    grads = expand_wide(place, len(wide_flips) // 2, more_flips, width, grads)
    grads, (last_top, last_low) = fenced([grads, [last_top, last_low]])

    wide_last = with_flips([jnp.concatenate([last_top, last_low], axis=0)])
    grad_up, grad_down, grad_out = expand_wide(
        place, chips - 1, wide_last, width, grads
    )
    grad_time, *vectors = small_sums(
        who, own_embed, other_embed, wide_flips + more_flips + wide_last,
        wide.shape[0] - lines * width // 128, lines, width,
    )
    return (
        output[None],
        grad_tokens[None],
        grad_qkv,
        grad_out,
        grad_up,
        grad_down,
        grad_time,
        *[vector.reshape(-1) for vector in vectors],
    )


def solution(mesh):
    in_specs = (
        (P("fsdp", "ctx", None),)
        + (P("fsdp", None),) * 5
        + (P("fsdp"),) * 6
        + (P("fsdp", None), P("fsdp", None), P("fsdp", "ctx", None))
    )
    out_specs = (
        (P("fsdp", "ctx", None),) * 2 + (P("fsdp", None),) * 5 + (P("fsdp"),) * 6
    )
    ctx_size, fsdp_size = mesh.shape["ctx"], mesh.shape["fsdp"]
    paired = ctx_size == HEADS and fsdp_size == 2
    return jax.shard_map(
        functools.partial(body if paired else body_general, ctx_size, fsdp_size),
        mesh=mesh,
        in_specs=in_specs,
        out_specs=out_specs,
        check_vma=False,
    )
```

```python
import functools
import math

import jax
import jax.numpy as jnp
import numpy as np
from jax import lax
from jax.experimental import pallas as pl
from jax.experimental.pallas import tpu as pltpu
from jax.sharding import PartitionSpec as P

HEADS = 16
EPSILON = 1e-05
NEGATIVE = -1e30
HIGH = lax.Precision.HIGHEST
F32 = jnp.float32
BF16 = jnp.bfloat16
VMEM_BYTES = 56 << 20


def dims(left, right, left_dim, right_dim):
    return lax.dot_general(
        left, right, (((left_dim,), (right_dim,)), ((), ())), preferred_element_type=F32
    )


def segments(ends, index):
    return sum((index >= end).astype(jnp.int32) for end in ends)


def positions(ends, index, segment):
    begin = jnp.zeros_like(index)
    for at, end in enumerate(ends):
        begin = jnp.where(segment > at, end, begin)
    return index - begin


def embed(steps_given, embed_width):
    half_width = embed_width // 2
    freq = jnp.exp(-math.log(10000.0) * jnp.arange(half_width, dtype=F32) / half_width)
    angle = steps_given.astype(F32)[..., None] * freq
    return jnp.concatenate([jnp.sin(angle), jnp.cos(angle)], axis=-1)


def stats(values):
    centre = jnp.mean(values, axis=-1, keepdims=True)
    centered = values - centre
    spread = jnp.mean(centered * centered, axis=-1, keepdims=True)
    scale = lax.rsqrt(spread + EPSILON)
    return centered * scale, scale


def stats_back(grad, normal, scale):
    return (
        grad
        - jnp.mean(grad, axis=-1, keepdims=True)
        - normal * jnp.mean(grad * normal, axis=-1, keepdims=True)
    ) * scale


def gelu_parts(pre):
    below = 0.5 * (1.0 + lax.erf(pre * math.sqrt(0.5)))
    density = jnp.exp(-0.5 * pre * pre) * (1.0 / math.sqrt(2.0 * math.pi))
    return pre * below, below + pre * density


def qkv_kernel(
    rows, head_size, first, ends_ref, base_ref, tokens_ref, gains_ref, shifts_ref, w_ref,
    cos_ref, sin_ref, *refs,
):
    norm_ref, query_t_ref, key_ref, key_t_ref, value_t_ref, pair_ref = refs[-6:]
    step = pl.program_id(0) + first
    block = tokens_ref.shape[0]
    seq_count = ends_ref.shape[0]
    half = head_size // 2
    values = tokens_ref[...].astype(F32)
    normal, _ = stats(values)
    chunks = block // rows

    def token_index(shape, axis):
        within = lax.broadcasted_iota(jnp.int32, shape, axis)
        index = within + base_ref[step * chunks]
        for at in range(1, chunks):
            index = jnp.where(
                within >= at * rows,
                within - at * rows + base_ref[step * chunks + at],
                index,
            )
        return index

    ends = [ends_ref[s] for s in range(seq_count)]
    seg_col = segments(ends, token_index((block, 1), 0))
    seg_row = segments(ends, token_index((1, block), 1))
    gains = gains_ref[0:1, :]
    shifts = shifts_ref[0:1, :]
    for s in range(1, seq_count + 1):
        gains = jnp.where(seg_col == s, gains_ref[s : s + 1, :], gains)
        shifts = jnp.where(seg_col == s, shifts_ref[s : s + 1, :], shifts)
    norm = (normal * gains + shifts).astype(BF16)
    norm_ref[...] = norm
    mixed = jnp.dot(norm, w_ref[...], preferred_element_type=F32)
    turned = mixed.T
    cos = cos_ref[...]
    sin = sin_ref[...]

    def turn(at):
        upper = turned[at : at + half]
        lower = turned[at + half : at + head_size]
        return jnp.concatenate(
            [upper * cos - lower * sin, lower * cos + upper * sin], axis=0
        ).astype(BF16)

    query = turn(0).astype(F32) * (float(head_size) ** -0.5)
    key = turn(head_size).astype(F32)
    value = turned[2 * head_size : 3 * head_size].astype(BF16).astype(F32)
    spare = 128 - head_size
    row_id = lax.broadcasted_iota(jnp.int32, (spare, block), 0)
    same = row_id == seg_row
    used = row_id <= seq_count
    key_tail = jnp.where((same & used) | ((row_id >= 8) & (row_id < 11)), 1.0, 0.0)
    query_tail = jnp.where(used & jnp.logical_not(same), NEGATIVE, 0.0)
    query_t_ref[...] = jnp.concatenate([query, query_tail], axis=0).astype(BF16)
    key_t_ref[...] = key.astype(BF16)
    value_t_ref[...] = value.astype(BF16)
    key_ref[...] = jnp.concatenate([key, key_tail], axis=0).T.astype(BF16)
    pair_ref[...] = jnp.concatenate([value, query], axis=0).T.astype(BF16)


def attend_kernel(
    chunk, rows, place_ref, query_ref, key_ref, value_ref, out_ref, sent_ref, lse_ref, score_ref, top_ref,
):
    core = place_ref[0] % 2
    count = key_ref.shape[0]
    step = pl.program_id(0)
    now = step % 2
    before = 1 - now
    query = query_ref[...]
    last_top = top_ref[before]
    top = None
    total = jnp.zeros_like(last_top)
    out = jnp.zeros(out_ref.shape, F32)
    for at in range(0, count, chunk):
        part = slice(at, at + chunk)
        score = jnp.dot(key_ref[part, :], query, preferred_element_type=F32)
        weight = jnp.exp(score_ref[before, part, :] - last_top)
        score_ref[now, part, :] = score
        high = jnp.max(score, axis=0, keepdims=True)
        top = high if top is None else jnp.maximum(top, high)
        total = total + jnp.sum(weight, axis=0, keepdims=True)
        out = out + jnp.dot(
            value_ref[:, part], weight.astype(BF16), preferred_element_type=F32
        )
    top_ref[now] = top

    @pl.when(step > 0)
    def _():
        result = out / total
        out_ref[...] = result
        for at in range(sent_ref.shape[0]):
            sent_ref[at ^ core] = result[:, at * rows : (at + 1) * rows].astype(BF16)
        lse_ref[...] = last_top + jnp.log(total)


def attend_back_kernel(
    chunk, rows, head_size, place_ref, query_ref, grad_ref, out_ref, lse_ref, key_ref, key_t_ref, pair_ref,
    pair_block_ref, cos_block_ref, sin_block_ref, cos_ref, sin_ref, mixed_ref, sent_ref, acc_ref,
):
    step = pl.program_id(0)
    core = place_ref[0] % 2
    per_step = grad_ref.shape[0]
    count = key_ref.shape[0]
    block = query_ref.shape[1]
    half = head_size // 2
    scale = float(head_size) ** -0.5

    @pl.when(step == 0)
    def _():
        acc_ref[...] = jnp.zeros_like(acc_ref)

    rest = -lse_ref[...]
    query = query_ref[...].astype(F32)
    row_id = lax.broadcasted_iota(jnp.int32, query.shape, 0)
    for k in range(3):
        piece = rest.astype(BF16).astype(F32)
        query = jnp.where(row_id == head_size + 8 + k, piece, query)
        rest = rest - piece
    query = query.astype(BF16)
    grad = jnp.concatenate(
        [grad_ref[at ^ core] for at in range(per_step)], axis=1
    ).astype(F32)
    delta = jnp.sum(grad * out_ref[...], axis=0, keepdims=True)
    grad_t = jnp.concatenate([grad, jnp.zeros((128 - head_size, block), F32)], axis=0)
    pair = pair_block_ref[...]
    lane = lax.broadcasted_iota(jnp.int32, pair.shape, 1)
    queries = jnp.where(lane >= head_size, pair.astype(F32), 0.0).astype(BF16)
    both = jnp.concatenate([queries, grad_t.T.astype(BF16)], axis=0)
    grad_t = grad_t.astype(BF16)
    grad_query = jnp.zeros((head_size, block), F32)
    for at in range(0, count, chunk):
        part = slice(at, at + chunk)
        score = jnp.dot(key_ref[part, :], query, preferred_element_type=F32)
        prob = jnp.exp(score)
        grad_prob = jnp.dot(pair_ref[part, :], grad_t, preferred_element_type=F32)
        grad_score = (prob * (grad_prob - delta)).astype(BF16)
        grad_query = grad_query + jnp.dot(
            key_t_ref[:, part], grad_score, preferred_element_type=F32
        )
        acc_ref[part, :] += jnp.dot(
            jnp.concatenate([grad_score, prob.astype(BF16)], axis=1),
            both,
            preferred_element_type=F32,
        )

    def turn_back(values, cos, sin):
        upper = values[:half]
        lower = values[half:]
        return jnp.concatenate(
            [upper * cos + lower * sin, lower * cos - upper * sin], axis=0
        ).astype(BF16)

    at = pl.multiple_of(step * block, block)
    query_part = turn_back(
        grad_query * scale, cos_block_ref[...], sin_block_ref[...]
    )
    mixed_ref[0:head_size, pl.ds(at, block)] = query_part
    for k in range(per_step):
        sent_ref[place_ref[step * per_step + k], 0:head_size, :] = query_part[
            :, k * rows : (k + 1) * rows
        ]

    @pl.when(step == pl.num_programs(0) - 1)
    def _():
        acc = acc_ref[...].T
        key_part = turn_back(acc[head_size : 2 * head_size], cos_ref[...], sin_ref[...])
        value_part = acc[:head_size].astype(BF16)
        parts = jnp.concatenate([key_part, value_part], axis=0)
        mixed_ref[head_size : 3 * head_size, :] = parts
        for k in range(count // rows):
            sent_ref[place_ref[k], head_size : 3 * head_size, :] = parts[
                :, k * rows : (k + 1) * rows
            ]


def whole(shape):
    return pl.BlockSpec(shape, lambda i, *_: (0,) * len(shape))


def project(
    tokens, base, ends, gains, shifts, w_head, cos, sin, rows, head_size, first=0, earlier=None,
):
    width = tokens.shape[1]
    count = base.shape[0] * rows
    block = min(count, 2 * rows)
    earlier = list(earlier or ())
    grid_spec = pltpu.PrefetchScalarGridSpec(
        num_scalar_prefetch=2,
        grid=(tokens.shape[0] // block,),
        in_specs=[
            pl.BlockSpec((block, width), lambda i, *_: (i, 0)),
            whole(gains.shape),
            whole(shifts.shape),
            whole(w_head.shape),
            pl.BlockSpec((head_size // 2, block), lambda i, *_: (0, i + first)),
            pl.BlockSpec((head_size // 2, block), lambda i, *_: (0, i + first)),
        ]
        + [pl.BlockSpec(memory_space=pl.ANY)] * len(earlier),
        out_specs=[
            pl.BlockSpec((block, width), lambda i, *_: (i + first, 0)),
            pl.BlockSpec((128, block), lambda i, *_: (0, i + first)),
            pl.BlockSpec((block, 128), lambda i, *_: (i + first, 0)),
            pl.BlockSpec((head_size, block), lambda i, *_: (0, i + first)),
            pl.BlockSpec((head_size, block), lambda i, *_: (0, i + first)),
            pl.BlockSpec((block, 128), lambda i, *_: (i + first, 0)),
        ],
    )
    return pl.pallas_call(
        functools.partial(qkv_kernel, rows, head_size, first),
        grid_spec=grid_spec,
        out_shape=[
            jax.ShapeDtypeStruct((count, width), BF16),
            jax.ShapeDtypeStruct((128, count), BF16),
            jax.ShapeDtypeStruct((count, 128), BF16),
            jax.ShapeDtypeStruct((head_size, count), BF16),
            jax.ShapeDtypeStruct((head_size, count), BF16),
            jax.ShapeDtypeStruct((count, 128), BF16),
        ],
        input_output_aliases={8 + k: k for k in range(len(earlier))},
        compiler_params=pltpu.CompilerParams(vmem_limit_bytes=VMEM_BYTES),
        cost_estimate=pl.CostEstimate(
            flops=2 * tokens.shape[0] * width * 1024,
            bytes_accessed=4 * tokens.shape[0] * width,
            transcendentals=0,
        ),
        name="project_head",
    )(ends, base, tokens, gains, shifts, w_head, cos, sin, *earlier)


def project_chunks_kernel(rows, head_size, first, chunks, who_ref, ends_ref, base_ref, *refs):
    tokens = refs[:chunks]
    gains_ref, shifts_ref, own_ref, other_ref, cos_ref, sin_ref = refs[chunks : chunks + 6]
    block_ref, w_ref = refs[-2:]
    step = pl.program_id(0)
    size = own_ref.shape[0]

    @pl.when(step == 0)
    def _():
        w_ref[:, 128:] = jnp.zeros((2 * size, 128), BF16)
        shard = who_ref[1]
        own_at = pl.multiple_of(shard * size, size)
        other_at = pl.multiple_of((1 - shard) * size, size)
        width = own_ref.shape[1]
        w_ref[pl.ds(own_at, size), :width] = own_ref[...]
        w_ref[pl.ds(other_at, size), :width] = other_ref[...]

    for at in range(chunks // 2):

        @pl.when(step == at)
        def _():
            block_ref[:rows] = tokens[2 * at][...]
            block_ref[rows:] = tokens[2 * at + 1][...]

    qkv_kernel(
        rows, head_size, first, ends_ref, base_ref, block_ref, gains_ref, shifts_ref, w_ref,
        cos_ref, sin_ref, *refs[-8:-2],
    )


def project_chunks(
    who, tokens, base, ends, gains, shifts, w_own, w_other, cos, sin, head_size, first=0, earlier=None,
):
    rows, width = tokens[0].shape
    count = base.shape[0] * rows
    block = 2 * rows
    earlier = list(earlier or ())
    grid_spec = pltpu.PrefetchScalarGridSpec(
        num_scalar_prefetch=3,
        grid=(len(tokens) // 2,),
        in_specs=[whole((rows, width))] * len(tokens)
        + [
            whole(gains.shape),
            whole(shifts.shape),
            whole(w_own.shape),
            whole(w_other.shape),
            pl.BlockSpec((head_size // 2, block), lambda i, *_: (0, i + first)),
            pl.BlockSpec((head_size // 2, block), lambda i, *_: (0, i + first)),
        ]
        + [pl.BlockSpec(memory_space=pl.ANY)] * len(earlier),
        out_specs=[
            pl.BlockSpec((block, width), lambda i, *_: (i + first, 0)),
            pl.BlockSpec((128, block), lambda i, *_: (0, i + first)),
            pl.BlockSpec((block, 128), lambda i, *_: (i + first, 0)),
            pl.BlockSpec((head_size, block), lambda i, *_: (0, i + first)),
            pl.BlockSpec((head_size, block), lambda i, *_: (0, i + first)),
            pl.BlockSpec((block, 128), lambda i, *_: (i + first, 0)),
        ],
        scratch_shapes=[
            pltpu.VMEM((block, width), BF16),
            pltpu.VMEM((width, 256), BF16),
        ],
    )
    return pl.pallas_call(
        functools.partial(project_chunks_kernel, rows, head_size, first, len(tokens)),
        grid_spec=grid_spec,
        out_shape=[
            jax.ShapeDtypeStruct((count, width), BF16),
            jax.ShapeDtypeStruct((128, count), BF16),
            jax.ShapeDtypeStruct((count, 128), BF16),
            jax.ShapeDtypeStruct((head_size, count), BF16),
            jax.ShapeDtypeStruct((head_size, count), BF16),
            jax.ShapeDtypeStruct((count, 128), BF16),
        ],
        input_output_aliases={9 + len(tokens) + k: k for k in range(len(earlier))},
        compiler_params=pltpu.CompilerParams(vmem_limit_bytes=VMEM_BYTES),
        cost_estimate=pl.CostEstimate(
            flops=2 * len(tokens) * rows * width * 1024,
            bytes_accessed=4 * len(tokens) * rows * width,
            transcendentals=0,
        ),
        name="project_chunks",
    )(who, ends, base, *tokens, gains, shifts, w_own, w_other, cos, sin, *earlier)


def attend(place, query_t, key, value_t, rows):
    count = key.shape[0]
    head_size = value_t.shape[0]
    block = min(count, 2 * rows)
    chunk = min(count, 512)
    blocks = count // block

    def before(i):
        return jnp.maximum(i - 1, 0)

    grid_spec = pltpu.PrefetchScalarGridSpec(
        num_scalar_prefetch=1,
        grid=(blocks + 1,),
        in_specs=[
            pl.BlockSpec((128, block), lambda i, _: (0, jnp.minimum(i, blocks - 1))),
            whole((count, 128)),
            whole((head_size, count)),
        ],
        out_specs=[
            pl.BlockSpec((head_size, block), lambda i, _: (0, before(i))),
            pl.BlockSpec(
                (2, head_size, rows), lambda i, place: (place[2 * before(i)] // 2, 0, 0)
            ),
            pl.BlockSpec((1, block), lambda i, _: (0, before(i))),
        ],
        scratch_shapes=[
            pltpu.VMEM((2, count, block), F32),
            pltpu.VMEM((2, 1, block), F32),
        ],
    )
    return pl.pallas_call(
        functools.partial(attend_kernel, chunk, rows),
        grid_spec=grid_spec,
        out_shape=[
            jax.ShapeDtypeStruct((head_size, count), F32),
            jax.ShapeDtypeStruct((count // rows, head_size, rows), BF16),
            jax.ShapeDtypeStruct((1, count), F32),
        ],
        compiler_params=pltpu.CompilerParams(vmem_limit_bytes=VMEM_BYTES),
        cost_estimate=pl.CostEstimate(
            flops=8 * count * count * 128,
            bytes_accessed=8 * count * 128,
            transcendentals=count * count,
        ),
        name="attend_head",
    )(place, query_t, key, value_t)


def attend_back(place, query_t, grad, out, lse, key, key_t, pair, cos, sin, rows):
    count = key.shape[0]
    head_size = key_t.shape[0]
    half = head_size // 2
    block = min(count, 2 * rows)
    chunk = min(count, 512)
    grid_spec = pltpu.PrefetchScalarGridSpec(
        num_scalar_prefetch=1,
        grid=(count // block,),
        in_specs=[
            pl.BlockSpec((128, block), lambda i, _: (0, i)),
            pl.BlockSpec(
                (2, head_size, rows), lambda i, place: (place[2 * i] // 2, 0, 0)
            ),
            pl.BlockSpec((head_size, block), lambda i, _: (0, i)),
            pl.BlockSpec((1, block), lambda i, _: (0, i)),
            whole((count, 128)),
            whole((head_size, count)),
            whole((count, 128)),
            pl.BlockSpec((block, 128), lambda i, _: (i, 0)),
            pl.BlockSpec((half, block), lambda i, _: (0, i)),
            pl.BlockSpec((half, block), lambda i, _: (0, i)),
            whole((half, count)),
            whole((half, count)),
        ],
        out_specs=[
            whole((3 * head_size, count)),
            whole((count // rows, 3 * head_size, rows)),
        ],
        scratch_shapes=[pltpu.VMEM((count, 128), F32)],
    )
    return pl.pallas_call(
        functools.partial(attend_back_kernel, chunk, rows, head_size),
        grid_spec=grid_spec,
        out_shape=[
            jax.ShapeDtypeStruct((3 * head_size, count), BF16),
            jax.ShapeDtypeStruct((count // rows, 3 * head_size, rows), BF16),
        ],
        compiler_params=pltpu.CompilerParams(vmem_limit_bytes=VMEM_BYTES),
        cost_estimate=pl.CostEstimate(
            flops=20 * count * count * 128,
            bytes_accessed=16 * count * 128,
            transcendentals=count * count,
        ),
        name="attend_head_back",
    )(place, query_t, grad, out, lse, key, key_t, pair, pair, cos, sin, cos, sin)


def slices_kernel(
    who_ref, norm_ref, grad_ref, up_own, up_other, down_own, down_other, bias_ref, keep_ref,
    give_ref, down_w, down_acc, up_acc, up_t,
):
    step = pl.program_id(0)
    shard = who_ref[1]
    size, units = up_own.shape
    width = 2 * size
    half = units // 2
    own_at = pl.multiple_of(shard * size, size)
    other_at = pl.multiple_of((1 - shard) * size, size)

    @pl.when(step == 0)
    def _():
        down_w[:half] = down_own[...]
        down_w[half:] = down_other[...]
        down_acc[...] = jnp.zeros_like(down_acc)
        up_acc[...] = jnp.zeros_like(up_acc)

    pre = jnp.dot(
        norm_ref[:, pl.ds(own_at, size)], up_own[...], preferred_element_type=F32
    )
    pre = pre + jnp.dot(
        norm_ref[:, pl.ds(other_at, size)], up_other[...], preferred_element_type=F32
    )
    act, slope = gelu_parts(pre + bias_ref[...])
    grad_y = grad_ref[...]
    grad = dims(grad_y, down_w[...], 1, 1) * slope
    down_acc[...] += jnp.dot(act.T.astype(BF16), grad_y, preferred_element_type=F32)
    up_acc[...] += jnp.dot(
        grad.T.astype(BF16), norm_ref[...], preferred_element_type=F32
    )

    @pl.when(step == pl.num_programs(0) - 1)
    def _():
        up_t[...] = up_acc[...].T
        for at, (rows, out_ref) in enumerate(((own_at, keep_ref), (other_at, give_ref))):
            values = up_t[pl.ds(rows, size), :].astype(out_ref.dtype)
            out_ref[pl.ds(own_at, size), :] = values[:, :half]
            out_ref[pl.ds(other_at, size), :] = values[:, half:]
            for k in range(width // half):
                out_ref[width + k * half : width + (k + 1) * half, :] = down_acc[
                    at * half : (at + 1) * half, k * half : (k + 1) * half
                ].astype(out_ref.dtype)


def slices(
    who, norm, grad_y, up_own, up_other, down_own, down_other, bias,
):
    count, width = norm.shape
    size, units = up_own.shape
    block = 256
    tall = 2 * width
    token = pl.BlockSpec((block, width), lambda i: (i, 0))
    return pl.pallas_call(
        slices_kernel,
        grid=(count // block,),
        in_specs=[pl.BlockSpec(memory_space=pltpu.SMEM), token, token]
        + [
            pl.BlockSpec(v.shape, lambda i: (0, 0))
            for v in (up_own, up_other, down_own, down_other, bias)
        ],
        out_specs=[pl.BlockSpec((tall, units // 2), lambda i: (0, 0))] * 2,
        out_shape=[
            jax.ShapeDtypeStruct((tall, units // 2), F32),
            jax.ShapeDtypeStruct((tall, units // 2), BF16),
        ],
        scratch_shapes=[
            pltpu.VMEM((units, width), BF16),
            pltpu.VMEM((units, width), F32),
            pltpu.VMEM((units, width), F32),
            pltpu.VMEM((width, units), F32),
        ],
        compiler_params=pltpu.CompilerParams(vmem_limit_bytes=VMEM_BYTES),
        cost_estimate=pl.CostEstimate(
            flops=8 * count * width * units,
            bytes_accessed=6 * count * width,
            transcendentals=2 * count * units,
        ),
        name="weight_slices",
    )(
        who, norm, grad_y, up_own, up_other, down_own, down_other, bias
    )


def head_of(device, devices):
    return device % 2 * (devices // 2) + device // 2


def row_starts(who_ref, size):
    core = who_ref[0] % 2
    shard = who_ref[1]
    half = size // 2
    other = (1 - shard) * size
    return (
        pl.multiple_of(shard * size, size),
        pl.multiple_of(other + core * half, half),
        pl.multiple_of(other + (1 - core) * half, half),
    )


def middle_kernel(
    who_ref, att_ref, own_ref, mine_ref, flip_ref, tokens_ref, gain_ref, bias_ref,
    resid_ref, normal_ref, scale_ref, norm_ref, turned,
):
    devices, head_size, _ = att_ref.shape
    for d in range(devices):
        at = head_of(d, devices) * head_size
        turned[:, at : at + head_size] = att_ref[d].astype(F32).T.astype(BF16)
    resid = tokens_ref[...].astype(F32)
    pieces = (own_ref, mine_ref, flip_ref)
    for at, piece in zip(row_starts(who_ref, own_ref.shape[0]), pieces):
        resid = resid + jnp.dot(
            turned[:, pl.ds(at, piece.shape[0])],
            piece[...],
            preferred_element_type=F32,
        )
    resid_ref[...] = resid
    normal, scale = stats(resid)
    normal_ref[...] = normal
    scale_ref[...] = scale
    norm_ref[...] = (normal * gain_ref[...] + bias_ref[...]).astype(BF16)


def middle(who, attended, pieces, tokens, gain, bias):
    rows, width = tokens.shape
    vmem = pl.BlockSpec(memory_space=pltpu.VMEM)
    return pl.pallas_call(
        middle_kernel,
        in_specs=[pl.BlockSpec(memory_space=pltpu.SMEM)] + [vmem] * 7,
        out_specs=[vmem] * 4,
        out_shape=[
            jax.ShapeDtypeStruct((rows, width), F32),
            jax.ShapeDtypeStruct((rows, width), F32),
            jax.ShapeDtypeStruct((rows, 1), F32),
            jax.ShapeDtypeStruct((rows, width), BF16),
        ],
        scratch_shapes=[pltpu.VMEM((rows, width), BF16)],
        compiler_params=pltpu.CompilerParams(vmem_limit_bytes=VMEM_BYTES),
        cost_estimate=pl.CostEstimate(
            flops=8 * rows * width * width,
            bytes_accessed=4 * width * width,
            transcendentals=0,
        ),
        name="output_projection",
    )(who, attended, *pieces, tokens, gain, bias)


def feed_kernel(parts, who_ref, norm_ref, own_ref, *refs):
    pieces = refs[: 4 * parts]
    (
        near_ref, far_ref, bias_ref, normal_ref, scale_ref, gain_ref, grad_y_ref, out_own, out_mine,
        out_flip, act_ref, resid_ref, resid_b_ref, sent_ref, sums_ref, grad_ref, att_ref,
    ) = refs[4 * parts :]
    side = who_ref[0] % 4
    shard = who_ref[1]
    size, hidden = own_ref.shape
    quarter = hidden // 4
    deep = size // parts
    own_at = pl.multiple_of(shard * size, size)
    other_at = pl.multiple_of((1 - shard) * size, size)
    own_norm = norm_ref[:, pl.ds(own_at, size)]
    part_at = [pl.multiple_of(other_at + p * deep, deep) for p in range(parts)]
    norms = [norm_ref[:, pl.ds(at, deep)] for at in part_at]
    for k in range(4):
        block = side ^ k
        columns = pl.ds(pl.multiple_of(block * quarter, quarter), quarter)
        weight = own_ref[:, columns]
        pre = jnp.dot(own_norm, weight, preferred_element_type=F32)
        for p in range(parts):
            pre = pre + jnp.dot(
                norms[p], pieces[4 * p + k][...], preferred_element_type=F32
            )
        act, slope = gelu_parts(pre + bias_ref[:, columns])
        act_ref[:, columns] = act.astype(BF16)
        within = pl.ds(pl.multiple_of((block % 2) * quarter, quarter), quarter)
        near = near_ref[:, within]
        far = far_ref[:, within].astype(F32)
        grad = jnp.where(block // 2 == shard, near, far) * slope
        sums_ref[pl.ds(3 + block, 1), :] = jnp.sum(grad, axis=0, keepdims=True)
        grad = grad.astype(BF16)
        terms = [(own_at, size, weight)]
        terms += [(part_at[p], deep, pieces[4 * p + k][...]) for p in range(parts)]
        for at, length, piece in terms:
            term = dims(grad, piece, 1, 1)
            if k == 0:
                grad_ref[:, pl.ds(at, length)] = term
            else:
                grad_ref[:, pl.ds(at, length)] += term
    grad = grad_ref[...]
    normal = normal_ref[...]
    grad_y = grad_y_ref[...].astype(F32)
    sums_ref[0:1, :] = jnp.sum(grad * normal, axis=0, keepdims=True)
    sums_ref[1:2, :] = jnp.sum(grad, axis=0, keepdims=True)
    sums_ref[2:3, :] = jnp.sum(grad_y, axis=0, keepdims=True)
    sums_ref[7:8, :] = jnp.zeros((1, quarter), F32)
    resid = grad_y + stats_back(grad * gain_ref[...], normal, scale_ref[...])
    resid_ref[...] = resid
    resid = resid.astype(BF16)
    resid_b_ref[...] = resid
    out_pieces = (out_own, out_mine, out_flip)
    for at, piece in zip(row_starts(who_ref, out_own.shape[0]), out_pieces):
        att_ref[pl.ds(at, piece.shape[0]), :] = dims(piece[...], resid, 1, 1).astype(
            BF16
        )
    devices, head_size, _ = sent_ref.shape
    for d in range(devices):
        at = head_of(d, devices) * head_size
        sent_ref[d] = att_ref[at : at + head_size, :]


def feed(who, norm, own, pieces, near, far, bias, normal, scale, gain, grad_y, out_pieces):
    rows, width = norm.shape
    hidden = own.shape[1]
    vmem = pl.BlockSpec(memory_space=pltpu.VMEM)
    return pl.pallas_call(
        functools.partial(feed_kernel, len(pieces) // 4),
        in_specs=[pl.BlockSpec(memory_space=pltpu.SMEM)] + [vmem] * (12 + len(pieces)),
        out_specs=[vmem] * 5,
        out_shape=[
            jax.ShapeDtypeStruct((rows, hidden), BF16),
            jax.ShapeDtypeStruct((rows, width), F32),
            jax.ShapeDtypeStruct((rows, width), BF16),
            jax.ShapeDtypeStruct((HEADS, width // HEADS, rows), BF16),
            jax.ShapeDtypeStruct((8, width), F32),
        ],
        scratch_shapes=[pltpu.VMEM((rows, width), F32), pltpu.VMEM((width, rows), BF16)],
        compiler_params=pltpu.CompilerParams(vmem_limit_bytes=VMEM_BYTES),
        cost_estimate=pl.CostEstimate(
            flops=16 * rows * width * hidden,
            bytes_accessed=4 * width * hidden,
            transcendentals=2 * rows * hidden,
        ),
        name="feed_forward",
    )(who, norm, own, *pieces, near, far, bias, normal, scale, gain, grad_y, *out_pieces)


def first_back_kernel(
    head_size, who_ref, ends_ref, got_ref, own_ref, mine_0, mine_1, flip_0, flip_1, tokens_ref,
    resid_ref, gains_ref, sums_ref, grad_ref, total_ref, mixed, turned,
):
    heads = got_ref.shape[0]
    rows, width = tokens_ref.shape
    seq_count = ends_ref.shape[0]
    for d in range(heads):
        for k in range(3):
            at = k * width + head_of(d, heads) * head_size
            mixed[at : at + head_size, :] = got_ref[
                d, k * head_size : (k + 1) * head_size, :
            ]
    own_at, mine_at, flip_at = row_starts(who_ref, own_ref.shape[0])
    part = mine_0.shape[0]
    starts = (own_at, mine_at, mine_at + part, flip_at, flip_at + part)
    for at, piece in zip(starts, (own_ref, mine_0, mine_1, flip_0, flip_1)):
        turned[pl.ds(at, piece.shape[0]), :] = jnp.dot(
            piece[...], mixed[...], preferred_element_type=F32
        )
    grad = turned[...].T
    normal, scale = stats(tokens_ref[...].astype(F32))
    index = who_ref[0] * rows + lax.broadcasted_iota(jnp.int32, (rows, 1), 0)
    segment = segments([ends_ref[s] for s in range(seq_count)], index)
    gains = gains_ref[0:1, :]
    for s in range(1, seq_count + 1):
        gains = jnp.where(segment == s, gains_ref[s : s + 1, :], gains)
    grad_ref[...] = (
        resid_ref[...] + stats_back(grad * gains, normal, scale)
    ).astype(BF16)
    total_ref[0:8, :] = sums_ref[...]
    product = grad * normal
    for s in range(seq_count + 1):
        here = segment == s
        for k, terms in enumerate((product, grad)):
            total_ref[8 + 2 * s + k : 9 + 2 * s + k, :] = jnp.sum(
                jnp.where(here, terms, 0.0), axis=0, keepdims=True
            )


def first_back(who, ends, got, pieces, tokens, resid, gains, sums):
    rows, width = tokens.shape
    heads, tall, _ = got.shape
    seq_count = ends.shape[0]
    lines = 8 + 2 * (seq_count + 1)
    vmem = pl.BlockSpec(memory_space=pltpu.VMEM)
    return pl.pallas_call(
        functools.partial(first_back_kernel, tall // 3),
        in_specs=[pl.BlockSpec(memory_space=pltpu.SMEM)] * 2 + [vmem] * 10,
        out_specs=[vmem] * 2,
        out_shape=[
            jax.ShapeDtypeStruct((rows, width), BF16),
            jax.ShapeDtypeStruct((lines, width), F32),
        ],
        scratch_shapes=[
            pltpu.VMEM((3 * width, rows), BF16),
            pltpu.VMEM((width, rows), F32),
        ],
        compiler_params=pltpu.CompilerParams(vmem_limit_bytes=VMEM_BYTES),
        cost_estimate=pl.CostEstimate(
            flops=12 * rows * width * width,
            bytes_accessed=8 * width * width,
            transcendentals=0,
        ),
        name="first_norm_back",
    )(who, ends, got, *pieces, tokens, resid, gains, sums)


def small_kernel(seq_count, chunks, who_ref, own_embed, other_embed, *refs):
    parts = refs[:chunks]
    (
        time_ref, gain_one, bias_one, gain_two, bias_two, bias_up, bias_down, total,
    ) = refs[chunks:]
    lines, width = total.shape
    half = width // 2
    shard = who_ref[1]
    for k in range(width // 128):
        at = k * lines
        value = parts[0][at : at + lines, :].astype(F32)
        for ref in parts[1:]:
            value = value + ref[at : at + lines, :].astype(F32)
        total[:, k * 128 : (k + 1) * 128] = value
    part = pl.ds(pl.multiple_of(shard * half, half), half)
    gain_two[...] = total[0:1, part]
    bias_two[...] = total[1:2, part]
    bias_down[...] = total[2:3, part]
    bias_up[:, :width] = total[pl.ds(3 + 2 * shard, 1), :]
    bias_up[:, width:] = total[pl.ds(4 + 2 * shard, 1), :]
    films = 2 * (seq_count + 1)
    gain = total[8:9, part]
    bias = total[9:10, part]
    for s in range(1, films):
        gain = gain + total[8 + 2 * s : 9 + 2 * s, part]
        bias = bias + total[9 + 2 * s : 10 + 2 * s, part]
    gain_one[...] = gain
    bias_one[...] = bias
    embeds = []
    for embed_ref in (own_embed, other_embed):
        columns = []
        for s in range(seq_count):
            line = embed_ref[s : s + 1, :]
            columns.append(jnp.broadcast_to(line, (8, line.shape[1])).T[:, 0:1])
        embeds.append(columns)
    for k in range(2):
        value = None
        for g, columns in enumerate(embeds):
            for s in range(seq_count):
                line = 8 + g * films + 2 * s + k
                term = columns[s] * total[line : line + 1, :]
                value = term if value is None else value + term
        time_ref[:, k * width : (k + 1) * width] = value


def small_sums(who, own_embed, other_embed, parts, top, lines, width):
    vmem = pl.BlockSpec(memory_space=pltpu.VMEM)
    tall = lines * width // 128
    tail = pl.BlockSpec((tall, 128), lambda i: (top // tall, 0))
    return pl.pallas_call(
        functools.partial(small_kernel, own_embed.shape[0], len(parts)),
        grid=(1,),
        in_specs=[pl.BlockSpec(memory_space=pltpu.SMEM)]
        + [vmem] * 2
        + [tail] * len(parts),
        out_specs=[vmem] * 7,
        out_shape=[jax.ShapeDtypeStruct((own_embed.shape[1], 2 * width), F32)]
        + [jax.ShapeDtypeStruct((1, width // 2), F32)] * 4
        + [
            jax.ShapeDtypeStruct((1, 2 * width), F32),
            jax.ShapeDtypeStruct((1, width // 2), F32),
        ],
        scratch_shapes=[pltpu.VMEM((lines, width), F32)],
        compiler_params=pltpu.CompilerParams(vmem_limit_bytes=VMEM_BYTES),
        cost_estimate=pl.CostEstimate(
            flops=1000000, bytes_accessed=2000000, transcendentals=0
        ),
        name="small_gradients",
    )(who, own_embed, other_embed, *parts)


def stream(chips, copies_of, fill):
    pending = [None, None]
    for at in range(chips):
        slot = at % 2
        if pending[slot] is not None:
            for copy in pending[slot]:
                copy.wait()
        fill(at, slot)
        pending[slot] = copies_of(at, slot)
        for copy in pending[slot]:
            copy.start()
    for copies in pending:
        if copies is not None:
            for copy in copies:
                copy.wait()


def wide_kernel(first, chunks, place_ref, *refs):
    parts = refs[:chunks]
    up_ref, down_ref, out_ref, up_slots, down_slots, out_slots, sems = refs[-7:]
    core = place_ref[0] % 2
    deep = out_slots.shape[1] // 2
    size = up_ref.shape[0]
    hidden = up_ref.shape[1]
    width = down_ref.shape[1]

    def fill(at, slot):
        for j in range(2):
            ref = parts[2 * at + j]
            column = pl.ds(pl.multiple_of((j ^ core) * 128, 128), 128)
            for k in range(2):
                up_slots[slot, k, :, column] = ref[k * size : (k + 1) * size, :].astype(
                    F32
                )
            row = pl.ds(pl.multiple_of((j ^ core) * 128, 128), 128)
            for k in range(width // 128):
                top = 2 * size + k * 128
                down_slots[slot, row, k * 128 : (k + 1) * 128] = ref[
                    top : top + 128, :
                ].astype(F32)
            row = pl.ds(pl.multiple_of((j ^ core) * deep, deep), deep)
            for k in range(width // 128):
                top = 2 * size + width + k * deep
                out_slots[slot, row, k * 128 : (k + 1) * 128] = ref[
                    top : top + deep, :
                ].astype(F32)

    def copies_of(at, slot):
        chip = place_ref[2 * (at + first)] // 2
        copies = []
        for k in range(2):
            column = pl.multiple_of(k * (hidden // 2) + chip * 256, 256)
            copies.append(
                pltpu.make_async_copy(
                    up_slots.at[slot, k],
                    up_ref.at[:, pl.ds(column, 256)],
                    sems.at[slot, k],
                )
            )
        row = pl.multiple_of(chip * 256, 256)
        copies.append(
            pltpu.make_async_copy(
                down_slots.at[slot], down_ref.at[pl.ds(row, 256), :], sems.at[slot, 2]
            )
        )
        row = pl.multiple_of(chip * 2 * deep, 2 * deep)
        copies.append(
            pltpu.make_async_copy(
                out_slots.at[slot], out_ref.at[pl.ds(row, 2 * deep), :], sems.at[slot, 3]
            )
        )
        return copies

    stream(chunks // 2, copies_of, fill)


def expand_wide(place, first, parts, width, earlier):
    devices = place.shape[0]
    size = width // 2
    vmem = pl.BlockSpec(memory_space=pltpu.VMEM)
    hbm = pl.BlockSpec(memory_space=pl.ANY)
    return pl.pallas_call(
        functools.partial(wide_kernel, first, len(parts)),
        in_specs=[pl.BlockSpec(memory_space=pltpu.SMEM)]
        + [vmem] * len(parts)
        + [hbm] * len(earlier),
        out_specs=[hbm, hbm, hbm],
        out_shape=[
            jax.ShapeDtypeStruct((size, 2 * devices * 128), F32),
            jax.ShapeDtypeStruct((devices * 128, width), F32),
            jax.ShapeDtypeStruct((size, width), F32),
        ],
        scratch_shapes=[
            pltpu.VMEM((2, 2, size, 256), F32),
            pltpu.VMEM((2, 256, width), F32),
            pltpu.VMEM((2, 2 * size // devices, width), F32),
            pltpu.SemaphoreType.DMA((2, 4)),
        ],
        input_output_aliases={1 + len(parts) + k: k for k in range(len(earlier))},
        compiler_params=pltpu.CompilerParams(vmem_limit_bytes=VMEM_BYTES),
        cost_estimate=pl.CostEstimate(
            flops=parts[0].size * len(parts),
            bytes_accessed=6 * parts[0].size * len(parts),
            transcendentals=0,
        ),
        name="expand_wide",
    )(place, *parts, *earlier)


def last_kernel(head_size, in_ref, out_ref):
    pairs = []
    for j in range(2):
        for k in range(in_ref.shape[0] // 4):
            pairs.append((in_ref[4 * k + j], in_ref[4 * k + 2 + j]))
    for at, (first, second) in enumerate(pairs):
        both = jnp.concatenate([first, second], axis=0).astype(F32)
        out_ref[:, at * 2 * head_size : (at + 1) * 2 * head_size] = both.T


def expand_last(parts, head_size):
    devices, tall, depth = parts.shape
    width = devices * head_size
    return pl.pallas_call(
        functools.partial(last_kernel, head_size),
        grid=(3,),
        in_specs=[pl.BlockSpec((devices, head_size, depth), lambda k: (0, k, 0))],
        out_specs=pl.BlockSpec((depth, width), lambda k: (0, k)),
        out_shape=jax.ShapeDtypeStruct((depth, 3 * width), F32),
        compiler_params=pltpu.CompilerParams(vmem_limit_bytes=VMEM_BYTES),
        cost_estimate=pl.CostEstimate(
            flops=parts.size, bytes_accessed=6 * parts.size, transcendentals=0
        ),
        name="expand_last",
    )(parts)


def times_rows(values, pieces):
    return sum(
        jnp.dot(
            lax.dynamic_slice_in_dim(values, at, piece.shape[0], 1),
            piece,
            preferred_element_type=F32,
        )
        for piece, at in pieces
    )


def times_rows_t(values_t, pieces):
    return sum(
        dims(lax.dynamic_slice_in_dim(values_t, at, piece.shape[0], 0), piece, 0, 0)
        for piece, at in pieces
    )


def joined(parts, pieces, dim):
    if len(parts) == 1:
        return parts[0]
    shape = list(parts[0].shape)
    shape[dim] = sum(part.shape[dim] for part in parts)
    out = jnp.zeros(shape, parts[0].dtype)
    for part, (_, at) in zip(parts, pieces):
        out = lax.dynamic_update_slice_in_dim(out, part, at, dim)
    return out


def rows_of(pieces, start, size):
    out = None
    for piece, at in pieces:
        length = piece.shape[0]
        local = jnp.clip(start - at, 0, length - size)
        found = lax.dynamic_slice_in_dim(piece, local, size, 0)
        inside = (start >= at) & (start < at + length)
        out = found if out is None else jnp.where(inside, found, out)
    return out


def body_general(
    ctx_size, fsdp_size,
    tokens, w_qkv, w_out, w_up, w_down, w_time, gain_one, bias_one, gain_two, bias_two, bias_up,
    bias_down, lengths, time_steps, cotangent,
):
    me = lax.axis_index("ctx")
    shard = lax.axis_index("fsdp")
    rows = tokens.shape[1]
    width = tokens.shape[2]
    count = rows * ctx_size
    head_size = width // HEADS
    repeats = ctx_size // HEADS
    columns = head_size // repeats
    seq_count = lengths.shape[1]
    hidden = w_up.shape[1]

    def gather_small(values):
        return lax.all_gather(values, "fsdp", axis=0, tiled=True)

    def fetch(weight):
        return [(gather_small(weight), 0)]

    def scatter_sum(values, dim):
        return lax.psum_scatter(
            values.astype(BF16), "fsdp", scatter_dimension=dim, tiled=True
        )

    def gather(values):
        return lax.all_gather(values, "ctx", axis=0, tiled=False)

    ends = []
    for s in range(seq_count):
        ends.append(lengths[0, s] + (ends[-1] if ends else 0))
    ends_vector = jnp.stack(ends)
    index = me * rows + jnp.arange(rows, dtype=jnp.int32)
    segment = segments(ends, index)
    live = (segment < seq_count).astype(F32)[:, None]
    all_index = jnp.arange(count, dtype=jnp.int32)
    all_position = positions(ends, all_index, segments(ends, all_index))
    half_width = head_size // 2
    inverse = jnp.exp(
        -math.log(10000.0) * jnp.arange(half_width, dtype=F32) / half_width
    )
    angle = inverse[:, None] * all_position.astype(F32)[None, :]
    cos = jnp.cos(angle)
    sin = jnp.sin(angle)

    all_tokens = gather(tokens[0]).reshape(count, width)
    inputs = tokens[0].astype(F32)
    grad_y = cotangent[0].astype(F32) * live
    grad_y_b = grad_y.astype(BF16)
    all_grad_y = gather(grad_y_b).reshape(count, width)

    small = [gain_one, bias_one, gain_two, bias_two, bias_down, bias_up]
    packed = gather_small(jnp.concatenate(small)[None, :])
    vectors = []
    at = 0
    for vector in small:
        size = vector.shape[0]
        vectors.append(packed[:, at : at + size].reshape(1, -1).astype(F32))
        at += size
    gain_first, bias_first, gain_second, bias_second, bias_output, bias_hidden = vectors

    all_steps = lax.all_gather(time_steps.astype(F32), "fsdp", axis=0, tiled=True)
    all_embedded = embed(all_steps, w_time.shape[0] * fsdp_size).astype(BF16)
    embedded = lax.dynamic_index_in_dim(all_embedded, shard, 0, keepdims=False)
    film = times_rows(embedded, fetch(w_time))
    film = jnp.concatenate([film, jnp.zeros((1, 2 * width), F32)], axis=0)
    gains = gain_first + film[:, :width]
    shifts = bias_first + film[:, width:]

    head = me // repeats
    w_head = jnp.concatenate(
        [
            lax.dynamic_slice_in_dim(w_qkv, k * width + head * head_size, head_size, 1)
            for k in range(3)
        ]
        + [jnp.zeros((w_qkv.shape[0], head_size), BF16)],
        axis=1,
    )
    w_head = gather_small(w_head)

    base = jnp.arange(ctx_size, dtype=jnp.int32) * rows
    all_norm, query_t, key, key_t, value_t, pair = project(
        all_tokens, base, ends_vector, gains, shifts, w_head, cos, sin, rows, head_size
    )
    place = jnp.arange(ctx_size, dtype=jnp.int32)
    out_t, sent, lse = attend(place, query_t, key, value_t, rows)

    part = (me % repeats) * columns
    if repeats > 1:
        sent = lax.dynamic_slice_in_dim(sent, part, columns, 1)
    attended_t = lax.all_to_all(sent, "ctx", 0, 0, tiled=True).reshape(width, rows)

    out_pieces = fetch(w_out)
    up_pieces = fetch(w_up)
    down_pieces = fetch(w_down)
    qkv_pieces = fetch(w_qkv)
    resid = inputs + times_rows_t(attended_t, out_pieces)
    normal_two, scale_two = stats(resid)
    norm_two_b = (normal_two * gain_second + bias_second).astype(BF16)
    all_norm_two = gather(norm_two_b).reshape(count, width)
    pre = times_rows(norm_two_b, up_pieces) + bias_hidden
    act, slope = gelu_parts(pre)
    branch = times_rows(act.astype(BF16), down_pieces) + bias_output
    output = (live * (resid + branch)).astype(BF16)
    grad_act = joined([dims(grad_y_b, p, 1, 1) for p, _ in down_pieces], down_pieces, 1)
    grad_pre = grad_act * slope
    grad_bias_up = jnp.sum(grad_pre, axis=0)
    grad_pre_b = grad_pre.astype(BF16)
    grad_norm_two = joined([dims(grad_pre_b, p, 1, 1) for p, _ in up_pieces], up_pieces, 1)
    grad_resid = grad_y + stats_back(grad_norm_two * gain_second, normal_two, scale_two)
    grad_resid_b = grad_resid.astype(BF16)
    grad_att_t = joined(
        [dims(p, grad_resid_b, 1, 1) for p, _ in out_pieces], out_pieces, 0
    ).astype(BF16)
    grad_att_t = grad_att_t.reshape(HEADS, head_size, rows)
    if repeats > 1:
        grad_att_t = jnp.repeat(grad_att_t, repeats, axis=0)
    grad_att = lax.all_to_all(grad_att_t, "ctx", 0, 0, tiled=True)

    mixed_t, _ = attend_back(
        place, query_t, grad_att, out_t, lse, key, key_t, pair, cos, sin, rows
    )
    mixed_t = mixed_t.reshape(3, head_size, count)
    if repeats > 1:
        mixed_t = lax.dynamic_slice_in_dim(mixed_t, part, columns, 1)
    mixed_t = mixed_t.reshape(3 * columns, count)
    mixed_sent = mixed_t.reshape(3 * columns, ctx_size, rows).transpose(1, 0, 2)
    mixed_got = lax.all_to_all(mixed_sent, "ctx", 0, 0, tiled=True)
    grad_mixed_t = (
        mixed_got.reshape(ctx_size, 3, columns, rows)
        .transpose(1, 0, 2, 3)
        .reshape(3 * width, rows)
    )
    grad_norm_one = joined(
        [dims(grad_mixed_t, p, 0, 1) for p, _ in qkv_pieces], qkv_pieces, 1
    )
    normal_one, scale_one = stats(inputs)
    seg_col = segment[:, None]
    gain_tok = gains[0:1]
    for s in range(1, seq_count + 1):
        gain_tok = jnp.where(seg_col == s, gains[s : s + 1], gain_tok)
    grad_tokens = (
        grad_resid + stats_back(grad_norm_one * gain_tok, normal_one, scale_one)
    ).astype(BF16)
    film_terms = jnp.concatenate([grad_norm_one * normal_one, grad_norm_one], axis=1)
    film_sums = [
        jnp.sum(jnp.where(seg_col == s, film_terms, 0.0), axis=0)
        for s in range(seq_count + 1)
    ]

    sums = [
        jnp.sum(grad_norm_two * normal_two, axis=0),
        jnp.sum(grad_norm_two, axis=0),
        jnp.sum(grad_y, axis=0),
        grad_bias_up,
    ] + film_sums
    sizes = [vector.shape[0] for vector in sums]
    total = lax.psum(jnp.concatenate(sums)[None, :], "ctx")
    total = lax.all_gather(total, "fsdp", axis=0, tiled=True)
    split = []
    at = 0
    for size in sizes:
        split.append(total[:, at : at + size])
        at += size

    def own(vector):
        size = vector.shape[0] // fsdp_size
        return lax.dynamic_slice_in_dim(vector, shard * size, size, 0)

    sum_gain_two, sum_bias_two, sum_bias_down, sum_bias_up = (
        own(jnp.sum(vector, axis=0)) for vector in split[:4]
    )
    film_all = jnp.sum(sum(split[4:]), axis=0)
    sum_gain_one = own(film_all[:width])
    sum_bias_one = own(film_all[width:])
    film_grad = jnp.stack(split[4 : 4 + seq_count], axis=1).reshape(-1, 2 * width)
    embedded_rows = lax.dynamic_slice_in_dim(
        all_embedded.astype(F32).reshape(film_grad.shape[0], -1),
        shard * w_time.shape[0],
        w_time.shape[0],
        1,
    )
    grad_time = sum(
        embedded_rows[g][:, None] * film_grad[g][None, :]
        for g in range(film_grad.shape[0])
    )

    slice_width = hidden // (ctx_size * fsdp_size)
    starts = [
        k * (hidden // fsdp_size) + me * slice_width for k in range(fsdp_size)
    ]
    w_up_cols = []
    for piece, _ in up_pieces:
        w_up_cols.append(
            jnp.concatenate(
                [
                    lax.dynamic_slice_in_dim(piece, start, slice_width, 1)
                    for start in starts
                ],
                axis=1,
            )
        )
    w_up_slice = joined(w_up_cols, up_pieces, 0)
    w_down_slice = jnp.concatenate(
        [rows_of(down_pieces, start, slice_width) for start in starts], axis=0
    )
    bias_slice = jnp.concatenate(
        [
            lax.dynamic_slice_in_dim(bias_hidden, start, slice_width, 1)
            for start in starts
        ],
        axis=1,
    )
    pre_slice = dims(all_norm_two, w_up_slice, 1, 0) + bias_slice
    act_slice, slope_slice = gelu_parts(pre_slice)
    grad_pre_slice = (dims(all_grad_y, w_down_slice, 1, 1) * slope_slice).astype(BF16)
    down_slice = dims(act_slice.astype(BF16), all_grad_y, 0, 0)
    up_slice = dims(all_norm_two, grad_pre_slice, 0, 0)
    grad_down = gather(scatter_sum(down_slice, 0)).reshape(-1, width).astype(F32)
    up_parts = gather(scatter_sum(up_slice, 0))
    grad_up = (
        up_parts.reshape(ctx_size, width // fsdp_size, fsdp_size, slice_width)
        .transpose(1, 2, 0, 3)
        .reshape(width // fsdp_size, hidden)
        .astype(F32)
    )
    out_part = jnp.dot(attended_t, grad_resid_b, preferred_element_type=F32)
    out_rows = lax.psum_scatter(
        out_part.astype(BF16), ("fsdp", "ctx"), scatter_dimension=0, tiled=True
    )
    grad_out = gather(out_rows).reshape(-1, width).astype(F32)
    qkv_slice = jnp.dot(mixed_t, all_norm, preferred_element_type=F32)
    qkv_parts = gather(scatter_sum(qkv_slice, 1))
    grad_qkv = (
        qkv_parts.reshape(ctx_size, 3, columns, width // fsdp_size)
        .transpose(3, 1, 0, 2)
        .reshape(width // fsdp_size, 3 * width)
        .astype(F32)
    )
    return (
        output[None],
        grad_tokens[None],
        grad_qkv,
        grad_out,
        grad_up,
        grad_down,
        grad_time,
        sum_gain_one,
        sum_bias_one,
        sum_gain_two,
        sum_bias_two,
        sum_bias_up,
        sum_bias_down,
    )


def ring_tables(ctx_size):
    chips = ctx_size // 2
    order = list(range(0, chips, 2)) + list(range(1, chips, 2))[::-1]
    offsets = [0]
    for step in range(1, chips // 2 + 1):
        offsets.append(-step)
        if step <= (chips - 1) // 2:
            offsets.append(step)
    place = np.zeros((ctx_size, ctx_size), np.int32)
    for me in range(ctx_size):
        at = order.index(me // 2)
        for k, offset in enumerate(offsets):
            chip = order[(at + offset) % chips]
            place[me, 2 * k] = 2 * chip + me % 2
            place[me, 2 * k + 1] = 2 * chip + 1 - me % 2
    return order, place


def fence(*values):
    return lax.optimization_barrier(values)


def after(values, *earlier):
    return lax.optimization_barrier((values, *earlier))[0]


def body(
    ctx_size, fsdp_size,
    tokens, w_qkv, w_out, w_up, w_down, w_time, gain_one, bias_one, gain_two, bias_two, bias_up,
    bias_down, lengths, time_steps, cotangent,
):
    me = lax.axis_index("ctx")
    shard = lax.axis_index("fsdp")
    core = me % 2
    rows = tokens.shape[1]
    width = tokens.shape[2]
    head_size = width // HEADS
    seq_count = lengths.shape[1]
    hidden = w_up.shape[1]
    other = 1 - shard
    chips = ctx_size // 2
    half = width // 2
    units = hidden // (ctx_size * fsdp_size)
    order, place_table = ring_tables(ctx_size)
    place = jnp.asarray(place_table)[me]
    who = jnp.stack([me, shard]).astype(jnp.int32)

    def across(values):
        return lax.ppermute(values, "fsdp", [(0, 1), (1, 0)])

    def gather(values):
        return lax.all_gather(values, "ctx", axis=0, tiled=True)

    def flip(values, bit=0):
        return lax.ppermute(
            values, "ctx", [(i, i ^ (1 << bit)) for i in range(ctx_size)]
        )

    def hop(values, step):
        return lax.ppermute(
            values,
            "ctx",
            [
                (2 * order[at] + c, 2 * order[(at + step) % chips] + c)
                for at in range(chips)
                for c in range(2)
            ],
        )

    def by_shard(mine, others, axis):
        first = jnp.where(shard == 0, mine, others)
        second = jnp.where(shard == 0, others, mine)
        return jnp.concatenate([first, second], axis=axis)

    def cut(values, start, size, axis):
        return lax.dynamic_slice_in_dim(values, start, size, axis)

    def halve(values, axis, mine, send):
        keep = lax.dynamic_index_in_dim(values, mine, axis, keepdims=False)
        give = lax.dynamic_index_in_dim(values, 1 - mine, axis, keepdims=False)
        return keep + send(give.astype(BF16)).astype(F32)

    ends = []
    for s in range(seq_count):
        ends.append(lengths[0, s] + (ends[-1] if ends else 0))
    ends_vector = jnp.stack(ends)
    base = place * rows
    index = me * rows + jnp.arange(rows, dtype=jnp.int32)
    segment = segments(ends, index)
    seg_col = segment[:, None]
    live = (segment < seq_count).astype(F32)[:, None]
    own_tokens = tokens[0]
    steps_row = time_steps.reshape(1, seq_count)
    high = (steps_row // 256).astype(BF16)
    low = (steps_row % 256).astype(BF16)
    head = core * chips + me // 2
    w_head = jnp.concatenate(
        [cut(w_qkv, k * width + head * head_size, head_size, 1) for k in range(3)], axis=1
    )
    class Ring:
        def __init__(self, values):
            self.right = self.left = values
            self.parts = [values]
            self.step = 0

        def go(self, *earlier):
            right, left = self.right, self.left
            if earlier:
                right, left = (
                    after(right, *earlier),
                    after(left, *earlier),
                )
            self.step += 1
            self.right = hop(right, 1)
            if self.step <= (chips - 1) // 2:
                self.left = hop(left, -1)
                return [self.right, self.left]
            return [self.right]

        def came(self, values):
            self.right = values[0]
            if len(values) > 1:
                self.left = values[1]
            self.parts += values

    def fenced(groups):
        flat = [v for group in groups for v in group]
        flat = list(fence(*flat))
        out = []
        for group in groups:
            out.append(flat[: len(group)])
            flat = flat[len(group) :]
        return out

    def with_flips(values):
        return [part for v in values for part in (v, flip(v))]

    tok = Ring(own_tokens)
    tok_new = tok.go()
    packed = jnp.concatenate([gain_one[None, :], bias_one[None, :], high, low], axis=1)
    tok_new, (packed, w_head) = fenced([tok_new, [packed, w_head]])
    tok.came(tok_new)

    tok_new = tok.go()
    packed_other = across(packed)
    w_head_other = across(w_head)
    me_1 = after(me, packed)
    place = jnp.asarray(place_table)[me_1]
    who = jnp.stack([me_1, shard]).astype(jnp.int32)
    base = place * rows
    all_index = (base[:, None] + jnp.arange(rows, dtype=jnp.int32)[None, :]).reshape(-1)
    all_position = positions(ends, all_index, segments(ends, all_index))
    half_width = head_size // 2
    inverse = jnp.exp(
        -math.log(10000.0) * jnp.arange(half_width, dtype=F32) / half_width
    )
    angle = inverse[:, None] * all_position.astype(F32)[None, :]
    cos = jnp.cos(angle)
    sin = jnp.sin(angle)

    inputs = own_tokens.astype(F32)
    grad_y = cotangent[0].astype(F32) * live
    grad_y_b = grad_y.astype(BF16)
    out_half = w_out.shape[0] // 2
    tok_new, (packed_other, w_head, cos, sin, grad_y_b, me_2, place, who, base, w_head_other) = fenced(
        [tok_new, [packed_other, w_head, cos, sin, grad_y_b, me, place, who, base, w_head_other]]
    )
    tok.came(tok_new)

    tok_new = tok.go()
    packed_all = by_shard(packed, packed_other, 0)

    def vector_of(values, at, size):
        return values[:, at : at + size].reshape(1, -1).astype(F32)

    gain_first = vector_of(packed_all, 0, half)
    bias_first = vector_of(packed_all, half, half)
    all_steps = packed_all[:, width : width + seq_count].astype(F32) * 256.0 + packed_all[
        :, width + seq_count :
    ].astype(F32)
    all_embedded = embed(all_steps, w_time.shape[0] * fsdp_size).astype(BF16)
    own_part = cut(all_embedded, shard * w_time.shape[0], w_time.shape[0], 2)
    film_part = jnp.dot(
        own_part.reshape(fsdp_size * seq_count, -1), w_time, preferred_element_type=F32
    ).reshape(fsdp_size, seq_count, 2 * width)
    film_other = across(lax.dynamic_index_in_dim(film_part, other, 0, keepdims=False))
    film = film_other + lax.dynamic_index_in_dim(film_part, shard, 0, keepdims=False)
    film = jnp.concatenate([film, jnp.zeros((1, 2 * width), F32)], axis=0)
    gains = gain_first + film[:, :width]
    shifts = bias_first + film[:, width:]
    up_parts = 2
    up_deep = w_up.shape[0] // up_parts
    quarter = hidden // 4
    up_send = [
        lax.dynamic_slice(w_up, (p * up_deep, (me_2 % 4) * quarter), (up_deep, quarter))
        for p in range(up_parts)
    ]
    tok_new, (gains, shifts), up_send = fenced([tok_new, [gains, shifts], up_send])
    tok_flips = with_flips(tok.parts)
    tok.came(tok_new)

    tok_last = tok.go()
    all_grad_y = gather(after(grad_y_b, gains))
    grad_y_other = across(grad_y_b)
    up_mine = [across(after(up_send[0], gains))]
    tok_flips += with_flips(tok_new)
    constants = (base, ends_vector, gains, shifts, w_head, w_head_other, cos, sin, head_size)
    head_values = project_chunks(who, tok_flips, *constants)
    head_values, tok_last, (grad_y_other, gain_two, up_send[1]) = fenced(
        [head_values, tok_last, [grad_y_other, gain_two, up_send[1]]]
    )

    up_mine.append(across(up_send[1]))
    far_send = dims(grad_y_other, w_down, 1, 1).astype(BF16)
    all_norm, query_t, key, key_t, value_t, pair = project_chunks(
        who, with_flips(tok_last), *constants, first=chips - 1, earlier=head_values
    )
    out_t, sent, lse = attend(place, query_t, key, value_t, rows)
    rest = jnp.concatenate(
        [v[None, :] for v in (gain_two, bias_two, bias_down, bias_up)], axis=1
    )
    out_t, sent, lse, *up_mine, rest, me_5, far_send = fence(
        out_t, sent, lse, *up_mine, rest, me, far_send
    )

    attended = lax.all_to_all(sent, "ctx", 0, 0, tiled=True)
    rest_other = across(rest)
    up_side = [flip(up_mine[0], 1), flip(up_mine[1], 1)]
    qkv_half = w_qkv.shape[0] // 2
    qkv_send = [
        cut(w_qkv, (me_5 % 2) * qkv_half + k * (qkv_half // 2), qkv_half // 2, 0)
        for k in range(2)
    ]
    out_mine = across(cut(w_out, (me_5 % 2) * out_half, out_half, 0))
    far_grad = across(far_send)
    near_grad = dims(after(grad_y_b, lse), w_down, 1, 1)
    pieces = [with_flips([v]) for v in up_mine]
    rest_5 = [out_mine, rest_other, me_5, qkv_send[1], qkv_send[0]]
    (attended, up_side[0], near_grad), rest_5, *pieces = fenced(
        [[attended, up_side[0], near_grad], rest_5, *pieces]
    )
    out_mine, rest_other, me_6, qkv_send[1], qkv_send[0] = rest_5

    rest = by_shard(rest, rest_other, 0)
    gain_second = vector_of(rest, 0, half)
    bias_second = vector_of(rest, half, half)
    bias_output = vector_of(rest, width, half)
    bias_hidden = vector_of(rest, width + half, hidden // 2)
    out_pieces = (w_out, out_mine, flip(out_mine))
    resid, normal_two, scale_two, norm_two_b = middle(
        who, attended, out_pieces, own_tokens, gain_second, bias_second
    )
    first_units = shard * (hidden // 2) + me_6 * units
    second_units = other * (hidden // 2) + me_6 * units
    up_first = cut(w_up, first_units, units, 1)
    up_second = cut(w_up, second_units, units, 1)
    up_own = jnp.concatenate([up_first, up_second], axis=1)
    down_own = cut(w_down, me_6 * units, units, 0)
    up_give = jnp.concatenate([up_second, up_first], axis=1)
    pieces[0] = pieces[0] + with_flips([up_side[0]])
    rest_6 = [up_own, up_give, down_own]
    (norm_two_b, far_grad, up_side[1]), rest_6, *pieces = fenced(
        [[norm_two_b, far_grad, up_side[1]], rest_6, *pieces]
    )
    up_own, up_give, down_own = rest_6
    pieces = pieces[0] + pieces[1] + with_flips([up_side[1]])

    all_norm_two = gather(norm_two_b)
    up_other = across(after(up_give, norm_two_b))
    down_other = across(after(down_own, norm_two_b))
    act_b, grad_resid, grad_resid_b, grad_att, sums = feed(
        who, norm_two_b, w_up, pieces, near_grad, far_grad, bias_hidden, normal_two, scale_two,
        gain_second, grad_y_b, out_pieces,
    )
    grad_att, grad_resid_b, me_8, up_other, down_other = fence(
        grad_att, grad_resid_b, me, up_other, down_other
    )

    grad_att = grad_att.reshape(HEADS, head_size, rows)
    grad_att = lax.all_to_all(grad_att, "ctx", 0, 0, tiled=True)
    qkv_mine = [across(after(qkv_send[0], up_other, down_other))]
    deep = width // (ctx_size * fsdp_size)
    by_core = attended.reshape(chips, fsdp_size, 2, deep, rows)

    def out_rows_of(which):
        some = lax.dynamic_index_in_dim(by_core, which, 2, keepdims=False)
        return jnp.dot(
            some.reshape(half, rows), grad_resid_b, preferred_element_type=F32
        )

    out_part = out_rows_of(core) + flip(out_rows_of(1 - core).astype(BF16)).astype(F32)
    out_part = out_part.reshape(chips, fsdp_size, deep, width)
    down_half = w_down.shape[0] // 2
    down_send = cut(w_down, (me_8 % 2) * down_half, down_half, 0)
    grad_att, down_send, out_part = fence(grad_att, down_send, out_part)

    out_part = halve(out_part, 1, shard, across)
    qkv_mine.append(across(after(qkv_send[1], out_part)))
    mixed, mixed_sent = attend_back(
        place, query_t, grad_att, out_t, lse, key, key_t, pair, cos, sin, rows
    )
    mixed, mixed_sent, out_part, qkv_mine[0] = fence(
        mixed, mixed_sent, out_part, qkv_mine[0]
    )

    mixed_got = lax.all_to_all(mixed_sent, "ctx", 0, 0, tiled=True)
    qkv_slice = jnp.dot(mixed, all_norm, preferred_element_type=F32)
    qkv_keep = cut(qkv_slice, shard * half, half, 1)
    qkv_give = cut(qkv_slice, other * half, half, 1).astype(BF16)
    bias_slice = jnp.concatenate(
        [cut(bias_hidden, at, units, 1) for at in (first_units, second_units)], axis=1
    )
    qkv_other = across(qkv_give)
    out_part = halve(
        out_part.reshape(-1, 2, deep, width), 1, (me >> 1) % 2, lambda v: flip(v, 1)
    )
    qkv_sum = (qkv_keep + qkv_other.astype(F32)).astype(BF16)
    qkv_sum, bias_slice, all_norm_two, all_grad_y, out_part = fence(
        qkv_sum, bias_slice, all_norm_two, all_grad_y, out_part
    )

    all_qkv = gather(qkv_sum)
    out_part = halve(
        out_part.reshape(-1, 2, deep, width), 1, (me >> 2) % 2, lambda v: flip(v, 2)
    )
    wide_keep, wide_give = slices(
        who, all_norm_two, all_grad_y, up_own, up_other, down_own, down_other, bias_slice
    )
    wide_keep, wide_give, mixed_got, out_part = fence(
        wide_keep, wide_give, mixed_got, out_part
    )

    wide_other = across(wide_give)
    qkv_mine = fence(*qkv_mine, wide_give)[:-1]
    qkv_pieces = (w_qkv, *qkv_mine, *[flip(v) for v in qkv_mine])
    grad_tokens, total = first_back(
        who, ends_vector, mixed_got, qkv_pieces, own_tokens, grad_resid, gains, sums
    )
    total_other = across(total)
    out_part = halve(
        out_part.reshape(-1, 2, deep, width), 1, (me >> 3) % 2, lambda v: flip(v, 3)
    )
    wide_other, total, total_other, out_part = fence(
        wide_other, total, total_other, out_part
    )

    total = jnp.concatenate(
        [total[:8] + total_other[:8], total[8:], total_other[8:]], axis=0
    )
    total = jnp.pad(total, ((0, -total.shape[0] % 16), (0, 0))).astype(BF16)
    lines = total.shape[0]

    def narrow(values):
        return [values[:, k * 128 : (k + 1) * 128] for k in range(width // 128)]

    wide = jnp.concatenate(
        [(wide_keep + wide_other.astype(F32)).astype(BF16)]
        + narrow(out_part.reshape(deep, width).astype(BF16))
        + narrow(total),
        axis=0,
    )
    wide_ring = Ring(wide)
    wide_new = wide_ring.go()
    down_mine = across(after(down_send, wide))
    wide_new = list(fence(*wide_new))
    wide_flips = with_flips(wide_ring.parts)
    wide_ring.came(wide_new)

    wide_flips += with_flips(wide_new)
    wide_new = wide_ring.go()
    grads = expand_wide(place, 0, wide_flips, width, ())
    own_embed = lax.dynamic_index_in_dim(own_part, shard, 0, keepdims=False)
    other_embed = lax.dynamic_index_in_dim(own_part, other, 0, keepdims=False)
    own_embed = own_embed.astype(F32)
    other_embed = other_embed.astype(F32)
    wide_new, grads, (down_mine, own_embed, other_embed, all_qkv) = fenced(
        [wide_new, grads, [down_mine, own_embed, other_embed, all_qkv]]
    )
    wide_ring.came(wide_new)

    more_flips = with_flips(wide_new)
    wide_new = wide_ring.go()
    grad_qkv = expand_last(all_qkv.reshape(ctx_size, 3 * head_size, half), head_size)
    down_flip = flip(down_mine)
    branch = bias_output
    for b, row in (
        (w_down, shard * (hidden // 2)),
        (down_mine, other * (hidden // 2) + core * down_half),
        (down_flip, other * (hidden // 2) + (1 - core) * down_half),
    ):
        branch = branch + jnp.dot(
            cut(act_b, row, b.shape[0], 1), b, preferred_element_type=F32
        )
    output = (live * (resid + branch)).astype(BF16)
    wide_new, (output, grad_qkv), more_flips = fenced(
        [wide_new, [output, grad_qkv], more_flips]
    )

    tall = wide.shape[0] // 2
    last_top = hop(wide_new[0][:tall], 1)
    last_low = hop(wide_new[1][tall:], -1)
    more_flips += with_flips(wide_new)
    grads = expand_wide(place, len(wide_flips) // 2, more_flips, width, grads)
    grads, (last_top, last_low) = fenced([grads, [last_top, last_low]])

    wide_last = with_flips([jnp.concatenate([last_top, last_low], axis=0)])
    grad_up, grad_down, grad_out = expand_wide(
        place, chips - 1, wide_last, width, grads
    )
    grad_time, *vectors = small_sums(
        who, own_embed, other_embed, wide_flips + more_flips + wide_last,
        wide.shape[0] - lines * width // 128, lines, width,
    )
    return (
        output[None],
        grad_tokens[None],
        grad_qkv,
        grad_out,
        grad_up,
        grad_down,
        grad_time,
        *[vector.reshape(-1) for vector in vectors],
    )


def solution(mesh):
    in_specs = (
        (P("fsdp", "ctx", None),)
        + (P("fsdp", None),) * 5
        + (P("fsdp"),) * 6
        + (P("fsdp", None), P("fsdp", None), P("fsdp", "ctx", None))
    )
    out_specs = (
        (P("fsdp", "ctx", None),) * 2 + (P("fsdp", None),) * 5 + (P("fsdp"),) * 6
    )
    ctx_size, fsdp_size = mesh.shape["ctx"], mesh.shape["fsdp"]
    paired = ctx_size == HEADS and fsdp_size == 2
    return jax.shard_map(
        functools.partial(body if paired else body_general, ctx_size, fsdp_size),
        mesh=mesh,
        in_specs=in_specs,
        out_specs=out_specs,
        check_vma=False,
    )
```

```python
import functools
import math

import jax
import jax.numpy as jnp
import numpy as np
from jax import lax
from jax.experimental import pallas as pl
from jax.experimental.pallas import tpu as pltpu
from jax.sharding import PartitionSpec as P

HEADS = 16
EPSILON = 1e-05
NEGATIVE = -1e30
HIGH = lax.Precision.HIGHEST
F32 = jnp.float32
BF16 = jnp.bfloat16
VMEM_BYTES = 56 << 20


def dims(left, right, left_dim, right_dim):
    return lax.dot_general(
        left, right, (((left_dim,), (right_dim,)), ((), ())), preferred_element_type=F32
    )


def segments(ends, index):
    return sum((index >= end).astype(jnp.int32) for end in ends)


def positions(ends, index, segment):
    begin = jnp.zeros_like(index)
    for at, end in enumerate(ends):
        begin = jnp.where(segment > at, end, begin)
    return index - begin


def embed(steps_given, embed_width):
    half_width = embed_width // 2
    freq = jnp.exp(-math.log(10000.0) * jnp.arange(half_width, dtype=F32) / half_width)
    angle = steps_given.astype(F32)[..., None] * freq
    return jnp.concatenate([jnp.sin(angle), jnp.cos(angle)], axis=-1)


def stats(values):
    centre = jnp.mean(values, axis=-1, keepdims=True)
    centered = values - centre
    spread = jnp.mean(centered * centered, axis=-1, keepdims=True)
    scale = lax.rsqrt(spread + EPSILON)
    return centered * scale, scale


def stats_back(grad, normal, scale):
    return (
        grad
        - jnp.mean(grad, axis=-1, keepdims=True)
        - normal * jnp.mean(grad * normal, axis=-1, keepdims=True)
    ) * scale


def gelu_parts(pre):
    below = 0.5 * (1.0 + lax.erf(pre * math.sqrt(0.5)))
    density = jnp.exp(-0.5 * pre * pre) * (1.0 / math.sqrt(2.0 * math.pi))
    return pre * below, below + pre * density


def qkv_kernel(
    rows, head_size, first, ends_ref, base_ref, tokens_ref, gains_ref, shifts_ref, w_ref,
    cos_ref, sin_ref, *refs,
):
    norm_ref, query_t_ref, key_ref, key_t_ref, value_t_ref, pair_ref = refs[-6:]
    step = pl.program_id(0) + first
    block = tokens_ref.shape[0]
    seq_count = ends_ref.shape[0]
    half = head_size // 2
    values = tokens_ref[...].astype(F32)
    normal, _ = stats(values)
    chunks = block // rows

    def token_index(shape, axis):
        within = lax.broadcasted_iota(jnp.int32, shape, axis)
        index = within + base_ref[step * chunks]
        for at in range(1, chunks):
            index = jnp.where(
                within >= at * rows,
                within - at * rows + base_ref[step * chunks + at],
                index,
            )
        return index

    ends = [ends_ref[s] for s in range(seq_count)]
    seg_col = segments(ends, token_index((block, 1), 0))
    seg_row = segments(ends, token_index((1, block), 1))
    gains = gains_ref[0:1, :]
    shifts = shifts_ref[0:1, :]
    for s in range(1, seq_count + 1):
        gains = jnp.where(seg_col == s, gains_ref[s : s + 1, :], gains)
        shifts = jnp.where(seg_col == s, shifts_ref[s : s + 1, :], shifts)
    norm = (normal * gains + shifts).astype(BF16)
    norm_ref[...] = norm
    mixed = jnp.dot(norm, w_ref[...], preferred_element_type=F32)
    turned = mixed.T
    cos = cos_ref[...]
    sin = sin_ref[...]

    def turn(at):
        upper = turned[at : at + half]
        lower = turned[at + half : at + head_size]
        return jnp.concatenate(
            [upper * cos - lower * sin, lower * cos + upper * sin], axis=0
        ).astype(BF16)

    query = turn(0).astype(F32) * (float(head_size) ** -0.5)
    key = turn(head_size).astype(F32)
    value = turned[2 * head_size : 3 * head_size].astype(BF16).astype(F32)
    spare = 128 - head_size
    row_id = lax.broadcasted_iota(jnp.int32, (spare, block), 0)
    same = row_id == seg_row
    used = row_id <= seq_count
    key_tail = jnp.where((same & used) | ((row_id >= 8) & (row_id < 11)), 1.0, 0.0)
    query_tail = jnp.where(used & jnp.logical_not(same), NEGATIVE, 0.0)
    query_t_ref[...] = jnp.concatenate([query, query_tail], axis=0).astype(BF16)
    key_t_ref[...] = key.astype(BF16)
    value_t_ref[...] = value.astype(BF16)
    key_ref[...] = jnp.concatenate([key, key_tail], axis=0).T.astype(BF16)
    pair_ref[...] = jnp.concatenate([value, query], axis=0).T.astype(BF16)


def attend_kernel(
    chunk, rows, place_ref, query_ref, key_ref, value_ref, out_ref, sent_ref, lse_ref, score_ref, top_ref,
):
    core = place_ref[0] % 2
    count = key_ref.shape[0]
    step = pl.program_id(0)
    now = step % 2
    before = 1 - now
    query = query_ref[...]
    last_top = top_ref[before]
    top = None
    total = jnp.zeros_like(last_top)
    out = jnp.zeros(out_ref.shape, F32)
    for at in range(0, count, chunk):
        part = slice(at, at + chunk)
        score = jnp.dot(key_ref[part, :], query, preferred_element_type=F32)
        weight = jnp.exp(score_ref[before, part, :] - last_top)
        score_ref[now, part, :] = score
        high = jnp.max(score, axis=0, keepdims=True)
        top = high if top is None else jnp.maximum(top, high)
        total = total + jnp.sum(weight, axis=0, keepdims=True)
        out = out + jnp.dot(
            value_ref[:, part], weight.astype(BF16), preferred_element_type=F32
        )
    top_ref[now] = top

    @pl.when(step > 0)
    def _():
        result = out / total
        out_ref[...] = result
        for at in range(sent_ref.shape[0]):
            sent_ref[at ^ core] = result[:, at * rows : (at + 1) * rows].astype(BF16)
        lse_ref[...] = last_top + jnp.log(total)


def attend_back_kernel(
    chunk, rows, head_size, place_ref, query_ref, grad_ref, out_ref, lse_ref, key_ref, key_t_ref, pair_ref,
    pair_block_ref, cos_block_ref, sin_block_ref, cos_ref, sin_ref, mixed_ref, sent_ref, acc_ref,
):
    step = pl.program_id(0)
    core = place_ref[0] % 2
    per_step = grad_ref.shape[0]
    count = key_ref.shape[0]
    block = query_ref.shape[1]
    half = head_size // 2
    scale = float(head_size) ** -0.5

    @pl.when(step == 0)
    def _():
        acc_ref[...] = jnp.zeros_like(acc_ref)

    rest = -lse_ref[...]
    query = query_ref[...].astype(F32)
    row_id = lax.broadcasted_iota(jnp.int32, query.shape, 0)
    for k in range(3):
        piece = rest.astype(BF16).astype(F32)
        query = jnp.where(row_id == head_size + 8 + k, piece, query)
        rest = rest - piece
    query = query.astype(BF16)
    grad = jnp.concatenate(
        [grad_ref[at ^ core] for at in range(per_step)], axis=1
    ).astype(F32)
    delta = jnp.sum(grad * out_ref[...], axis=0, keepdims=True)
    grad_t = jnp.concatenate([grad, jnp.zeros((128 - head_size, block), F32)], axis=0)
    pair = pair_block_ref[...]
    lane = lax.broadcasted_iota(jnp.int32, pair.shape, 1)
    queries = jnp.where(lane >= head_size, pair.astype(F32), 0.0).astype(BF16)
    both = jnp.concatenate([queries, grad_t.T.astype(BF16)], axis=0)
    grad_t = grad_t.astype(BF16)
    grad_query = jnp.zeros((head_size, block), F32)
    for at in range(0, count, chunk):
        part = slice(at, at + chunk)
        score = jnp.dot(key_ref[part, :], query, preferred_element_type=F32)
        prob = jnp.exp(score)
        grad_prob = jnp.dot(pair_ref[part, :], grad_t, preferred_element_type=F32)
        grad_score = (prob * (grad_prob - delta)).astype(BF16)
        grad_query = grad_query + jnp.dot(
            key_t_ref[:, part], grad_score, preferred_element_type=F32
        )
        acc_ref[part, :] += jnp.dot(
            jnp.concatenate([grad_score, prob.astype(BF16)], axis=1),
            both,
            preferred_element_type=F32,
        )

    def turn_back(values, cos, sin):
        upper = values[:half]
        lower = values[half:]
        return jnp.concatenate(
            [upper * cos + lower * sin, lower * cos - upper * sin], axis=0
        ).astype(BF16)

    at = pl.multiple_of(step * block, block)
    query_part = turn_back(
        grad_query * scale, cos_block_ref[...], sin_block_ref[...]
    )
    mixed_ref[0:head_size, pl.ds(at, block)] = query_part
    for k in range(per_step):
        sent_ref[place_ref[step * per_step + k], 0:head_size, :] = query_part[
            :, k * rows : (k + 1) * rows
        ]

    @pl.when(step == pl.num_programs(0) - 1)
    def _():
        acc = acc_ref[...].T
        key_part = turn_back(acc[head_size : 2 * head_size], cos_ref[...], sin_ref[...])
        value_part = acc[:head_size].astype(BF16)
        parts = jnp.concatenate([key_part, value_part], axis=0)
        mixed_ref[head_size : 3 * head_size, :] = parts
        for k in range(count // rows):
            sent_ref[place_ref[k], head_size : 3 * head_size, :] = parts[
                :, k * rows : (k + 1) * rows
            ]


def whole(shape):
    return pl.BlockSpec(shape, lambda i, *_: (0,) * len(shape))


def project(
    tokens, base, ends, gains, shifts, w_head, cos, sin, rows, head_size, first=0, earlier=None,
):
    width = tokens.shape[1]
    count = base.shape[0] * rows
    block = min(count, 2 * rows)
    earlier = list(earlier or ())
    grid_spec = pltpu.PrefetchScalarGridSpec(
        num_scalar_prefetch=2,
        grid=(tokens.shape[0] // block,),
        in_specs=[
            pl.BlockSpec((block, width), lambda i, *_: (i, 0)),
            whole(gains.shape),
            whole(shifts.shape),
            whole(w_head.shape),
            pl.BlockSpec((head_size // 2, block), lambda i, *_: (0, i + first)),
            pl.BlockSpec((head_size // 2, block), lambda i, *_: (0, i + first)),
        ]
        + [pl.BlockSpec(memory_space=pl.ANY)] * len(earlier),
        out_specs=[
            pl.BlockSpec((block, width), lambda i, *_: (i + first, 0)),
            pl.BlockSpec((128, block), lambda i, *_: (0, i + first)),
            pl.BlockSpec((block, 128), lambda i, *_: (i + first, 0)),
            pl.BlockSpec((head_size, block), lambda i, *_: (0, i + first)),
            pl.BlockSpec((head_size, block), lambda i, *_: (0, i + first)),
            pl.BlockSpec((block, 128), lambda i, *_: (i + first, 0)),
        ],
    )
    return pl.pallas_call(
        functools.partial(qkv_kernel, rows, head_size, first),
        grid_spec=grid_spec,
        out_shape=[
            jax.ShapeDtypeStruct((count, width), BF16),
            jax.ShapeDtypeStruct((128, count), BF16),
            jax.ShapeDtypeStruct((count, 128), BF16),
            jax.ShapeDtypeStruct((head_size, count), BF16),
            jax.ShapeDtypeStruct((head_size, count), BF16),
            jax.ShapeDtypeStruct((count, 128), BF16),
        ],
        input_output_aliases={8 + k: k for k in range(len(earlier))},
        compiler_params=pltpu.CompilerParams(vmem_limit_bytes=VMEM_BYTES),
        cost_estimate=pl.CostEstimate(
            flops=2 * tokens.shape[0] * width * 1024,
            bytes_accessed=4 * tokens.shape[0] * width,
            transcendentals=0,
        ),
        name="project_head",
    )(ends, base, tokens, gains, shifts, w_head, cos, sin, *earlier)


def project_chunks_kernel(rows, head_size, first, chunks, who_ref, ends_ref, base_ref, *refs):
    tokens = refs[:chunks]
    gains_ref, shifts_ref, own_ref, other_ref, cos_ref, sin_ref = refs[chunks : chunks + 6]
    block_ref, w_ref = refs[-2:]
    step = pl.program_id(0)
    size = own_ref.shape[0]

    @pl.when(step == 0)
    def _():
        w_ref[:, 128:] = jnp.zeros((2 * size, 128), BF16)
        shard = who_ref[1]
        own_at = pl.multiple_of(shard * size, size)
        other_at = pl.multiple_of((1 - shard) * size, size)
        width = own_ref.shape[1]
        w_ref[pl.ds(own_at, size), :width] = own_ref[...]
        w_ref[pl.ds(other_at, size), :width] = other_ref[...]

    for at in range(chunks // 2):

        @pl.when(step == at)
        def _():
            block_ref[:rows] = tokens[2 * at][...]
            block_ref[rows:] = tokens[2 * at + 1][...]

    qkv_kernel(
        rows, head_size, first, ends_ref, base_ref, block_ref, gains_ref, shifts_ref, w_ref,
        cos_ref, sin_ref, *refs[-8:-2],
    )


def project_chunks(
    who, tokens, base, ends, gains, shifts, w_own, w_other, cos, sin, head_size, first=0, earlier=None,
):
    rows, width = tokens[0].shape
    count = base.shape[0] * rows
    block = 2 * rows
    earlier = list(earlier or ())
    grid_spec = pltpu.PrefetchScalarGridSpec(
        num_scalar_prefetch=3,
        grid=(len(tokens) // 2,),
        in_specs=[whole((rows, width))] * len(tokens)
        + [
            whole(gains.shape),
            whole(shifts.shape),
            whole(w_own.shape),
            whole(w_other.shape),
            pl.BlockSpec((head_size // 2, block), lambda i, *_: (0, i + first)),
            pl.BlockSpec((head_size // 2, block), lambda i, *_: (0, i + first)),
        ]
        + [pl.BlockSpec(memory_space=pl.ANY)] * len(earlier),
        out_specs=[
            pl.BlockSpec((block, width), lambda i, *_: (i + first, 0)),
            pl.BlockSpec((128, block), lambda i, *_: (0, i + first)),
            pl.BlockSpec((block, 128), lambda i, *_: (i + first, 0)),
            pl.BlockSpec((head_size, block), lambda i, *_: (0, i + first)),
            pl.BlockSpec((head_size, block), lambda i, *_: (0, i + first)),
            pl.BlockSpec((block, 128), lambda i, *_: (i + first, 0)),
        ],
        scratch_shapes=[
            pltpu.VMEM((block, width), BF16),
            pltpu.VMEM((width, 256), BF16),
        ],
    )
    return pl.pallas_call(
        functools.partial(project_chunks_kernel, rows, head_size, first, len(tokens)),
        grid_spec=grid_spec,
        out_shape=[
            jax.ShapeDtypeStruct((count, width), BF16),
            jax.ShapeDtypeStruct((128, count), BF16),
            jax.ShapeDtypeStruct((count, 128), BF16),
            jax.ShapeDtypeStruct((head_size, count), BF16),
            jax.ShapeDtypeStruct((head_size, count), BF16),
            jax.ShapeDtypeStruct((count, 128), BF16),
        ],
        input_output_aliases={9 + len(tokens) + k: k for k in range(len(earlier))},
        compiler_params=pltpu.CompilerParams(vmem_limit_bytes=VMEM_BYTES),
        cost_estimate=pl.CostEstimate(
            flops=2 * len(tokens) * rows * width * 1024,
            bytes_accessed=4 * len(tokens) * rows * width,
            transcendentals=0,
        ),
        name="project_chunks",
    )(who, ends, base, *tokens, gains, shifts, w_own, w_other, cos, sin, *earlier)


def attend(place, query_t, key, value_t, rows):
    count = key.shape[0]
    head_size = value_t.shape[0]
    block = min(count, 2 * rows)
    chunk = min(count, 1024)
    blocks = count // block

    def before(i):
        return jnp.maximum(i - 1, 0)

    grid_spec = pltpu.PrefetchScalarGridSpec(
        num_scalar_prefetch=1,
        grid=(blocks + 1,),
        in_specs=[
            pl.BlockSpec((128, block), lambda i, _: (0, jnp.minimum(i, blocks - 1))),
            whole((count, 128)),
            whole((head_size, count)),
        ],
        out_specs=[
            pl.BlockSpec((head_size, block), lambda i, _: (0, before(i))),
            pl.BlockSpec(
                (2, head_size, rows), lambda i, place: (place[2 * before(i)] // 2, 0, 0)
            ),
            pl.BlockSpec((1, block), lambda i, _: (0, before(i))),
        ],
        scratch_shapes=[
            pltpu.VMEM((2, count, block), F32),
            pltpu.VMEM((2, 1, block), F32),
        ],
    )
    return pl.pallas_call(
        functools.partial(attend_kernel, chunk, rows),
        grid_spec=grid_spec,
        out_shape=[
            jax.ShapeDtypeStruct((head_size, count), F32),
            jax.ShapeDtypeStruct((count // rows, head_size, rows), BF16),
            jax.ShapeDtypeStruct((1, count), F32),
        ],
        compiler_params=pltpu.CompilerParams(vmem_limit_bytes=VMEM_BYTES),
        cost_estimate=pl.CostEstimate(
            flops=8 * count * count * 128,
            bytes_accessed=8 * count * 128,
            transcendentals=count * count,
        ),
        name="attend_head",
    )(place, query_t, key, value_t)


def attend_back(place, query_t, grad, out, lse, key, key_t, pair, cos, sin, rows):
    count = key.shape[0]
    head_size = key_t.shape[0]
    half = head_size // 2
    block = min(count, 2 * rows)
    chunk = min(count, 1024)
    grid_spec = pltpu.PrefetchScalarGridSpec(
        num_scalar_prefetch=1,
        grid=(count // block,),
        in_specs=[
            pl.BlockSpec((128, block), lambda i, _: (0, i)),
            pl.BlockSpec(
                (2, head_size, rows), lambda i, place: (place[2 * i] // 2, 0, 0)
            ),
            pl.BlockSpec((head_size, block), lambda i, _: (0, i)),
            pl.BlockSpec((1, block), lambda i, _: (0, i)),
            whole((count, 128)),
            whole((head_size, count)),
            whole((count, 128)),
            pl.BlockSpec((block, 128), lambda i, _: (i, 0)),
            pl.BlockSpec((half, block), lambda i, _: (0, i)),
            pl.BlockSpec((half, block), lambda i, _: (0, i)),
            whole((half, count)),
            whole((half, count)),
        ],
        out_specs=[
            whole((3 * head_size, count)),
            whole((count // rows, 3 * head_size, rows)),
        ],
        scratch_shapes=[pltpu.VMEM((count, 128), F32)],
    )
    return pl.pallas_call(
        functools.partial(attend_back_kernel, chunk, rows, head_size),
        grid_spec=grid_spec,
        out_shape=[
            jax.ShapeDtypeStruct((3 * head_size, count), BF16),
            jax.ShapeDtypeStruct((count // rows, 3 * head_size, rows), BF16),
        ],
        compiler_params=pltpu.CompilerParams(vmem_limit_bytes=VMEM_BYTES),
        cost_estimate=pl.CostEstimate(
            flops=20 * count * count * 128,
            bytes_accessed=16 * count * 128,
            transcendentals=count * count,
        ),
        name="attend_head_back",
    )(place, query_t, grad, out, lse, key, key_t, pair, pair, cos, sin, cos, sin)


def slices_kernel(
    who_ref, norm_ref, grad_ref, up_own, up_other, down_own, down_other, bias_ref, keep_ref,
    give_ref, down_w, down_acc, up_acc, up_t,
):
    step = pl.program_id(0)
    shard = who_ref[1]
    size, units = up_own.shape
    width = 2 * size
    half = units // 2
    own_at = pl.multiple_of(shard * size, size)
    other_at = pl.multiple_of((1 - shard) * size, size)

    @pl.when(step == 0)
    def _():
        down_w[:half] = down_own[...]
        down_w[half:] = down_other[...]
        down_acc[...] = jnp.zeros_like(down_acc)
        up_acc[...] = jnp.zeros_like(up_acc)

    pre = jnp.dot(
        norm_ref[:, pl.ds(own_at, size)], up_own[...], preferred_element_type=F32
    )
    pre = pre + jnp.dot(
        norm_ref[:, pl.ds(other_at, size)], up_other[...], preferred_element_type=F32
    )
    act, slope = gelu_parts(pre + bias_ref[...])
    grad_y = grad_ref[...]
    grad = dims(grad_y, down_w[...], 1, 1) * slope
    down_acc[...] += jnp.dot(act.T.astype(BF16), grad_y, preferred_element_type=F32)
    up_acc[...] += jnp.dot(
        grad.T.astype(BF16), norm_ref[...], preferred_element_type=F32
    )

    @pl.when(step == pl.num_programs(0) - 1)
    def _():
        up_t[...] = up_acc[...].T
        for at, (rows, out_ref) in enumerate(((own_at, keep_ref), (other_at, give_ref))):
            values = up_t[pl.ds(rows, size), :].astype(out_ref.dtype)
            out_ref[pl.ds(own_at, size), :] = values[:, :half]
            out_ref[pl.ds(other_at, size), :] = values[:, half:]
            for k in range(width // half):
                out_ref[width + k * half : width + (k + 1) * half, :] = down_acc[
                    at * half : (at + 1) * half, k * half : (k + 1) * half
                ].astype(out_ref.dtype)


def slices(
    who, norm, grad_y, up_own, up_other, down_own, down_other, bias,
):
    count, width = norm.shape
    size, units = up_own.shape
    block = 256
    tall = 2 * width
    token = pl.BlockSpec((block, width), lambda i: (i, 0))
    return pl.pallas_call(
        slices_kernel,
        grid=(count // block,),
        in_specs=[pl.BlockSpec(memory_space=pltpu.SMEM), token, token]
        + [
            pl.BlockSpec(v.shape, lambda i: (0, 0))
            for v in (up_own, up_other, down_own, down_other, bias)
        ],
        out_specs=[pl.BlockSpec((tall, units // 2), lambda i: (0, 0))] * 2,
        out_shape=[
            jax.ShapeDtypeStruct((tall, units // 2), F32),
            jax.ShapeDtypeStruct((tall, units // 2), BF16),
        ],
        scratch_shapes=[
            pltpu.VMEM((units, width), BF16),
            pltpu.VMEM((units, width), F32),
            pltpu.VMEM((units, width), F32),
            pltpu.VMEM((width, units), F32),
        ],
        compiler_params=pltpu.CompilerParams(vmem_limit_bytes=VMEM_BYTES),
        cost_estimate=pl.CostEstimate(
            flops=8 * count * width * units,
            bytes_accessed=6 * count * width,
            transcendentals=2 * count * units,
        ),
        name="weight_slices",
    )(
        who, norm, grad_y, up_own, up_other, down_own, down_other, bias
    )


def head_of(device, devices):
    return device % 2 * (devices // 2) + device // 2


def row_starts(who_ref, size):
    core = who_ref[0] % 2
    shard = who_ref[1]
    half = size // 2
    other = (1 - shard) * size
    return (
        pl.multiple_of(shard * size, size),
        pl.multiple_of(other + core * half, half),
        pl.multiple_of(other + (1 - core) * half, half),
    )


def middle_kernel(
    who_ref, att_ref, own_ref, mine_ref, flip_ref, tokens_ref, gain_ref, bias_ref,
    resid_ref, normal_ref, scale_ref, norm_ref, turned,
):
    devices, head_size, _ = att_ref.shape
    for d in range(devices):
        at = head_of(d, devices) * head_size
        turned[:, at : at + head_size] = att_ref[d].astype(F32).T.astype(BF16)
    resid = tokens_ref[...].astype(F32)
    pieces = (own_ref, mine_ref, flip_ref)
    for at, piece in zip(row_starts(who_ref, own_ref.shape[0]), pieces):
        resid = resid + jnp.dot(
            turned[:, pl.ds(at, piece.shape[0])],
            piece[...],
            preferred_element_type=F32,
        )
    resid_ref[...] = resid
    normal, scale = stats(resid)
    normal_ref[...] = normal
    scale_ref[...] = scale
    norm_ref[...] = (normal * gain_ref[...] + bias_ref[...]).astype(BF16)


def middle(who, attended, pieces, tokens, gain, bias):
    rows, width = tokens.shape
    vmem = pl.BlockSpec(memory_space=pltpu.VMEM)
    return pl.pallas_call(
        middle_kernel,
        in_specs=[pl.BlockSpec(memory_space=pltpu.SMEM)] + [vmem] * 7,
        out_specs=[vmem] * 4,
        out_shape=[
            jax.ShapeDtypeStruct((rows, width), F32),
            jax.ShapeDtypeStruct((rows, width), F32),
            jax.ShapeDtypeStruct((rows, 1), F32),
            jax.ShapeDtypeStruct((rows, width), BF16),
        ],
        scratch_shapes=[pltpu.VMEM((rows, width), BF16)],
        compiler_params=pltpu.CompilerParams(vmem_limit_bytes=VMEM_BYTES),
        cost_estimate=pl.CostEstimate(
            flops=8 * rows * width * width,
            bytes_accessed=4 * width * width,
            transcendentals=0,
        ),
        name="output_projection",
    )(who, attended, *pieces, tokens, gain, bias)


def feed_kernel(parts, who_ref, norm_ref, own_ref, *refs):
    pieces = refs[: 4 * parts]
    (
        near_ref, far_ref, bias_ref, normal_ref, scale_ref, gain_ref, grad_y_ref, out_own, out_mine,
        out_flip, act_ref, resid_ref, resid_b_ref, sent_ref, sums_ref, grad_ref, att_ref,
    ) = refs[4 * parts :]
    side = who_ref[0] % 4
    shard = who_ref[1]
    size, hidden = own_ref.shape
    quarter = hidden // 4
    deep = size // parts
    own_at = pl.multiple_of(shard * size, size)
    other_at = pl.multiple_of((1 - shard) * size, size)
    own_norm = norm_ref[:, pl.ds(own_at, size)]
    part_at = [pl.multiple_of(other_at + p * deep, deep) for p in range(parts)]
    norms = [norm_ref[:, pl.ds(at, deep)] for at in part_at]
    for k in range(4):
        block = side ^ k
        columns = pl.ds(pl.multiple_of(block * quarter, quarter), quarter)
        weight = own_ref[:, columns]
        pre = jnp.dot(own_norm, weight, preferred_element_type=F32)
        for p in range(parts):
            pre = pre + jnp.dot(
                norms[p], pieces[4 * p + k][...], preferred_element_type=F32
            )
        act, slope = gelu_parts(pre + bias_ref[:, columns])
        act_ref[:, columns] = act.astype(BF16)
        within = pl.ds(pl.multiple_of((block % 2) * quarter, quarter), quarter)
        near = near_ref[:, within]
        far = far_ref[:, within].astype(F32)
        grad = jnp.where(block // 2 == shard, near, far) * slope
        sums_ref[pl.ds(3 + block, 1), :] = jnp.sum(grad, axis=0, keepdims=True)
        grad = grad.astype(BF16)
        terms = [(own_at, size, weight)]
        terms += [(part_at[p], deep, pieces[4 * p + k][...]) for p in range(parts)]
        for at, length, piece in terms:
            term = dims(grad, piece, 1, 1)
            if k == 0:
                grad_ref[:, pl.ds(at, length)] = term
            else:
                grad_ref[:, pl.ds(at, length)] += term
    grad = grad_ref[...]
    normal = normal_ref[...]
    grad_y = grad_y_ref[...].astype(F32)
    sums_ref[0:1, :] = jnp.sum(grad * normal, axis=0, keepdims=True)
    sums_ref[1:2, :] = jnp.sum(grad, axis=0, keepdims=True)
    sums_ref[2:3, :] = jnp.sum(grad_y, axis=0, keepdims=True)
    sums_ref[7:8, :] = jnp.zeros((1, quarter), F32)
    resid = grad_y + stats_back(grad * gain_ref[...], normal, scale_ref[...])
    resid_ref[...] = resid
    resid = resid.astype(BF16)
    resid_b_ref[...] = resid
    out_pieces = (out_own, out_mine, out_flip)
    for at, piece in zip(row_starts(who_ref, out_own.shape[0]), out_pieces):
        att_ref[pl.ds(at, piece.shape[0]), :] = dims(piece[...], resid, 1, 1).astype(
            BF16
        )
    devices, head_size, _ = sent_ref.shape
    for d in range(devices):
        at = head_of(d, devices) * head_size
        sent_ref[d] = att_ref[at : at + head_size, :]


def feed(who, norm, own, pieces, near, far, bias, normal, scale, gain, grad_y, out_pieces):
    rows, width = norm.shape
    hidden = own.shape[1]
    vmem = pl.BlockSpec(memory_space=pltpu.VMEM)
    return pl.pallas_call(
        functools.partial(feed_kernel, len(pieces) // 4),
        in_specs=[pl.BlockSpec(memory_space=pltpu.SMEM)] + [vmem] * (12 + len(pieces)),
        out_specs=[vmem] * 5,
        out_shape=[
            jax.ShapeDtypeStruct((rows, hidden), BF16),
            jax.ShapeDtypeStruct((rows, width), F32),
            jax.ShapeDtypeStruct((rows, width), BF16),
            jax.ShapeDtypeStruct((HEADS, width // HEADS, rows), BF16),
            jax.ShapeDtypeStruct((8, width), F32),
        ],
        scratch_shapes=[pltpu.VMEM((rows, width), F32), pltpu.VMEM((width, rows), BF16)],
        compiler_params=pltpu.CompilerParams(vmem_limit_bytes=VMEM_BYTES),
        cost_estimate=pl.CostEstimate(
            flops=16 * rows * width * hidden,
            bytes_accessed=4 * width * hidden,
            transcendentals=2 * rows * hidden,
        ),
        name="feed_forward",
    )(who, norm, own, *pieces, near, far, bias, normal, scale, gain, grad_y, *out_pieces)


def first_back_kernel(
    head_size, who_ref, ends_ref, got_ref, own_ref, mine_0, mine_1, flip_0, flip_1, tokens_ref,
    resid_ref, gains_ref, sums_ref, grad_ref, total_ref, mixed, turned,
):
    heads = got_ref.shape[0]
    rows, width = tokens_ref.shape
    seq_count = ends_ref.shape[0]
    for d in range(heads):
        for k in range(3):
            at = k * width + head_of(d, heads) * head_size
            mixed[at : at + head_size, :] = got_ref[
                d, k * head_size : (k + 1) * head_size, :
            ]
    own_at, mine_at, flip_at = row_starts(who_ref, own_ref.shape[0])
    part = mine_0.shape[0]
    starts = (own_at, mine_at, mine_at + part, flip_at, flip_at + part)
    for at, piece in zip(starts, (own_ref, mine_0, mine_1, flip_0, flip_1)):
        turned[pl.ds(at, piece.shape[0]), :] = jnp.dot(
            piece[...], mixed[...], preferred_element_type=F32
        )
    grad = turned[...].T
    normal, scale = stats(tokens_ref[...].astype(F32))
    index = who_ref[0] * rows + lax.broadcasted_iota(jnp.int32, (rows, 1), 0)
    segment = segments([ends_ref[s] for s in range(seq_count)], index)
    gains = gains_ref[0:1, :]
    for s in range(1, seq_count + 1):
        gains = jnp.where(segment == s, gains_ref[s : s + 1, :], gains)
    grad_ref[...] = (
        resid_ref[...] + stats_back(grad * gains, normal, scale)
    ).astype(BF16)
    total_ref[0:8, :] = sums_ref[...]
    product = grad * normal
    for s in range(seq_count + 1):
        here = segment == s
        for k, terms in enumerate((product, grad)):
            total_ref[8 + 2 * s + k : 9 + 2 * s + k, :] = jnp.sum(
                jnp.where(here, terms, 0.0), axis=0, keepdims=True
            )


def first_back(who, ends, got, pieces, tokens, resid, gains, sums):
    rows, width = tokens.shape
    heads, tall, _ = got.shape
    seq_count = ends.shape[0]
    lines = 8 + 2 * (seq_count + 1)
    vmem = pl.BlockSpec(memory_space=pltpu.VMEM)
    return pl.pallas_call(
        functools.partial(first_back_kernel, tall // 3),
        in_specs=[pl.BlockSpec(memory_space=pltpu.SMEM)] * 2 + [vmem] * 10,
        out_specs=[vmem] * 2,
        out_shape=[
            jax.ShapeDtypeStruct((rows, width), BF16),
            jax.ShapeDtypeStruct((lines, width), F32),
        ],
        scratch_shapes=[
            pltpu.VMEM((3 * width, rows), BF16),
            pltpu.VMEM((width, rows), F32),
        ],
        compiler_params=pltpu.CompilerParams(vmem_limit_bytes=VMEM_BYTES),
        cost_estimate=pl.CostEstimate(
            flops=12 * rows * width * width,
            bytes_accessed=8 * width * width,
            transcendentals=0,
        ),
        name="first_norm_back",
    )(who, ends, got, *pieces, tokens, resid, gains, sums)


def small_kernel(seq_count, chunks, who_ref, own_embed, other_embed, *refs):
    parts = refs[:chunks]
    (
        time_ref, gain_one, bias_one, gain_two, bias_two, bias_up, bias_down, total,
    ) = refs[chunks:]
    lines, width = total.shape
    half = width // 2
    shard = who_ref[1]
    for k in range(width // 128):
        at = k * lines
        value = parts[0][at : at + lines, :].astype(F32)
        for ref in parts[1:]:
            value = value + ref[at : at + lines, :].astype(F32)
        total[:, k * 128 : (k + 1) * 128] = value
    part = pl.ds(pl.multiple_of(shard * half, half), half)
    gain_two[...] = total[0:1, part]
    bias_two[...] = total[1:2, part]
    bias_down[...] = total[2:3, part]
    bias_up[:, :width] = total[pl.ds(3 + 2 * shard, 1), :]
    bias_up[:, width:] = total[pl.ds(4 + 2 * shard, 1), :]
    films = 2 * (seq_count + 1)
    gain = total[8:9, part]
    bias = total[9:10, part]
    for s in range(1, films):
        gain = gain + total[8 + 2 * s : 9 + 2 * s, part]
        bias = bias + total[9 + 2 * s : 10 + 2 * s, part]
    gain_one[...] = gain
    bias_one[...] = bias
    embeds = []
    for embed_ref in (own_embed, other_embed):
        columns = []
        for s in range(seq_count):
            line = embed_ref[s : s + 1, :]
            columns.append(jnp.broadcast_to(line, (8, line.shape[1])).T[:, 0:1])
        embeds.append(columns)
    for k in range(2):
        value = None
        for g, columns in enumerate(embeds):
            for s in range(seq_count):
                line = 8 + g * films + 2 * s + k
                term = columns[s] * total[line : line + 1, :]
                value = term if value is None else value + term
        time_ref[:, k * width : (k + 1) * width] = value


def small_sums(who, own_embed, other_embed, parts, top, lines, width):
    vmem = pl.BlockSpec(memory_space=pltpu.VMEM)
    tall = lines * width // 128
    tail = pl.BlockSpec((tall, 128), lambda i: (top // tall, 0))
    return pl.pallas_call(
        functools.partial(small_kernel, own_embed.shape[0], len(parts)),
        grid=(1,),
        in_specs=[pl.BlockSpec(memory_space=pltpu.SMEM)]
        + [vmem] * 2
        + [tail] * len(parts),
        out_specs=[vmem] * 7,
        out_shape=[jax.ShapeDtypeStruct((own_embed.shape[1], 2 * width), F32)]
        + [jax.ShapeDtypeStruct((1, width // 2), F32)] * 4
        + [
            jax.ShapeDtypeStruct((1, 2 * width), F32),
            jax.ShapeDtypeStruct((1, width // 2), F32),
        ],
        scratch_shapes=[pltpu.VMEM((lines, width), F32)],
        compiler_params=pltpu.CompilerParams(vmem_limit_bytes=VMEM_BYTES),
        cost_estimate=pl.CostEstimate(
            flops=1000000, bytes_accessed=2000000, transcendentals=0
        ),
        name="small_gradients",
    )(who, own_embed, other_embed, *parts)


def stream(chips, copies_of, fill):
    pending = [None, None]
    for at in range(chips):
        slot = at % 2
        if pending[slot] is not None:
            for copy in pending[slot]:
                copy.wait()
        fill(at, slot)
        pending[slot] = copies_of(at, slot)
        for copy in pending[slot]:
            copy.start()
    for copies in pending:
        if copies is not None:
            for copy in copies:
                copy.wait()


def wide_kernel(first, chunks, place_ref, *refs):
    parts = refs[:chunks]
    up_ref, down_ref, out_ref, up_slots, down_slots, out_slots, sems = refs[-7:]
    core = place_ref[0] % 2
    deep = out_slots.shape[1] // 2
    size = up_ref.shape[0]
    hidden = up_ref.shape[1]
    width = down_ref.shape[1]

    def fill(at, slot):
        for j in range(2):
            ref = parts[2 * at + j]
            column = pl.ds(pl.multiple_of((j ^ core) * 128, 128), 128)
            for k in range(2):
                up_slots[slot, k, :, column] = ref[k * size : (k + 1) * size, :].astype(
                    F32
                )
            row = pl.ds(pl.multiple_of((j ^ core) * 128, 128), 128)
            for k in range(width // 128):
                top = 2 * size + k * 128
                down_slots[slot, row, k * 128 : (k + 1) * 128] = ref[
                    top : top + 128, :
                ].astype(F32)
            row = pl.ds(pl.multiple_of((j ^ core) * deep, deep), deep)
            for k in range(width // 128):
                top = 2 * size + width + k * deep
                out_slots[slot, row, k * 128 : (k + 1) * 128] = ref[
                    top : top + deep, :
                ].astype(F32)

    def copies_of(at, slot):
        chip = place_ref[2 * (at + first)] // 2
        copies = []
        for k in range(2):
            column = pl.multiple_of(k * (hidden // 2) + chip * 256, 256)
            copies.append(
                pltpu.make_async_copy(
                    up_slots.at[slot, k],
                    up_ref.at[:, pl.ds(column, 256)],
                    sems.at[slot, k],
                )
            )
        row = pl.multiple_of(chip * 256, 256)
        copies.append(
            pltpu.make_async_copy(
                down_slots.at[slot], down_ref.at[pl.ds(row, 256), :], sems.at[slot, 2]
            )
        )
        row = pl.multiple_of(chip * 2 * deep, 2 * deep)
        copies.append(
            pltpu.make_async_copy(
                out_slots.at[slot], out_ref.at[pl.ds(row, 2 * deep), :], sems.at[slot, 3]
            )
        )
        return copies

    stream(chunks // 2, copies_of, fill)


def expand_wide(place, first, parts, width, earlier):
    devices = place.shape[0]
    size = width // 2
    vmem = pl.BlockSpec(memory_space=pltpu.VMEM)
    hbm = pl.BlockSpec(memory_space=pl.ANY)
    return pl.pallas_call(
        functools.partial(wide_kernel, first, len(parts)),
        in_specs=[pl.BlockSpec(memory_space=pltpu.SMEM)]
        + [vmem] * len(parts)
        + [hbm] * len(earlier),
        out_specs=[hbm, hbm, hbm],
        out_shape=[
            jax.ShapeDtypeStruct((size, 2 * devices * 128), F32),
            jax.ShapeDtypeStruct((devices * 128, width), F32),
            jax.ShapeDtypeStruct((size, width), F32),
        ],
        scratch_shapes=[
            pltpu.VMEM((2, 2, size, 256), F32),
            pltpu.VMEM((2, 256, width), F32),
            pltpu.VMEM((2, 2 * size // devices, width), F32),
            pltpu.SemaphoreType.DMA((2, 4)),
        ],
        input_output_aliases={1 + len(parts) + k: k for k in range(len(earlier))},
        compiler_params=pltpu.CompilerParams(vmem_limit_bytes=VMEM_BYTES),
        cost_estimate=pl.CostEstimate(
            flops=parts[0].size * len(parts),
            bytes_accessed=6 * parts[0].size * len(parts),
            transcendentals=0,
        ),
        name="expand_wide",
    )(place, *parts, *earlier)


def last_kernel(head_size, in_ref, out_ref):
    pairs = []
    for j in range(2):
        for k in range(in_ref.shape[0] // 4):
            pairs.append((in_ref[4 * k + j], in_ref[4 * k + 2 + j]))
    for at, (first, second) in enumerate(pairs):
        both = jnp.concatenate([first, second], axis=0).astype(F32)
        out_ref[:, at * 2 * head_size : (at + 1) * 2 * head_size] = both.T


def expand_last(parts, head_size):
    devices, tall, depth = parts.shape
    width = devices * head_size
    return pl.pallas_call(
        functools.partial(last_kernel, head_size),
        grid=(3,),
        in_specs=[pl.BlockSpec((devices, head_size, depth), lambda k: (0, k, 0))],
        out_specs=pl.BlockSpec((depth, width), lambda k: (0, k)),
        out_shape=jax.ShapeDtypeStruct((depth, 3 * width), F32),
        compiler_params=pltpu.CompilerParams(vmem_limit_bytes=VMEM_BYTES),
        cost_estimate=pl.CostEstimate(
            flops=parts.size, bytes_accessed=6 * parts.size, transcendentals=0
        ),
        name="expand_last",
    )(parts)


def times_rows(values, pieces):
    return sum(
        jnp.dot(
            lax.dynamic_slice_in_dim(values, at, piece.shape[0], 1),
            piece,
            preferred_element_type=F32,
        )
        for piece, at in pieces
    )


def times_rows_t(values_t, pieces):
    return sum(
        dims(lax.dynamic_slice_in_dim(values_t, at, piece.shape[0], 0), piece, 0, 0)
        for piece, at in pieces
    )


def joined(parts, pieces, dim):
    if len(parts) == 1:
        return parts[0]
    shape = list(parts[0].shape)
    shape[dim] = sum(part.shape[dim] for part in parts)
    out = jnp.zeros(shape, parts[0].dtype)
    for part, (_, at) in zip(parts, pieces):
        out = lax.dynamic_update_slice_in_dim(out, part, at, dim)
    return out


def rows_of(pieces, start, size):
    out = None
    for piece, at in pieces:
        length = piece.shape[0]
        local = jnp.clip(start - at, 0, length - size)
        found = lax.dynamic_slice_in_dim(piece, local, size, 0)
        inside = (start >= at) & (start < at + length)
        out = found if out is None else jnp.where(inside, found, out)
    return out


def body_general(
    ctx_size, fsdp_size,
    tokens, w_qkv, w_out, w_up, w_down, w_time, gain_one, bias_one, gain_two, bias_two, bias_up,
    bias_down, lengths, time_steps, cotangent,
):
    me = lax.axis_index("ctx")
    shard = lax.axis_index("fsdp")
    rows = tokens.shape[1]
    width = tokens.shape[2]
    count = rows * ctx_size
    head_size = width // HEADS
    repeats = ctx_size // HEADS
    columns = head_size // repeats
    seq_count = lengths.shape[1]
    hidden = w_up.shape[1]

    def gather_small(values):
        return lax.all_gather(values, "fsdp", axis=0, tiled=True)

    def fetch(weight):
        return [(gather_small(weight), 0)]

    def scatter_sum(values, dim):
        return lax.psum_scatter(
            values.astype(BF16), "fsdp", scatter_dimension=dim, tiled=True
        )

    def gather(values):
        return lax.all_gather(values, "ctx", axis=0, tiled=False)

    ends = []
    for s in range(seq_count):
        ends.append(lengths[0, s] + (ends[-1] if ends else 0))
    ends_vector = jnp.stack(ends)
    index = me * rows + jnp.arange(rows, dtype=jnp.int32)
    segment = segments(ends, index)
    live = (segment < seq_count).astype(F32)[:, None]
    all_index = jnp.arange(count, dtype=jnp.int32)
    all_position = positions(ends, all_index, segments(ends, all_index))
    half_width = head_size // 2
    inverse = jnp.exp(
        -math.log(10000.0) * jnp.arange(half_width, dtype=F32) / half_width
    )
    angle = inverse[:, None] * all_position.astype(F32)[None, :]
    cos = jnp.cos(angle)
    sin = jnp.sin(angle)

    all_tokens = gather(tokens[0]).reshape(count, width)
    inputs = tokens[0].astype(F32)
    grad_y = cotangent[0].astype(F32) * live
    grad_y_b = grad_y.astype(BF16)
    all_grad_y = gather(grad_y_b).reshape(count, width)

    small = [gain_one, bias_one, gain_two, bias_two, bias_down, bias_up]
    packed = gather_small(jnp.concatenate(small)[None, :])
    vectors = []
    at = 0
    for vector in small:
        size = vector.shape[0]
        vectors.append(packed[:, at : at + size].reshape(1, -1).astype(F32))
        at += size
    gain_first, bias_first, gain_second, bias_second, bias_output, bias_hidden = vectors

    all_steps = lax.all_gather(time_steps.astype(F32), "fsdp", axis=0, tiled=True)
    all_embedded = embed(all_steps, w_time.shape[0] * fsdp_size).astype(BF16)
    embedded = lax.dynamic_index_in_dim(all_embedded, shard, 0, keepdims=False)
    film = times_rows(embedded, fetch(w_time))
    film = jnp.concatenate([film, jnp.zeros((1, 2 * width), F32)], axis=0)
    gains = gain_first + film[:, :width]
    shifts = bias_first + film[:, width:]

    head = me // repeats
    w_head = jnp.concatenate(
        [
            lax.dynamic_slice_in_dim(w_qkv, k * width + head * head_size, head_size, 1)
            for k in range(3)
        ]
        + [jnp.zeros((w_qkv.shape[0], head_size), BF16)],
        axis=1,
    )
    w_head = gather_small(w_head)

    base = jnp.arange(ctx_size, dtype=jnp.int32) * rows
    all_norm, query_t, key, key_t, value_t, pair = project(
        all_tokens, base, ends_vector, gains, shifts, w_head, cos, sin, rows, head_size
    )
    place = jnp.arange(ctx_size, dtype=jnp.int32)
    out_t, sent, lse = attend(place, query_t, key, value_t, rows)

    part = (me % repeats) * columns
    if repeats > 1:
        sent = lax.dynamic_slice_in_dim(sent, part, columns, 1)
    attended_t = lax.all_to_all(sent, "ctx", 0, 0, tiled=True).reshape(width, rows)

    out_pieces = fetch(w_out)
    up_pieces = fetch(w_up)
    down_pieces = fetch(w_down)
    qkv_pieces = fetch(w_qkv)
    resid = inputs + times_rows_t(attended_t, out_pieces)
    normal_two, scale_two = stats(resid)
    norm_two_b = (normal_two * gain_second + bias_second).astype(BF16)
    all_norm_two = gather(norm_two_b).reshape(count, width)
    pre = times_rows(norm_two_b, up_pieces) + bias_hidden
    act, slope = gelu_parts(pre)
    branch = times_rows(act.astype(BF16), down_pieces) + bias_output
    output = (live * (resid + branch)).astype(BF16)
    grad_act = joined([dims(grad_y_b, p, 1, 1) for p, _ in down_pieces], down_pieces, 1)
    grad_pre = grad_act * slope
    grad_bias_up = jnp.sum(grad_pre, axis=0)
    grad_pre_b = grad_pre.astype(BF16)
    grad_norm_two = joined([dims(grad_pre_b, p, 1, 1) for p, _ in up_pieces], up_pieces, 1)
    grad_resid = grad_y + stats_back(grad_norm_two * gain_second, normal_two, scale_two)
    grad_resid_b = grad_resid.astype(BF16)
    grad_att_t = joined(
        [dims(p, grad_resid_b, 1, 1) for p, _ in out_pieces], out_pieces, 0
    ).astype(BF16)
    grad_att_t = grad_att_t.reshape(HEADS, head_size, rows)
    if repeats > 1:
        grad_att_t = jnp.repeat(grad_att_t, repeats, axis=0)
    grad_att = lax.all_to_all(grad_att_t, "ctx", 0, 0, tiled=True)

    mixed_t, _ = attend_back(
        place, query_t, grad_att, out_t, lse, key, key_t, pair, cos, sin, rows
    )
    mixed_t = mixed_t.reshape(3, head_size, count)
    if repeats > 1:
        mixed_t = lax.dynamic_slice_in_dim(mixed_t, part, columns, 1)
    mixed_t = mixed_t.reshape(3 * columns, count)
    mixed_sent = mixed_t.reshape(3 * columns, ctx_size, rows).transpose(1, 0, 2)
    mixed_got = lax.all_to_all(mixed_sent, "ctx", 0, 0, tiled=True)
    grad_mixed_t = (
        mixed_got.reshape(ctx_size, 3, columns, rows)
        .transpose(1, 0, 2, 3)
        .reshape(3 * width, rows)
    )
    grad_norm_one = joined(
        [dims(grad_mixed_t, p, 0, 1) for p, _ in qkv_pieces], qkv_pieces, 1
    )
    normal_one, scale_one = stats(inputs)
    seg_col = segment[:, None]
    gain_tok = gains[0:1]
    for s in range(1, seq_count + 1):
        gain_tok = jnp.where(seg_col == s, gains[s : s + 1], gain_tok)
    grad_tokens = (
        grad_resid + stats_back(grad_norm_one * gain_tok, normal_one, scale_one)
    ).astype(BF16)
    film_terms = jnp.concatenate([grad_norm_one * normal_one, grad_norm_one], axis=1)
    film_sums = [
        jnp.sum(jnp.where(seg_col == s, film_terms, 0.0), axis=0)
        for s in range(seq_count + 1)
    ]

    sums = [
        jnp.sum(grad_norm_two * normal_two, axis=0),
        jnp.sum(grad_norm_two, axis=0),
        jnp.sum(grad_y, axis=0),
        grad_bias_up,
    ] + film_sums
    sizes = [vector.shape[0] for vector in sums]
    total = lax.psum(jnp.concatenate(sums)[None, :], "ctx")
    total = lax.all_gather(total, "fsdp", axis=0, tiled=True)
    split = []
    at = 0
    for size in sizes:
        split.append(total[:, at : at + size])
        at += size

    def own(vector):
        size = vector.shape[0] // fsdp_size
        return lax.dynamic_slice_in_dim(vector, shard * size, size, 0)

    sum_gain_two, sum_bias_two, sum_bias_down, sum_bias_up = (
        own(jnp.sum(vector, axis=0)) for vector in split[:4]
    )
    film_all = jnp.sum(sum(split[4:]), axis=0)
    sum_gain_one = own(film_all[:width])
    sum_bias_one = own(film_all[width:])
    film_grad = jnp.stack(split[4 : 4 + seq_count], axis=1).reshape(-1, 2 * width)
    embedded_rows = lax.dynamic_slice_in_dim(
        all_embedded.astype(F32).reshape(film_grad.shape[0], -1),
        shard * w_time.shape[0],
        w_time.shape[0],
        1,
    )
    grad_time = sum(
        embedded_rows[g][:, None] * film_grad[g][None, :]
        for g in range(film_grad.shape[0])
    )

    slice_width = hidden // (ctx_size * fsdp_size)
    starts = [
        k * (hidden // fsdp_size) + me * slice_width for k in range(fsdp_size)
    ]
    w_up_cols = []
    for piece, _ in up_pieces:
        w_up_cols.append(
            jnp.concatenate(
                [
                    lax.dynamic_slice_in_dim(piece, start, slice_width, 1)
                    for start in starts
                ],
                axis=1,
            )
        )
    w_up_slice = joined(w_up_cols, up_pieces, 0)
    w_down_slice = jnp.concatenate(
        [rows_of(down_pieces, start, slice_width) for start in starts], axis=0
    )
    bias_slice = jnp.concatenate(
        [
            lax.dynamic_slice_in_dim(bias_hidden, start, slice_width, 1)
            for start in starts
        ],
        axis=1,
    )
    pre_slice = dims(all_norm_two, w_up_slice, 1, 0) + bias_slice
    act_slice, slope_slice = gelu_parts(pre_slice)
    grad_pre_slice = (dims(all_grad_y, w_down_slice, 1, 1) * slope_slice).astype(BF16)
    down_slice = dims(act_slice.astype(BF16), all_grad_y, 0, 0)
    up_slice = dims(all_norm_two, grad_pre_slice, 0, 0)
    grad_down = gather(scatter_sum(down_slice, 0)).reshape(-1, width).astype(F32)
    up_parts = gather(scatter_sum(up_slice, 0))
    grad_up = (
        up_parts.reshape(ctx_size, width // fsdp_size, fsdp_size, slice_width)
        .transpose(1, 2, 0, 3)
        .reshape(width // fsdp_size, hidden)
        .astype(F32)
    )
    out_part = jnp.dot(attended_t, grad_resid_b, preferred_element_type=F32)
    out_rows = lax.psum_scatter(
        out_part.astype(BF16), ("fsdp", "ctx"), scatter_dimension=0, tiled=True
    )
    grad_out = gather(out_rows).reshape(-1, width).astype(F32)
    qkv_slice = jnp.dot(mixed_t, all_norm, preferred_element_type=F32)
    qkv_parts = gather(scatter_sum(qkv_slice, 1))
    grad_qkv = (
        qkv_parts.reshape(ctx_size, 3, columns, width // fsdp_size)
        .transpose(3, 1, 0, 2)
        .reshape(width // fsdp_size, 3 * width)
        .astype(F32)
    )
    return (
        output[None],
        grad_tokens[None],
        grad_qkv,
        grad_out,
        grad_up,
        grad_down,
        grad_time,
        sum_gain_one,
        sum_bias_one,
        sum_gain_two,
        sum_bias_two,
        sum_bias_up,
        sum_bias_down,
    )


def ring_tables(ctx_size):
    chips = ctx_size // 2
    order = list(range(0, chips, 2)) + list(range(1, chips, 2))[::-1]
    offsets = [0]
    for step in range(1, chips // 2 + 1):
        offsets.append(-step)
        if step <= (chips - 1) // 2:
            offsets.append(step)
    place = np.zeros((ctx_size, ctx_size), np.int32)
    for me in range(ctx_size):
        at = order.index(me // 2)
        for k, offset in enumerate(offsets):
            chip = order[(at + offset) % chips]
            place[me, 2 * k] = 2 * chip + me % 2
            place[me, 2 * k + 1] = 2 * chip + 1 - me % 2
    return order, place


def fence(*values):
    return lax.optimization_barrier(values)


def after(values, *earlier):
    return lax.optimization_barrier((values, *earlier))[0]


def body(
    ctx_size, fsdp_size,
    tokens, w_qkv, w_out, w_up, w_down, w_time, gain_one, bias_one, gain_two, bias_two, bias_up,
    bias_down, lengths, time_steps, cotangent,
):
    me = lax.axis_index("ctx")
    shard = lax.axis_index("fsdp")
    core = me % 2
    rows = tokens.shape[1]
    width = tokens.shape[2]
    head_size = width // HEADS
    seq_count = lengths.shape[1]
    hidden = w_up.shape[1]
    other = 1 - shard
    chips = ctx_size // 2
    half = width // 2
    units = hidden // (ctx_size * fsdp_size)
    order, place_table = ring_tables(ctx_size)
    place = jnp.asarray(place_table)[me]
    who = jnp.stack([me, shard]).astype(jnp.int32)

    def across(values):
        return lax.ppermute(values, "fsdp", [(0, 1), (1, 0)])

    def gather(values):
        return lax.all_gather(values, "ctx", axis=0, tiled=True)

    def flip(values, bit=0):
        return lax.ppermute(
            values, "ctx", [(i, i ^ (1 << bit)) for i in range(ctx_size)]
        )

    def hop(values, step):
        return lax.ppermute(
            values,
            "ctx",
            [
                (2 * order[at] + c, 2 * order[(at + step) % chips] + c)
                for at in range(chips)
                for c in range(2)
            ],
        )

    def by_shard(mine, others, axis):
        first = jnp.where(shard == 0, mine, others)
        second = jnp.where(shard == 0, others, mine)
        return jnp.concatenate([first, second], axis=axis)

    def cut(values, start, size, axis):
        return lax.dynamic_slice_in_dim(values, start, size, axis)

    def halve(values, axis, mine, send):
        keep = lax.dynamic_index_in_dim(values, mine, axis, keepdims=False)
        give = lax.dynamic_index_in_dim(values, 1 - mine, axis, keepdims=False)
        return keep + send(give.astype(BF16)).astype(F32)

    ends = []
    for s in range(seq_count):
        ends.append(lengths[0, s] + (ends[-1] if ends else 0))
    ends_vector = jnp.stack(ends)
    base = place * rows
    index = me * rows + jnp.arange(rows, dtype=jnp.int32)
    segment = segments(ends, index)
    seg_col = segment[:, None]
    live = (segment < seq_count).astype(F32)[:, None]
    own_tokens = tokens[0]
    steps_row = time_steps.reshape(1, seq_count)
    high = (steps_row // 256).astype(BF16)
    low = (steps_row % 256).astype(BF16)
    head = core * chips + me // 2
    w_head = jnp.concatenate(
        [cut(w_qkv, k * width + head * head_size, head_size, 1) for k in range(3)], axis=1
    )
    class Ring:
        def __init__(self, values):
            self.right = self.left = values
            self.parts = [values]
            self.step = 0

        def go(self, *earlier):
            right, left = self.right, self.left
            if earlier:
                right, left = (
                    after(right, *earlier),
                    after(left, *earlier),
                )
            self.step += 1
            self.right = hop(right, 1)
            if self.step <= (chips - 1) // 2:
                self.left = hop(left, -1)
                return [self.right, self.left]
            return [self.right]

        def came(self, values):
            self.right = values[0]
            if len(values) > 1:
                self.left = values[1]
            self.parts += values

    def fenced(groups):
        flat = [v for group in groups for v in group]
        flat = list(fence(*flat))
        out = []
        for group in groups:
            out.append(flat[: len(group)])
            flat = flat[len(group) :]
        return out

    def with_flips(values):
        return [part for v in values for part in (v, flip(v))]

    tok = Ring(own_tokens)
    tok_new = tok.go()
    packed = jnp.concatenate([gain_one[None, :], bias_one[None, :], high, low], axis=1)
    tok_new, (packed, w_head) = fenced([tok_new, [packed, w_head]])
    tok.came(tok_new)

    tok_new = tok.go()
    packed_other = across(packed)
    w_head_other = across(w_head)
    me_1 = after(me, packed)
    place = jnp.asarray(place_table)[me_1]
    who = jnp.stack([me_1, shard]).astype(jnp.int32)
    base = place * rows
    all_index = (base[:, None] + jnp.arange(rows, dtype=jnp.int32)[None, :]).reshape(-1)
    all_position = positions(ends, all_index, segments(ends, all_index))
    half_width = head_size // 2
    inverse = jnp.exp(
        -math.log(10000.0) * jnp.arange(half_width, dtype=F32) / half_width
    )
    angle = inverse[:, None] * all_position.astype(F32)[None, :]
    cos = jnp.cos(angle)
    sin = jnp.sin(angle)

    inputs = own_tokens.astype(F32)
    grad_y = cotangent[0].astype(F32) * live
    grad_y_b = grad_y.astype(BF16)
    out_half = w_out.shape[0] // 2
    tok_new, (packed_other, w_head, cos, sin, grad_y_b, me_2, place, who, base, w_head_other) = fenced(
        [tok_new, [packed_other, w_head, cos, sin, grad_y_b, me, place, who, base, w_head_other]]
    )
    tok.came(tok_new)

    tok_new = tok.go()
    packed_all = by_shard(packed, packed_other, 0)

    def vector_of(values, at, size):
        return values[:, at : at + size].reshape(1, -1).astype(F32)

    gain_first = vector_of(packed_all, 0, half)
    bias_first = vector_of(packed_all, half, half)
    all_steps = packed_all[:, width : width + seq_count].astype(F32) * 256.0 + packed_all[
        :, width + seq_count :
    ].astype(F32)
    all_embedded = embed(all_steps, w_time.shape[0] * fsdp_size).astype(BF16)
    own_part = cut(all_embedded, shard * w_time.shape[0], w_time.shape[0], 2)
    film_part = jnp.dot(
        own_part.reshape(fsdp_size * seq_count, -1), w_time, preferred_element_type=F32
    ).reshape(fsdp_size, seq_count, 2 * width)
    film_other = across(lax.dynamic_index_in_dim(film_part, other, 0, keepdims=False))
    film = film_other + lax.dynamic_index_in_dim(film_part, shard, 0, keepdims=False)
    film = jnp.concatenate([film, jnp.zeros((1, 2 * width), F32)], axis=0)
    gains = gain_first + film[:, :width]
    shifts = bias_first + film[:, width:]
    up_parts = 2
    up_deep = w_up.shape[0] // up_parts
    quarter = hidden // 4
    up_send = [
        lax.dynamic_slice(w_up, (p * up_deep, (me_2 % 4) * quarter), (up_deep, quarter))
        for p in range(up_parts)
    ]
    tok_new, (gains, shifts), up_send = fenced([tok_new, [gains, shifts], up_send])
    tok_flips = with_flips(tok.parts)
    tok.came(tok_new)

    tok_last = tok.go()
    all_grad_y = gather(after(grad_y_b, gains))
    grad_y_other = across(grad_y_b)
    up_mine = [across(after(up_send[0], gains))]
    tok_flips += with_flips(tok_new)
    constants = (base, ends_vector, gains, shifts, w_head, w_head_other, cos, sin, head_size)
    head_values = project_chunks(who, tok_flips, *constants)
    head_values, tok_last, (grad_y_other, gain_two, up_send[1]) = fenced(
        [head_values, tok_last, [grad_y_other, gain_two, up_send[1]]]
    )

    up_mine.append(across(up_send[1]))
    far_send = dims(grad_y_other, w_down, 1, 1).astype(BF16)
    all_norm, query_t, key, key_t, value_t, pair = project_chunks(
        who, with_flips(tok_last), *constants, first=chips - 1, earlier=head_values
    )
    out_t, sent, lse = attend(place, query_t, key, value_t, rows)
    rest = jnp.concatenate(
        [v[None, :] for v in (gain_two, bias_two, bias_down, bias_up)], axis=1
    )
    out_t, sent, lse, *up_mine, rest, me_5, far_send = fence(
        out_t, sent, lse, *up_mine, rest, me, far_send
    )

    attended = lax.all_to_all(sent, "ctx", 0, 0, tiled=True)
    rest_other = across(rest)
    up_side = [flip(up_mine[0], 1), flip(up_mine[1], 1)]
    qkv_half = w_qkv.shape[0] // 2
    qkv_send = [
        cut(w_qkv, (me_5 % 2) * qkv_half + k * (qkv_half // 2), qkv_half // 2, 0)
        for k in range(2)
    ]
    out_mine = across(cut(w_out, (me_5 % 2) * out_half, out_half, 0))
    far_grad = across(far_send)
    near_grad = dims(after(grad_y_b, lse), w_down, 1, 1)
    pieces = [with_flips([v]) for v in up_mine]
    rest_5 = [out_mine, rest_other, me_5, qkv_send[1], qkv_send[0]]
    (attended, up_side[0], near_grad), rest_5, *pieces = fenced(
        [[attended, up_side[0], near_grad], rest_5, *pieces]
    )
    out_mine, rest_other, me_6, qkv_send[1], qkv_send[0] = rest_5

    rest = by_shard(rest, rest_other, 0)
    gain_second = vector_of(rest, 0, half)
    bias_second = vector_of(rest, half, half)
    bias_output = vector_of(rest, width, half)
    bias_hidden = vector_of(rest, width + half, hidden // 2)
    out_pieces = (w_out, out_mine, flip(out_mine))
    resid, normal_two, scale_two, norm_two_b = middle(
        who, attended, out_pieces, own_tokens, gain_second, bias_second
    )
    first_units = shard * (hidden // 2) + me_6 * units
    second_units = other * (hidden // 2) + me_6 * units
    up_first = cut(w_up, first_units, units, 1)
    up_second = cut(w_up, second_units, units, 1)
    up_own = jnp.concatenate([up_first, up_second], axis=1)
    down_own = cut(w_down, me_6 * units, units, 0)
    up_give = jnp.concatenate([up_second, up_first], axis=1)
    pieces[0] = pieces[0] + with_flips([up_side[0]])
    rest_6 = [up_own, up_give, down_own]
    (norm_two_b, far_grad, up_side[1]), rest_6, *pieces = fenced(
        [[norm_two_b, far_grad, up_side[1]], rest_6, *pieces]
    )
    up_own, up_give, down_own = rest_6
    pieces = pieces[0] + pieces[1] + with_flips([up_side[1]])

    all_norm_two = gather(norm_two_b)
    up_other = across(after(up_give, norm_two_b))
    down_other = across(after(down_own, norm_two_b))
    act_b, grad_resid, grad_resid_b, grad_att, sums = feed(
        who, norm_two_b, w_up, pieces, near_grad, far_grad, bias_hidden, normal_two, scale_two,
        gain_second, grad_y_b, out_pieces,
    )
    grad_att, grad_resid_b, me_8, up_other, down_other = fence(
        grad_att, grad_resid_b, me, up_other, down_other
    )

    grad_att = grad_att.reshape(HEADS, head_size, rows)
    grad_att = lax.all_to_all(grad_att, "ctx", 0, 0, tiled=True)
    qkv_mine = [across(after(qkv_send[0], up_other, down_other))]
    deep = width // (ctx_size * fsdp_size)
    by_core = attended.reshape(chips, fsdp_size, 2, deep, rows)

    def out_rows_of(which):
        some = lax.dynamic_index_in_dim(by_core, which, 2, keepdims=False)
        return jnp.dot(
            some.reshape(half, rows), grad_resid_b, preferred_element_type=F32
        )

    out_part = out_rows_of(core) + flip(out_rows_of(1 - core).astype(BF16)).astype(F32)
    out_part = out_part.reshape(chips, fsdp_size, deep, width)
    down_half = w_down.shape[0] // 2
    down_send = cut(w_down, (me_8 % 2) * down_half, down_half, 0)
    grad_att, down_send, out_part = fence(grad_att, down_send, out_part)

    out_part = halve(out_part, 1, shard, across)
    qkv_mine.append(across(after(qkv_send[1], out_part)))
    mixed, mixed_sent = attend_back(
        place, query_t, grad_att, out_t, lse, key, key_t, pair, cos, sin, rows
    )
    mixed, mixed_sent, out_part, qkv_mine[0] = fence(
        mixed, mixed_sent, out_part, qkv_mine[0]
    )

    mixed_got = lax.all_to_all(mixed_sent, "ctx", 0, 0, tiled=True)
    qkv_slice = jnp.dot(mixed, all_norm, preferred_element_type=F32)
    qkv_keep = cut(qkv_slice, shard * half, half, 1)
    qkv_give = cut(qkv_slice, other * half, half, 1).astype(BF16)
    bias_slice = jnp.concatenate(
        [cut(bias_hidden, at, units, 1) for at in (first_units, second_units)], axis=1
    )
    qkv_other = across(qkv_give)
    out_part = halve(
        out_part.reshape(-1, 2, deep, width), 1, (me >> 1) % 2, lambda v: flip(v, 1)
    )
    qkv_sum = (qkv_keep + qkv_other.astype(F32)).astype(BF16)
    qkv_sum, bias_slice, all_norm_two, all_grad_y, out_part = fence(
        qkv_sum, bias_slice, all_norm_two, all_grad_y, out_part
    )

    all_qkv = gather(qkv_sum)
    out_part = halve(
        out_part.reshape(-1, 2, deep, width), 1, (me >> 2) % 2, lambda v: flip(v, 2)
    )
    wide_keep, wide_give = slices(
        who, all_norm_two, all_grad_y, up_own, up_other, down_own, down_other, bias_slice
    )
    wide_keep, wide_give, mixed_got, out_part = fence(
        wide_keep, wide_give, mixed_got, out_part
    )

    wide_other = across(wide_give)
    qkv_mine = fence(*qkv_mine, wide_give)[:-1]
    qkv_pieces = (w_qkv, *qkv_mine, *[flip(v) for v in qkv_mine])
    grad_tokens, total = first_back(
        who, ends_vector, mixed_got, qkv_pieces, own_tokens, grad_resid, gains, sums
    )
    total_other = across(total)
    out_part = halve(
        out_part.reshape(-1, 2, deep, width), 1, (me >> 3) % 2, lambda v: flip(v, 3)
    )
    wide_other, total, total_other, out_part = fence(
        wide_other, total, total_other, out_part
    )

    total = jnp.concatenate(
        [total[:8] + total_other[:8], total[8:], total_other[8:]], axis=0
    )
    total = jnp.pad(total, ((0, -total.shape[0] % 16), (0, 0))).astype(BF16)
    lines = total.shape[0]

    def narrow(values):
        return [values[:, k * 128 : (k + 1) * 128] for k in range(width // 128)]

    wide = jnp.concatenate(
        [(wide_keep + wide_other.astype(F32)).astype(BF16)]
        + narrow(out_part.reshape(deep, width).astype(BF16))
        + narrow(total),
        axis=0,
    )
    wide_ring = Ring(wide)
    wide_new = wide_ring.go()
    down_mine = across(after(down_send, wide))
    wide_new = list(fence(*wide_new))
    wide_flips = with_flips(wide_ring.parts)
    wide_ring.came(wide_new)

    wide_flips += with_flips(wide_new)
    wide_new = wide_ring.go()
    grads = expand_wide(place, 0, wide_flips, width, ())
    own_embed = lax.dynamic_index_in_dim(own_part, shard, 0, keepdims=False)
    other_embed = lax.dynamic_index_in_dim(own_part, other, 0, keepdims=False)
    own_embed = own_embed.astype(F32)
    other_embed = other_embed.astype(F32)
    wide_new, grads, (down_mine, own_embed, other_embed, all_qkv) = fenced(
        [wide_new, grads, [down_mine, own_embed, other_embed, all_qkv]]
    )
    wide_ring.came(wide_new)

    more_flips = with_flips(wide_new)
    wide_new = wide_ring.go()
    grad_qkv = expand_last(all_qkv.reshape(ctx_size, 3 * head_size, half), head_size)
    down_flip = flip(down_mine)
    branch = bias_output
    for b, row in (
        (w_down, shard * (hidden // 2)),
        (down_mine, other * (hidden // 2) + core * down_half),
        (down_flip, other * (hidden // 2) + (1 - core) * down_half),
    ):
        branch = branch + jnp.dot(
            cut(act_b, row, b.shape[0], 1), b, preferred_element_type=F32
        )
    output = (live * (resid + branch)).astype(BF16)
    wide_new, (output, grad_qkv), more_flips = fenced(
        [wide_new, [output, grad_qkv], more_flips]
    )

    tall = wide.shape[0] // 2
    last_top = hop(wide_new[0][:tall], 1)
    last_low = hop(wide_new[1][tall:], -1)
    more_flips += with_flips(wide_new)
    grads = expand_wide(place, len(wide_flips) // 2, more_flips, width, grads)
    grads, (last_top, last_low) = fenced([grads, [last_top, last_low]])

    wide_last = with_flips([jnp.concatenate([last_top, last_low], axis=0)])
    grad_up, grad_down, grad_out = expand_wide(
        place, chips - 1, wide_last, width, grads
    )
    grad_time, *vectors = small_sums(
        who, own_embed, other_embed, wide_flips + more_flips + wide_last,
        wide.shape[0] - lines * width // 128, lines, width,
    )
    return (
        output[None],
        grad_tokens[None],
        grad_qkv,
        grad_out,
        grad_up,
        grad_down,
        grad_time,
        *[vector.reshape(-1) for vector in vectors],
    )


def solution(mesh):
    in_specs = (
        (P("fsdp", "ctx", None),)
        + (P("fsdp", None),) * 5
        + (P("fsdp"),) * 6
        + (P("fsdp", None), P("fsdp", None), P("fsdp", "ctx", None))
    )
    out_specs = (
        (P("fsdp", "ctx", None),) * 2 + (P("fsdp", None),) * 5 + (P("fsdp"),) * 6
    )
    ctx_size, fsdp_size = mesh.shape["ctx"], mesh.shape["fsdp"]
    paired = ctx_size == HEADS and fsdp_size == 2
    return jax.shard_map(
        functools.partial(body if paired else body_general, ctx_size, fsdp_size),
        mesh=mesh,
        in_specs=in_specs,
        out_specs=out_specs,
        check_vma=False,
    )
```
